32 devices in a mesh: dp: 16 (over z, y, x), tensor: 2 (over core).
Axes of the slice: x: 2, y: 2, z: 4, core: 2. Of those that a mesh axis runs over, the one named last changes fastest.
Arguments:
- tokens: bfloat16 [16, 1024, 640], P('dp'), may hold values from -6 to 6
- document_numbers: int32 [16, 1024], P('dp'), may hold values from 0 to 3, never falling along the last dimension, each value on 1 to 800 neighbouring positions
- input_norm_gain: float32 [640], replicated, may hold values from 0.1 to 1.9
- after_attention_gain: float32 [640], replicated, may hold values from 0.1 to 1.9
- before_feedforward_gain: float32 [640], replicated, may hold values from 0.1 to 1.9
- after_feedforward_gain: float32 [640], replicated, may hold values from 0.1 to 1.9
- query_norm_gain: float32 [256], replicated, may hold values from 0.1 to 1.9
- key_norm_gain: float32 [256], replicated, may hold values from 0.1 to 1.9
- query_weight: bfloat16 [640, 1024], P(None, 'tensor'), may hold values from -0.25 to 0.25
- keyvalue_weight: bfloat16 [640, 512], replicated, may hold values from -0.25 to 0.25
- output_weight: bfloat16 [1024, 640], P('tensor'), may hold values from -0.1875 to 0.1875
- gateup_weight: bfloat16 [2, 640, 2048], P(None, None, 'tensor'), may hold values from -0.25 to 0.25
- down_weight: bfloat16 [2048, 640], P('tensor'), may hold values from -0.125 to 0.125
- query_adapter_first: bfloat16 [640, 256], replicated, may hold values from -0.25 to 0.25
- query_adapter_second: bfloat16 [256, 1024], replicated, may hold values from -0.1875 to 0.1875
- keyvalue_adapter_first: bfloat16 [640, 512], replicated, may hold values from -0.25 to 0.25
- keyvalue_adapter_second: bfloat16 [2, 256, 256], replicated, may hold values from -0.1875 to 0.1875
- output_adapter_first: bfloat16 [1024, 256], replicated, may hold values from -0.1875 to 0.1875
- output_adapter_second: bfloat16 [256, 640], replicated, may hold values from -0.1875 to 0.1875
- gateup_adapter_first: bfloat16 [640, 512], replicated, may hold values from -0.25 to 0.25
- gateup_adapter_second: bfloat16 [2, 256, 2048], replicated, may hold values from -0.1875 to 0.1875
- down_adapter_first: bfloat16 [2048, 256], replicated, may hold values from -0.125 to 0.125
- down_adapter_second: bfloat16 [256, 640], replicated, may hold values from -0.1875 to 0.1875
- cotangent: bfloat16 [16, 1024, 640], P('dp'), may hold values from -6 to 6
Outputs:
- out: bfloat16 [16, 1024, 640], P('dp')
- gradient_token_input: float32 [16, 1024, 640], P('dp')
- gradient_input_gain: float32 [640], replicated
- gradient_after_attention: float32 [640], replicated
- gradient_before_feedforward: float32 [640], replicated
- gradient_after_feedforward: float32 [640], replicated
- gradient_query_norm_gain: float32 [256], replicated
- gradient_key_norm_gain: float32 [256], replicated
- gradient_query_weight: float32 [640, 1024], P(None, 'tensor')
- gradient_keyvalue_weight: float32 [640, 512], replicated
- gradient_output_weight: float32 [1024, 640], P('tensor')
- gradient_gateup_weight: float32 [2, 640, 2048], P(None, None, 'tensor')
- gradient_down_weight: float32 [2048, 640], P('tensor')
- gradient_query_adapter_first: float32 [640, 256], replicated
- gradient_query_adapter_second: float32 [256, 1024], replicated
- gradient_keyvalue_adapter_first: float32 [640, 512], replicated
- gradient_keyvalue_adapter_second: float32 [2, 256, 256], replicated
- gradient_output_adapter_first: float32 [1024, 256], replicated
- gradient_output_adapter_second: float32 [256, 640], replicated
- gradient_gateup_adapter_first: float32 [640, 512], replicated
- gradient_gateup_adapter_second: float32 [2, 256, 2048], replicated
- gradient_down_adapter_first: float32 [2048, 256], replicated
- gradient_down_adapter_second: float32 [256, 640], replicated
The draws below stay inside these ranges and needn't reach their ends.
Inputs may be any that keep to these rules, and one draw needn't show every extreme that they name: `document_numbers`: each sequence packs 4 documents numbered in order, each of 1 to 800 tokens; some document has exactly 800 tokens.
All inputs are finite; a program needn't handle non-finite values.
Results may differ from the reference program's by a relative error of at most 0.019.
Values sent between devices are 32-bit elements; how exact they have to be, the bound alone decides.
A program may use at most 192 MiB of HBM per device.

```python
import math
import jax
import jax.numpy as jnp
import numpy as np
from jax import lax

MODEL_WIDTH = 640
QUERY_HEADS = 4
HEAD_WIDTH = 256
HIDDEN_UNITS = 2048
ADAPTER_RANK = 256
SEQ_LEN = 1024
DOCS = 4
DOC_MAX = 800
SEQS = 16
N_TENSOR = 2


def shard_levels(key, extent, cuts, least, high):
    def one(dim, shards_of):
        steps = jax.random.uniform(jax.random.fold_in(jax.random.fold_in(key, 6), dim), (shards_of,), jnp.float32, least / len(cuts), high / len(cuts))
        return jnp.repeat(jnp.exp(steps), extent[dim] // shards_of).reshape((-1,) + (1,) * (len(extent) - dim - 1))

    factor_of = one(*cuts[0])
    for cut in cuts[1:]:
        factor_of = factor_of * one(*cut)
    return factor_of


def split_up(count, total, reach, lean):
    weights = [(1 << 20) // math.isqrt(rank ** lean) + 1 for rank in range(2, count + 1)]
    surplus, holding = total - reach - (count - 1), [1] * (count - 1)
    while surplus > 0:
        candidates = [i for i in range(count - 1) if holding[i] < reach]
        mass, budget = sum([weights[i] for i in candidates]), surplus
        for i in candidates:
            extra = min(reach - holding[i], max(1, budget * weights[i] // mass), surplus)
            holding[i] = holding[i] + extra
            surplus = surplus - extra
    return np.array([reach] + holding)


def ragged_sizes(own_key, amount, total, bound, lean):
    if amount == 2:
        one = jax.random.randint(own_key, (), max(1, total - bound), min(bound, total - 1) + 1)
        return jnp.stack([one, total - one])
    tallies = jnp.asarray(split_up(amount, total, bound, lean), jnp.int32)
    twos = (amount - 1) // 2
    giver, receiver = tallies[1:1 + 2 * twos:2], tallies[2:2 + 2 * twos:2]
    margin = jnp.minimum(giver - 1, bound - receiver)
    passed = jax.random.randint(jax.random.fold_in(own_key, 1), (twos,), 0, 1 << 20) % (margin + 1)
    tallies = tallies.at[1:1 + 2 * twos:2].set(giver - passed).at[2:2 + 2 * twos:2].set(receiver + passed)
    return tallies[jax.random.permutation(jax.random.fold_in(own_key, 2), amount)]


def scatter_about(rng, shape, scale, bound, shards=(), held_as=jnp.bfloat16):
    array = jax.random.normal(rng, shape, jnp.float32) * scale
    if len(shards) > 0:
        array = shard_levels(rng, shape, shards, -0.22, 0.18) * array
    return jnp.clip(array, min=-bound, max=bound).astype(held_as)


def setup_inputs(seed: int = 0) -> dict:
    key_of = jax.random.split(jax.random.key(seed), 25)
    tokens = scatter_about(key_of[0], (SEQS, SEQ_LEN, MODEL_WIDTH), 1.0, 6.0, ((0, 16),))
    document_numbers = jax.vmap(lambda own: jnp.searchsorted(jnp.cumsum(ragged_sizes(own, DOCS, SEQ_LEN, DOC_MAX, 0)), jnp.arange(SEQ_LEN), side="right"))(jax.random.split(key_of[1], SEQS)).reshape((SEQS, SEQ_LEN)).astype(jnp.int32)
    input_norm_gain = jnp.clip(1.0 + 0.18 * jax.random.normal(key_of[2], (MODEL_WIDTH,), jnp.float32), 0.1, 1.9)
    after_attention_gain = jnp.clip(1.0 + 0.18 * jax.random.normal(key_of[3], (MODEL_WIDTH,), jnp.float32), 0.1, 1.9)
    before_feedforward_gain = jnp.clip(1.0 + 0.18 * jax.random.normal(key_of[4], (MODEL_WIDTH,), jnp.float32), 0.1, 1.9)
    after_feedforward_gain = jnp.clip(1.0 + 0.18 * jax.random.normal(key_of[5], (MODEL_WIDTH,), jnp.float32), 0.1, 1.9)
    query_norm_gain = jnp.clip(1.0 + 0.18 * jax.random.normal(key_of[6], (HEAD_WIDTH,), jnp.float32), 0.1, 1.9)
    key_norm_gain = jnp.clip(1.0 + 0.18 * jax.random.normal(key_of[7], (HEAD_WIDTH,), jnp.float32), 0.1, 1.9)
    query_weight = scatter_about(key_of[8], (MODEL_WIDTH, QUERY_HEADS * HEAD_WIDTH), MODEL_WIDTH ** -0.5, 0.25, ((1, 2),))
    keyvalue_weight = scatter_about(key_of[9], (MODEL_WIDTH, 2 * HEAD_WIDTH), MODEL_WIDTH ** -0.5, 0.25)
    output_weight = scatter_about(key_of[10], (QUERY_HEADS * HEAD_WIDTH, MODEL_WIDTH), (QUERY_HEADS * HEAD_WIDTH) ** -0.5, 0.1875, ((0, 2),))
    gateup_weight = scatter_about(key_of[11], (2, MODEL_WIDTH, HIDDEN_UNITS), MODEL_WIDTH ** -0.5, 0.25, ((2, 2),))
    down_weight = scatter_about(key_of[12], (HIDDEN_UNITS, MODEL_WIDTH), HIDDEN_UNITS ** -0.5, 0.125, ((0, 2),))
    query_adapter_first = scatter_about(key_of[13], (MODEL_WIDTH, ADAPTER_RANK), MODEL_WIDTH ** -0.5, 0.25)
    query_adapter_second = scatter_about(key_of[14], (ADAPTER_RANK, QUERY_HEADS * HEAD_WIDTH), (4 * ADAPTER_RANK) ** -0.5, 0.1875)
    keyvalue_adapter_first = scatter_about(key_of[15], (MODEL_WIDTH, 2 * ADAPTER_RANK), MODEL_WIDTH ** -0.5, 0.25)
    keyvalue_adapter_second = scatter_about(key_of[16], (2, ADAPTER_RANK, HEAD_WIDTH), (4 * ADAPTER_RANK) ** -0.5, 0.1875)
    output_adapter_first = scatter_about(key_of[17], (QUERY_HEADS * HEAD_WIDTH, ADAPTER_RANK), (QUERY_HEADS * HEAD_WIDTH) ** -0.5, 0.1875)
    output_adapter_second = scatter_about(key_of[18], (ADAPTER_RANK, MODEL_WIDTH), (4 * ADAPTER_RANK) ** -0.5, 0.1875)
    gateup_adapter_first = scatter_about(key_of[19], (MODEL_WIDTH, 2 * ADAPTER_RANK), MODEL_WIDTH ** -0.5, 0.25)
    gateup_adapter_second = scatter_about(key_of[20], (2, ADAPTER_RANK, HIDDEN_UNITS), (4 * ADAPTER_RANK) ** -0.5, 0.1875)
    down_adapter_first = scatter_about(key_of[21], (HIDDEN_UNITS, ADAPTER_RANK), HIDDEN_UNITS ** -0.5, 0.125)
    down_adapter_second = scatter_about(key_of[22], (ADAPTER_RANK, MODEL_WIDTH), (4 * ADAPTER_RANK) ** -0.5, 0.1875)
    cotangent = scatter_about(key_of[23], (SEQS, SEQ_LEN, MODEL_WIDTH), 1.0, 6.0, ((0, 16),))
    return dict(tokens=tokens, document_numbers=document_numbers, input_norm_gain=input_norm_gain, after_attention_gain=after_attention_gain, before_feedforward_gain=before_feedforward_gain, after_feedforward_gain=after_feedforward_gain, query_norm_gain=query_norm_gain, key_norm_gain=key_norm_gain, query_weight=query_weight, keyvalue_weight=keyvalue_weight, output_weight=output_weight, gateup_weight=gateup_weight, down_weight=down_weight, query_adapter_first=query_adapter_first, query_adapter_second=query_adapter_second, keyvalue_adapter_first=keyvalue_adapter_first, keyvalue_adapter_second=keyvalue_adapter_second, output_adapter_first=output_adapter_first, output_adapter_second=output_adapter_second, gateup_adapter_first=gateup_adapter_first, gateup_adapter_second=gateup_adapter_second, down_adapter_first=down_adapter_first, down_adapter_second=down_adapter_second, cotangent=cotangent)


EPS = 1e-06
THETA = 1000000.0
MASKED = -1e+30
PRECISE = lax.Precision.HIGHEST

@jax.custom_vjp
def lowrank_product(v):
    return lax.optimization_barrier(v.astype(jnp.bfloat16)).astype(jnp.float32)

@jax.custom_vjp
def lowrank_backward_pass(v):
    return v

def low_keep(v):
    return (lowrank_product(v), None)

def low_pass(kept, grad):
    return (grad,)

def back_keep(v):
    return (v, None)

def back_low(kept, grad):
    return (lowrank_product(grad),)
lowrank_product.defvjp(low_keep, low_pass)
lowrank_backward_pass.defvjp(back_keep, back_low)

def matrix_product(left_side, right_side):
    return jnp.dot(left_side, right_side, precision=PRECISE)

def rms_scale(values, scale_gain):
    return values * lax.rsqrt(lax.optimization_barrier(jnp.mean(values * values, axis=-1, keepdims=True)) + EPS) * scale_gain

def positions_of(segments):
    length = segments.shape[0]
    indices = jnp.arange(length, dtype=jnp.int32)
    before = jnp.concatenate([jnp.full((1,), -1, jnp.int32), segments[:-1]])
    starts = lax.cummax(jnp.where(segments != before, indices, jnp.zeros_like(indices)), axis=0)
    return indices - starts

def rotate(values, positions):
    half_dim = values.shape[-1] // 2
    frequency = THETA ** (-jnp.arange(half_dim, dtype=jnp.float32) * 2.0 / values.shape[-1])
    angles = positions.astype(jnp.float32)[:, None] * frequency[None, :]
    cosine = jnp.cos(angles)
    sine_part = jnp.sin(angles)
    if values.ndim == 3:
        cosine = cosine[:, None, :]
        sine_part = sine_part[:, None, :]
    leading = values[..., :half_dim]
    trailing = values[..., half_dim:]
    return jnp.concatenate([leading * cosine - trailing * sine_part, trailing * cosine + leading * sine_part], axis=-1)

def attend(q_rot, k_rot, values, allowed):
    scores = jnp.einsum('qhd,kd->hqk', q_rot, k_rot, precision=PRECISE)
    scores = lowrank_backward_pass(scores)
    scores = jnp.where(allowed[None], scores, MASKED)
    probs = jax.nn.softmax(scores, axis=-1)
    return jnp.einsum('hqk,kd->qhd', lowrank_product(probs), values, precision=PRECISE)

def layer(parameter_tuple, inputs, segments):
    input_norm_gain, after_attention_gain, before_feedforward_gain, after_feedforward_gain, query_norm_gain, key_norm_gain, query_weight, keyvalue_weight, output_weight, gateup_weight, down_weight, query_adapter_first, query_adapter_second, keyvalue_adapter_first, keyvalue_adapter_second, output_adapter_first, output_adapter_second, gateup_adapter_first, gateup_adapter_second, down_adapter_first, down_adapter_second = parameter_tuple
    length = inputs.shape[0]
    positions = positions_of(segments)
    indices = jnp.arange(length, dtype=jnp.int32)
    allowed = (segments[:, None] == segments[None, :]) & (indices[:, None] >= indices[None, :])
    head_group = QUERY_HEADS // N_TENSOR
    query_columns = head_group * HEAD_WIDTH
    hidden_columns = HIDDEN_UNITS // N_TENSOR
    normalized_rows = lowrank_product(rms_scale(inputs, input_norm_gain))
    query_lowrank = lowrank_product(matrix_product(normalized_rows, query_adapter_first))
    keyvalue_lowrank = lowrank_product(matrix_product(normalized_rows, keyvalue_adapter_first))
    kv_base = matrix_product(normalized_rows, keyvalue_weight)
    branch_output = jnp.zeros((length, MODEL_WIDTH), jnp.float32)
    for group_position in range(N_TENSOR):
        column_span = slice(group_position * query_columns, (group_position + 1) * query_columns)
        query_group = lowrank_backward_pass(query_lowrank)
        query_rows = lowrank_backward_pass(matrix_product(normalized_rows, query_weight[:, column_span]) + matrix_product(query_group, query_adapter_second[:, column_span]))
        keyvalue_group = lowrank_backward_pass(keyvalue_lowrank)
        adapter_pair = jnp.concatenate([matrix_product(keyvalue_group[:, :ADAPTER_RANK], keyvalue_adapter_second[0]), matrix_product(keyvalue_group[:, ADAPTER_RANK:], keyvalue_adapter_second[1])], axis=1)
        keyvalue = lowrank_backward_pass(kv_base + adapter_pair)
        q_heads = rms_scale(query_rows.reshape(length, head_group, HEAD_WIDTH), query_norm_gain)
        q_rot = lowrank_product(rotate(q_heads, positions) * HEAD_WIDTH ** (-0.5))
        k_rot = lowrank_product(rotate(rms_scale(keyvalue[:, :HEAD_WIDTH], key_norm_gain), positions))
        values = lowrank_product(keyvalue[:, HEAD_WIDTH:])
        attended_rows = lowrank_backward_pass(lowrank_product(attend(q_rot, k_rot, values, allowed).reshape(length, query_columns)))
        output_lowrank = lowrank_backward_pass(lowrank_product(matrix_product(attended_rows, output_adapter_first[column_span])))
        branch_output = branch_output + matrix_product(attended_rows, output_weight[column_span]) + matrix_product(output_lowrank, output_adapter_second)
    attention_before = lowrank_backward_pass(branch_output)
    residual = inputs + rms_scale(attention_before, after_attention_gain)
    feedforward_lowrank = lowrank_product(rms_scale(residual, before_feedforward_gain))
    gateup_lowrank = lowrank_product(matrix_product(feedforward_lowrank, gateup_adapter_first))
    feedforward_branch = jnp.zeros((length, MODEL_WIDTH), jnp.float32)
    for group_position in range(N_TENSOR):
        column_span = slice(group_position * hidden_columns, (group_position + 1) * hidden_columns)
        gateup_group = lowrank_backward_pass(gateup_lowrank)
        gate_values = lowrank_backward_pass(matrix_product(feedforward_lowrank, gateup_weight[0][:, column_span]) + matrix_product(gateup_group[:, :ADAPTER_RANK], gateup_adapter_second[0][:, column_span]))
        up_portion = lowrank_backward_pass(matrix_product(feedforward_lowrank, gateup_weight[1][:, column_span]) + matrix_product(gateup_group[:, ADAPTER_RANK:], gateup_adapter_second[1][:, column_span]))
        hidden_activation = lowrank_product(jax.nn.gelu(gate_values, approximate=True) * up_portion)
        down_lowrank = lowrank_backward_pass(lowrank_product(matrix_product(hidden_activation, down_adapter_first[column_span])))
        feedforward_branch = feedforward_branch + matrix_product(hidden_activation, down_weight[column_span]) + matrix_product(down_lowrank, down_adapter_second)
    feedforward_before = lowrank_backward_pass(feedforward_branch)
    return residual + rms_scale(feedforward_before, after_feedforward_gain)

def reference(tokens, document_numbers, input_norm_gain, after_attention_gain, before_feedforward_gain, after_feedforward_gain, query_norm_gain, key_norm_gain, query_weight, keyvalue_weight, output_weight, gateup_weight, down_weight, query_adapter_first, query_adapter_second, keyvalue_adapter_first, keyvalue_adapter_second, output_adapter_first, output_adapter_second, gateup_adapter_first, gateup_adapter_second, down_adapter_first, down_adapter_second, cotangent):
    parameter_tuple = tuple((entry_value.astype(jnp.float32) for entry_value in (input_norm_gain, after_attention_gain, before_feedforward_gain, after_feedforward_gain, query_norm_gain, key_norm_gain, query_weight, keyvalue_weight, output_weight, gateup_weight, down_weight, query_adapter_first, query_adapter_second, keyvalue_adapter_first, keyvalue_adapter_second, output_adapter_first, output_adapter_second, gateup_adapter_first, gateup_adapter_second, down_adapter_first, down_adapter_second)))
    inputs = tokens.astype(jnp.float32)

    def forward(weights, activations):

        def one_sequence(pair):
            return layer(weights, pair[0], pair[1])
        return lax.map(jax.checkpoint(one_sequence), (activations, document_numbers))
    result_value, pullback = jax.vjp(forward, parameter_tuple, inputs)
    gradient_tuple, gradient_token_input = pullback(cotangent.astype(jnp.float32))
    gradient_input_gain, gradient_after_attention, gradient_before_feedforward, gradient_after_feedforward, gradient_query_norm_gain, gradient_key_norm_gain, gradient_query_weight, gradient_keyvalue_weight, gradient_output_weight, gradient_gateup_weight, gradient_down_weight, gradient_query_adapter_first, gradient_query_adapter_second, gradient_keyvalue_adapter_first, gradient_keyvalue_adapter_second, gradient_output_adapter_first, gradient_output_adapter_second, gradient_gateup_adapter_first, gradient_gateup_adapter_second, gradient_down_adapter_first, gradient_down_adapter_second = gradient_tuple
    return (result_value.astype(jnp.bfloat16), gradient_token_input, gradient_input_gain, gradient_after_attention, gradient_before_feedforward, gradient_after_feedforward, gradient_query_norm_gain, gradient_key_norm_gain, gradient_query_weight, gradient_keyvalue_weight, gradient_output_weight, gradient_gateup_weight, gradient_down_weight, gradient_query_adapter_first, gradient_query_adapter_second, gradient_keyvalue_adapter_first, gradient_keyvalue_adapter_second, gradient_output_adapter_first, gradient_output_adapter_second, gradient_gateup_adapter_first, gradient_gateup_adapter_second, gradient_down_adapter_first, gradient_down_adapter_second)
```

```python
import jax
import jax.numpy as jnp
from jax import lax
from jax.sharding import PartitionSpec as P

EPS = 1e-06
THETA = 1000000.0
MASKED = -1e30


def matrix_product(left_side, right_side):
    return jnp.dot(left_side, right_side, preferred_element_type=jnp.float32)


def left_transposed(left_side, right_side):
    return lax.dot_general(
        left_side, right_side, (((0,), (0,)), ((), ())), preferred_element_type=jnp.float32
    )


def right_transposed(left_side, right_side):
    return lax.dot_general(
        left_side, right_side, (((1,), (1,)), ((), ())), preferred_element_type=jnp.float32
    )


def rms_scale(values, scale_gain):
    return values * lax.rsqrt(jnp.mean(values * values, axis=-1, keepdims=True) + EPS) * scale_gain


def positions_of(segments):
    length = segments.shape[0]
    indices = jnp.arange(length, dtype=jnp.int32)
    before = jnp.concatenate([jnp.full((1,), -1, jnp.int32), segments[:-1]])
    starts = lax.cummax(jnp.where(segments != before, indices, jnp.zeros_like(indices)), axis=0)
    return indices - starts


def rotate(values, positions):
    half_dim = values.shape[-1] // 2
    frequency = THETA ** (-jnp.arange(half_dim, dtype=jnp.float32) * 2.0 / values.shape[-1])
    angles = positions.astype(jnp.float32)[:, None] * frequency[None, :]
    cosine = jnp.cos(angles)
    sine_part = jnp.sin(angles)
    if values.ndim == 3:
        cosine = cosine[:, None, :]
        sine_part = sine_part[:, None, :]
    leading = values[..., :half_dim]
    trailing = values[..., half_dim:]
    return jnp.concatenate(
        [leading * cosine - trailing * sine_part, trailing * cosine + leading * sine_part], axis=-1
    )


def exact_product(left_side, right_side, contract):
    return lax.dot_general(
        left_side,
        right_side.astype(jnp.float32),
        (contract, ((), ())),
        precision=lax.Precision.HIGHEST,
        preferred_element_type=jnp.float32,
    )


def activate(gate_in, up_in):
    return jax.nn.gelu(gate_in, approximate=True) * up_in


def on_device(
    tokens,
    document_numbers,
    input_norm_gain,
    after_attention_gain,
    before_feedforward_gain,
    after_feedforward_gain,
    query_norm_gain,
    key_norm_gain,
    query_weight,
    keyvalue_weight,
    output_weight,
    gateup_weight,
    down_weight,
    query_adapter_first,
    query_adapter_second,
    keyvalue_adapter_first,
    keyvalue_adapter_second,
    output_adapter_first,
    output_adapter_second,
    gateup_adapter_first,
    gateup_adapter_second,
    down_adapter_first,
    down_adapter_second,
    cotangent,
):
    inputs = tokens[0].astype(jnp.float32)
    segments = document_numbers[0]
    length = inputs.shape[0]
    head_width = keyvalue_adapter_second.shape[2]
    adapter_rank = query_adapter_first.shape[1]
    query_columns = query_weight.shape[1]
    hidden_columns = down_weight.shape[0]
    heads_local = query_columns // head_width
    group_position = lax.axis_index("tensor")
    query_piece = lax.dynamic_slice_in_dim(
        query_adapter_second, group_position * query_columns, query_columns, 1
    )
    output_rows = lax.dynamic_slice_in_dim(
        output_adapter_first, group_position * query_columns, query_columns, 0
    )
    gateup_piece = lax.dynamic_slice_in_dim(
        gateup_adapter_second, group_position * hidden_columns, hidden_columns, 2
    )
    down_rows = lax.dynamic_slice_in_dim(
        down_adapter_first, group_position * hidden_columns, hidden_columns, 0
    )
    query_merged = (
        query_weight.astype(jnp.float32) + matrix_product(query_adapter_first, query_piece)
    ).astype(jnp.bfloat16)
    keyvalue_merged = (
        keyvalue_weight.astype(jnp.float32)
        + jnp.concatenate(
            [
                matrix_product(keyvalue_adapter_first[:, :adapter_rank], keyvalue_adapter_second[0]),
                matrix_product(keyvalue_adapter_first[:, adapter_rank:], keyvalue_adapter_second[1]),
            ],
            axis=1,
        )
    ).astype(jnp.bfloat16)
    output_merged = (
        output_weight.astype(jnp.float32) + matrix_product(output_rows, output_adapter_second)
    ).astype(jnp.bfloat16)
    gate_merged = (
        gateup_weight[0].astype(jnp.float32)
        + matrix_product(gateup_adapter_first[:, :adapter_rank], gateup_piece[0])
    ).astype(jnp.bfloat16)
    up_merged = (
        gateup_weight[1].astype(jnp.float32)
        + matrix_product(gateup_adapter_first[:, adapter_rank:], gateup_piece[1])
    ).astype(jnp.bfloat16)
    down_merged = (
        down_weight.astype(jnp.float32) + matrix_product(down_rows, down_adapter_second)
    ).astype(jnp.bfloat16)
    positions = positions_of(segments)
    key_index = jnp.arange(length, dtype=jnp.int32)
    block_rows = min(512, length)
    normalized_rows, in_back = jax.vjp(rms_scale, inputs, input_norm_gain)
    normalized_lowrank = normalized_rows.astype(jnp.bfloat16)
    query_rows = matrix_product(normalized_lowrank, query_merged)
    keyvalue = matrix_product(normalized_lowrank, keyvalue_merged)

    def prepare(q_in, kv_in, q_scale, k_scale):
        q_heads = rms_scale(q_in.reshape(length, heads_local, head_width), q_scale)
        q_out = rotate(q_heads, positions) * head_width ** (-0.5)
        k_out = rotate(rms_scale(kv_in[:, :head_width], k_scale), positions)
        return (q_out, k_out, kv_in[:, head_width:])

    prepared, prepare_back = jax.vjp(prepare, query_rows, keyvalue, query_norm_gain, key_norm_gain)
    q_rot = prepared[0].astype(jnp.bfloat16)
    k_rot = prepared[1].astype(jnp.bfloat16)
    v_low = prepared[2].astype(jnp.bfloat16)

    def scores_of(row_start):
        rows = q_rot[row_start : row_start + block_rows]
        raw = jnp.einsum("qhd,kd->hqk", rows, k_rot, preferred_element_type=jnp.float32)
        row_index = row_start + jnp.arange(block_rows, dtype=jnp.int32)
        allowed = (segments[row_start : row_start + block_rows][:, None] == segments[None, :]) & (
            row_index[:, None] >= key_index[None, :]
        )
        return jnp.where(allowed[None], raw, MASKED)

    outputs = []
    log_totals = []
    for row_start in range(0, length, block_rows):
        scores = scores_of(row_start)
        row_peak = jnp.max(scores, axis=-1, keepdims=True)
        weights = jnp.exp(scores - row_peak)
        row_total = jnp.sum(weights, axis=-1, keepdims=True)
        log_totals.append(row_peak + jnp.log(row_total))
        probs_low = (weights / row_total).astype(jnp.bfloat16)
        outputs.append(
            jnp.einsum("hqk,kd->qhd", probs_low, v_low, preferred_element_type=jnp.float32)
        )
    attended_rows = (
        jnp.concatenate(outputs, axis=0).reshape(length, query_columns).astype(jnp.bfloat16)
    )
    attention_before = lax.psum(matrix_product(attended_rows, output_merged), "tensor")
    attn_post, post_attn_back = jax.vjp(rms_scale, attention_before, after_attention_gain)
    residual = inputs + attn_post
    normed_ff, pre_ff_back = jax.vjp(rms_scale, residual, before_feedforward_gain)
    feedforward_lowrank = normed_ff.astype(jnp.bfloat16)
    gate_portion = matrix_product(feedforward_lowrank, gate_merged)
    up_portion = matrix_product(feedforward_lowrank, up_merged)
    hidden_full, activate_back = jax.vjp(activate, gate_portion, up_portion)
    hidden_activation = hidden_full.astype(jnp.bfloat16)
    feedforward_before = lax.psum(matrix_product(hidden_activation, down_merged), "tensor")
    mlp_post, post_ff_back = jax.vjp(rms_scale, feedforward_before, after_feedforward_gain)
    result_value = (residual + mlp_post).astype(jnp.bfloat16)[None]
    grad_out = cotangent[0].astype(jnp.float32)
    grad_mlp_pre, gradient_after_feedforward = post_ff_back(grad_out)
    gradient_feedforward_lowrank = grad_mlp_pre.astype(jnp.bfloat16)
    gradient_down_weight = left_transposed(hidden_activation, gradient_feedforward_lowrank)
    grad_hidden = right_transposed(gradient_feedforward_lowrank, down_merged)
    grad_gate, grad_up = activate_back(grad_hidden)
    gate_lowrank = grad_gate.astype(jnp.bfloat16)
    up_lowrank = grad_up.astype(jnp.bfloat16)
    gradient_gateup_weight = jnp.stack(
        [
            left_transposed(feedforward_lowrank, gate_lowrank),
            left_transposed(feedforward_lowrank, up_lowrank),
        ]
    )
    grad_ff_part = right_transposed(gate_lowrank, gate_merged) + right_transposed(
        up_lowrank, up_merged
    )
    grad_normed_ff = lax.psum(grad_ff_part, "tensor")
    grad_residual_ff, gradient_before_feedforward = pre_ff_back(grad_normed_ff)
    grad_residual = grad_out + grad_residual_ff
    grad_attn_pre, gradient_after_attention = post_attn_back(grad_residual)
    gradient_attention_lowrank = grad_attn_pre.astype(jnp.bfloat16)
    gradient_output_weight = left_transposed(attended_rows, gradient_attention_lowrank)
    grad_attended = right_transposed(gradient_attention_lowrank, output_merged).astype(jnp.bfloat16)
    grad_attended = grad_attended.reshape(length, heads_local, head_width)
    grad_q_blocks = []
    grad_k_rot = jnp.zeros((length, head_width), jnp.float32)
    grad_values = jnp.zeros((length, head_width), jnp.float32)
    for block_index, row_start in enumerate(range(0, length, block_rows)):
        scores = scores_of(row_start)
        probs = jnp.exp(scores - log_totals[block_index])
        grad_rows = grad_attended[row_start : row_start + block_rows]
        grad_probs = jnp.einsum("qhd,kd->hqk", grad_rows, v_low, preferred_element_type=jnp.float32)
        grad_scores = (
            probs * (grad_probs - jnp.sum(probs * grad_probs, axis=-1, keepdims=True))
        ).astype(jnp.bfloat16)
        grad_q_blocks.append(
            jnp.einsum("hqk,kd->qhd", grad_scores, k_rot, preferred_element_type=jnp.float32)
        )
        grad_k_rot = grad_k_rot + jnp.einsum(
            "hqk,qhd->kd",
            grad_scores,
            q_rot[row_start : row_start + block_rows],
            preferred_element_type=jnp.float32,
        )
        grad_values = grad_values + jnp.einsum(
            "hqk,qhd->kd", probs.astype(jnp.bfloat16), grad_rows, preferred_element_type=jnp.float32
        )
    grad_queries, grad_keyvalue, gradient_query_norm_gain, gradient_key_norm_gain = prepare_back(
        (jnp.concatenate(grad_q_blocks, axis=0), grad_k_rot, grad_values)
    )
    query_low = grad_queries.astype(jnp.bfloat16)
    keyvalue_gradient_lowrank = grad_keyvalue.astype(jnp.bfloat16)
    gradient_query_weight = left_transposed(normalized_lowrank, query_low)
    gradient_keyvalue_weight = left_transposed(normalized_lowrank, keyvalue_gradient_lowrank)
    grad_in_part = right_transposed(query_low, query_merged) + right_transposed(
        keyvalue_gradient_lowrank, keyvalue_merged
    )
    grad_normed = lax.psum(grad_in_part, "tensor")
    grad_inputs_add, gradient_input_gain = in_back(grad_normed)
    gradient_token_input = (grad_residual + grad_inputs_add)[None]
    lead_mask = (group_position == 0).astype(jnp.float32)
    lead_in = gradient_input_gain * lead_mask
    lead_post_attn = gradient_after_attention * lead_mask
    lead_pre_ff = gradient_before_feedforward * lead_mask
    lead_post_ff = gradient_after_feedforward * lead_mask
    sum_w_query, sum_w_out, sum_w_gate_up, sum_w_down = lax.psum(
        (
            gradient_query_weight,
            gradient_output_weight,
            gradient_gateup_weight,
            gradient_down_weight,
        ),
        "dp",
    )
    (
        sum_gain_in,
        sum_post_attn,
        sum_pre_ff,
        sum_post_ff,
        sum_query_gain,
        sum_key_gain,
        sum_w_keyvalue,
    ) = lax.psum(
        (
            lead_in,
            lead_post_attn,
            lead_pre_ff,
            lead_post_ff,
            gradient_query_norm_gain,
            gradient_key_norm_gain,
            gradient_keyvalue_weight,
        ),
        ("dp", "tensor"),
    )
    rows_rows = ((0,), (0,))
    columns_columns = ((1,), (1,))
    sum_kv_b = jnp.stack(
        [
            exact_product(
                sum_w_keyvalue[:, i * head_width : (i + 1) * head_width],
                keyvalue_adapter_first[:, i * adapter_rank : (i + 1) * adapter_rank],
                rows_rows,
            ).T
            for i in range(2)
        ]
    )
    sum_kv_a = jnp.concatenate(
        [
            exact_product(
                sum_w_keyvalue[:, i * head_width : (i + 1) * head_width],
                keyvalue_adapter_second[i],
                columns_columns,
            )
            for i in range(2)
        ],
        axis=1,
    )
    part_q_b = exact_product(sum_w_query, query_adapter_first, rows_rows).T
    part_q_a = exact_product(sum_w_query, query_piece, columns_columns)
    part_o_a = exact_product(sum_w_out, output_adapter_second, columns_columns)
    part_o_b = exact_product(sum_w_out, output_rows, rows_rows).T
    part_gu_b = jnp.stack(
        [
            exact_product(
                sum_w_gate_up[i],
                gateup_adapter_first[:, i * adapter_rank : (i + 1) * adapter_rank],
                rows_rows,
            ).T
            for i in range(2)
        ]
    )
    part_gu_a = jnp.concatenate(
        [exact_product(sum_w_gate_up[i], gateup_piece[i], columns_columns) for i in range(2)],
        axis=1,
    )
    part_d_a = exact_product(sum_w_down, down_adapter_second, columns_columns)
    part_d_b = exact_product(sum_w_down, down_rows, rows_rows).T
    sum_q_a, sum_o_b, sum_gu_a, sum_d_b = lax.psum(
        (part_q_a, part_o_b, part_gu_a, part_d_b), "tensor"
    )
    sum_q_b = lax.all_gather(part_q_b, "tensor", axis=1, tiled=True)
    sum_o_a = lax.all_gather(part_o_a, "tensor", axis=0, tiled=True)
    sum_gu_b = lax.all_gather(part_gu_b, "tensor", axis=2, tiled=True)
    sum_d_a = lax.all_gather(part_d_a, "tensor", axis=0, tiled=True)
    return (
        result_value,
        gradient_token_input,
        sum_gain_in,
        sum_post_attn,
        sum_pre_ff,
        sum_post_ff,
        sum_query_gain,
        sum_key_gain,
        sum_w_query,
        sum_w_keyvalue,
        sum_w_out,
        sum_w_gate_up,
        sum_w_down,
        sum_q_a,
        sum_q_b,
        sum_kv_a,
        sum_kv_b,
        sum_o_a,
        sum_o_b,
        sum_gu_a,
        sum_gu_b,
        sum_d_a,
        sum_d_b,
    )


def solution(mesh):
    in_specs = (
        P("dp", None, None),
        P("dp", None),
        P(),
        P(),
        P(),
        P(),
        P(),
        P(),
        P(None, "tensor"),
        P(),
        P("tensor", None),
        P(None, None, "tensor"),
        P("tensor", None),
        P(),
        P(),
        P(),
        P(),
        P(),
        P(),
        P(),
        P(),
        P(),
        P(),
        P("dp", None, None),
    )
    out_specs = (
        P("dp", None, None),
        P("dp", None, None),
        P(),
        P(),
        P(),
        P(),
        P(),
        P(),
        P(None, "tensor"),
        P(),
        P("tensor", None),
        P(None, None, "tensor"),
        P("tensor", None),
        P(),
        P(),
        P(),
        P(),
        P(),
        P(),
        P(),
        P(),
        P(),
        P(),
    )
    return jax.shard_map(
        on_device, mesh=mesh, in_specs=in_specs, out_specs=out_specs, check_vma=False
    )
```

```python
import functools

import jax
import jax.numpy as jnp
from jax import lax
from jax.experimental import pallas as pl
from jax.experimental.pallas import tpu as pltpu
from jax.sharding import PartitionSpec as P

EPS = 1e-06
THETA = 1000000.0
MASKED = -1e30


def matrix_product(left_side, right_side):
    return jnp.dot(left_side, right_side, preferred_element_type=jnp.float32)


def left_transposed(left_side, right_side):
    return lax.dot_general(
        left_side, right_side, (((0,), (0,)), ((), ())), preferred_element_type=jnp.float32
    )


def right_transposed(left_side, right_side):
    return lax.dot_general(
        left_side, right_side, (((1,), (1,)), ((), ())), preferred_element_type=jnp.float32
    )


def rms_scale(values, scale_gain):
    return values * lax.rsqrt(jnp.mean(values * values, axis=-1, keepdims=True) + EPS) * scale_gain


def positions_of(segments):
    length = segments.shape[0]
    indices = jnp.arange(length, dtype=jnp.int32)
    before = jnp.concatenate([jnp.full((1,), -1, jnp.int32), segments[:-1]])
    starts = lax.cummax(jnp.where(segments != before, indices, jnp.zeros_like(indices)), axis=0)
    return indices - starts


def rotate(values, positions):
    half_dim = values.shape[-1] // 2
    frequency = THETA ** (-jnp.arange(half_dim, dtype=jnp.float32) * 2.0 / values.shape[-1])
    angles = positions.astype(jnp.float32)[:, None] * frequency[None, :]
    cosine = jnp.cos(angles)
    sine_part = jnp.sin(angles)
    if values.ndim == 3:
        cosine = cosine[:, None, :]
        sine_part = sine_part[:, None, :]
    leading = values[..., :half_dim]
    trailing = values[..., half_dim:]
    return jnp.concatenate(
        [leading * cosine - trailing * sine_part, trailing * cosine + leading * sine_part], axis=-1
    )


def exact_product(left_side, right_side, contract):
    return lax.dot_general(
        left_side,
        right_side.astype(jnp.float32),
        (contract, ((), ())),
        precision=lax.Precision.HIGHEST,
        preferred_element_type=jnp.float32,
    )


def activate(gate_in, up_in):
    return jax.nn.gelu(gate_in, approximate=True) * up_in


MESH_ID = pl.DeviceIdType.MESH


class Place:
    def __init__(self):
        me = lax.axis_index("dp")
        core = lax.axis_index("tensor")
        bit_x = lax.rem(me, 2)
        bit_y = lax.rem(me // 2, 2)
        level = me // 4
        across_x = me + 1 - 2 * bit_x
        across_y = me + 2 - 4 * bit_y
        self.core = core
        self.side = level // 2
        self.level = level
        self.outer = jnp.logical_or(level == 0, level == 3)
        self.inner = jnp.logical_not(self.outer)
        self.bit_one = jnp.where(core == 0, bit_x, bit_y)
        self.bit_two = jnp.where(core == 0, bit_y, bit_x)
        self.one = (jnp.where(core == 0, across_x, across_y), core)
        self.two = (jnp.where(core == 0, across_y, across_x), core)
        column = lax.rem(me, 4)
        self.near = ((level + 1 - 2 * lax.rem(level, 2)) * 4 + column, core)
        self.middle = ((3 - level) * 4 + column, core)
        self.sibling = (me, 1 - core)


def add_rows(target, target_row, extra, extra_row, count):
    step = 32 if count % 32 == 0 else (16 if count % 16 == 0 else 8)

    def body(index, carry):
        rows = pl.ds(pl.multiple_of(target_row + index * step, 8), step)
        target[rows] = target[rows] + extra[pl.ds(pl.multiple_of(extra_row + index * step, 8), step)]
        return carry

    lax.fori_loop(0, count // step, body, 0)


class Sums:
    def __init__(self, place, sends, receives, freed):
        self.place = place
        self.sends = sends
        self.receives = receives
        self.freed = freed
        self.used = 0
        self.credits = 0

    def credit(self):
        self.credits += 1
        return self.freed.at[self.credits - 1]

    def copy(self, source, target, device):
        slot = self.used
        self.used += 1
        return pltpu.make_async_remote_copy(
            src_ref=source,
            dst_ref=target,
            send_sem=self.sends.at[slot],
            recv_sem=self.receives.at[slot],
            device_id=device,
            device_id_type=MESH_ID,
        )


def signal(semaphore, device):
    pl.semaphore_signal(semaphore, inc=1, device_id=device, device_id_type=MESH_ID)


def rows_at(ref, start, count):
    return ref.at[pl.ds(pl.multiple_of(start, 8), count)]


def plane_first(sums, total, row, count, landing, landing_row, finish):
    place = sums.place
    half, quarter = count // 2, count // 4
    kept = row + place.bit_one * half
    given = row + (1 - place.bit_one) * half
    mine = kept + place.bit_two * quarter
    other = kept + (1 - place.bit_two) * quarter
    land_one = rows_at(landing, landing_row, half)
    land_two = rows_at(landing, landing_row + half, quarter)
    land_near = rows_at(landing, landing_row + half + quarter, quarter)
    land_mid = rows_at(landing, landing_row + 2 * half, quarter)
    ours = rows_at(total, mine, quarter)
    copy_one = sums.copy(rows_at(total, given, half), land_one, place.one)
    copy_two = sums.copy(rows_at(total, other, quarter), land_two, place.two)
    copy_in = sums.copy(ours, land_near, place.near)
    copy_mid = sums.copy(ours, land_mid, place.middle)
    copy_out = sums.copy(ours, ours, place.near)
    back_two = sums.copy(ours, ours, place.two)
    back_one = sums.copy(rows_at(total, kept, half), rows_at(total, kept, half), place.one)

    free_one, free_two, free_in = sums.credit(), sums.credit(), sums.credit()

    def step0():
        copy_one.start()

    def step1():
        copy_one.wait_recv()
        add_rows(total, kept, landing, landing_row, half)
        copy_two.start()

    def step2():
        copy_two.wait_recv()
        add_rows(total, mine, landing, landing_row + half, quarter)

        @pl.when(place.outer)
        def _():
            copy_in.start()

        copy_one.wait_send()
        signal(free_one, place.one)

    def step3():
        @pl.when(place.inner)
        def _():
            copy_in.wait_recv()
            add_rows(total, mine, landing, landing_row + half + quarter, quarter)
            copy_mid.start()

        copy_two.wait_send()
        signal(free_two, place.two)

        @pl.when(place.outer)
        def _():
            copy_in.wait_send()
            signal(free_in, place.near)

    def step4():
        @pl.when(place.inner)
        def _():
            copy_mid.wait()
            add_rows(total, mine, landing, landing_row + 2 * half, quarter)
            pl.semaphore_wait(free_in, 1)
            copy_out.start()
            pl.semaphore_wait(free_two, 1)
            back_two.start()

    def step5():
        @pl.when(place.outer)
        def _():
            copy_out.wait_recv()
            pl.semaphore_wait(free_two, 1)
            back_two.start()

    def step6():
        back_two.wait_recv()
        pl.semaphore_wait(free_one, 1)
        back_one.start()

    def step7():
        back_one.wait_recv()
        back_two.wait_send()
        back_one.wait_send()

        @pl.when(place.inner)
        def _():
            copy_out.wait_send()

        finish()

    return [step0, step1, step2, step3, step4, step5, step6, step7]


def line_first(sums, total, row, count, landing, landing_row, finish):
    place = sums.place
    quarter = count // 4
    side = place.side
    three = row + (1 - side) * quarter
    far_pair = row + (1 - side) * 2 * quarter
    own_pair = row + side * 2 * quarter
    outer_quarter = row + 3 * side * quarter
    mine = row + place.level * quarter
    ours = rows_at(total, mine, quarter)
    land_three = rows_at(landing, landing_row, 3 * quarter)
    land_pair = rows_at(landing, landing_row + 3 * quarter, 2 * quarter)
    land_back = rows_at(landing, landing_row, quarter)
    land_one = rows_at(landing, landing_row + 5 * quarter, quarter)
    land_two = rows_at(landing, landing_row + 6 * quarter, quarter)
    copy_three = sums.copy(rows_at(total, three, 3 * quarter), land_three, place.near)
    copy_pair = sums.copy(rows_at(total, far_pair, 2 * quarter), land_pair, place.middle)
    outers = rows_at(total, outer_quarter, quarter)
    copy_back = sums.copy(outers, land_back, place.near)
    copy_one = sums.copy(ours, land_one, place.one)
    copy_two = sums.copy(ours, land_two, place.two)
    spread_in = sums.copy(ours, ours, place.near)
    spread_out = sums.copy(ours, ours, place.near)
    spread_mid = sums.copy(ours, ours, place.middle)
    forward_mid = sums.copy(outers, outers, place.middle)
    far_rows = rows_at(total, far_pair, 2 * quarter)
    forward_out = sums.copy(far_rows, far_rows, place.near)

    free_three, free_pair, free_back = sums.credit(), sums.credit(), sums.credit()

    def step0():
        @pl.when(place.outer)
        def _():
            copy_three.start()

    def step1():
        @pl.when(place.inner)
        def _():
            copy_three.wait_recv()
            add_rows(total, three, landing, landing_row, 3 * quarter)
            copy_pair.start()

    def step2():
        @pl.when(place.inner)
        def _():
            copy_pair.wait_recv()
            add_rows(total, own_pair, landing, landing_row + 3 * quarter, 2 * quarter)
            copy_back.start()
            copy_one.start()

    def step3():
        @pl.when(place.outer)
        def _():
            copy_back.wait_recv()
            add_rows(total, mine, landing, landing_row, quarter)
            copy_one.start()
            copy_three.wait_send()
            signal(free_three, place.near)

        @pl.when(place.inner)
        def _():
            copy_pair.wait_send()
            signal(free_pair, place.middle)
            copy_back.wait_send()
            signal(free_back, place.near)

    def step4():
        copy_one.wait()
        add_rows(total, mine, landing, landing_row + 5 * quarter, quarter)
        copy_two.start()

    def step5():
        copy_two.wait()
        add_rows(total, mine, landing, landing_row + 6 * quarter, quarter)

        @pl.when(place.outer)
        def _():
            pl.semaphore_wait(free_back, 1)
            spread_in.start()

        @pl.when(place.inner)
        def _():
            pl.semaphore_wait(free_three, 1)
            spread_out.start()
            pl.semaphore_wait(free_pair, 1)
            spread_mid.start()

    def step6():
        @pl.when(place.inner)
        def _():
            spread_in.wait_recv()
            forward_mid.start()

    def step7():
        @pl.when(place.inner)
        def _():
            spread_mid.wait_recv()
            forward_mid.wait_recv()
            forward_out.start()

    def step8():
        @pl.when(place.outer)
        def _():
            spread_out.wait_recv()
            forward_out.wait_recv()
            spread_in.wait_send()

        @pl.when(place.inner)
        def _():
            spread_out.wait_send()
            spread_mid.wait_send()
            forward_mid.wait_send()
            forward_out.wait_send()

        finish()

    return [step0, step1, step2, step3, step4, step5, step6, step7, step8]


def greet(place):
    barrier = pltpu.get_barrier_semaphore()
    for device in (place.one, place.two, place.near, place.sibling):
        pl.semaphore_signal(barrier, inc=1, device_id=device, device_id_type=MESH_ID)

    @pl.when(place.inner)
    def _():
        pl.semaphore_signal(barrier, inc=1, device_id=place.middle, device_id_type=MESH_ID)
        pl.semaphore_wait(barrier, 5)

    @pl.when(place.outer)
    def _():
        pl.semaphore_wait(barrier, 4)

ANYWHERE = pl.BlockSpec(memory_space=pl.ANY)


def chunk_plan(shapes):
    cuts = {
        "d": ("L", 224, "P", 288, "L", 192, "P", 320),
        "g": ("L", 128, "P", 192, "L", 128, "P", 192),
        "u": ("L", 128, "P", 192, "L", 128, "P", 192),
        "o": ("L", 192, "P", 160, "P", 160),
        "q": ("L", 256, "P", 192, "P", 192),
        "k": ("P", 160, "P", 160),
        "s": ("P", 32),
    }
    plan = []
    for name, (rows, columns) in shapes.items():
        parts = list(zip(cuts[name][0::2], cuts[name][1::2]))
        assert sum(count for _, count in parts) == rows
        plan.append((name, rows, columns, parts))
    return plan


def landing_rows(kind, count):
    return count // 4 * (5 if kind == "P" else 7)


def reduce_kernel(plan, *refs):
    names = [entry[0] for entry in plan]
    split = [name for name in names if name not in "ks"]
    refs = list(refs)

    def take(keys):
        return {key: refs.pop(0) for key in keys}

    source = take(names)
    own = take(names)
    both = take(split)
    total = take(names)
    landing = take(names)
    swapped = take("ks")
    sends, receives, local, freed = refs
    place = Place()
    greet(place)
    sums = Sums(place, sends, receives, freed)
    loads = {}
    swaps = {}
    for index, name in enumerate(names):
        piece = source[name]
        if name == "k":
            half = total["k"].shape[0]
            swaps["k"] = sums.copy(
                rows_at(piece, (1 - place.core) * half, half), swapped["k"], place.sibling
            )
            piece = rows_at(piece, place.core * half, half)
        if name == "s":
            swaps["s"] = sums.copy(piece, swapped["s"], place.sibling)
        loads[name] = pltpu.make_async_copy(piece, total[name], local.at[index])
        loads[name].start()
    for swap in swaps.values():
        swap.start()
    chunks = []
    leaving = []
    slots = len(names)
    for name, rows, columns, parts in plan:
        row = 0
        land_row = 0
        for kind, count in parts:

            def finish(name=name, row=row, count=count, slot=slots):
                rows = pl.ds(row, count)
                done = total[name].at[rows]
                if name == "k":
                    home = rows_at(own["k"], place.core * total["k"].shape[0] + row, count)
                    moves = [
                        pltpu.make_async_copy(done, home, local.at[slot]),
                        sums.copy(done, home, place.sibling),
                    ]
                elif name == "s":
                    moves = [pltpu.make_async_copy(done, own["s"], local.at[slot])]
                else:
                    home = both[name].at[place.core, rows]
                    moves = [
                        pltpu.make_async_copy(done, own[name].at[rows], local.at[slot]),
                        pltpu.make_async_copy(done, home, local.at[slot + 1]),
                        sums.copy(done, home, place.sibling),
                    ]
                for move in moves:
                    move.start()
                leaving.extend(moves)

            build = plane_first if kind == "P" else line_first
            steps = build(sums, total[name], row, count, landing[name], land_row, finish)
            if row == 0:

                def enter(name=name, first=steps[0]):
                    loads[name].wait()
                    if name in swaps:
                        swaps[name].wait()
                        add_rows(total[name], 0, swapped[name], 0, total[name].shape[0])
                    first()

                steps = [enter] + steps[1:]
            chunks.append(steps)
            slots += 2
            row += count
            land_row += landing_rows(kind, count)
    active = []
    while chunks or active:
        active += chunks[:2]
        chunks = chunks[2:]
        for steps in list(active):
            steps.pop(0)()
            if not steps:
                active.remove(steps)
    for move in leaving:
        move.wait()


def reduce_over_chips(pieces):
    shapes = {name: piece.shape for name, piece in pieces.items()}
    shapes["k"] = (shapes["k"][0] // 2, shapes["k"][1])
    plan = chunk_plan(shapes)
    split = [name for name in pieces if name not in "ks"]
    outs = [jax.ShapeDtypeStruct(piece.shape, jnp.float32) for piece in pieces.values()]
    outs += [jax.ShapeDtypeStruct((2,) + pieces[name].shape, jnp.float32) for name in split]
    scratch = [pltpu.VMEM((rows, columns), jnp.float32) for _, rows, columns, _ in plan]
    scratch += [
        pltpu.VMEM((sum(landing_rows(*part) for part in parts), columns), jnp.float32)
        for _, _, columns, parts in plan
    ]
    scratch += [pltpu.VMEM(shapes[name], jnp.float32) for name in "ks"]
    count = sum(len(parts) for _, _, _, parts in plan)
    scratch += [
        pltpu.SemaphoreType.DMA((count * 11 + 4,)),
        pltpu.SemaphoreType.DMA((count * 11 + 4,)),
        pltpu.SemaphoreType.DMA((len(plan) + 2 * count,)),
        pltpu.SemaphoreType.REGULAR((count * 3,)),
    ]
    results = pl.pallas_call(
        functools.partial(reduce_kernel, plan),
        out_shape=outs,
        in_specs=[ANYWHERE] * len(plan),
        out_specs=[ANYWHERE] * len(outs),
        scratch_shapes=scratch,
        compiler_params=pltpu.CompilerParams(
            collective_id=0, has_side_effects=True, vmem_limit_bytes=62 * 2**20
        ),
    )(*pieces.values())
    own = dict(zip(pieces, results[: len(plan)]))
    both = dict(zip(split, results[len(plan) :]))
    return own, both


def on_device(
    fast,
    tokens,
    document_numbers,
    input_norm_gain,
    after_attention_gain,
    before_feedforward_gain,
    after_feedforward_gain,
    query_norm_gain,
    key_norm_gain,
    query_weight,
    keyvalue_weight,
    output_weight,
    gateup_weight,
    down_weight,
    query_adapter_first,
    query_adapter_second,
    keyvalue_adapter_first,
    keyvalue_adapter_second,
    output_adapter_first,
    output_adapter_second,
    gateup_adapter_first,
    gateup_adapter_second,
    down_adapter_first,
    down_adapter_second,
    cotangent,
):
    inputs = tokens[0].astype(jnp.float32)
    segments = document_numbers[0]
    length = inputs.shape[0]
    head_width = keyvalue_adapter_second.shape[2]
    adapter_rank = query_adapter_first.shape[1]
    query_columns = query_weight.shape[1]
    hidden_columns = down_weight.shape[0]
    heads_local = query_columns // head_width
    group_position = lax.axis_index("tensor")
    query_piece = lax.dynamic_slice_in_dim(
        query_adapter_second, group_position * query_columns, query_columns, 1
    )
    output_rows = lax.dynamic_slice_in_dim(
        output_adapter_first, group_position * query_columns, query_columns, 0
    )
    gateup_piece = lax.dynamic_slice_in_dim(
        gateup_adapter_second, group_position * hidden_columns, hidden_columns, 2
    )
    down_rows = lax.dynamic_slice_in_dim(
        down_adapter_first, group_position * hidden_columns, hidden_columns, 0
    )
    query_merged = (
        query_weight.astype(jnp.float32) + matrix_product(query_adapter_first, query_piece)
    ).astype(jnp.bfloat16)
    keyvalue_merged = (
        keyvalue_weight.astype(jnp.float32)
        + jnp.concatenate(
            [
                matrix_product(keyvalue_adapter_first[:, :adapter_rank], keyvalue_adapter_second[0]),
                matrix_product(keyvalue_adapter_first[:, adapter_rank:], keyvalue_adapter_second[1]),
            ],
            axis=1,
        )
    ).astype(jnp.bfloat16)
    output_merged = (
        output_weight.astype(jnp.float32) + matrix_product(output_rows, output_adapter_second)
    ).astype(jnp.bfloat16)
    gate_merged = (
        gateup_weight[0].astype(jnp.float32)
        + matrix_product(gateup_adapter_first[:, :adapter_rank], gateup_piece[0])
    ).astype(jnp.bfloat16)
    up_merged = (
        gateup_weight[1].astype(jnp.float32)
        + matrix_product(gateup_adapter_first[:, adapter_rank:], gateup_piece[1])
    ).astype(jnp.bfloat16)
    down_merged = (
        down_weight.astype(jnp.float32) + matrix_product(down_rows, down_adapter_second)
    ).astype(jnp.bfloat16)
    positions = positions_of(segments)
    key_index = jnp.arange(length, dtype=jnp.int32)
    block_rows = min(512, length)
    normalized_rows, in_back = jax.vjp(rms_scale, inputs, input_norm_gain)
    normalized_lowrank = normalized_rows.astype(jnp.bfloat16)
    query_rows = matrix_product(normalized_lowrank, query_merged)
    keyvalue = matrix_product(normalized_lowrank, keyvalue_merged)

    def prepare(q_in, kv_in, q_scale, k_scale):
        q_heads = rms_scale(q_in.reshape(length, heads_local, head_width), q_scale)
        q_out = rotate(q_heads, positions) * head_width ** (-0.5)
        k_out = rotate(rms_scale(kv_in[:, :head_width], k_scale), positions)
        return (q_out, k_out, kv_in[:, head_width:])

    prepared, prepare_back = jax.vjp(prepare, query_rows, keyvalue, query_norm_gain, key_norm_gain)
    q_rot = prepared[0].astype(jnp.bfloat16)
    k_rot = prepared[1].astype(jnp.bfloat16)
    v_low = prepared[2].astype(jnp.bfloat16)

    def scores_of(row_start):
        rows = q_rot[row_start : row_start + block_rows]
        raw = jnp.einsum("qhd,kd->hqk", rows, k_rot, preferred_element_type=jnp.float32)
        row_index = row_start + jnp.arange(block_rows, dtype=jnp.int32)
        allowed = (segments[row_start : row_start + block_rows][:, None] == segments[None, :]) & (
            row_index[:, None] >= key_index[None, :]
        )
        return jnp.where(allowed[None], raw, MASKED)

    outputs = []
    log_totals = []
    for row_start in range(0, length, block_rows):
        scores = scores_of(row_start)
        row_peak = jnp.max(scores, axis=-1, keepdims=True)
        weights = jnp.exp(scores - row_peak)
        row_total = jnp.sum(weights, axis=-1, keepdims=True)
        log_totals.append(row_peak + jnp.log(row_total))
        probs_low = (weights / row_total).astype(jnp.bfloat16)
        outputs.append(
            jnp.einsum("hqk,kd->qhd", probs_low, v_low, preferred_element_type=jnp.float32)
        )
    attended_rows = (
        jnp.concatenate(outputs, axis=0).reshape(length, query_columns).astype(jnp.bfloat16)
    )
    attention_before = lax.psum(matrix_product(attended_rows, output_merged), "tensor")
    attn_post, post_attn_back = jax.vjp(rms_scale, attention_before, after_attention_gain)
    residual = inputs + attn_post
    normed_ff, pre_ff_back = jax.vjp(rms_scale, residual, before_feedforward_gain)
    feedforward_lowrank = normed_ff.astype(jnp.bfloat16)
    gate_portion = matrix_product(feedforward_lowrank, gate_merged)
    up_portion = matrix_product(feedforward_lowrank, up_merged)
    hidden_full, activate_back = jax.vjp(activate, gate_portion, up_portion)
    hidden_activation = hidden_full.astype(jnp.bfloat16)
    feedforward_before = lax.psum(matrix_product(hidden_activation, down_merged), "tensor")
    mlp_post, post_ff_back = jax.vjp(rms_scale, feedforward_before, after_feedforward_gain)
    result_value = (residual + mlp_post).astype(jnp.bfloat16)[None]
    grad_out = cotangent[0].astype(jnp.float32)
    grad_mlp_pre, gradient_after_feedforward = post_ff_back(grad_out)
    gradient_feedforward_lowrank = grad_mlp_pre.astype(jnp.bfloat16)
    gradient_down_weight = left_transposed(hidden_activation, gradient_feedforward_lowrank)
    grad_hidden = right_transposed(gradient_feedforward_lowrank, down_merged)
    grad_gate, grad_up = activate_back(grad_hidden)
    gate_lowrank = grad_gate.astype(jnp.bfloat16)
    up_lowrank = grad_up.astype(jnp.bfloat16)
    gradient_gateup_weight = jnp.stack(
        [
            left_transposed(feedforward_lowrank, gate_lowrank),
            left_transposed(feedforward_lowrank, up_lowrank),
        ]
    )
    grad_ff_part = right_transposed(gate_lowrank, gate_merged) + right_transposed(
        up_lowrank, up_merged
    )
    grad_normed_ff = lax.psum(grad_ff_part, "tensor")
    grad_residual_ff, gradient_before_feedforward = pre_ff_back(grad_normed_ff)
    grad_residual = grad_out + grad_residual_ff
    grad_attn_pre, gradient_after_attention = post_attn_back(grad_residual)
    gradient_attention_lowrank = grad_attn_pre.astype(jnp.bfloat16)
    gradient_output_weight = left_transposed(attended_rows, gradient_attention_lowrank)
    grad_attended = right_transposed(gradient_attention_lowrank, output_merged).astype(jnp.bfloat16)
    grad_attended = grad_attended.reshape(length, heads_local, head_width)
    grad_q_blocks = []
    grad_k_rot = jnp.zeros((length, head_width), jnp.float32)
    grad_values = jnp.zeros((length, head_width), jnp.float32)
    for block_index, row_start in enumerate(range(0, length, block_rows)):
        scores = scores_of(row_start)
        probs = jnp.exp(scores - log_totals[block_index])
        grad_rows = grad_attended[row_start : row_start + block_rows]
        grad_probs = jnp.einsum("qhd,kd->hqk", grad_rows, v_low, preferred_element_type=jnp.float32)
        grad_scores = (
            probs * (grad_probs - jnp.sum(probs * grad_probs, axis=-1, keepdims=True))
        ).astype(jnp.bfloat16)
        grad_q_blocks.append(
            jnp.einsum("hqk,kd->qhd", grad_scores, k_rot, preferred_element_type=jnp.float32)
        )
        grad_k_rot = grad_k_rot + jnp.einsum(
            "hqk,qhd->kd",
            grad_scores,
            q_rot[row_start : row_start + block_rows],
            preferred_element_type=jnp.float32,
        )
        grad_values = grad_values + jnp.einsum(
            "hqk,qhd->kd", probs.astype(jnp.bfloat16), grad_rows, preferred_element_type=jnp.float32
        )
    grad_queries, grad_keyvalue, gradient_query_norm_gain, gradient_key_norm_gain = prepare_back(
        (jnp.concatenate(grad_q_blocks, axis=0), grad_k_rot, grad_values)
    )
    query_low = grad_queries.astype(jnp.bfloat16)
    keyvalue_gradient_lowrank = grad_keyvalue.astype(jnp.bfloat16)
    gradient_query_weight = left_transposed(normalized_lowrank, query_low)
    gradient_keyvalue_weight = left_transposed(normalized_lowrank, keyvalue_gradient_lowrank)
    grad_in_part = right_transposed(query_low, query_merged) + right_transposed(
        keyvalue_gradient_lowrank, keyvalue_merged
    )
    grad_normed = lax.psum(grad_in_part, "tensor")
    grad_inputs_add, gradient_input_gain = in_back(grad_normed)
    gradient_token_input = (grad_residual + grad_inputs_add)[None]
    lead_mask = (group_position == 0).astype(jnp.float32)
    lead_in = gradient_input_gain * lead_mask
    lead_post_attn = gradient_after_attention * lead_mask
    lead_pre_ff = gradient_before_feedforward * lead_mask
    lead_post_ff = gradient_after_feedforward * lead_mask
    if fast:
        small = jnp.concatenate(
            [lead_in, lead_post_attn, lead_pre_ff, lead_post_ff]
            + [gradient_query_norm_gain, gradient_key_norm_gain]
        ).reshape(-1, 128)
        own, both = reduce_over_chips(
            {
                "d": gradient_down_weight,
                "g": gradient_gateup_weight[0],
                "u": gradient_gateup_weight[1],
                "o": gradient_output_weight,
                "q": gradient_query_weight,
                "k": gradient_keyvalue_weight,
                "s": jnp.pad(small, ((0, 8), (0, 0))),
            }
        )
        width = input_norm_gain.shape[0]
        sums_flat = own["s"].reshape(-1)
        sum_gain_in = sums_flat[:width]
        sum_post_attn = sums_flat[width : 2 * width]
        sum_pre_ff = sums_flat[2 * width : 3 * width]
        sum_post_ff = sums_flat[3 * width : 4 * width]
        sum_query_gain = sums_flat[4 * width : 4 * width + head_width]
        sum_key_gain = sums_flat[4 * width + head_width : 4 * width + 2 * head_width]
        sum_w_keyvalue = own["k"]
        sum_w_query = own["q"]
        sum_w_out = own["o"]
        sum_w_down = own["d"]
        sum_w_gate_up = jnp.stack([own["g"], own["u"]])
    else:
        sum_w_query, sum_w_out, sum_w_gate_up, sum_w_down = lax.psum(
            (
                gradient_query_weight,
                gradient_output_weight,
                gradient_gateup_weight,
                gradient_down_weight,
            ),
            "dp",
        )
        (
            sum_gain_in,
            sum_post_attn,
            sum_pre_ff,
            sum_post_ff,
            sum_query_gain,
            sum_key_gain,
            sum_w_keyvalue,
        ) = lax.psum(
            (
                lead_in,
                lead_post_attn,
                lead_pre_ff,
                lead_post_ff,
                gradient_query_norm_gain,
                gradient_key_norm_gain,
                gradient_keyvalue_weight,
            ),
            ("dp", "tensor"),
        )
    rows_rows = ((0,), (0,))
    columns_columns = ((1,), (1,))
    sum_kv_b = jnp.stack(
        [
            exact_product(
                sum_w_keyvalue[:, i * head_width : (i + 1) * head_width],
                keyvalue_adapter_first[:, i * adapter_rank : (i + 1) * adapter_rank],
                rows_rows,
            ).T
            for i in range(2)
        ]
    )
    sum_kv_a = jnp.concatenate(
        [
            exact_product(
                sum_w_keyvalue[:, i * head_width : (i + 1) * head_width],
                keyvalue_adapter_second[i],
                columns_columns,
            )
            for i in range(2)
        ],
        axis=1,
    )
    if fast:
        groups = range(2)

        def first_rows(array, group, axis=0):
            size = array.shape[axis] // 2
            return lax.slice_in_dim(array, group * size, (group + 1) * size, axis=axis)

        sum_q_b = jnp.concatenate(
            [exact_product(both["q"][g], query_adapter_first, rows_rows).T for g in groups], axis=1
        )
        sum_q_a = sum(
            exact_product(both["q"][g], first_rows(query_adapter_second, g, 1), columns_columns)
            for g in groups
        )
        sum_o_a = jnp.concatenate(
            [exact_product(both["o"][g], output_adapter_second, columns_columns) for g in groups]
        )
        sum_o_b = sum(
            exact_product(both["o"][g], first_rows(output_adapter_first, g), rows_rows).T
            for g in groups
        )
        sum_gu_b = jnp.stack(
            [
                jnp.concatenate(
                    [
                        exact_product(
                            both[name][g],
                            gateup_adapter_first[:, i * adapter_rank : (i + 1) * adapter_rank],
                            rows_rows,
                        ).T
                        for g in groups
                    ],
                    axis=1,
                )
                for i, name in enumerate("gu")
            ]
        )
        sum_gu_a = jnp.concatenate(
            [
                sum(
                    exact_product(
                        both[name][g], first_rows(gateup_adapter_second[i], g, 1), columns_columns
                    )
                    for g in groups
                )
                for i, name in enumerate("gu")
            ],
            axis=1,
        )
        sum_d_a = jnp.concatenate(
            [exact_product(both["d"][g], down_adapter_second, columns_columns) for g in groups]
        )
        sum_d_b = sum(
            exact_product(both["d"][g], first_rows(down_adapter_first, g), rows_rows).T
            for g in groups
        )
    else:
        part_q_b = exact_product(sum_w_query, query_adapter_first, rows_rows).T
        part_q_a = exact_product(sum_w_query, query_piece, columns_columns)
        part_o_a = exact_product(sum_w_out, output_adapter_second, columns_columns)
        part_o_b = exact_product(sum_w_out, output_rows, rows_rows).T
        part_gu_b = jnp.stack(
            [
                exact_product(
                    sum_w_gate_up[i],
                    gateup_adapter_first[:, i * adapter_rank : (i + 1) * adapter_rank],
                    rows_rows,
                ).T
                for i in range(2)
            ]
        )
        part_gu_a = jnp.concatenate(
            [exact_product(sum_w_gate_up[i], gateup_piece[i], columns_columns) for i in range(2)],
            axis=1,
        )
        part_d_a = exact_product(sum_w_down, down_adapter_second, columns_columns)
        part_d_b = exact_product(sum_w_down, down_rows, rows_rows).T
        sum_q_a, sum_o_b, sum_gu_a, sum_d_b = lax.psum(
            (part_q_a, part_o_b, part_gu_a, part_d_b), "tensor"
        )
        sum_q_b = lax.all_gather(part_q_b, "tensor", axis=1, tiled=True)
        sum_o_a = lax.all_gather(part_o_a, "tensor", axis=0, tiled=True)
        sum_gu_b = lax.all_gather(part_gu_b, "tensor", axis=2, tiled=True)
        sum_d_a = lax.all_gather(part_d_a, "tensor", axis=0, tiled=True)
    return (
        result_value,
        gradient_token_input,
        sum_gain_in,
        sum_post_attn,
        sum_pre_ff,
        sum_post_ff,
        sum_query_gain,
        sum_key_gain,
        sum_w_query,
        sum_w_keyvalue,
        sum_w_out,
        sum_w_gate_up,
        sum_w_down,
        sum_q_a,
        sum_q_b,
        sum_kv_a,
        sum_kv_b,
        sum_o_a,
        sum_o_b,
        sum_gu_a,
        sum_gu_b,
        sum_d_a,
        sum_d_b,
    )


def solution(mesh):
    in_specs = (
        P("dp", None, None),
        P("dp", None),
        P(),
        P(),
        P(),
        P(),
        P(),
        P(),
        P(None, "tensor"),
        P(),
        P("tensor", None),
        P(None, None, "tensor"),
        P("tensor", None),
        P(),
        P(),
        P(),
        P(),
        P(),
        P(),
        P(),
        P(),
        P(),
        P(),
        P("dp", None, None),
    )
    out_specs = (
        P("dp", None, None),
        P("dp", None, None),
        P(),
        P(),
        P(),
        P(),
        P(),
        P(),
        P(None, "tensor"),
        P(),
        P("tensor", None),
        P(None, None, "tensor"),
        P("tensor", None),
        P(),
        P(),
        P(),
        P(),
        P(),
        P(),
        P(),
        P(),
        P(),
        P(),
    )
    fast = mesh.shape["dp"] == 16 and mesh.shape["tensor"] == 2
    return jax.shard_map(
        functools.partial(on_device, fast), mesh=mesh, in_specs=in_specs, out_specs=out_specs, check_vma=False
    )
```

```python
import functools

import jax
import jax.numpy as jnp
from jax import lax
from jax.experimental import pallas as pl
from jax.experimental.pallas import tpu as pltpu
from jax.sharding import PartitionSpec as P

EPS = 1e-06
THETA = 1000000.0
MASKED = -1e30


def matrix_product(left_side, right_side):
    return jnp.dot(left_side, right_side, preferred_element_type=jnp.float32)


def left_transposed(left_side, right_side):
    return lax.dot_general(
        left_side, right_side, (((0,), (0,)), ((), ())), preferred_element_type=jnp.float32
    )


def right_transposed(left_side, right_side):
    return lax.dot_general(
        left_side, right_side, (((1,), (1,)), ((), ())), preferred_element_type=jnp.float32
    )


def rms_scale(values, scale_gain):
    return values * lax.rsqrt(jnp.mean(values * values, axis=-1, keepdims=True) + EPS) * scale_gain


def positions_of(segments):
    length = segments.shape[0]
    indices = jnp.arange(length, dtype=jnp.int32)
    before = jnp.concatenate([jnp.full((1,), -1, jnp.int32), segments[:-1]])
    starts = lax.cummax(jnp.where(segments != before, indices, jnp.zeros_like(indices)), axis=0)
    return indices - starts


def rotation_of(positions, head_width):
    half_dim = head_width // 2
    frequency = THETA ** (-jnp.arange(half_dim, dtype=jnp.float32) * 2.0 / head_width)
    angles = positions.astype(jnp.float32)[:, None] * frequency[None, :]
    return jnp.cos(angles), jnp.sin(angles)


def rotate(values, rotation):
    half_dim = values.shape[-1] // 2
    cosine, sine_part = rotation
    if values.ndim == 3:
        cosine = cosine[:, None, :]
        sine_part = sine_part[:, None, :]
    leading = values[..., :half_dim]
    trailing = values[..., half_dim:]
    return jnp.concatenate(
        [leading * cosine - trailing * sine_part, trailing * cosine + leading * sine_part], axis=-1
    )


def exact_product(left_side, right_side, contract):
    return lax.dot_general(
        left_side,
        right_side.astype(jnp.float32),
        (contract, ((), ())),
        precision=lax.Precision.HIGHEST,
        preferred_element_type=jnp.float32,
    )


def activate(gate_in, up_in):
    return jax.nn.gelu(gate_in, approximate=True) * up_in


MESH_ID = pl.DeviceIdType.MESH


class Place:
    def __init__(self):
        me = lax.axis_index("dp")
        core = lax.axis_index("tensor")
        bit_x = lax.rem(me, 2)
        bit_y = lax.rem(me // 2, 2)
        level = me // 4
        across_x = me + 1 - 2 * bit_x
        across_y = me + 2 - 4 * bit_y
        self.core = core
        self.side = level // 2
        self.level = level
        self.outer = jnp.logical_or(level == 0, level == 3)
        self.inner = jnp.logical_not(self.outer)
        self.bits = (jnp.where(core == 0, bit_x, bit_y), jnp.where(core == 0, bit_y, bit_x))
        self.across = (
            (jnp.where(core == 0, across_x, across_y), core),
            (jnp.where(core == 0, across_y, across_x), core),
        )
        column = lax.rem(me, 4)
        self.near = ((level + 1 - 2 * lax.rem(level, 2)) * 4 + column, core)
        self.middle = ((3 - level) * 4 + column, core)
        self.sibling = (me, 1 - core)


def add_rows(target, target_row, extra, extra_row, count):
    step = 32 if count % 32 == 0 else (16 if count % 16 == 0 else 8)

    def body(index, carry):
        rows = pl.ds(pl.multiple_of(target_row + index * step, 8), step)
        target[rows] = target[rows] + extra[pl.ds(pl.multiple_of(extra_row + index * step, 8), step)]
        return carry

    lax.fori_loop(0, count // step, body, 0)


class Sums:
    def __init__(self, place, sends, receives, freed):
        self.place = place
        self.sends = sends
        self.receives = receives
        self.freed = freed
        self.used = 0
        self.credits = 0

    def credit(self):
        self.credits += 1
        return self.freed.at[self.credits - 1]

    def copy(self, source, target, device):
        slot = self.used
        self.used += 1
        return pltpu.make_async_remote_copy(
            src_ref=source,
            dst_ref=target,
            send_sem=self.sends.at[slot],
            recv_sem=self.receives.at[slot],
            device_id=device,
            device_id_type=MESH_ID,
        )


def signal(semaphore, device):
    pl.semaphore_signal(semaphore, inc=1, device_id=device, device_id_type=MESH_ID)


def rows_at(ref, start, count):
    return ref.at[pl.ds(pl.multiple_of(start, 8), count)]


def plane_first(sums, total, row, count, landing, landing_row, finish, turned):
    place = sums.place
    half, quarter = count // 2, count // 4
    bit_one, bit_two = place.bits[turned], place.bits[1 - turned]
    one, two = place.across[turned], place.across[1 - turned]
    kept = row + bit_one * half
    given = row + (1 - bit_one) * half
    mine = kept + bit_two * quarter
    other = kept + (1 - bit_two) * quarter
    land_one = rows_at(landing, landing_row, half)
    land_two = rows_at(landing, landing_row + half, quarter)
    land_near = rows_at(landing, landing_row + half + quarter, quarter)
    land_mid = rows_at(landing, landing_row + 2 * half, quarter)
    ours = rows_at(total, mine, quarter)
    copy_one = sums.copy(rows_at(total, given, half), land_one, one)
    copy_two = sums.copy(rows_at(total, other, quarter), land_two, two)
    copy_in = sums.copy(ours, land_near, place.near)
    copy_mid = sums.copy(ours, land_mid, place.middle)
    copy_out = sums.copy(ours, ours, place.near)
    back_two = sums.copy(ours, ours, two)
    back_one = sums.copy(rows_at(total, kept, half), rows_at(total, kept, half), one)

    free_one, free_two, free_in = sums.credit(), sums.credit(), sums.credit()

    def step0():
        copy_one.start()

    def step1():
        copy_one.wait_recv()
        add_rows(total, kept, landing, landing_row, half)
        copy_two.start()

    def step2():
        copy_two.wait_recv()
        add_rows(total, mine, landing, landing_row + half, quarter)

        @pl.when(place.outer)
        def _():
            copy_in.start()

        copy_one.wait_send()
        signal(free_one, one)

    def step3():
        @pl.when(place.inner)
        def _():
            copy_in.wait_recv()
            add_rows(total, mine, landing, landing_row + half + quarter, quarter)
            copy_mid.start()

        copy_two.wait_send()
        signal(free_two, two)

        @pl.when(place.outer)
        def _():
            copy_in.wait_send()
            signal(free_in, place.near)

    def step4():
        @pl.when(place.inner)
        def _():
            copy_mid.wait()
            add_rows(total, mine, landing, landing_row + 2 * half, quarter)
            pl.semaphore_wait(free_in, 1)
            copy_out.start()
            pl.semaphore_wait(free_two, 1)
            back_two.start()

    def step5():
        @pl.when(place.outer)
        def _():
            copy_out.wait_recv()
            pl.semaphore_wait(free_two, 1)
            back_two.start()

    def step6():
        back_two.wait_recv()
        pl.semaphore_wait(free_one, 1)
        back_one.start()

    def step7():
        back_one.wait_recv()
        back_two.wait_send()
        back_one.wait_send()

        @pl.when(place.inner)
        def _():
            copy_out.wait_send()

        finish()

    return [step0, step1, step2, step3, step4, step5, step6, step7]


def line_first(sums, total, row, count, landing, landing_row, finish, turned):
    place = sums.place
    one, two = place.across[turned], place.across[1 - turned]
    quarter = count // 4
    side = place.side
    three = row + (1 - side) * quarter
    far_pair = row + (1 - side) * 2 * quarter
    own_pair = row + side * 2 * quarter
    outer_quarter = row + 3 * side * quarter
    mine = row + place.level * quarter
    ours = rows_at(total, mine, quarter)
    land_three = rows_at(landing, landing_row, 3 * quarter)
    land_pair = rows_at(landing, landing_row + 3 * quarter, 2 * quarter)
    land_back = rows_at(landing, landing_row, quarter)
    land_one = rows_at(landing, landing_row + 5 * quarter, quarter)
    land_two = rows_at(landing, landing_row + 6 * quarter, quarter)
    copy_three = sums.copy(rows_at(total, three, 3 * quarter), land_three, place.near)
    copy_pair = sums.copy(rows_at(total, far_pair, 2 * quarter), land_pair, place.middle)
    outers = rows_at(total, outer_quarter, quarter)
    copy_back = sums.copy(outers, land_back, place.near)
    copy_one = sums.copy(ours, land_one, one)
    copy_two = sums.copy(ours, land_two, two)
    spread_in = sums.copy(ours, ours, place.near)
    spread_out = sums.copy(ours, ours, place.near)
    spread_mid = sums.copy(ours, ours, place.middle)
    forward_mid = sums.copy(outers, outers, place.middle)
    far_rows = rows_at(total, far_pair, 2 * quarter)
    forward_out = sums.copy(far_rows, far_rows, place.near)

    free_three, free_pair, free_back = sums.credit(), sums.credit(), sums.credit()

    def step0():
        @pl.when(place.outer)
        def _():
            copy_three.start()

    def step1():
        @pl.when(place.inner)
        def _():
            copy_three.wait_recv()
            add_rows(total, three, landing, landing_row, 3 * quarter)
            copy_pair.start()

    def step2():
        @pl.when(place.inner)
        def _():
            copy_pair.wait_recv()
            add_rows(total, own_pair, landing, landing_row + 3 * quarter, 2 * quarter)
            copy_back.start()
            copy_one.start()

    def step3():
        @pl.when(place.outer)
        def _():
            copy_back.wait_recv()
            add_rows(total, mine, landing, landing_row, quarter)
            copy_one.start()
            copy_three.wait_send()
            signal(free_three, place.near)

        @pl.when(place.inner)
        def _():
            copy_pair.wait_send()
            signal(free_pair, place.middle)
            copy_back.wait_send()
            signal(free_back, place.near)

    def step4():
        copy_one.wait()
        add_rows(total, mine, landing, landing_row + 5 * quarter, quarter)
        copy_two.start()

    def step5():
        copy_two.wait()
        add_rows(total, mine, landing, landing_row + 6 * quarter, quarter)

        @pl.when(place.outer)
        def _():
            pl.semaphore_wait(free_back, 1)
            spread_in.start()

        @pl.when(place.inner)
        def _():
            pl.semaphore_wait(free_three, 1)
            spread_out.start()
            pl.semaphore_wait(free_pair, 1)
            spread_mid.start()

    def step6():
        @pl.when(place.inner)
        def _():
            spread_in.wait_recv()
            forward_mid.start()

    def step7():
        @pl.when(place.inner)
        def _():
            spread_mid.wait_recv()
            forward_mid.wait_recv()
            forward_out.start()

    def step8():
        @pl.when(place.outer)
        def _():
            spread_out.wait_recv()
            forward_out.wait_recv()
            spread_in.wait_send()

        @pl.when(place.inner)
        def _():
            spread_out.wait_send()
            spread_mid.wait_send()
            forward_mid.wait_send()
            forward_out.wait_send()

        finish()

    return [step0, step1, step2, step3, step4, step5, step6, step7, step8]


def greet(place):
    barrier = pltpu.get_barrier_semaphore()
    for device in (*place.across, place.near, place.sibling):
        pl.semaphore_signal(barrier, inc=1, device_id=device, device_id_type=MESH_ID)

    @pl.when(place.inner)
    def _():
        pl.semaphore_signal(barrier, inc=1, device_id=place.middle, device_id_type=MESH_ID)
        pl.semaphore_wait(barrier, 5)

    @pl.when(place.outer)
    def _():
        pl.semaphore_wait(barrier, 4)

ANYWHERE = pl.BlockSpec(memory_space=pl.ANY)


def landing_rows(kind, count):
    return count // 4 * (5 if kind == "P" else 7)


ROWS = 256


def row_loop(count, body, start=0):
    def step(index, carry):
        body(pl.ds(pl.multiple_of(index * ROWS, ROWS), ROWS), index)
        return carry

    lax.fori_loop(start, count, step, 0)


def inverse_rms(values):
    return lax.rsqrt(jnp.mean(values * values, axis=-1, keepdims=True) + EPS)


def rms_back(incoming, gain, normed, inverse):
    scaled = incoming * gain
    return inverse * (scaled - normed * jnp.mean(scaled * normed, axis=-1, keepdims=True))


def add_gain(target, terms):
    width = terms.shape[1]
    target[...] = target[...] + jnp.sum(terms.reshape(-1, 8, width), axis=0)


def gelu_parts(gate):
    inner = 0.7978845608028654 * gate * (1.0 + 0.044715 * gate * gate)
    bent = jnp.tanh(inner)
    half = 0.5 * (1.0 + bent)
    slope = half + 0.5 * gate * (1.0 - bent * bent) * 0.7978845608028654 * (
        1.0 + 0.134145 * gate * gate
    )
    return gate * half, slope


def turn_back(values, cosine, sine):
    half = values.shape[1] // 2
    leading, trailing = values[:, :half], values[:, half:]
    return jnp.concatenate(
        [leading * cosine + trailing * sine, trailing * cosine - leading * sine], axis=1
    )


def backward_kernel(setup, *refs):
    plan, order, inputs, split = setup
    refs = list(refs)

    def take(keys):
        return {key: refs.pop(0) for key in keys}

    names = [entry[0] for entry in plan]
    source = take(inputs)
    out_home, token_home = refs.pop(0), refs.pop(0)
    own = take("ks")
    both = take(split)
    held = take(inputs)
    total = take(names)
    landing = take(names)
    swapped = take("ks")
    work = take(["low", "gate", "up", "part", "other", "dq", "gains", "gain_q", "gain_k", "result"])
    loads, sends, receives, local, freed, handed = refs
    place = Place()
    core = place.core
    sums = Sums(place, sends, receives, freed)
    arrivals = {
        name: pltpu.make_async_copy(source[name], held[name], loads.at[index])
        for index, name in enumerate(inputs)
    }
    for name in inputs:
        arrivals[name].start()
    greet(place)
    length = held["attn"].shape[0]
    blocks = length // ROWS
    width = held["attn"].shape[1]
    head = held["k_rot"].shape[1]
    heads = held["q_rot"].shape[1] // head
    hidden_columns = held["hidden"].shape[1]
    here = set()

    def need(*keys):
        for key in keys:
            if key not in here:
                here.add(key)
                arrivals[key].wait()

    for name in ("gains", "gain_q", "gain_k"):
        work[name][...] = jnp.zeros_like(work[name])
    gain_in, gain_pa, gain_pf, gain_pff = (work["gains"].at[i] for i in range(4))
    low, part, other = work["low"], work["part"], work["other"]
    leaving = []

    def residual_of(rows):
        attn = held["attn"][rows, :]
        inverse = inverse_rms(attn)
        normed = attn * inverse
        return held["tokens"][rows, :].astype(jnp.float32) + normed * held["pa"][...], normed, inverse

    def finish_forward():
        need("mlp", "attn", "tokens", "cot", "pa", "pff")

        def body(rows, index):
            residual, _, _ = residual_of(rows)
            mlp = held["mlp"][rows, :]
            inverse = inverse_rms(mlp)
            normed = mlp * inverse
            work["result"][rows, :] = (residual + normed * held["pff"][...]).astype(jnp.bfloat16)
            incoming = held["cot"][rows, :].astype(jnp.float32)
            add_gain(gain_pff, incoming * normed)
            low[rows, :] = rms_back(incoming, held["pff"][...], normed, inverse).astype(jnp.bfloat16)

        row_loop(blocks, body)
        move = pltpu.make_async_copy(work["result"], out_home, local.at[0])
        move.start()
        leaving.append(move)

    def down_gradient():
        need("hidden")
        for index in range(hidden_columns // ROWS):
            columns = pl.ds(index * ROWS, ROWS)
            total["d"][columns, :] = left_transposed(held["hidden"][:, columns], low[...])

    def gate_block(index):
        def run():
            need("ff", "w_g", "w_u", "w_d")
            columns = pl.ds(index * ROWS, ROWS)

            def body(rows, _):
                entering = held["ff"][rows, :]
                gate = matrix_product(entering, held["w_g"][:, columns])
                up = matrix_product(entering, held["w_u"][:, columns])
                incoming = right_transposed(low[rows, :], held["w_d"][columns, :])
                bent, slope = gelu_parts(gate)
                grad_gate = (incoming * up * slope).astype(jnp.bfloat16)
                grad_up = (incoming * bent).astype(jnp.bfloat16)
                work["gate"][rows, :] = grad_gate
                work["up"][rows, :] = grad_up
                share = right_transposed(grad_gate, held["w_g"][:, columns]) + right_transposed(
                    grad_up, held["w_u"][:, columns]
                )
                part[rows, :] = share if index == 0 else part[rows, :] + share

            row_loop(blocks, body)
            total["g"][:, columns] = left_transposed(held["ff"][...], work["gate"][...])
            total["u"][:, columns] = left_transposed(held["ff"][...], work["up"][...])

        return run

    exchange = {}

    def send_parts(key):
        copies = []
        for index in range(blocks):
            rows = pl.ds(index * ROWS, ROWS)
            copies.append(sums.copy(part.at[rows], other.at[rows], place.sibling))
        for copy in copies:
            copy.start()
        exchange[key] = copies

    def residual_back():
        need("pf", "w_o")
        for index in range(blocks):
            exchange["ff"][index].wait_recv()
            rows = pl.ds(index * ROWS, ROWS)
            residual, normed_attn, inverse_attn = residual_of(rows)
            incoming = part[rows, :] + other[rows, :]
            inverse = inverse_rms(residual)
            normed = residual * inverse
            add_gain(gain_pf, incoming * normed)
            grad = held["cot"][rows, :].astype(jnp.float32) + rms_back(
                incoming, held["pf"][...], normed, inverse
            )
            held["mlp"][rows, :] = grad
            add_gain(gain_pa, grad * normed_attn)
            low[rows, :] = rms_back(grad, held["pa"][...], normed_attn, inverse_attn).astype(
                jnp.bfloat16
            )
        for copy in exchange["ff"]:
            copy.wait_send()
        signal(handed, place.sibling)
        grad_attended = held["ff"]

        def body(rows, _):
            grad_attended[rows, : heads * head] = right_transposed(
                low[rows, :], held["w_o"][...]
            ).astype(jnp.bfloat16)

        row_loop(blocks, body)

    def output_gradient():
        need("attended")
        for index in range(heads * head // ROWS):
            columns = pl.ds(index * ROWS, ROWS)
            total["o"][columns, :] = left_transposed(held["attended"][:, columns], low[...])

    grad_key = held["attn"].at[:, :head]
    grad_value = held["attn"].at[:, head : 2 * head]
    grad_query_low = held["hidden"].at[:, : heads * head]
    grad_keyvalue_low = held["hidden"].at[:, heads * head : heads * head + 2 * head]

    def attention_rows(which, start, stop):
        def run():
            need("q_rot", "k_rot", "values", "seg_c", "seg_r", "lse", "cos", "sin", "normed", "w_q")
            need("gq")
            columns = pl.ds(which * head, head)
            if which == 0 and start == 0:
                held["attn"][...] = jnp.zeros_like(held["attn"])

            def body(rows, index):
                query = held["q_rot"][rows, columns]
                grad = held["ff"][rows, columns]
                attended = held["attended"][rows, columns]
                weight = jnp.sum(
                    grad.astype(jnp.float32) * attended.astype(jnp.float32), axis=1, keepdims=True
                )
                lse = held["lse"][which, rows, :]
                segment = held["seg_c"][rows, :]
                work["dq"][...] = jnp.zeros_like(work["dq"])

                def inner(at, carry):
                    others = pl.ds(pl.multiple_of(at * ROWS, ROWS), ROWS)
                    key = held["k_rot"][others, :]
                    value = held["values"][others, :]
                    scores = right_transposed(query, key)
                    row_index = index * ROWS + lax.broadcasted_iota(jnp.int32, scores.shape, 0)
                    column_index = at * ROWS + lax.broadcasted_iota(jnp.int32, scores.shape, 1)
                    allowed = (segment == held["seg_r"][at]) & (row_index >= column_index)
                    probs = jnp.where(allowed, jnp.exp(scores - lse), 0.0)
                    grad_probs = right_transposed(grad, value)
                    grad_scores = (probs * (grad_probs - weight)).astype(jnp.bfloat16)
                    work["dq"][...] += matrix_product(grad_scores, key)
                    grad_key[others, :] = grad_key[others, :] + left_transposed(grad_scores, query)
                    grad_value[others, :] = grad_value[others, :] + left_transposed(
                        probs.astype(jnp.bfloat16), grad
                    )
                    return carry

                lax.fori_loop(0, index + 1, inner, 0)
                turned = turn_back(work["dq"][...], held["cos"][rows, :], held["sin"][rows, :])
                turned = turned * head ** (-0.5)
                raw = matrix_product(held["normed"][rows, :], held["w_q"][:, columns])
                inverse = inverse_rms(raw)
                normed = raw * inverse
                add_gain(work["gain_q"], turned * normed)
                grad_query_low[rows, columns] = rms_back(
                    turned, held["gq"][...], normed, inverse
                ).astype(jnp.bfloat16)

            row_loop(stop, body, start)

        return run

    def key_back():
        need("w_kv", "gk")

        def body(rows, _):
            turned = turn_back(grad_key[rows, :], held["cos"][rows, :], held["sin"][rows, :])
            raw = matrix_product(held["normed"][rows, :], held["w_kv"][:, :head])
            inverse = inverse_rms(raw)
            normed = raw * inverse
            add_gain(work["gain_k"], turned * normed)
            grad_keyvalue_low[rows, :head] = rms_back(
                turned, held["gk"][...], normed, inverse
            ).astype(jnp.bfloat16)
            grad_keyvalue_low[rows, head:] = grad_value[rows, :].astype(jnp.bfloat16)

        row_loop(blocks, body)

    def query_gradient():
        for index in range(heads * head // ROWS):
            columns = pl.ds(index * ROWS, ROWS)
            total["q"][:, columns] = left_transposed(held["normed"][...], grad_query_low[:, columns])

    half_rows = swapped["k"].shape[0]
    swaps = {}

    def keyvalue_gradient():
        for index in range(2 * head // ROWS):
            columns = pl.ds(index * ROWS, ROWS)
            total["k"][:, columns] = left_transposed(
                held["normed"][...], grad_keyvalue_low[:, columns]
            )
        swaps["k"] = sums.copy(
            rows_at(total["k"], (1 - core) * half_rows, half_rows), swapped["k"], place.sibling
        )
        swaps["k"].start()

    def input_parts():
        def body(rows, _):
            part[rows, :] = right_transposed(
                grad_query_low[rows, :], held["w_q"][...]
            ) + right_transposed(grad_keyvalue_low[rows, :], held["w_kv"][...])

        row_loop(blocks, body)
        pl.semaphore_wait(handed, 1)
        send_parts("in")

    def input_back():
        need("gin")
        for index in range(blocks):
            exchange["in"][index].wait_recv()
            rows = pl.ds(index * ROWS, ROWS)
            incoming = part[rows, :] + other[rows, :]
            tokens = held["tokens"][rows, :].astype(jnp.float32)
            inverse = inverse_rms(tokens)
            normed = tokens * inverse
            add_gain(gain_in, incoming * normed)
            held["mlp"][rows, :] = held["mlp"][rows, :] + rms_back(
                incoming, held["gin"][...], normed, inverse
            )
            move = pltpu.make_async_copy(held["mlp"].at[rows], token_home.at[rows], local.at[1 + index])
            move.start()
            leaving.append(move)
        for copy in exchange["in"]:
            copy.wait_send()
        small = total["s"]
        small[...] = jnp.zeros_like(small)
        lead = jnp.where(core == 0, 1.0, 0.0)
        row = 0
        for index in range(4):
            vector = jnp.sum(work["gains"][index], axis=0, keepdims=True) * lead
            for at in range(width // 128):
                small[row : row + 1, :] = vector[:, at * 128 : (at + 1) * 128]
                row += 1
        for name in ("gain_q", "gain_k"):
            vector = jnp.sum(work[name][...], axis=0, keepdims=True)
            for at in range(head // 128):
                small[row : row + 1, :] = vector[:, at * 128 : (at + 1) * 128]
                row += 1
        swaps["s"] = sums.copy(small, swapped["s"], place.sibling)
        swaps["s"].start()

    tasks = {
        "C0": lambda: (finish_forward(), down_gradient()),
        "G0": gate_block(0),
        "G1": gate_block(1),
        "G2": gate_block(2),
        "G3": lambda: (gate_block(3)(), send_parts("ff")),
        "R": residual_back,
        "O": output_gradient,
        "A0": attention_rows(0, 0, 3),
        "A1": attention_rows(0, 3, 4),
        "A2": attention_rows(1, 0, 3),
        "A3": attention_rows(1, 3, 4),
        "K": key_back,
        "WK": keyvalue_gradient,
        "WQ": query_gradient,
        "I0": input_parts,
        "I1": input_back,
    }
    chunks = []
    slots = 1 + blocks
    for name, rows, columns, parts in plan:
        row = 0
        land_row = 0
        base = core * half_rows if name == "k" else 0
        for kind, count, turned in parts:

            def finish(name=name, row=row, base=base, count=count, slot=slots):
                done = rows_at(total[name], base + row, count)
                if name == "s":
                    moves = [pltpu.make_async_copy(done, own["s"], local.at[slot])]
                else:
                    if name == "k":
                        home = rows_at(own["k"], base + row, count)
                    else:
                        home = both[name].at[core, pl.ds(row, count)]
                    moves = [
                        pltpu.make_async_copy(done, home, local.at[slot]),
                        sums.copy(done, home, place.sibling),
                    ]
                for move in moves:
                    move.start()
                leaving.extend(moves)

            build = plane_first if kind == "P" else line_first
            steps = build(
                sums, total[name], base + row, count, landing[name], land_row, finish, turned
            )
            if name in "ks":

                def enter(name=name, base=base, first=steps[0]):
                    if name in swaps:
                        swaps.pop(name).wait()
                        add_rows(total[name], base, swapped[name], 0, swapped[name].shape[0])
                    first()

                steps = [enter] + steps[1:]
            chunks.append(steps)
            slots += 1
            row += count
            land_row += landing_rows(kind, count)
    for entry in order:
        if isinstance(entry, str):
            tasks[entry]()
        else:
            chunks[entry[0]][entry[1]]()
    for move in leaving:
        move.wait()


CUTS = {
    "d": (("L", 320, 0), ("P", 384, 0), ("P", 320, 1)),
    "g": (("L", 96, 1), ("P", 128, 0), ("L", 96, 0), ("P", 224, 1), ("P", 96, 0)),
    "u": (("L", 192, 0), ("P", 192, 0), ("P", 96, 0), ("P", 160, 1)),
    "o": (("L", 224, 0), ("P", 288, 0)),
    "q": (("L", 128, 1), ("P", 288, 1), ("P", 224, 0)),
    "k": (("P", 128, 1), ("P", 192, 1)),
    "s": (("P", 32, 0),),
}
ORDER = (
    "C0", (1, 0), (0, 0), "G0", "G1", "G2", "G3", (3, 0), (4, 0), (1, 1), (2, 0), (4, 1), (6, 0),
    (0, 1), (1, 2), (10, 0), (2, 1), (5, 0), (0, 2), (3, 1), (4, 2), (9, 0), (2, 2), (0, 3),
    (1, 3), (3, 2), (5, 1), (7, 0), (3, 3), (0, 4), (4, 3), (1, 4), (5, 2), (2, 3), (8, 0),
    (6, 1), "R", "O", (13, 0), (7, 1), (0, 5), (1, 5), (3, 4), (10, 1), (2, 4), (5, 3), (6, 2),
    (9, 1), (7, 2), (2, 5), (8, 1), (9, 2), (5, 4), (1, 6), "A0", "A1", "A2", "A3", "K", "WK",
    "WQ", (14, 0), (0, 6), (11, 0), (3, 5), (4, 4), (2, 6), (4, 5), (5, 5), (7, 3), (12, 0),
    (6, 3), (8, 2), (0, 7), (11, 1), (7, 4), (15, 0), (9, 3), (10, 2), (13, 1), (6, 4), (8, 3),
    (3, 6), (14, 1), (3, 7), (11, 2), (9, 4), (8, 4), (12, 1), (5, 6), (18, 0), (0, 8), (4, 6),
    (7, 5), (15, 1), (13, 2), "I0", "I1", (19, 0), (10, 3), (1, 7), (6, 5), (12, 2), (2, 7),
    (3, 8), (15, 2), (4, 7), (5, 7), (14, 2), (16, 0), (11, 3), (13, 3), (17, 0), (6, 6), (7, 6),
    (10, 4), (11, 4), (9, 5), (8, 5), (18, 1), (12, 3), (7, 7), (16, 1), (11, 5), (17, 1), (9, 6),
    (14, 3), (12, 4), (13, 4), (8, 6), (10, 5), (19, 1), (8, 7), (17, 2), (15, 3), (6, 7),
    (18, 2), (16, 2), (15, 4), (13, 5), (12, 5), (14, 4), (16, 3), (10, 6), (11, 6), (18, 3),
    (9, 7), (15, 5), (17, 3), (17, 4), (16, 4), (18, 4), (19, 2), (13, 6), (10, 7), (12, 6),
    (19, 3), (15, 6), (17, 5), (14, 5), (19, 4), (12, 7), (18, 5), (14, 6), (8, 8), (14, 7),
    (16, 5), (11, 7), (17, 6), (16, 6), (5, 8), (19, 5), (18, 6), (13, 7), (12, 8), (19, 6),
    (15, 7), (17, 7), (16, 7), (14, 8), (19, 7), (18, 7),
)


def backward_and_sums(values, shapes, order, cuts):
    length, width = values["tokens"].shape
    head = values["k_rot"].shape[1]
    plan = [(name, *shape, cuts[name]) for name, shape in shapes.items()]
    split = [name for name in shapes if name not in "ks"]
    inputs = list(values)
    outs = [
        jax.ShapeDtypeStruct((length, width), jnp.bfloat16),
        jax.ShapeDtypeStruct((length, width), jnp.float32),
    ]
    outs += [jax.ShapeDtypeStruct(shapes[name], jnp.float32) for name in "ks"]
    outs += [jax.ShapeDtypeStruct((2,) + shapes[name], jnp.float32) for name in split]
    scratch = [pltpu.VMEM(array.shape, array.dtype) for array in values.values()]
    scratch += [pltpu.VMEM(shape, jnp.float32) for shape in shapes.values()]
    scratch += [
        pltpu.VMEM((sum(landing_rows(kind, count) for kind, count, _ in parts), columns), jnp.float32)
        for _, _, columns, parts in plan
    ]
    half = (shapes["k"][0] // 2, shapes["k"][1])
    scratch += [pltpu.VMEM(half, jnp.float32), pltpu.VMEM(shapes["s"], jnp.float32)]
    count = sum(len(parts) for _, _, _, parts in plan)
    blocks = length // ROWS
    scratch += [
        pltpu.VMEM((length, width), jnp.bfloat16),
        pltpu.VMEM((length, ROWS), jnp.bfloat16),
        pltpu.VMEM((length, ROWS), jnp.bfloat16),
        pltpu.VMEM((length, width), jnp.float32),
        pltpu.VMEM((length, width), jnp.float32),
        pltpu.VMEM((ROWS, head), jnp.float32),
        pltpu.VMEM((4, 8, width), jnp.float32),
        pltpu.VMEM((8, head), jnp.float32),
        pltpu.VMEM((8, head), jnp.float32),
        pltpu.VMEM((length, width), jnp.bfloat16),
        pltpu.SemaphoreType.DMA((len(inputs),)),
        pltpu.SemaphoreType.DMA((count * 11 + 2 * blocks + 4,)),
        pltpu.SemaphoreType.DMA((count * 11 + 2 * blocks + 4,)),
        pltpu.SemaphoreType.DMA((count + blocks + 2,)),
        pltpu.SemaphoreType.REGULAR((count * 3,)),
        pltpu.SemaphoreType.REGULAR,
    ]
    results = pl.pallas_call(
        functools.partial(backward_kernel, (plan, order, inputs, split)),
        out_shape=outs,
        in_specs=[ANYWHERE] * len(inputs),
        out_specs=[ANYWHERE] * len(outs),
        scratch_shapes=scratch,
        compiler_params=pltpu.CompilerParams(
            collective_id=0, has_side_effects=True, vmem_limit_bytes=67043328
        ),
    )(*values.values())
    own = dict(zip("ks", results[2:4]))
    both = dict(zip(split, results[4:]))
    return results[0], results[1], own, both


def derive_kernel(names, *refs):
    refs = list(refs)

    def take(keys):
        return {key: refs.pop(0) for key in keys}

    source = take(names["sums"] + names["weights"])
    target = take(names["outs"])
    held = take(names["sums"] + names["weights"])
    made = take(names["made"])
    loaded, stored = refs
    core = lax.axis_index("tensor")
    arrivals = {}
    for index, name in enumerate(names["sums"] + names["weights"]):
        arrivals[name] = pltpu.make_async_copy(source[name], held[name], loaded.at[index])
    order = ["down_a", "down_b", "d", "gateup_a", "gateup_b", "g", "u"]
    order += ["output_a", "output_b", "o", "query_a", "query_b", "q", "keyvalue_a", "keyvalue_b", "k"]
    for name in order:
        arrivals[name].start()
    arrived = set()
    leaving = []

    def need(*keys):
        for key in keys:
            if key not in arrived:
                arrived.add(key)
                arrivals[key].wait()

    def leave(piece, home):
        move = pltpu.make_async_copy(piece, home, stored.at[len(leaving)])
        move.start()
        leaving.append(move)

    def factors(total, first, second, out_first, out_second, add_first=False, add_second=False):
        count, columns = total.shape
        step = 256 if count % 256 == 0 else 320
        width = 512 if columns % 512 == 0 else columns // 2
        if not add_second:
            out_second[...] = jnp.zeros(out_second.shape, jnp.float32)
        for at in range(columns // width):
            part = pl.ds(at * width, width)

            def body(index, carry):
                block = pl.ds(pl.multiple_of(index * step, 64), step)
                value = total[block, part]
                high = value.astype(jnp.bfloat16)
                low = (value - high.astype(jnp.float32)).astype(jnp.bfloat16)
                other = second[:, part]
                product = right_transposed(high, other) + right_transposed(low, other)
                if add_first or at > 0:
                    product = product + out_first[block, :]
                out_first[block, :] = product
                this = first[block, :]
                out_second[:, part] = (
                    out_second[:, part] + left_transposed(this, high) + left_transposed(this, low)
                )
                return carry

            lax.fori_loop(0, count // step, body, 0)

    rank = made["query_a"].shape[1]

    def columns_of(ref, part, size):
        return ref.at[:, pl.ds(part * size, size)]

    def rows_of(ref, part, size):
        return ref.at[pl.ds(part * size, size)]

    need("down_a", "down_b", "d")
    leave(held["d"].at[core], target["down"])
    for group in range(2):
        total = held["d"].at[group]
        size = total.shape[0]
        first = rows_of(held["down_a"], group, size)
        out = rows_of(made["down_a"], group, size)
        factors(total, first, held["down_b"], out, made["down_b"], False, group > 0)
    leave(made["down_a"], target["down_a"])
    leave(made["down_b"], target["down_b"])
    need("gateup_a", "gateup_b")
    for part, name in enumerate("gu"):
        need(name)
        leave(held[name].at[core], target["gateup"].at[part])
        for group in range(2):
            total = held[name].at[group]
            size = total.shape[1]
            second = columns_of(held["gateup_b"].at[part], group, size)
            first = columns_of(held["gateup_a"], part, rank)
            out_first = columns_of(made["gateup_a"], part, rank)
            out_second = columns_of(made["gateup_b"].at[part], group, size)
            factors(total, first, second, out_first, out_second, group > 0, False)
        leave(made["gateup_b"].at[part], target["gateup_b"].at[part])
    leave(made["gateup_a"], target["gateup_a"])
    need("output_a", "output_b", "o")
    leave(held["o"].at[core], target["output"])
    for group in range(2):
        total = held["o"].at[group]
        size = total.shape[0]
        first = rows_of(held["output_a"], group, size)
        out = rows_of(made["output_a"], group, size)
        factors(total, first, held["output_b"], out, made["output_b"], False, group > 0)
    leave(made["output_a"], target["output_a"])
    leave(made["output_b"], target["output_b"])
    need("query_a", "query_b", "q")
    leave(held["q"].at[core], target["query"])
    for group in range(2):
        total = held["q"].at[group]
        size = total.shape[1]
        second = columns_of(held["query_b"], group, size)
        out = columns_of(made["query_b"], group, size)
        factors(total, held["query_a"], second, made["query_a"], out, group > 0, False)
    leave(made["query_a"], target["query_a"])
    leave(made["query_b"], target["query_b"])
    need("keyvalue_a", "keyvalue_b", "k")
    leave(held["k"], target["keyvalue"])
    for part in range(2):
        width = made["keyvalue_b"].shape[2]
        total = columns_of(held["k"], part, width)
        out = columns_of(made["keyvalue_a"], part, rank)
        first = columns_of(held["keyvalue_a"], part, rank)
        factors(total, first, held["keyvalue_b"].at[part], out, made["keyvalue_b"].at[part])
    leave(made["keyvalue_a"], target["keyvalue_a"])
    leave(made["keyvalue_b"], target["keyvalue_b"])
    for move in leaving:
        move.wait()


def derive_adapters(sums, weights):
    made = {name: weights[name] for name in weights}
    plain = {
        "down": sums["d"].shape[1:],
        "gateup": (2,) + sums["g"].shape[1:],
        "output": sums["o"].shape[1:],
        "query": sums["q"].shape[1:],
        "keyvalue": sums["k"].shape,
    }
    names = {
        "sums": list(sums),
        "weights": list(weights),
        "outs": list(plain) + list(made),
        "made": list(made),
    }
    outs = [jax.ShapeDtypeStruct(shape, jnp.float32) for shape in plain.values()]
    outs += [jax.ShapeDtypeStruct(array.shape, jnp.float32) for array in made.values()]
    inputs = list(sums.values()) + list(weights.values())
    results = pl.pallas_call(
        functools.partial(derive_kernel, names),
        out_shape=outs,
        in_specs=[ANYWHERE] * len(inputs),
        out_specs=[ANYWHERE] * len(outs),
        scratch_shapes=[pltpu.VMEM(array.shape, array.dtype) for array in inputs]
        + [pltpu.VMEM(array.shape, jnp.float32) for array in made.values()]
        + [pltpu.SemaphoreType.DMA((len(inputs),)), pltpu.SemaphoreType.DMA((len(outs) + 2,))],
        compiler_params=pltpu.CompilerParams(vmem_limit_bytes=63 * 2**20),
    )(*inputs)
    return dict(zip(names["outs"], results))


def on_device(
    fast,
    tokens,
    document_numbers,
    input_norm_gain,
    after_attention_gain,
    before_feedforward_gain,
    after_feedforward_gain,
    query_norm_gain,
    key_norm_gain,
    query_weight,
    keyvalue_weight,
    output_weight,
    gateup_weight,
    down_weight,
    query_adapter_first,
    query_adapter_second,
    keyvalue_adapter_first,
    keyvalue_adapter_second,
    output_adapter_first,
    output_adapter_second,
    gateup_adapter_first,
    gateup_adapter_second,
    down_adapter_first,
    down_adapter_second,
    cotangent,
):
    inputs = tokens[0].astype(jnp.float32)
    segments = document_numbers[0]
    length = inputs.shape[0]
    head_width = keyvalue_adapter_second.shape[2]
    adapter_rank = query_adapter_first.shape[1]
    query_columns = query_weight.shape[1]
    hidden_columns = down_weight.shape[0]
    heads_local = query_columns // head_width
    group_position = lax.axis_index("tensor")
    query_piece = lax.dynamic_slice_in_dim(
        query_adapter_second, group_position * query_columns, query_columns, 1
    )
    output_rows = lax.dynamic_slice_in_dim(
        output_adapter_first, group_position * query_columns, query_columns, 0
    )
    gateup_piece = lax.dynamic_slice_in_dim(
        gateup_adapter_second, group_position * hidden_columns, hidden_columns, 2
    )
    down_rows = lax.dynamic_slice_in_dim(
        down_adapter_first, group_position * hidden_columns, hidden_columns, 0
    )
    query_merged = (
        query_weight.astype(jnp.float32) + matrix_product(query_adapter_first, query_piece)
    ).astype(jnp.bfloat16)
    keyvalue_merged = (
        keyvalue_weight.astype(jnp.float32)
        + jnp.concatenate(
            [
                matrix_product(keyvalue_adapter_first[:, :adapter_rank], keyvalue_adapter_second[0]),
                matrix_product(keyvalue_adapter_first[:, adapter_rank:], keyvalue_adapter_second[1]),
            ],
            axis=1,
        )
    ).astype(jnp.bfloat16)
    output_merged = (
        output_weight.astype(jnp.float32) + matrix_product(output_rows, output_adapter_second)
    ).astype(jnp.bfloat16)
    gate_merged = (
        gateup_weight[0].astype(jnp.float32)
        + matrix_product(gateup_adapter_first[:, :adapter_rank], gateup_piece[0])
    ).astype(jnp.bfloat16)
    up_merged = (
        gateup_weight[1].astype(jnp.float32)
        + matrix_product(gateup_adapter_first[:, adapter_rank:], gateup_piece[1])
    ).astype(jnp.bfloat16)
    down_merged = (
        down_weight.astype(jnp.float32) + matrix_product(down_rows, down_adapter_second)
    ).astype(jnp.bfloat16)
    positions = positions_of(segments)
    rotation = rotation_of(positions, head_width)
    key_index = jnp.arange(length, dtype=jnp.int32)
    block_rows = min(512, length)
    normalized_rows, in_back = jax.vjp(rms_scale, inputs, input_norm_gain)
    normalized_lowrank = normalized_rows.astype(jnp.bfloat16)
    query_rows = matrix_product(normalized_lowrank, query_merged)
    keyvalue = matrix_product(normalized_lowrank, keyvalue_merged)

    def prepare(q_in, kv_in, q_scale, k_scale):
        q_heads = rms_scale(q_in.reshape(length, heads_local, head_width), q_scale)
        q_out = rotate(q_heads, rotation) * head_width ** (-0.5)
        k_out = rotate(rms_scale(kv_in[:, :head_width], k_scale), rotation)
        return (q_out, k_out, kv_in[:, head_width:])

    prepared, prepare_back = jax.vjp(prepare, query_rows, keyvalue, query_norm_gain, key_norm_gain)
    q_rot = prepared[0].astype(jnp.bfloat16)
    k_rot = prepared[1].astype(jnp.bfloat16)
    v_low = prepared[2].astype(jnp.bfloat16)

    def scores_of(row_start):
        rows = q_rot[row_start : row_start + block_rows]
        raw = jnp.einsum("qhd,kd->hqk", rows, k_rot, preferred_element_type=jnp.float32)
        row_index = row_start + jnp.arange(block_rows, dtype=jnp.int32)
        allowed = (segments[row_start : row_start + block_rows][:, None] == segments[None, :]) & (
            row_index[:, None] >= key_index[None, :]
        )
        return jnp.where(allowed[None], raw, MASKED)

    outputs = []
    log_totals = []
    for row_start in range(0, length, block_rows):
        scores = scores_of(row_start)
        row_peak = jnp.max(scores, axis=-1, keepdims=True)
        weights = jnp.exp(scores - row_peak)
        row_total = jnp.sum(weights, axis=-1, keepdims=True)
        log_totals.append(row_peak + jnp.log(row_total))
        probs_low = (weights / row_total).astype(jnp.bfloat16)
        outputs.append(
            jnp.einsum("hqk,kd->qhd", probs_low, v_low, preferred_element_type=jnp.float32)
        )
    attended_rows = (
        jnp.concatenate(outputs, axis=0).reshape(length, query_columns).astype(jnp.bfloat16)
    )
    attention_before = lax.psum(matrix_product(attended_rows, output_merged), "tensor")
    attn_post, post_attn_back = jax.vjp(rms_scale, attention_before, after_attention_gain)
    residual = inputs + attn_post
    normed_ff, pre_ff_back = jax.vjp(rms_scale, residual, before_feedforward_gain)
    feedforward_lowrank = normed_ff.astype(jnp.bfloat16)
    gate_portion = matrix_product(feedforward_lowrank, gate_merged)
    up_portion = matrix_product(feedforward_lowrank, up_merged)
    hidden_full, activate_back = jax.vjp(activate, gate_portion, up_portion)
    hidden_activation = hidden_full.astype(jnp.bfloat16)
    feedforward_before = lax.psum(matrix_product(hidden_activation, down_merged), "tensor")
    if fast:
        cosine, sine_part = rotation
        row_block = ROWS
        values = {
            "mlp": feedforward_before,
            "attn": attention_before,
            "tokens": tokens[0],
            "cot": cotangent[0],
            "pa": after_attention_gain[None],
            "pff": after_feedforward_gain[None],
            "hidden": hidden_activation,
            "ff": feedforward_lowrank,
            "w_g": gate_merged,
            "w_u": up_merged,
            "w_d": down_merged,
            "pf": before_feedforward_gain[None],
            "w_o": output_merged,
            "attended": attended_rows,
            "q_rot": q_rot.reshape(length, query_columns),
            "k_rot": k_rot,
            "values": v_low,
            "seg_c": segments[:, None],
            "seg_r": segments.reshape(-1, 1, row_block),
            "lse": jnp.concatenate(log_totals, axis=1),
            "cos": cosine,
            "sin": sine_part,
            "normed": normalized_lowrank,
            "w_q": query_merged,
            "gq": query_norm_gain[None],
            "w_kv": keyvalue_merged,
            "gk": key_norm_gain[None],
            "gin": input_norm_gain[None],
        }
        width = input_norm_gain.shape[0]
        shapes = {
            "d": down_weight.shape,
            "g": gateup_weight.shape[1:],
            "u": gateup_weight.shape[1:],
            "o": output_weight.shape,
            "q": query_weight.shape,
            "k": keyvalue_weight.shape,
            "s": (32, 128),
        }
        result_value, gradient_token_input, own, both = backward_and_sums(
            values, shapes, ORDER, CUTS
        )
        result_value = result_value[None]
        gradient_token_input = gradient_token_input[None]
        sums_flat = own["s"].reshape(-1)
        sum_gain_in = sums_flat[:width]
        sum_post_attn = sums_flat[width : 2 * width]
        sum_pre_ff = sums_flat[2 * width : 3 * width]
        sum_post_ff = sums_flat[3 * width : 4 * width]
        sum_query_gain = sums_flat[4 * width : 4 * width + head_width]
        sum_key_gain = sums_flat[4 * width + head_width : 4 * width + 2 * head_width]
        derived = derive_adapters(
            {**both, "k": own["k"]},
            {
                "query_a": query_adapter_first,
                "query_b": query_adapter_second,
                "keyvalue_a": keyvalue_adapter_first,
                "keyvalue_b": keyvalue_adapter_second,
                "output_a": output_adapter_first,
                "output_b": output_adapter_second,
                "gateup_a": gateup_adapter_first,
                "gateup_b": gateup_adapter_second,
                "down_a": down_adapter_first,
                "down_b": down_adapter_second,
            },
        )
        sum_w_query, sum_w_keyvalue, sum_w_out = (
            derived["query"],
            derived["keyvalue"],
            derived["output"],
        )
        sum_w_gate_up, sum_w_down = derived["gateup"], derived["down"]
        sum_q_a, sum_q_b = derived["query_a"], derived["query_b"]
        sum_kv_a, sum_kv_b = derived["keyvalue_a"], derived["keyvalue_b"]
        sum_o_a, sum_o_b = derived["output_a"], derived["output_b"]
        sum_gu_a, sum_gu_b = derived["gateup_a"], derived["gateup_b"]
        sum_d_a, sum_d_b = derived["down_a"], derived["down_b"]
    else:
        mlp_post, post_ff_back = jax.vjp(rms_scale, feedforward_before, after_feedforward_gain)
        result_value = (residual + mlp_post).astype(jnp.bfloat16)[None]
        grad_out = cotangent[0].astype(jnp.float32)
        grad_mlp_pre, gradient_after_feedforward = post_ff_back(grad_out)
        gradient_feedforward_lowrank = grad_mlp_pre.astype(jnp.bfloat16)
        gradient_down_weight = left_transposed(hidden_activation, gradient_feedforward_lowrank)
        grad_hidden = right_transposed(gradient_feedforward_lowrank, down_merged)
        grad_gate, grad_up = activate_back(grad_hidden)
        gate_lowrank = grad_gate.astype(jnp.bfloat16)
        up_lowrank = grad_up.astype(jnp.bfloat16)
        gradient_gateup_weight = jnp.stack(
            [
                left_transposed(feedforward_lowrank, gate_lowrank),
                left_transposed(feedforward_lowrank, up_lowrank),
            ]
        )
        grad_ff_part = right_transposed(gate_lowrank, gate_merged) + right_transposed(
            up_lowrank, up_merged
        )
        grad_normed_ff = lax.psum(grad_ff_part, "tensor")
        grad_residual_ff, gradient_before_feedforward = pre_ff_back(grad_normed_ff)
        grad_residual = grad_out + grad_residual_ff
        grad_attn_pre, gradient_after_attention = post_attn_back(grad_residual)
        gradient_attention_lowrank = grad_attn_pre.astype(jnp.bfloat16)
        gradient_output_weight = left_transposed(attended_rows, gradient_attention_lowrank)
        grad_attended = right_transposed(gradient_attention_lowrank, output_merged).astype(jnp.bfloat16)
        grad_attended = grad_attended.reshape(length, heads_local, head_width)
        grad_q_blocks = []
        grad_k_rot = jnp.zeros((length, head_width), jnp.float32)
        grad_values = jnp.zeros((length, head_width), jnp.float32)
        for block_index, row_start in enumerate(range(0, length, block_rows)):
            scores = scores_of(row_start)
            probs = jnp.exp(scores - log_totals[block_index])
            grad_rows = grad_attended[row_start : row_start + block_rows]
            grad_probs = jnp.einsum("qhd,kd->hqk", grad_rows, v_low, preferred_element_type=jnp.float32)
            grad_scores = (
                probs * (grad_probs - jnp.sum(probs * grad_probs, axis=-1, keepdims=True))
            ).astype(jnp.bfloat16)
            grad_q_blocks.append(
                jnp.einsum("hqk,kd->qhd", grad_scores, k_rot, preferred_element_type=jnp.float32)
            )
            grad_k_rot = grad_k_rot + jnp.einsum(
                "hqk,qhd->kd",
                grad_scores,
                q_rot[row_start : row_start + block_rows],
                preferred_element_type=jnp.float32,
            )
            grad_values = grad_values + jnp.einsum(
                "hqk,qhd->kd", probs.astype(jnp.bfloat16), grad_rows, preferred_element_type=jnp.float32
            )
        grad_queries, grad_keyvalue, gradient_query_norm_gain, gradient_key_norm_gain = prepare_back(
            (jnp.concatenate(grad_q_blocks, axis=0), grad_k_rot, grad_values)
        )
        query_low = grad_queries.astype(jnp.bfloat16)
        keyvalue_gradient_lowrank = grad_keyvalue.astype(jnp.bfloat16)
        gradient_query_weight = left_transposed(normalized_lowrank, query_low)
        gradient_keyvalue_weight = left_transposed(normalized_lowrank, keyvalue_gradient_lowrank)
        grad_in_part = right_transposed(query_low, query_merged) + right_transposed(
            keyvalue_gradient_lowrank, keyvalue_merged
        )
        grad_normed = lax.psum(grad_in_part, "tensor")
        grad_inputs_add, gradient_input_gain = in_back(grad_normed)
        gradient_token_input = (grad_residual + grad_inputs_add)[None]
        lead_mask = (group_position == 0).astype(jnp.float32)
        lead_in = gradient_input_gain * lead_mask
        lead_post_attn = gradient_after_attention * lead_mask
        lead_pre_ff = gradient_before_feedforward * lead_mask
        lead_post_ff = gradient_after_feedforward * lead_mask
        sum_w_query, sum_w_out, sum_w_gate_up, sum_w_down = lax.psum(
            (
                gradient_query_weight,
                gradient_output_weight,
                gradient_gateup_weight,
                gradient_down_weight,
            ),
            "dp",
        )
        (
            sum_gain_in,
            sum_post_attn,
            sum_pre_ff,
            sum_post_ff,
            sum_query_gain,
            sum_key_gain,
            sum_w_keyvalue,
        ) = lax.psum(
            (
                lead_in,
                lead_post_attn,
                lead_pre_ff,
                lead_post_ff,
                gradient_query_norm_gain,
                gradient_key_norm_gain,
                gradient_keyvalue_weight,
            ),
            ("dp", "tensor"),
        )
        rows_rows = ((0,), (0,))
        columns_columns = ((1,), (1,))
        sum_kv_b = jnp.stack(
            [
                exact_product(
                    sum_w_keyvalue[:, i * head_width : (i + 1) * head_width],
                    keyvalue_adapter_first[:, i * adapter_rank : (i + 1) * adapter_rank],
                    rows_rows,
                ).T
                for i in range(2)
            ]
        )
        sum_kv_a = jnp.concatenate(
            [
                exact_product(
                    sum_w_keyvalue[:, i * head_width : (i + 1) * head_width],
                    keyvalue_adapter_second[i],
                    columns_columns,
                )
                for i in range(2)
            ],
            axis=1,
        )
        part_q_b = exact_product(sum_w_query, query_adapter_first, rows_rows).T
        part_q_a = exact_product(sum_w_query, query_piece, columns_columns)
        part_o_a = exact_product(sum_w_out, output_adapter_second, columns_columns)
        part_o_b = exact_product(sum_w_out, output_rows, rows_rows).T
        part_gu_b = jnp.stack(
            [
                exact_product(
                    sum_w_gate_up[i],
                    gateup_adapter_first[:, i * adapter_rank : (i + 1) * adapter_rank],
                    rows_rows,
                ).T
                for i in range(2)
            ]
        )
        part_gu_a = jnp.concatenate(
            [exact_product(sum_w_gate_up[i], gateup_piece[i], columns_columns) for i in range(2)],
            axis=1,
        )
        part_d_a = exact_product(sum_w_down, down_adapter_second, columns_columns)
        part_d_b = exact_product(sum_w_down, down_rows, rows_rows).T
        sum_q_a, sum_o_b, sum_gu_a, sum_d_b = lax.psum(
            (part_q_a, part_o_b, part_gu_a, part_d_b), "tensor"
        )
        sum_q_b = lax.all_gather(part_q_b, "tensor", axis=1, tiled=True)
        sum_o_a = lax.all_gather(part_o_a, "tensor", axis=0, tiled=True)
        sum_gu_b = lax.all_gather(part_gu_b, "tensor", axis=2, tiled=True)
        sum_d_a = lax.all_gather(part_d_a, "tensor", axis=0, tiled=True)
    return (
        result_value,
        gradient_token_input,
        sum_gain_in,
        sum_post_attn,
        sum_pre_ff,
        sum_post_ff,
        sum_query_gain,
        sum_key_gain,
        sum_w_query,
        sum_w_keyvalue,
        sum_w_out,
        sum_w_gate_up,
        sum_w_down,
        sum_q_a,
        sum_q_b,
        sum_kv_a,
        sum_kv_b,
        sum_o_a,
        sum_o_b,
        sum_gu_a,
        sum_gu_b,
        sum_d_a,
        sum_d_b,
    )


def solution(mesh):
    in_specs = (
        P("dp", None, None),
        P("dp", None),
        P(),
        P(),
        P(),
        P(),
        P(),
        P(),
        P(None, "tensor"),
        P(),
        P("tensor", None),
        P(None, None, "tensor"),
        P("tensor", None),
        P(),
        P(),
        P(),
        P(),
        P(),
        P(),
        P(),
        P(),
        P(),
        P(),
        P("dp", None, None),
    )
    out_specs = (
        P("dp", None, None),
        P("dp", None, None),
        P(),
        P(),
        P(),
        P(),
        P(),
        P(),
        P(None, "tensor"),
        P(),
        P("tensor", None),
        P(None, None, "tensor"),
        P("tensor", None),
        P(),
        P(),
        P(),
        P(),
        P(),
        P(),
        P(),
        P(),
        P(),
        P(),
    )
    fast = mesh.shape["dp"] == 16 and mesh.shape["tensor"] == 2
    return jax.shard_map(
        functools.partial(on_device, fast), mesh=mesh, in_specs=in_specs, out_specs=out_specs, check_vma=False
    )
```

```python
import functools
from typing import NamedTuple

import jax
import jax.numpy as jnp
import numpy as np
from jax import lax
from jax.experimental import pallas as pl
from jax.experimental.pallas import tpu as pltpu
from jax.sharding import PartitionSpec as P

EPS = 1e-06
THETA = 1000000.0
MASKED = -1e30
GELU = 0.7978845608028654
DP, TENSOR = "dp", "tensor"
ROWS = 256
MESH_ID = pl.DeviceIdType.MESH
ANYWHERE = pl.BlockSpec(memory_space=pl.ANY)


def matrix_product(left_side, right_side):
    return jnp.dot(left_side, right_side, preferred_element_type=jnp.float32)


def left_transposed(left_side, right_side):
    return lax.dot_general(
        left_side, right_side, (((0,), (0,)), ((), ())), preferred_element_type=jnp.float32
    )


def right_transposed(left_side, right_side):
    return lax.dot_general(
        left_side, right_side, (((1,), (1,)), ((), ())), preferred_element_type=jnp.float32
    )


def rms_scale(values, scale_gain):
    return values * lax.rsqrt(jnp.mean(values * values, axis=-1, keepdims=True) + EPS) * scale_gain


def positions_of(segments):
    length = segments.shape[0]
    indices = jnp.arange(length, dtype=jnp.int32)
    before = jnp.concatenate([jnp.full((1,), -1, jnp.int32), segments[:-1]])
    starts = lax.cummax(jnp.where(segments != before, indices, jnp.zeros_like(indices)), axis=0)
    return indices - starts


def rotate(values, positions):
    half_dim = values.shape[-1] // 2
    frequency = THETA ** (-jnp.arange(half_dim, dtype=jnp.float32) * 2.0 / values.shape[-1])
    angles = positions.astype(jnp.float32)[:, None] * frequency[None, :]
    cosine = jnp.cos(angles)
    sine_part = jnp.sin(angles)
    if values.ndim == 3:
        cosine = cosine[:, None, :]
        sine_part = sine_part[:, None, :]
    leading = values[..., :half_dim]
    trailing = values[..., half_dim:]
    return jnp.concatenate(
        [leading * cosine - trailing * sine_part, trailing * cosine + leading * sine_part], axis=-1
    )


def exact_product(left_side, right_side, contract):
    return lax.dot_general(
        left_side,
        right_side.astype(jnp.float32),
        (contract, ((), ())),
        precision=lax.Precision.HIGHEST,
        preferred_element_type=jnp.float32,
    )


def activate(gate_in, up_in):
    return jax.nn.gelu(gate_in, approximate=True) * up_in


class Place:
    def __init__(self):
        me = lax.axis_index(DP)
        core = lax.axis_index(TENSOR)
        bit_x = lax.rem(me, 2)
        bit_y = lax.rem(me // 2, 2)
        level = me // 4
        across_x = me + 1 - 2 * bit_x
        across_y = me + 2 - 4 * bit_y
        self.core = core
        self.side = level // 2
        self.level = level
        self.outer = jnp.logical_or(level == 0, level == 3)
        self.inner = jnp.logical_not(self.outer)
        self.bits = (jnp.where(core == 0, bit_x, bit_y), jnp.where(core == 0, bit_y, bit_x))
        self.across = (
            (jnp.where(core == 0, across_x, across_y), core),
            (jnp.where(core == 0, across_y, across_x), core),
        )
        column = lax.rem(me, 4)
        self.near = ((level + 1 - 2 * lax.rem(level, 2)) * 4 + column, core)
        self.middle = ((3 - level) * 4 + column, core)
        self.sibling = (me, 1 - core)


def add_rows(target, target_row, extra, extra_row, count):
    step = 32 if count % 32 == 0 else (16 if count % 16 == 0 else 8)

    def body(index, carry):
        rows = pl.ds(pl.multiple_of(target_row + index * step, 8), step)
        target[rows] = target[rows] + extra[pl.ds(pl.multiple_of(extra_row + index * step, 8), step)]
        return carry

    lax.fori_loop(0, count // step, body, 0)


class Sums:
    def __init__(self, place, sends, receives, freed):
        self.place = place
        self.sends = sends
        self.receives = receives
        self.freed = freed
        self.used = 0
        self.credits = 0

    def credit(self):
        self.credits += 1
        return self.freed.at[self.credits - 1]

    def copy(self, source, target, device):
        slot = self.used
        self.used += 1
        return pltpu.make_async_remote_copy(
            src_ref=source,
            dst_ref=target,
            send_sem=self.sends.at[slot],
            recv_sem=self.receives.at[slot],
            device_id=device,
            device_id_type=MESH_ID,
        )


def signal(semaphore, device):
    pl.semaphore_signal(semaphore, inc=1, device_id=device, device_id_type=MESH_ID)


def rows_at(ref, start, count):
    return ref.at[pl.ds(pl.multiple_of(start, 8), count)]


def plane_first(sums, total, row, count, landing, landing_row, finish, turned):
    place = sums.place
    half, quarter = count // 2, count // 4
    bit_one, bit_two = place.bits[turned], place.bits[1 - turned]
    one, two = place.across[turned], place.across[1 - turned]
    kept = row + bit_one * half
    given = row + (1 - bit_one) * half
    mine = kept + bit_two * quarter
    other = kept + (1 - bit_two) * quarter
    land_one = rows_at(landing, landing_row, half)
    land_two = rows_at(landing, landing_row + half, quarter)
    land_near = rows_at(landing, landing_row + half + quarter, quarter)
    land_mid = rows_at(landing, landing_row + 2 * half, quarter)
    ours = rows_at(total, mine, quarter)
    copy_one = sums.copy(rows_at(total, given, half), land_one, one)
    copy_two = sums.copy(rows_at(total, other, quarter), land_two, two)
    copy_in = sums.copy(ours, land_near, place.near)
    copy_mid = sums.copy(ours, land_mid, place.middle)
    copy_out = sums.copy(ours, ours, place.near)
    back_two = sums.copy(ours, ours, two)
    back_one = sums.copy(rows_at(total, kept, half), rows_at(total, kept, half), one)

    free_one, free_two, free_in = sums.credit(), sums.credit(), sums.credit()

    def step0():
        copy_one.start()

    def step1():
        copy_one.wait_recv()
        add_rows(total, kept, landing, landing_row, half)
        copy_two.start()

    def step2():
        copy_two.wait_recv()
        add_rows(total, mine, landing, landing_row + half, quarter)

        @pl.when(place.outer)
        def _():
            copy_in.start()

        copy_one.wait_send()
        signal(free_one, one)

    def step3():
        @pl.when(place.inner)
        def _():
            copy_in.wait_recv()
            add_rows(total, mine, landing, landing_row + half + quarter, quarter)
            copy_mid.start()

        copy_two.wait_send()
        signal(free_two, two)

        @pl.when(place.outer)
        def _():
            copy_in.wait_send()
            signal(free_in, place.near)

    def step4():
        @pl.when(place.inner)
        def _():
            copy_mid.wait()
            add_rows(total, mine, landing, landing_row + 2 * half, quarter)
            pl.semaphore_wait(free_in, 1)
            copy_out.start()
            pl.semaphore_wait(free_two, 1)
            back_two.start()

    def step5():
        @pl.when(place.outer)
        def _():
            copy_out.wait_recv()
            pl.semaphore_wait(free_two, 1)
            back_two.start()

    def step6():
        back_two.wait_recv()
        pl.semaphore_wait(free_one, 1)
        back_one.start()

    def step7():
        back_one.wait_recv()
        back_two.wait_send()
        back_one.wait_send()

        @pl.when(place.inner)
        def _():
            copy_out.wait_send()

        finish()

    return [step0, step1, step2, step3, step4, step5, step6, step7]


def line_first(sums, total, row, count, landing, landing_row, finish, turned):
    place = sums.place
    one, two = place.across[turned], place.across[1 - turned]
    quarter = count // 4
    side = place.side
    three = row + (1 - side) * quarter
    far_pair = row + (1 - side) * 2 * quarter
    own_pair = row + side * 2 * quarter
    outer_quarter = row + 3 * side * quarter
    mine = row + place.level * quarter
    ours = rows_at(total, mine, quarter)
    land_three = rows_at(landing, landing_row, 3 * quarter)
    land_pair = rows_at(landing, landing_row + 3 * quarter, 2 * quarter)
    land_back = rows_at(landing, landing_row, quarter)
    land_one = rows_at(landing, landing_row + 5 * quarter, quarter)
    land_two = rows_at(landing, landing_row + 6 * quarter, quarter)
    copy_three = sums.copy(rows_at(total, three, 3 * quarter), land_three, place.near)
    copy_pair = sums.copy(rows_at(total, far_pair, 2 * quarter), land_pair, place.middle)
    outers = rows_at(total, outer_quarter, quarter)
    copy_back = sums.copy(outers, land_back, place.near)
    copy_one = sums.copy(ours, land_one, one)
    copy_two = sums.copy(ours, land_two, two)
    spread_in = sums.copy(ours, ours, place.near)
    spread_out = sums.copy(ours, ours, place.near)
    spread_mid = sums.copy(ours, ours, place.middle)
    forward_mid = sums.copy(outers, outers, place.middle)
    far_rows = rows_at(total, far_pair, 2 * quarter)
    forward_out = sums.copy(far_rows, far_rows, place.near)

    free_three, free_pair, free_back = sums.credit(), sums.credit(), sums.credit()

    def step0():
        @pl.when(place.outer)
        def _():
            copy_three.start()

    def step1():
        @pl.when(place.inner)
        def _():
            copy_three.wait_recv()
            add_rows(total, three, landing, landing_row, 3 * quarter)
            copy_pair.start()

    def step2():
        @pl.when(place.inner)
        def _():
            copy_pair.wait_recv()
            add_rows(total, own_pair, landing, landing_row + 3 * quarter, 2 * quarter)
            copy_back.start()
            copy_one.start()

    def step3():
        @pl.when(place.outer)
        def _():
            copy_back.wait_recv()
            add_rows(total, mine, landing, landing_row, quarter)
            copy_one.start()
            copy_three.wait_send()
            signal(free_three, place.near)

        @pl.when(place.inner)
        def _():
            copy_pair.wait_send()
            signal(free_pair, place.middle)
            copy_back.wait_send()
            signal(free_back, place.near)

    def step4():
        copy_one.wait()
        add_rows(total, mine, landing, landing_row + 5 * quarter, quarter)
        copy_two.start()

    def step5():
        copy_two.wait()
        add_rows(total, mine, landing, landing_row + 6 * quarter, quarter)

        @pl.when(place.outer)
        def _():
            pl.semaphore_wait(free_back, 1)
            spread_in.start()

        @pl.when(place.inner)
        def _():
            pl.semaphore_wait(free_three, 1)
            spread_out.start()
            pl.semaphore_wait(free_pair, 1)
            spread_mid.start()

    def step6():
        @pl.when(place.inner)
        def _():
            spread_in.wait_recv()
            forward_mid.start()

    def step7():
        @pl.when(place.inner)
        def _():
            spread_mid.wait_recv()
            forward_mid.wait_recv()
            forward_out.start()

    def step8():
        @pl.when(place.outer)
        def _():
            spread_out.wait_recv()
            forward_out.wait_recv()
            spread_in.wait_send()

        @pl.when(place.inner)
        def _():
            spread_out.wait_send()
            spread_mid.wait_send()
            forward_mid.wait_send()
            forward_out.wait_send()

        finish()

    return [step0, step1, step2, step3, step4, step5, step6, step7, step8]


def greet(place):
    barrier = pltpu.get_barrier_semaphore()
    for device in (*place.across, place.near, place.sibling):
        pl.semaphore_signal(barrier, inc=1, device_id=device, device_id_type=MESH_ID)

    @pl.when(place.inner)
    def _():
        pl.semaphore_signal(barrier, inc=1, device_id=place.middle, device_id_type=MESH_ID)
        pl.semaphore_wait(barrier, 5)

    @pl.when(place.outer)
    def _():
        pl.semaphore_wait(barrier, 4)


class BackwardInputs(NamedTuple):
    mlp: object
    attn: object
    tokens: object
    cot: object
    pa: object
    pff: object
    hidden: object
    ff: object
    w_g: object
    w_u: object
    w_d: object
    pf: object
    w_o: object
    attended: object
    q_rot: object
    k_rot: object
    values: object
    segments: object
    lse: object
    cosine: object
    sine: object
    normed: object
    w_q: object
    gq: object
    w_kv: object
    gk: object
    gin: object


class Pieces(NamedTuple):
    d: object
    g: object
    u: object
    o: object
    q: object
    k: object
    s: object


PIECE_K, PIECE_S = 5, 6


class Work(NamedTuple):
    low: object
    gate: object
    up: object
    part: object
    other: object
    dq: object
    gains: object
    gain_q: object
    gain_k: object
    result: object


def row_loop(count, body, start=0):
    def step(index, carry):
        body(pl.ds(pl.multiple_of(index * ROWS, ROWS), ROWS), index)
        return carry

    lax.fori_loop(start, count, step, 0)


def row_at(segments, index):
    columns = pl.ds(pl.multiple_of(index * ROWS, ROWS), ROWS)
    return segments[:, columns].astype(jnp.float32)


def column_of(row):
    shape = (row.shape[1], row.shape[1])
    diagonal = lax.broadcasted_iota(jnp.int32, shape, 0) == lax.broadcasted_iota(jnp.int32, shape, 1)
    return jnp.sum(jnp.where(diagonal, row, 0.0), axis=1, keepdims=True)


def inverse_rms(values):
    return lax.rsqrt(jnp.mean(values * values, axis=-1, keepdims=True) + EPS)


def rms_back(incoming, gain, normed, inverse):
    scaled = incoming * gain
    return inverse * (scaled - normed * jnp.mean(scaled * normed, axis=-1, keepdims=True))


def add_gain(target, terms):
    width = terms.shape[1]
    target[...] = target[...] + jnp.sum(terms.reshape(-1, 8, width), axis=0)


def gelu_parts(gate):
    inner = 0.7978845608028654 * gate * (1.0 + 0.044715 * gate * gate)
    bent = jnp.tanh(inner)
    half = 0.5 * (1.0 + bent)
    slope = half + 0.5 * gate * (1.0 - bent * bent) * 0.7978845608028654 * (
        1.0 + 0.134145 * gate * gate
    )
    return gate * half, slope


def turn_back(values, cosine, sine):
    half = values.shape[1] // 2
    leading, trailing = values[:, :half], values[:, half:]
    return jnp.concatenate(
        [leading * cosine + trailing * sine, trailing * cosine - leading * sine], axis=1
    )


def backward_kernel(setup, *refs):
    plan, order = setup
    refs = list(refs)
    source = BackwardInputs(*refs[: len(BackwardInputs._fields)])
    refs = refs[len(source) :]
    out_home, token_home, own_k, own_s = refs[:4]
    both = refs[4 : 4 + len(Pieces._fields) - 2]
    refs = refs[4 + len(both) :]
    held = BackwardInputs(*refs[: len(source)])
    refs = refs[len(source) :]
    total = Pieces(*refs[: len(plan)])
    refs = refs[len(plan) :]
    landing = refs[: len(plan)]
    refs = refs[len(plan) :]
    swapped_k, swapped_s = refs[:2]
    work = Work(*refs[2 : 2 + len(Work._fields)])
    loads, sends, receives, local, freed, handed = refs[2 + len(work) :]
    place = Place()
    core = place.core
    sums = Sums(place, sends, receives, freed)
    arrivals = BackwardInputs(
        *(
            pltpu.make_async_copy(piece, home, loads.at[index])
            for index, (piece, home) in enumerate(zip(source, held))
        )
    )
    for arrival in arrivals[:7]:
        arrival.start()
    greet(place)
    length = held.attn.shape[0]
    blocks = length // ROWS
    width = held.attn.shape[1]
    head = held.k_rot.shape[1]
    heads = held.q_rot.shape[1] // head
    hidden_columns = held.hidden.shape[1]
    here = set()

    def need(*copies):
        for copy in copies:
            if id(copy) not in here:
                here.add(id(copy))
                copy.wait()

    for gains in (work.gains, work.gain_q, work.gain_k):
        gains[...] = jnp.zeros_like(gains)
    gain_in, gain_pa, gain_pf, gain_pff = (work.gains.at[i] for i in range(4))
    low, part, other = work.low, work.part, work.other
    leaving = []

    def residual_of(rows):
        attn = held.attn[rows, :]
        inverse = inverse_rms(attn)
        normed = attn * inverse
        return held.tokens[rows, :].astype(jnp.float32) + normed * held.pa[...], normed, inverse

    def finish_forward():
        need(arrivals.mlp, arrivals.attn, arrivals.tokens, arrivals.cot, arrivals.pa, arrivals.pff)
        for arrival in arrivals[7:13]:
            arrival.start()

        def body(rows, index):
            residual, _, _ = residual_of(rows)
            mlp = held.mlp[rows, :]
            inverse = inverse_rms(mlp)
            normed = mlp * inverse
            work.result[rows, :] = (residual + normed * held.pff[...]).astype(jnp.bfloat16)
            incoming = held.cot[rows, :].astype(jnp.float32)
            add_gain(gain_pff, incoming * normed)
            low[rows, :] = rms_back(incoming, held.pff[...], normed, inverse).astype(jnp.bfloat16)

        row_loop(blocks, body)
        move = pltpu.make_async_copy(work.result, out_home, local.at[0])
        move.start()
        leaving.append(move)

    def down_gradient():
        need(arrivals.hidden)
        for arrival in arrivals[13:]:
            arrival.start()
        for index in range(hidden_columns // ROWS):
            columns = pl.ds(index * ROWS, ROWS)
            total.d[columns, :] = left_transposed(held.hidden[:, columns], low[...])

    def gate_block(index):
        def run():
            need(arrivals.ff, arrivals.w_g, arrivals.w_u, arrivals.w_d)
            columns = pl.ds(index * ROWS, ROWS)

            def body(rows, _):
                entering = held.ff[rows, :]
                gate = matrix_product(entering, held.w_g[:, columns])
                up = matrix_product(entering, held.w_u[:, columns])
                incoming = right_transposed(low[rows, :], held.w_d[columns, :])
                bent, slope = gelu_parts(gate)
                grad_gate = (incoming * up * slope).astype(jnp.bfloat16)
                grad_up = (incoming * bent).astype(jnp.bfloat16)
                work.gate[rows, :] = grad_gate
                work.up[rows, :] = grad_up
                share = right_transposed(grad_gate, held.w_g[:, columns]) + right_transposed(
                    grad_up, held.w_u[:, columns]
                )
                part[rows, :] = share if index == 0 else part[rows, :] + share

            row_loop(blocks, body)
            total.g[:, columns] = left_transposed(held.ff[...], work.gate[...])
            total.u[:, columns] = left_transposed(held.ff[...], work.up[...])

        return run

    into_ff, into_input = [], []

    def send_parts(copies):
        for index in range(blocks):
            rows = pl.ds(index * ROWS, ROWS)
            copies.append(sums.copy(part.at[rows], other.at[rows], place.sibling))
        for copy in copies:
            copy.start()

    def residual_back():
        need(arrivals.pf, arrivals.w_o)
        for index in range(blocks):
            into_ff[index].wait_recv()
            rows = pl.ds(index * ROWS, ROWS)
            residual, normed_attn, inverse_attn = residual_of(rows)
            incoming = part[rows, :] + other[rows, :]
            inverse = inverse_rms(residual)
            normed = residual * inverse
            add_gain(gain_pf, incoming * normed)
            grad = held.cot[rows, :].astype(jnp.float32) + rms_back(
                incoming, held.pf[...], normed, inverse
            )
            held.mlp[rows, :] = grad
            add_gain(gain_pa, grad * normed_attn)
            low[rows, :] = rms_back(grad, held.pa[...], normed_attn, inverse_attn).astype(
                jnp.bfloat16
            )
        for copy in into_ff:
            copy.wait_send()
        signal(handed, place.sibling)
        grad_attended = held.ff

        def body(rows, _):
            grad_attended[rows, : heads * head] = right_transposed(
                low[rows, :], held.w_o[...]
            ).astype(jnp.bfloat16)

        row_loop(blocks, body)

    def output_gradient():
        need(arrivals.attended)
        for index in range(heads * head // ROWS):
            columns = pl.ds(index * ROWS, ROWS)
            total.o[columns, :] = left_transposed(held.attended[:, columns], low[...])

    grad_key = held.attn.at[:, :head]
    grad_value = held.attn.at[:, head : 2 * head]
    grad_query_low = held.hidden.at[:, : heads * head]
    grad_keyvalue_low = held.hidden.at[:, heads * head : heads * head + 2 * head]

    def attention_rows(which, start, stop):
        def run():
            need(arrivals.q_rot, arrivals.k_rot, arrivals.values, arrivals.segments, arrivals.lse, arrivals.cosine, arrivals.sine, arrivals.normed, arrivals.w_q)
            need(arrivals.gq)
            columns = pl.ds(which * head, head)
            if which == 0 and start == 0:
                held.attn[...] = jnp.zeros_like(held.attn)

            def body(rows, index):
                query = held.q_rot[rows, columns]
                grad = held.ff[rows, columns]
                attended = held.attended[rows, columns]
                weight = jnp.sum(
                    grad.astype(jnp.float32) * attended.astype(jnp.float32), axis=1, keepdims=True
                )
                lse = held.lse[which, rows, :]
                segment = column_of(row_at(held.segments, index))
                work.dq[...] = jnp.zeros_like(work.dq)

                def inner(at, carry):
                    others = pl.ds(pl.multiple_of(at * ROWS, ROWS), ROWS)
                    key = held.k_rot[others, :]
                    value = held.values[others, :]
                    scores = right_transposed(query, key)
                    row_index = index * ROWS + lax.broadcasted_iota(jnp.int32, scores.shape, 0)
                    column_index = at * ROWS + lax.broadcasted_iota(jnp.int32, scores.shape, 1)
                    allowed = (segment == row_at(held.segments, at)) & (row_index >= column_index)
                    probs = jnp.where(allowed, jnp.exp(scores - lse), 0.0)
                    grad_probs = right_transposed(grad, value)
                    grad_scores = (probs * (grad_probs - weight)).astype(jnp.bfloat16)
                    work.dq[...] += matrix_product(grad_scores, key)
                    grad_key[others, :] = grad_key[others, :] + left_transposed(grad_scores, query)
                    grad_value[others, :] = grad_value[others, :] + left_transposed(
                        probs.astype(jnp.bfloat16), grad
                    )
                    return carry

                lax.fori_loop(0, index + 1, inner, 0)
                turned = turn_back(work.dq[...], held.cosine[rows, :], held.sine[rows, :])
                turned = turned * head ** (-0.5)
                raw = matrix_product(held.normed[rows, :], held.w_q[:, columns])
                inverse = inverse_rms(raw)
                normed = raw * inverse
                add_gain(work.gain_q, turned * normed)
                grad_query_low[rows, columns] = rms_back(
                    turned, held.gq[...], normed, inverse
                ).astype(jnp.bfloat16)

            row_loop(stop, body, start)

        return run

    def key_back():
        need(arrivals.w_kv, arrivals.gk)

        def body(rows, _):
            turned = turn_back(grad_key[rows, :], held.cosine[rows, :], held.sine[rows, :])
            raw = matrix_product(held.normed[rows, :], held.w_kv[:, :head])
            inverse = inverse_rms(raw)
            normed = raw * inverse
            add_gain(work.gain_k, turned * normed)
            grad_keyvalue_low[rows, :head] = rms_back(
                turned, held.gk[...], normed, inverse
            ).astype(jnp.bfloat16)
            grad_keyvalue_low[rows, head:] = grad_value[rows, :].astype(jnp.bfloat16)

        row_loop(blocks, body)

    def query_gradient():
        for index in range(heads * head // ROWS):
            columns = pl.ds(index * ROWS, ROWS)
            total.q[:, columns] = left_transposed(held.normed[...], grad_query_low[:, columns])

    half_rows = swapped_k.shape[0]
    swap_k, swap_s = [], []

    def keyvalue_gradient():
        for index in range(2 * head // ROWS):
            columns = pl.ds(index * ROWS, ROWS)
            total.k[:, columns] = left_transposed(
                held.normed[...], grad_keyvalue_low[:, columns]
            )
        copy = sums.copy(
            rows_at(total.k, (1 - core) * half_rows, half_rows), swapped_k, place.sibling
        )
        copy.start()
        swap_k.append(copy)

    def input_parts():
        def body(rows, _):
            part[rows, :] = right_transposed(
                grad_query_low[rows, :], held.w_q[...]
            ) + right_transposed(grad_keyvalue_low[rows, :], held.w_kv[...])

        row_loop(blocks, body)
        pl.semaphore_wait(handed, 1)
        send_parts(into_input)

    def input_back():
        need(arrivals.gin)
        for index in range(blocks):
            into_input[index].wait_recv()
            rows = pl.ds(index * ROWS, ROWS)
            incoming = part[rows, :] + other[rows, :]
            tokens = held.tokens[rows, :].astype(jnp.float32)
            inverse = inverse_rms(tokens)
            normed = tokens * inverse
            add_gain(gain_in, incoming * normed)
            held.mlp[rows, :] = held.mlp[rows, :] + rms_back(
                incoming, held.gin[...], normed, inverse
            )
            move = pltpu.make_async_copy(held.mlp.at[rows], token_home.at[rows], local.at[1 + index])
            move.start()
            leaving.append(move)
        for copy in into_input:
            copy.wait_send()
        small = total.s
        small[...] = jnp.zeros_like(small)
        lead = jnp.where(core == 0, 1.0, 0.0)
        row = 0
        for index in range(4):
            vector = jnp.sum(work.gains[index], axis=0, keepdims=True) * lead
            for at in range(width // 128):
                small[row : row + 1, :] = vector[:, at * 128 : (at + 1) * 128]
                row += 1
        for gains in (work.gain_q, work.gain_k):
            vector = jnp.sum(gains[...], axis=0, keepdims=True)
            for at in range(head // 128):
                small[row : row + 1, :] = vector[:, at * 128 : (at + 1) * 128]
                row += 1
        copy = sums.copy(small, swapped_s, place.sibling)
        copy.start()
        swap_s.append(copy)

    tasks = (
        lambda: (finish_forward(), down_gradient()),
        gate_block(0),
        gate_block(1),
        gate_block(2),
        lambda: (gate_block(3)(), send_parts(into_ff)),
        residual_back,
        output_gradient,
        attention_rows(0, 0, 3),
        attention_rows(0, 3, 4),
        attention_rows(1, 0, 3),
        attention_rows(1, 3, 4),
        key_back,
        keyvalue_gradient,
        query_gradient,
        input_parts,
        input_back,
    )
    chunks = []
    slots = 1 + blocks
    for piece, parts in enumerate(plan):
        row = 0
        land_row = 0
        base = core * half_rows if piece == PIECE_K else 0
        for line, count, turned in parts:

            def finish(piece=piece, row=row, base=base, count=count, slot=slots):
                done = rows_at(total[piece], base + row, count)
                if piece == PIECE_S:
                    moves = [pltpu.make_async_copy(done, own_s, local.at[slot])]
                else:
                    if piece == PIECE_K:
                        home = rows_at(own_k, base + row, count)
                    else:
                        home = both[piece].at[core, pl.ds(row, count)]
                    moves = [
                        pltpu.make_async_copy(done, home, local.at[slot]),
                        sums.copy(done, home, place.sibling),
                    ]
                for move in moves:
                    move.start()
                leaving.extend(moves)

            build = line_first if line else plane_first
            steps = build(
                sums, total[piece], base + row, count, landing[piece], land_row, finish, turned
            )
            if piece >= PIECE_K:
                swap, landed = (swap_k, swapped_k) if piece == PIECE_K else (swap_s, swapped_s)

                def enter(swap=swap, landed=landed, out=total[piece], base=base, first=steps[0]):
                    if swap:
                        swap.pop().wait()
                        add_rows(out, base, landed, 0, landed.shape[0])
                    first()

                steps = [enter] + steps[1:]
            chunks.append(steps)
            slots += 1
            row += count
            land_row += landing_rows(line, count)
    for entry in order:
        if entry < 0:
            tasks[-1 - entry]()
        else:
            chunks[entry // 10][entry % 10]()
    for move in leaving:
        move.wait()


def backward_and_sums(values, shapes):
    length, width = values.tokens.shape
    head = values.k_rot.shape[1]
    full, low = jnp.float32, jnp.bfloat16
    outs = [((length, width), low), ((length, width), full), (shapes.k, full), (shapes.s, full)]
    outs += [((2,) + shape, full) for shape in shapes[:PIECE_K]]
    scratch = [pltpu.VMEM(array.shape, array.dtype) for array in values]
    scratch += [pltpu.VMEM(shape, full) for shape in shapes]
    scratch += [
        pltpu.VMEM((sum(landing_rows(line, count) for line, count, _ in parts), shape[1]), full)
        for shape, parts in zip(shapes, CUTS)
    ]
    scratch += [pltpu.VMEM((shapes.k[0] // 2, shapes.k[1]), full), pltpu.VMEM(shapes.s, full)]
    scratch += Work(
        low=pltpu.VMEM((length, width), low),
        gate=pltpu.VMEM((length, ROWS), low),
        up=pltpu.VMEM((length, ROWS), low),
        part=pltpu.VMEM((length, width), full),
        other=pltpu.VMEM((length, width), full),
        dq=pltpu.VMEM((ROWS, head), full),
        gains=pltpu.VMEM((4, 8, width), full),
        gain_q=pltpu.VMEM((8, head), full),
        gain_k=pltpu.VMEM((8, head), full),
        result=pltpu.VMEM((length, width), low),
    )
    count = sum(len(parts) for parts in CUTS)
    blocks = length // ROWS
    scratch += [
        pltpu.SemaphoreType.DMA((len(values),)),
        pltpu.SemaphoreType.DMA((count * 11 + 2 * blocks + 4,)),
        pltpu.SemaphoreType.DMA((count * 11 + 2 * blocks + 4,)),
        pltpu.SemaphoreType.DMA((count + blocks + 2,)),
        pltpu.SemaphoreType.REGULAR((count * 3,)),
        pltpu.SemaphoreType.REGULAR,
    ]
    results = pl.pallas_call(
        functools.partial(backward_kernel, (CUTS, ORDER)),
        out_shape=[jax.ShapeDtypeStruct(*out) for out in outs],
        in_specs=[ANYWHERE] * len(values),
        out_specs=[ANYWHERE] * len(outs),
        scratch_shapes=scratch,
        compiler_params=pltpu.CompilerParams(
            collective_id=0, has_side_effects=True, vmem_limit_bytes=67043328
        ),
    )(*values)
    return results[:4], results[4:]


CUTS = (
    ((1, 96, 0), (0, 224, 0), (1, 160, 0), (0, 192, 0), (1, 128, 1), (0, 224, 0),),
    ((1, 224, 1), (0, 192, 0), (0, 128, 0), (0, 96, 1),),
    ((1, 128, 0), (0, 192, 0), (1, 96, 0), (0, 224, 1),),
    ((1, 192, 1), (0, 320, 1),),
    ((1, 96, 1), (0, 544, 1),),
    ((0, 320, 1),),
    ((0, 32, 0),),
)
ORDER = (
    -1, 0, 10, 30, 20, -2, 50, 11, 1, 2, -3, 40, 12, 31, 3, 21, -4, 13, 22, 41, 4, 32, -5, 70, 51,
    42, 60, 23, 14, 90, 80, -6, 33, 43, 15, 71, 61, -7, 5, 52, 110, 44, 6, 34, -8, 53, 24, 91, 72,
    -9, 35, 62, 25, 16, -10, 26, 81, 7, 73, 100, 111, -11, 82, 36, 130, -12, 120, 54, 45, 92, 74,
    63, 101, 83, 112, 140, -13, 131, 121, 46, 17, 64, 102, 55, 27, -14, 56, 150, 93, 84, 8, -15,
    -16, 160, 170, 122, 113, 47, 103, 85, 37, 104, 151, 94, 75, 65, 123, 57, 124, 114, 141, 48,
    95, 132, 171, 66, 180, 142, 190, 105, 76, 115, 67, 133, 191, 172, 143, 106, 152, 96, 116, 181,
    134, 86, 161, 153, 162, 125, 163, 135, 192, 97, 28, 126, 68, 117, 173, 154, 144, 107, 136,
    182, 155, 174, 108, 164, 193, 127, 183, 156, 184, 145, 175, 165, 87, 194, 176, 146, 185, 157,
    128, 195, 186, 147, 166, 77, 167, 196, 148, 177, 137, 197, 168, 187,
)


def landing_rows(line, count):
    return count // 4 * (7 if line else 5)


class ForwardInputs(NamedTuple):
    tokens: object
    gin: object
    w_q: object
    a_q: object
    b_q: object
    w_kv: object
    a_kv: object
    b_kv: object
    table: object
    segments: object
    gq: object
    gk: object
    w_o: object
    a_o: object
    b_o: object
    pa: object
    pf: object
    w_gu: object
    a_gu: object
    b_gu: object
    w_d: object
    a_d: object
    b_d: object


class ForwardOutputs(NamedTuple):
    mlp: object
    attn: object
    hidden: object
    ff: object
    w_g: object
    w_u: object
    w_d: object
    w_o: object
    attended: object
    q_rot: object
    k_rot: object
    values: object
    lse: object
    cosine: object
    sine: object
    normed: object
    w_q: object
    w_kv: object


def turn(values, cosine, sine):
    half = values.shape[1] // 2
    leading, trailing = values[:, :half], values[:, half:]
    return jnp.concatenate(
        [leading * cosine - trailing * sine, trailing * cosine + leading * sine], axis=1
    )


def forward_kernel(*refs):
    refs = list(refs)
    source = ForwardInputs(*refs[: len(ForwardInputs._fields)])
    refs = refs[len(source) :]
    target = ForwardOutputs(*refs[: len(ForwardOutputs._fields)])
    refs = refs[len(target) :]
    held = ForwardInputs(*refs[: len(source)])
    refs = refs[len(source) :]
    made = ForwardOutputs(*refs[: len(target)])
    part, other, part_two, other_two, sums_at, loads, sends, receives, stores = refs[len(target) :]
    me = lax.axis_index(DP)
    core = lax.axis_index(TENSOR)
    sibling = (me, 1 - core)

    def own_part(ref, home, axis):
        size = home.shape[axis]
        span = pl.ds(pl.multiple_of(core * size, 256), size)
        index = [slice(None)] * len(home.shape)
        index[axis] = span
        return ref.at[tuple(index)]

    pieces = source._replace(
        b_q=own_part(source.b_q, held.b_q, 1),
        a_o=own_part(source.a_o, held.a_o, 0),
        b_gu=own_part(source.b_gu, held.b_gu, 2),
        a_d=own_part(source.a_d, held.a_d, 0),
    )
    arrivals = ForwardInputs(
        *(
            pltpu.make_async_copy(piece, home, loads.at[index])
            for index, (piece, home) in enumerate(zip(pieces, held))
        )
    )
    for arrival in arrivals[:8]:
        arrival.start()
    barrier = pltpu.get_barrier_semaphore()
    signal(barrier, sibling)
    pl.semaphore_wait(barrier, 1)
    leaving = []
    homes = {id(ref): (index, home) for index, (ref, home) in enumerate(zip(made, target))}

    def leave(*arrays):
        for ref in arrays:
            index, home = homes[id(ref)]
            move = pltpu.make_async_copy(ref, home, stores.at[index])
            move.start()
            leaving.append(move)

    def need(*copies):
        for copy in copies:
            copy.wait()

    length, width = held.tokens.shape
    blocks = length // ROWS
    head = held.gq.shape[0]
    heads = held.w_q.shape[1] // head
    rank = held.a_q.shape[1]

    def merge(out, weight, first, second):
        count = weight.shape[0]
        step = 256 if count % 256 == 0 else 320

        def body(index, carry):
            rows = pl.ds(pl.multiple_of(index * step, 64), step)
            out[rows, :] = (
                weight[rows, :].astype(jnp.float32) + matrix_product(first[rows, :], second[...])
            ).astype(jnp.bfloat16)
            return carry

        lax.fori_loop(0, count // step, body, 0)

    need(arrivals.tokens, arrivals.gin, arrivals.w_q, arrivals.a_q, arrivals.b_q)
    for arrival in arrivals[8:]:
        arrival.start()
    merge(made.w_q, held.w_q, held.a_q, held.b_q)
    need(arrivals.w_kv, arrivals.a_kv, arrivals.b_kv)
    for index in range(2):
        columns = pl.ds(index * head, head)
        merge(
            made.w_kv.at[:, columns],
            held.w_kv.at[:, columns],
            held.a_kv.at[:, pl.ds(index * rank, rank)],
            held.b_kv.at[index],
        )
    leave(made.w_q, made.w_kv)
    need(arrivals.table, arrivals.segments, arrivals.gq, arrivals.gk)
    before = jnp.zeros((8, 1), jnp.float32)
    number = lax.broadcasted_iota(jnp.int32, (8, ROWS), 0).astype(jnp.float32)
    for index in range(blocks):
        fewer = jnp.where(row_at(held.segments, index) < number, 1.0, 0.0)
        before = before + jnp.sum(fewer, axis=1, keepdims=True)
    at_token = lax.broadcasted_iota(jnp.int32, (8, length), 1).astype(jnp.float32)
    chosen = jnp.where(at_token == before, 1.0, 0.0)
    starts = jnp.dot(
        chosen, held.table[...], precision=lax.Precision.HIGHEST, preferred_element_type=jnp.float32
    )
    half = head // 2

    def project(rows, index):
        tokens = held.tokens[rows, :].astype(jnp.float32)
        normed = (tokens * inverse_rms(tokens) * held.gin[...]).astype(jnp.bfloat16)
        made.normed[rows, :] = normed
        segment = column_of(row_at(held.segments, index))
        start = starts[3:4, :]
        for document in (2, 1, 0):
            start = jnp.where(segment == document, starts[document : document + 1, :], start)
        start_cosine, start_sine = start[:, :half], start[:, half:]
        here = held.table[rows, :]
        here_cosine, here_sine = here[:, :half], here[:, half:]
        cosine = here_cosine * start_cosine + here_sine * start_sine
        sine = here_sine * start_cosine - here_cosine * start_sine
        made.cosine[rows, :] = cosine
        made.sine[rows, :] = sine
        for at in range(heads):
            columns = pl.ds(at * head, head)
            raw = matrix_product(normed, made.w_q[:, columns])
            query = turn(raw * inverse_rms(raw) * held.gq[...], cosine, sine) * head ** (-0.5)
            made.q_rot[rows, columns] = query.astype(jnp.bfloat16)
        raw = matrix_product(normed, made.w_kv[:, :head])
        key = turn(raw * inverse_rms(raw) * held.gk[...], cosine, sine)
        made.k_rot[rows, :] = key.astype(jnp.bfloat16)
        made.values[rows, :] = matrix_product(normed, made.w_kv[:, head:]).astype(jnp.bfloat16)

    row_loop(blocks, project)
    leave(made.normed, made.cosine, made.sine, made.q_rot, made.k_rot, made.values)
    need(arrivals.w_o, arrivals.a_o, arrivals.b_o)
    merge(made.w_o, held.w_o, held.a_o, held.b_o)
    leave(made.w_o)

    def exchange(key, index, mine, theirs):
        rows = pl.ds(index * ROWS, ROWS)
        slot = key * blocks + index
        return pltpu.make_async_remote_copy(
            src_ref=mine.at[rows],
            dst_ref=theirs.at[rows],
            send_sem=sends.at[slot],
            recv_sem=receives.at[slot],
            device_id=sibling,
            device_id_type=MESH_ID,
        )

    attention_copies = [exchange(0, index, part, other) for index in range(blocks)]
    mlp_copies = [exchange(1, index, part_two, other_two) for index in range(blocks)]

    def attend(index):
        rows = pl.ds(index * ROWS, ROWS)
        segment = column_of(row_at(held.segments, index))

        def one_head(which, carry):
            columns = pl.ds(pl.multiple_of(which * head, head), head)
            query = made.q_rot[rows, columns]
            sums_at[...] = jnp.zeros_like(sums_at)

            def inner(at, carry):
                peak, amount = carry
                others = pl.ds(pl.multiple_of(at * ROWS, ROWS), ROWS)
                scores = right_transposed(query, made.k_rot[others, :])
                row_index = index * ROWS + lax.broadcasted_iota(jnp.int32, scores.shape, 0)
                column_index = at * ROWS + lax.broadcasted_iota(jnp.int32, scores.shape, 1)
                allowed = (segment == row_at(held.segments, at)) & (row_index >= column_index)
                scores = jnp.where(allowed, scores, MASKED)
                higher = jnp.maximum(peak, jnp.max(scores, axis=1, keepdims=True))
                weights = jnp.where(allowed, jnp.exp(scores - higher), 0.0)
                shrink = jnp.exp(peak - higher)
                amount = amount * shrink + jnp.sum(weights, axis=1, keepdims=True)
                sums_at[...] = sums_at[...] * shrink + matrix_product(
                    weights.astype(jnp.bfloat16), made.values[others, :]
                )
                return higher, amount

            first = (jnp.full((ROWS, 1), MASKED, jnp.float32), jnp.zeros((ROWS, 1), jnp.float32))
            peak, amount = lax.fori_loop(0, index + 1, inner, first)
            made.attended[rows, columns] = (sums_at[...] / amount).astype(jnp.bfloat16)
            made.lse[which, rows, :] = peak + jnp.log(amount)
            return carry

        lax.fori_loop(0, heads, one_head, 0)
        part[rows, :] = matrix_product(made.attended[rows, :], made.w_o[...])
        attention_copies[index].start()

    for index in range(blocks):
        attend(index)
    leave(made.attended, made.lse)
    need(arrivals.w_gu, arrivals.a_gu, arrivals.b_gu, arrivals.w_d, arrivals.a_d, arrivals.b_d)
    for index, out in enumerate((made.w_g, made.w_u)):
        first = held.a_gu.at[:, pl.ds(index * rank, rank)]
        merge(out, held.w_gu.at[index], first, held.b_gu.at[index])
    merge(made.w_d, held.w_d, held.a_d, held.b_d)
    leave(made.w_g, made.w_u, made.w_d)
    need(arrivals.pa, arrivals.pf)
    hidden_columns = made.hidden.shape[1]

    def feed_forward(index):
        rows = pl.ds(index * ROWS, ROWS)
        attention_copies[index].wait_recv()
        attn = part[rows, :] + other[rows, :]
        made.attn[rows, :] = attn
        residual = held.tokens[rows, :].astype(jnp.float32) + attn * inverse_rms(attn) * held.pa[...]
        made.ff[rows, :] = (residual * inverse_rms(residual) * held.pf[...]).astype(jnp.bfloat16)

        def one_block(at, carry):
            columns = pl.ds(pl.multiple_of(at * ROWS, ROWS), ROWS)
            entering = made.ff[rows, :]
            gate = matrix_product(entering, made.w_g[:, columns])
            up = matrix_product(entering, made.w_u[:, columns])
            bent = 0.5 * gate * (1.0 + jnp.tanh(GELU * gate * (1.0 + 0.044715 * gate * gate)))
            made.hidden[rows, columns] = (bent * up).astype(jnp.bfloat16)
            return carry

        lax.fori_loop(0, hidden_columns // ROWS, one_block, 0)
        part_two[rows, :] = matrix_product(made.hidden[rows, :], made.w_d[...])
        mlp_copies[index].start()

    for index in range(blocks):
        feed_forward(index)
    leave(made.attn, made.ff, made.hidden)
    for index in range(blocks):
        rows = pl.ds(index * ROWS, ROWS)
        mlp_copies[index].wait_recv()
        made.mlp[rows, :] = part_two[rows, :] + other_two[rows, :]
    leave(made.mlp)
    for copy in attention_copies + mlp_copies:
        copy.wait_send()
    for move in leaving:
        move.wait()


def rotation_table(length, head):
    frequency = THETA ** (-np.arange(head // 2, dtype=np.float64) * 2.0 / head)
    angles = np.arange(length, dtype=np.float64)[:, None] * frequency[None, :]
    return jnp.asarray(np.concatenate([np.cos(angles), np.sin(angles)], axis=1).astype(np.float32))


def forward_pass(values):
    length, width = values.tokens.shape
    head = values.gq.shape[0]
    query_columns = values.w_q.shape[1]
    heads = query_columns // head
    hidden_columns = values.w_d.shape[0]
    rank = values.a_q.shape[1]
    low, full = jnp.bfloat16, jnp.float32
    shapes = ForwardOutputs(
        mlp=((length, width), full),
        attn=((length, width), full),
        hidden=((length, hidden_columns), low),
        ff=((length, width), low),
        w_g=((width, hidden_columns), low),
        w_u=((width, hidden_columns), low),
        w_d=((hidden_columns, width), low),
        w_o=((query_columns, width), low),
        attended=((length, query_columns), low),
        q_rot=((length, query_columns), low),
        k_rot=((length, head), low),
        values=((length, head), low),
        lse=((heads, length, 1), full),
        cosine=((length, head // 2), full),
        sine=((length, head // 2), full),
        normed=((length, width), low),
        w_q=((width, query_columns), low),
        w_kv=((width, 2 * head), low),
    )
    sizes = values._replace(
        b_q=jax.ShapeDtypeStruct((rank, query_columns), low),
        a_o=jax.ShapeDtypeStruct((query_columns, rank), low),
        b_gu=jax.ShapeDtypeStruct((2, rank, hidden_columns), low),
        a_d=jax.ShapeDtypeStruct((hidden_columns, rank), low),
    )
    slots = 2 * (length // ROWS)
    results = pl.pallas_call(
        forward_kernel,
        out_shape=[jax.ShapeDtypeStruct(*shape) for shape in shapes],
        in_specs=[ANYWHERE] * len(values),
        out_specs=[ANYWHERE] * len(shapes),
        scratch_shapes=[pltpu.VMEM(array.shape, array.dtype) for array in sizes]
        + [pltpu.VMEM(*shape) for shape in shapes]
        + [pltpu.VMEM((length, width), full)] * 4
        + [
            pltpu.VMEM((ROWS, head), full),
            pltpu.SemaphoreType.DMA((len(values),)),
            pltpu.SemaphoreType.DMA((slots,)),
            pltpu.SemaphoreType.DMA((slots,)),
            pltpu.SemaphoreType.DMA((len(shapes),)),
        ],
        compiler_params=pltpu.CompilerParams(
            collective_id=1, has_side_effects=True, vmem_limit_bytes=67043328
        ),
    )(*values)
    return ForwardOutputs(*results)


class Adapters(NamedTuple):
    down_a: object
    down_b: object
    gateup_a: object
    gateup_b: object
    output_a: object
    output_b: object
    query_a: object
    query_b: object
    keyvalue_a: object
    keyvalue_b: object


class DeriveInputs(NamedTuple):
    down_a: object
    down_b: object
    d: object
    gateup_a: object
    gateup_b: object
    g: object
    u: object
    output_a: object
    output_b: object
    o: object
    query_a: object
    query_b: object
    q: object
    keyvalue_a: object
    keyvalue_b: object
    k: object
    small: object
    result: object
    tokens: object


class DeriveOutputs(NamedTuple):
    down: object
    gateup: object
    output: object
    query: object
    keyvalue: object
    down_a: object
    down_b: object
    gateup_a: object
    gateup_b: object
    output_a: object
    output_b: object
    query_a: object
    query_b: object
    keyvalue_a: object
    keyvalue_b: object
    result: object
    tokens: object
    gain_in: object
    gain_pa: object
    gain_pf: object
    gain_pff: object
    gain_q: object
    gain_k: object


def derive_kernel(*refs):
    refs = list(refs)
    fields = len(DeriveInputs._fields)
    source = DeriveInputs(*refs[:fields])
    refs = refs[fields:]
    target = DeriveOutputs(*refs[: len(DeriveOutputs._fields)])
    refs = refs[len(target) :]
    held = DeriveInputs(*refs[:fields])
    refs = refs[fields:]
    made = Adapters(*refs[: len(Adapters._fields)])
    gains = refs[len(made) : len(made) + 6]
    loaded, stored = refs[len(made) + 6 :]
    core = lax.axis_index(TENSOR)
    arrivals = DeriveInputs(
        *(
            pltpu.make_async_copy(piece, home, loaded.at[index])
            for index, (piece, home) in enumerate(zip(source, held))
        )
    )
    for arrival in arrivals[:6]:
        arrival.start()
    behind = list(arrivals[6:])
    leaving = []

    def need(*copies):
        for copy in copies:
            copy.wait()
        for arrival in behind[:3]:
            arrival.start()
        del behind[:3]

    def leave(piece, home):
        move = pltpu.make_async_copy(piece, home, stored.at[len(leaving)])
        move.start()
        leaving.append(move)

    def factors(total, first, second, out_first, out_second, add_first=False, add_second=False):
        count, columns = total.shape
        step = 256 if count % 256 == 0 else 320
        width = 512 if columns % 512 == 0 else columns // 2
        if not add_second:
            out_second[...] = jnp.zeros(out_second.shape, jnp.float32)
        for at in range(columns // width):
            part = pl.ds(at * width, width)

            def body(index, carry):
                block = pl.ds(pl.multiple_of(index * step, 64), step)
                value = total[block, part]
                high = value.astype(jnp.bfloat16)
                low = (value - high.astype(jnp.float32)).astype(jnp.bfloat16)
                other = second[:, part]
                product = right_transposed(high, other) + right_transposed(low, other)
                if add_first or at > 0:
                    product = product + out_first[block, :]
                out_first[block, :] = product
                this = first[block, :]
                out_second[:, part] = (
                    out_second[:, part] + left_transposed(this, high) + left_transposed(this, low)
                )
                return carry

            lax.fori_loop(0, count // step, body, 0)

    rank = made.query_a.shape[1]

    def columns_of(ref, part, size):
        return ref.at[:, pl.ds(part * size, size)]

    def rows_of(ref, part, size):
        return ref.at[pl.ds(part * size, size)]

    need(arrivals.down_a, arrivals.down_b, arrivals.d)
    leave(held.d.at[core], target.down)
    for group in range(2):
        total = held.d.at[group]
        size = total.shape[0]
        first = rows_of(held.down_a, group, size)
        out = rows_of(made.down_a, group, size)
        factors(total, first, held.down_b, out, made.down_b, False, group > 0)
    leave(made.down_a, target.down_a)
    leave(made.down_b, target.down_b)
    need(arrivals.gateup_a, arrivals.gateup_b)
    for part, name in enumerate((held.g, held.u)):
        need((arrivals.g, arrivals.u)[part])
        leave(name.at[core], target.gateup.at[part])
        for group in range(2):
            total = name.at[group]
            size = total.shape[1]
            second = columns_of(held.gateup_b.at[part], group, size)
            first = columns_of(held.gateup_a, part, rank)
            out_first = columns_of(made.gateup_a, part, rank)
            out_second = columns_of(made.gateup_b.at[part], group, size)
            factors(total, first, second, out_first, out_second, group > 0, False)
        leave(made.gateup_b.at[part], target.gateup_b.at[part])
    leave(made.gateup_a, target.gateup_a)
    need(arrivals.output_a, arrivals.output_b, arrivals.o)
    leave(held.o.at[core], target.output)
    for group in range(2):
        total = held.o.at[group]
        size = total.shape[0]
        first = rows_of(held.output_a, group, size)
        out = rows_of(made.output_a, group, size)
        factors(total, first, held.output_b, out, made.output_b, False, group > 0)
    leave(made.output_a, target.output_a)
    leave(made.output_b, target.output_b)
    need(arrivals.query_a, arrivals.query_b, arrivals.q)
    leave(held.q.at[core], target.query)
    for group in range(2):
        total = held.q.at[group]
        size = total.shape[1]
        second = columns_of(held.query_b, group, size)
        out = columns_of(made.query_b, group, size)
        factors(total, held.query_a, second, made.query_a, out, group > 0, False)
    leave(made.query_a, target.query_a)
    leave(made.query_b, target.query_b)
    need(arrivals.keyvalue_a, arrivals.keyvalue_b, arrivals.k)
    leave(held.k, target.keyvalue)
    for part in range(2):
        width = made.keyvalue_b.shape[2]
        total = columns_of(held.k, part, width)
        out = columns_of(made.keyvalue_a, part, rank)
        first = columns_of(held.keyvalue_a, part, rank)
        factors(total, first, held.keyvalue_b.at[part], out, made.keyvalue_b.at[part])
    leave(made.keyvalue_a, target.keyvalue_a)
    leave(made.keyvalue_b, target.keyvalue_b)
    need(arrivals.small, arrivals.result, arrivals.tokens)
    leave(held.result, target.result)
    leave(held.tokens, target.tokens)
    row = 0
    for gain, home in zip(gains, target[-6:]):
        for at in range(gain.shape[0] // 128):
            gain[pl.ds(at * 128, 128)] = held.small[row]
            row += 1
        leave(gain, home)
    for move in leaving:
        move.wait()


def derive_adapters(values, widths):
    made = [getattr(values, name) for name in Adapters._fields]
    shapes = [
        values.d.shape[1:],
        (2,) + values.g.shape[1:],
        values.o.shape[1:],
        values.q.shape[1:],
        values.k.shape,
    ]
    shapes += [array.shape for array in made]
    shapes += [values.result.shape, values.tokens.shape] + [(width,) for width in widths]
    kinds = [jnp.float32] * len(shapes)
    kinds[len(made) + 5] = values.result.dtype
    results = pl.pallas_call(
        derive_kernel,
        out_shape=[jax.ShapeDtypeStruct(*out) for out in zip(shapes, kinds)],
        in_specs=[ANYWHERE] * len(values),
        out_specs=[ANYWHERE] * len(shapes),
        scratch_shapes=[pltpu.VMEM(array.shape, array.dtype) for array in values]
        + [pltpu.VMEM(array.shape, jnp.float32) for array in made]
        + [pltpu.VMEM((width,), jnp.float32) for width in widths]
        + [
            pltpu.SemaphoreType.DMA((len(values),)),
            pltpu.SemaphoreType.DMA((len(shapes) + 2,)),
        ],
        compiler_params=pltpu.CompilerParams(vmem_limit_bytes=67043328),
    )(*values)
    return DeriveOutputs(*results)


def on_device_general(
    tokens,
    document_numbers,
    input_norm_gain,
    after_attention_gain,
    before_feedforward_gain,
    after_feedforward_gain,
    query_norm_gain,
    key_norm_gain,
    query_weight,
    keyvalue_weight,
    output_weight,
    gateup_weight,
    down_weight,
    query_adapter_first,
    query_adapter_second,
    keyvalue_adapter_first,
    keyvalue_adapter_second,
    output_adapter_first,
    output_adapter_second,
    gateup_adapter_first,
    gateup_adapter_second,
    down_adapter_first,
    down_adapter_second,
    cotangent,
):
    inputs = tokens[0].astype(jnp.float32)
    segments = document_numbers[0]
    length = inputs.shape[0]
    head_width = keyvalue_adapter_second.shape[2]
    adapter_rank = query_adapter_first.shape[1]
    query_columns = query_weight.shape[1]
    hidden_columns = down_weight.shape[0]
    heads_local = query_columns // head_width
    group_position = lax.axis_index(TENSOR)
    query_piece = lax.dynamic_slice_in_dim(
        query_adapter_second, group_position * query_columns, query_columns, 1
    )
    output_rows = lax.dynamic_slice_in_dim(
        output_adapter_first, group_position * query_columns, query_columns, 0
    )
    gateup_piece = lax.dynamic_slice_in_dim(
        gateup_adapter_second, group_position * hidden_columns, hidden_columns, 2
    )
    down_rows = lax.dynamic_slice_in_dim(
        down_adapter_first, group_position * hidden_columns, hidden_columns, 0
    )
    query_merged = (
        query_weight.astype(jnp.float32) + matrix_product(query_adapter_first, query_piece)
    ).astype(jnp.bfloat16)
    keyvalue_merged = (
        keyvalue_weight.astype(jnp.float32)
        + jnp.concatenate(
            [
                matrix_product(keyvalue_adapter_first[:, :adapter_rank], keyvalue_adapter_second[0]),
                matrix_product(keyvalue_adapter_first[:, adapter_rank:], keyvalue_adapter_second[1]),
            ],
            axis=1,
        )
    ).astype(jnp.bfloat16)
    output_merged = (
        output_weight.astype(jnp.float32) + matrix_product(output_rows, output_adapter_second)
    ).astype(jnp.bfloat16)
    gate_merged = (
        gateup_weight[0].astype(jnp.float32)
        + matrix_product(gateup_adapter_first[:, :adapter_rank], gateup_piece[0])
    ).astype(jnp.bfloat16)
    up_merged = (
        gateup_weight[1].astype(jnp.float32)
        + matrix_product(gateup_adapter_first[:, adapter_rank:], gateup_piece[1])
    ).astype(jnp.bfloat16)
    down_merged = (
        down_weight.astype(jnp.float32) + matrix_product(down_rows, down_adapter_second)
    ).astype(jnp.bfloat16)
    positions = positions_of(segments)
    key_index = jnp.arange(length, dtype=jnp.int32)
    block_rows = min(512, length)
    normalized_rows, in_back = jax.vjp(rms_scale, inputs, input_norm_gain)
    normalized_lowrank = normalized_rows.astype(jnp.bfloat16)
    query_rows = matrix_product(normalized_lowrank, query_merged)
    keyvalue = matrix_product(normalized_lowrank, keyvalue_merged)

    def prepare(q_in, kv_in, q_scale, k_scale):
        q_heads = rms_scale(q_in.reshape(length, heads_local, head_width), q_scale)
        q_out = rotate(q_heads, positions) * head_width ** (-0.5)
        k_out = rotate(rms_scale(kv_in[:, :head_width], k_scale), positions)
        return (q_out, k_out, kv_in[:, head_width:])

    prepared, prepare_back = jax.vjp(prepare, query_rows, keyvalue, query_norm_gain, key_norm_gain)
    q_rot = prepared[0].astype(jnp.bfloat16)
    k_rot = prepared[1].astype(jnp.bfloat16)
    v_low = prepared[2].astype(jnp.bfloat16)

    def scores_of(row_start):
        rows = q_rot[row_start : row_start + block_rows]
        raw = jnp.einsum("qhd,kd->hqk", rows, k_rot, preferred_element_type=jnp.float32)
        row_index = row_start + jnp.arange(block_rows, dtype=jnp.int32)
        allowed = (segments[row_start : row_start + block_rows][:, None] == segments[None, :]) & (
            row_index[:, None] >= key_index[None, :]
        )
        return jnp.where(allowed[None], raw, MASKED)

    outputs = []
    log_totals = []
    for row_start in range(0, length, block_rows):
        scores = scores_of(row_start)
        row_peak = jnp.max(scores, axis=-1, keepdims=True)
        weights = jnp.exp(scores - row_peak)
        row_total = jnp.sum(weights, axis=-1, keepdims=True)
        log_totals.append(row_peak + jnp.log(row_total))
        probs_low = (weights / row_total).astype(jnp.bfloat16)
        outputs.append(
            jnp.einsum("hqk,kd->qhd", probs_low, v_low, preferred_element_type=jnp.float32)
        )
    attended_rows = (
        jnp.concatenate(outputs, axis=0).reshape(length, query_columns).astype(jnp.bfloat16)
    )
    attention_before = lax.psum(matrix_product(attended_rows, output_merged), TENSOR)
    attn_post, post_attn_back = jax.vjp(rms_scale, attention_before, after_attention_gain)
    residual = inputs + attn_post
    normed_ff, pre_ff_back = jax.vjp(rms_scale, residual, before_feedforward_gain)
    feedforward_lowrank = normed_ff.astype(jnp.bfloat16)
    gate_portion = matrix_product(feedforward_lowrank, gate_merged)
    up_portion = matrix_product(feedforward_lowrank, up_merged)
    hidden_full, activate_back = jax.vjp(activate, gate_portion, up_portion)
    hidden_activation = hidden_full.astype(jnp.bfloat16)
    feedforward_before = lax.psum(matrix_product(hidden_activation, down_merged), TENSOR)
    mlp_post, post_ff_back = jax.vjp(rms_scale, feedforward_before, after_feedforward_gain)
    result_value = (residual + mlp_post).astype(jnp.bfloat16)[None]
    grad_out = cotangent[0].astype(jnp.float32)
    grad_mlp_pre, gradient_after_feedforward = post_ff_back(grad_out)
    gradient_feedforward_lowrank = grad_mlp_pre.astype(jnp.bfloat16)
    gradient_down_weight = left_transposed(hidden_activation, gradient_feedforward_lowrank)
    grad_hidden = right_transposed(gradient_feedforward_lowrank, down_merged)
    grad_gate, grad_up = activate_back(grad_hidden)
    gate_lowrank = grad_gate.astype(jnp.bfloat16)
    up_lowrank = grad_up.astype(jnp.bfloat16)
    gradient_gateup_weight = jnp.stack(
        [
            left_transposed(feedforward_lowrank, gate_lowrank),
            left_transposed(feedforward_lowrank, up_lowrank),
        ]
    )
    grad_ff_part = right_transposed(gate_lowrank, gate_merged) + right_transposed(
        up_lowrank, up_merged
    )
    grad_normed_ff = lax.psum(grad_ff_part, TENSOR)
    grad_residual_ff, gradient_before_feedforward = pre_ff_back(grad_normed_ff)
    grad_residual = grad_out + grad_residual_ff
    grad_attn_pre, gradient_after_attention = post_attn_back(grad_residual)
    gradient_attention_lowrank = grad_attn_pre.astype(jnp.bfloat16)
    gradient_output_weight = left_transposed(attended_rows, gradient_attention_lowrank)
    grad_attended = right_transposed(gradient_attention_lowrank, output_merged).astype(jnp.bfloat16)
    grad_attended = grad_attended.reshape(length, heads_local, head_width)
    grad_q_blocks = []
    grad_k_rot = jnp.zeros((length, head_width), jnp.float32)
    grad_values = jnp.zeros((length, head_width), jnp.float32)
    for block_index, row_start in enumerate(range(0, length, block_rows)):
        scores = scores_of(row_start)
        probs = jnp.exp(scores - log_totals[block_index])
        grad_rows = grad_attended[row_start : row_start + block_rows]
        grad_probs = jnp.einsum("qhd,kd->hqk", grad_rows, v_low, preferred_element_type=jnp.float32)
        grad_scores = (
            probs * (grad_probs - jnp.sum(probs * grad_probs, axis=-1, keepdims=True))
        ).astype(jnp.bfloat16)
        grad_q_blocks.append(
            jnp.einsum("hqk,kd->qhd", grad_scores, k_rot, preferred_element_type=jnp.float32)
        )
        grad_k_rot = grad_k_rot + jnp.einsum(
            "hqk,qhd->kd",
            grad_scores,
            q_rot[row_start : row_start + block_rows],
            preferred_element_type=jnp.float32,
        )
        grad_values = grad_values + jnp.einsum(
            "hqk,qhd->kd", probs.astype(jnp.bfloat16), grad_rows, preferred_element_type=jnp.float32
        )
    grad_queries, grad_keyvalue, gradient_query_norm_gain, gradient_key_norm_gain = prepare_back(
        (jnp.concatenate(grad_q_blocks, axis=0), grad_k_rot, grad_values)
    )
    query_low = grad_queries.astype(jnp.bfloat16)
    keyvalue_gradient_lowrank = grad_keyvalue.astype(jnp.bfloat16)
    gradient_query_weight = left_transposed(normalized_lowrank, query_low)
    gradient_keyvalue_weight = left_transposed(normalized_lowrank, keyvalue_gradient_lowrank)
    grad_in_part = right_transposed(query_low, query_merged) + right_transposed(
        keyvalue_gradient_lowrank, keyvalue_merged
    )
    grad_normed = lax.psum(grad_in_part, TENSOR)
    grad_inputs_add, gradient_input_gain = in_back(grad_normed)
    gradient_token_input = (grad_residual + grad_inputs_add)[None]
    lead_mask = (group_position == 0).astype(jnp.float32)
    lead_in = gradient_input_gain * lead_mask
    lead_post_attn = gradient_after_attention * lead_mask
    lead_pre_ff = gradient_before_feedforward * lead_mask
    lead_post_ff = gradient_after_feedforward * lead_mask
    sum_w_query, sum_w_out, sum_w_gate_up, sum_w_down = lax.psum(
        (
            gradient_query_weight,
            gradient_output_weight,
            gradient_gateup_weight,
            gradient_down_weight,
        ),
        DP,
    )
    (
        sum_gain_in,
        sum_post_attn,
        sum_pre_ff,
        sum_post_ff,
        sum_query_gain,
        sum_key_gain,
        sum_w_keyvalue,
    ) = lax.psum(
        (
            lead_in,
            lead_post_attn,
            lead_pre_ff,
            lead_post_ff,
            gradient_query_norm_gain,
            gradient_key_norm_gain,
            gradient_keyvalue_weight,
        ),
        (DP, TENSOR),
    )
    rows_rows = ((0,), (0,))
    columns_columns = ((1,), (1,))
    sum_kv_b = jnp.stack(
        [
            exact_product(
                sum_w_keyvalue[:, i * head_width : (i + 1) * head_width],
                keyvalue_adapter_first[:, i * adapter_rank : (i + 1) * adapter_rank],
                rows_rows,
            ).T
            for i in range(2)
        ]
    )
    sum_kv_a = jnp.concatenate(
        [
            exact_product(
                sum_w_keyvalue[:, i * head_width : (i + 1) * head_width],
                keyvalue_adapter_second[i],
                columns_columns,
            )
            for i in range(2)
        ],
        axis=1,
    )
    part_q_b = exact_product(sum_w_query, query_adapter_first, rows_rows).T
    part_q_a = exact_product(sum_w_query, query_piece, columns_columns)
    part_o_a = exact_product(sum_w_out, output_adapter_second, columns_columns)
    part_o_b = exact_product(sum_w_out, output_rows, rows_rows).T
    part_gu_b = jnp.stack(
        [
            exact_product(
                sum_w_gate_up[i],
                gateup_adapter_first[:, i * adapter_rank : (i + 1) * adapter_rank],
                rows_rows,
            ).T
            for i in range(2)
        ]
    )
    part_gu_a = jnp.concatenate(
        [exact_product(sum_w_gate_up[i], gateup_piece[i], columns_columns) for i in range(2)],
        axis=1,
    )
    part_d_a = exact_product(sum_w_down, down_adapter_second, columns_columns)
    part_d_b = exact_product(sum_w_down, down_rows, rows_rows).T
    sum_q_a, sum_o_b, sum_gu_a, sum_d_b = lax.psum(
        (part_q_a, part_o_b, part_gu_a, part_d_b), TENSOR
    )
    sum_q_b = lax.all_gather(part_q_b, TENSOR, axis=1, tiled=True)
    sum_o_a = lax.all_gather(part_o_a, TENSOR, axis=0, tiled=True)
    sum_gu_b = lax.all_gather(part_gu_b, TENSOR, axis=2, tiled=True)
    sum_d_a = lax.all_gather(part_d_a, TENSOR, axis=0, tiled=True)
    return (
        result_value,
        gradient_token_input,
        sum_gain_in,
        sum_post_attn,
        sum_pre_ff,
        sum_post_ff,
        sum_query_gain,
        sum_key_gain,
        sum_w_query,
        sum_w_keyvalue,
        sum_w_out,
        sum_w_gate_up,
        sum_w_down,
        sum_q_a,
        sum_q_b,
        sum_kv_a,
        sum_kv_b,
        sum_o_a,
        sum_o_b,
        sum_gu_a,
        sum_gu_b,
        sum_d_a,
        sum_d_b,
    )


def on_device_fast(
    tokens,
    document_numbers,
    input_norm_gain,
    after_attention_gain,
    before_feedforward_gain,
    after_feedforward_gain,
    query_norm_gain,
    key_norm_gain,
    query_weight,
    keyvalue_weight,
    output_weight,
    gateup_weight,
    down_weight,
    query_adapter_first,
    query_adapter_second,
    keyvalue_adapter_first,
    keyvalue_adapter_second,
    output_adapter_first,
    output_adapter_second,
    gateup_adapter_first,
    gateup_adapter_second,
    down_adapter_first,
    down_adapter_second,
    cotangent,
):
    length = document_numbers.shape[1]
    head_width = keyvalue_adapter_second.shape[2]
    width = input_norm_gain.shape[0]
    ahead = forward_pass(
        ForwardInputs(
            tokens=tokens[0],
            gin=input_norm_gain,
            w_q=query_weight,
            a_q=query_adapter_first,
            b_q=query_adapter_second,
            w_kv=keyvalue_weight,
            a_kv=keyvalue_adapter_first,
            b_kv=keyvalue_adapter_second,
            table=rotation_table(length, head_width),
            segments=document_numbers,
            gq=query_norm_gain,
            gk=key_norm_gain,
            w_o=output_weight,
            a_o=output_adapter_first,
            b_o=output_adapter_second,
            pa=after_attention_gain,
            pf=before_feedforward_gain,
            w_gu=gateup_weight,
            a_gu=gateup_adapter_first,
            b_gu=gateup_adapter_second,
            w_d=down_weight,
            a_d=down_adapter_first,
            b_d=down_adapter_second,
        )
    )
    shapes = Pieces(
        d=down_weight.shape,
        g=gateup_weight.shape[1:],
        u=gateup_weight.shape[1:],
        o=output_weight.shape,
        q=query_weight.shape,
        k=keyvalue_weight.shape,
        s=(32, 128),
    )
    values = BackwardInputs(
        tokens=tokens[0],
        cot=cotangent[0],
        pa=after_attention_gain,
        pff=after_feedforward_gain,
        pf=before_feedforward_gain,
        segments=document_numbers,
        gq=query_norm_gain,
        gk=key_norm_gain,
        gin=input_norm_gain,
        **ahead._asdict(),
    )
    (result, grad_tokens, sum_k, sum_s), both = backward_and_sums(values, shapes)
    sum_d, sum_g, sum_u, sum_o, sum_q = both
    derived = derive_adapters(
        DeriveInputs(
            down_a=down_adapter_first,
            down_b=down_adapter_second,
            d=sum_d,
            gateup_a=gateup_adapter_first,
            gateup_b=gateup_adapter_second,
            g=sum_g,
            u=sum_u,
            output_a=output_adapter_first,
            output_b=output_adapter_second,
            o=sum_o,
            query_a=query_adapter_first,
            query_b=query_adapter_second,
            q=sum_q,
            keyvalue_a=keyvalue_adapter_first,
            keyvalue_b=keyvalue_adapter_second,
            k=sum_k,
            small=sum_s,
            result=result,
            tokens=grad_tokens,
        ),
        (width,) * 4 + (head_width,) * 2,
    )
    return (
        derived.result[None],
        derived.tokens[None],
        derived.gain_in,
        derived.gain_pa,
        derived.gain_pf,
        derived.gain_pff,
        derived.gain_q,
        derived.gain_k,
        derived.query,
        derived.keyvalue,
        derived.output,
        derived.gateup,
        derived.down,
        derived.query_a,
        derived.query_b,
        derived.keyvalue_a,
        derived.keyvalue_b,
        derived.output_a,
        derived.output_b,
        derived.gateup_a,
        derived.gateup_b,
        derived.down_a,
        derived.down_b,
    )


def solution(mesh):
    in_specs = (
        P(DP, None, None),
        P(DP, None),
        P(),
        P(),
        P(),
        P(),
        P(),
        P(),
        P(None, TENSOR),
        P(),
        P(TENSOR, None),
        P(None, None, TENSOR),
        P(TENSOR, None),
        P(),
        P(),
        P(),
        P(),
        P(),
        P(),
        P(),
        P(),
        P(),
        P(),
        P(DP, None, None),
    )
    out_specs = (
        P(DP, None, None),
        P(DP, None, None),
        P(),
        P(),
        P(),
        P(),
        P(),
        P(),
        P(None, TENSOR),
        P(),
        P(TENSOR, None),
        P(None, None, TENSOR),
        P(TENSOR, None),
        P(),
        P(),
        P(),
        P(),
        P(),
        P(),
        P(),
        P(),
        P(),
        P(),
    )
    fast = mesh.shape[DP] == 16 and mesh.shape[TENSOR] == 2
    return jax.shard_map(
        on_device_fast if fast else on_device_general,
        mesh=mesh, in_specs=in_specs, out_specs=out_specs, check_vma=False
    )
```

```python
import functools
from typing import NamedTuple

import jax
import jax.numpy as jnp
import numpy as np
from jax import lax
from jax.experimental import pallas as pl
from jax.experimental.pallas import tpu as pltpu
from jax.sharding import PartitionSpec as P

EPS = 1e-06
THETA = 1000000.0
MASKED = -1e30
GELU = 0.7978845608028654
DP, TENSOR = "dp", "tensor"
ROWS = 256
MESH_ID = pl.DeviceIdType.MESH
ANYWHERE = pl.BlockSpec(memory_space=pl.ANY)


def matrix_product(left_side, right_side):
    return jnp.dot(left_side, right_side, preferred_element_type=jnp.float32)


def left_transposed(left_side, right_side):
    return lax.dot_general(
        left_side, right_side, (((0,), (0,)), ((), ())), preferred_element_type=jnp.float32
    )


def right_transposed(left_side, right_side):
    return lax.dot_general(
        left_side, right_side, (((1,), (1,)), ((), ())), preferred_element_type=jnp.float32
    )


def rms_scale(values, scale_gain):
    return values * lax.rsqrt(jnp.mean(values * values, axis=-1, keepdims=True) + EPS) * scale_gain


def positions_of(segments):
    length = segments.shape[0]
    indices = jnp.arange(length, dtype=jnp.int32)
    before = jnp.concatenate([jnp.full((1,), -1, jnp.int32), segments[:-1]])
    starts = lax.cummax(jnp.where(segments != before, indices, jnp.zeros_like(indices)), axis=0)
    return indices - starts


def rotate(values, positions):
    half_dim = values.shape[-1] // 2
    frequency = THETA ** (-jnp.arange(half_dim, dtype=jnp.float32) * 2.0 / values.shape[-1])
    angles = positions.astype(jnp.float32)[:, None] * frequency[None, :]
    cosine = jnp.cos(angles)
    sine_part = jnp.sin(angles)
    if values.ndim == 3:
        cosine = cosine[:, None, :]
        sine_part = sine_part[:, None, :]
    leading = values[..., :half_dim]
    trailing = values[..., half_dim:]
    return jnp.concatenate(
        [leading * cosine - trailing * sine_part, trailing * cosine + leading * sine_part], axis=-1
    )


def exact_product(left_side, right_side, contract):
    return lax.dot_general(
        left_side,
        right_side.astype(jnp.float32),
        (contract, ((), ())),
        precision=lax.Precision.HIGHEST,
        preferred_element_type=jnp.float32,
    )


def activate(gate_in, up_in):
    return jax.nn.gelu(gate_in, approximate=True) * up_in


class Place:
    def __init__(self):
        me = lax.axis_index(DP)
        core = lax.axis_index(TENSOR)
        bit_x = lax.rem(me, 2)
        bit_y = lax.rem(me // 2, 2)
        level = me // 4
        across_x = me + 1 - 2 * bit_x
        across_y = me + 2 - 4 * bit_y
        self.core = core
        self.side = level // 2
        self.level = level
        self.outer = jnp.logical_or(level == 0, level == 3)
        self.inner = jnp.logical_not(self.outer)
        self.bits = (jnp.where(core == 0, bit_x, bit_y), jnp.where(core == 0, bit_y, bit_x))
        self.across = (
            (jnp.where(core == 0, across_x, across_y), core),
            (jnp.where(core == 0, across_y, across_x), core),
        )
        column = lax.rem(me, 4)
        self.near = ((level + 1 - 2 * lax.rem(level, 2)) * 4 + column, core)
        self.middle = ((3 - level) * 4 + column, core)
        self.sibling = (me, 1 - core)


def add_rows(target, target_row, extra, extra_row, count):
    step = 32 if count % 32 == 0 else (16 if count % 16 == 0 else 8)

    def body(index, carry):
        rows = pl.ds(pl.multiple_of(target_row + index * step, 8), step)
        target[rows] = target[rows] + extra[pl.ds(pl.multiple_of(extra_row + index * step, 8), step)]
        return carry

    lax.fori_loop(0, count // step, body, 0)


class Sums:
    def __init__(self, place, sends, receives, freed):
        self.place = place
        self.sends = sends
        self.receives = receives
        self.freed = freed
        self.used = 0
        self.credits = 0

    def credit(self):
        self.credits += 1
        return self.freed.at[self.credits - 1]

    def copy(self, source, target, device):
        slot = self.used
        self.used += 1
        return pltpu.make_async_remote_copy(
            src_ref=source,
            dst_ref=target,
            send_sem=self.sends.at[slot],
            recv_sem=self.receives.at[slot],
            device_id=device,
            device_id_type=MESH_ID,
        )


def signal(semaphore, device):
    pl.semaphore_signal(semaphore, inc=1, device_id=device, device_id_type=MESH_ID)


def rows_at(ref, start, count):
    return ref.at[pl.ds(pl.multiple_of(start, 8), count)]


def plane_first(sums, total, row, count, landing, landing_row, finish, turned):
    place = sums.place
    half, quarter = count // 2, count // 4
    bit_one, bit_two = place.bits[turned], place.bits[1 - turned]
    one, two = place.across[turned], place.across[1 - turned]
    kept = row + bit_one * half
    given = row + (1 - bit_one) * half
    mine = kept + bit_two * quarter
    other = kept + (1 - bit_two) * quarter
    land_one = rows_at(landing, landing_row, half)
    land_two = rows_at(landing, landing_row + half, quarter)
    land_near = rows_at(landing, landing_row + half + quarter, quarter)
    land_mid = rows_at(landing, landing_row + 2 * half, quarter)
    ours = rows_at(total, mine, quarter)
    copy_one = sums.copy(rows_at(total, given, half), land_one, one)
    copy_two = sums.copy(rows_at(total, other, quarter), land_two, two)
    copy_in = sums.copy(ours, land_near, place.near)
    copy_mid = sums.copy(ours, land_mid, place.middle)
    copy_out = sums.copy(ours, ours, place.near)
    back_two = sums.copy(ours, ours, two)
    back_one = sums.copy(rows_at(total, kept, half), rows_at(total, kept, half), one)

    free_one, free_two, free_in = sums.credit(), sums.credit(), sums.credit()

    def step0():
        copy_one.start()

    def step1():
        copy_one.wait_recv()
        add_rows(total, kept, landing, landing_row, half)
        copy_two.start()

    def step2():
        copy_two.wait_recv()
        add_rows(total, mine, landing, landing_row + half, quarter)

        @pl.when(place.outer)
        def _():
            copy_in.start()

        copy_one.wait_send()
        signal(free_one, one)

    def step3():
        @pl.when(place.inner)
        def _():
            copy_in.wait_recv()
            add_rows(total, mine, landing, landing_row + half + quarter, quarter)
            copy_mid.start()

        copy_two.wait_send()
        signal(free_two, two)

        @pl.when(place.outer)
        def _():
            copy_in.wait_send()
            signal(free_in, place.near)

    def step4():
        @pl.when(place.inner)
        def _():
            copy_mid.wait()
            add_rows(total, mine, landing, landing_row + 2 * half, quarter)
            pl.semaphore_wait(free_in, 1)
            copy_out.start()
            pl.semaphore_wait(free_two, 1)
            back_two.start()

    def step5():
        @pl.when(place.outer)
        def _():
            copy_out.wait_recv()
            pl.semaphore_wait(free_two, 1)
            back_two.start()

    def step6():
        back_two.wait_recv()
        pl.semaphore_wait(free_one, 1)
        back_one.start()

    def step7():
        back_one.wait_recv()
        back_two.wait_send()
        back_one.wait_send()

        @pl.when(place.inner)
        def _():
            copy_out.wait_send()

        finish()

    return [step0, step1, step2, step3, step4, step5, step6, step7]


def line_first(sums, total, row, count, landing, landing_row, finish, turned):
    place = sums.place
    one, two = place.across[turned], place.across[1 - turned]
    quarter = count // 4
    side = place.side
    three = row + (1 - side) * quarter
    far_pair = row + (1 - side) * 2 * quarter
    own_pair = row + side * 2 * quarter
    outer_quarter = row + 3 * side * quarter
    mine = row + place.level * quarter
    ours = rows_at(total, mine, quarter)
    land_three = rows_at(landing, landing_row, 3 * quarter)
    land_pair = rows_at(landing, landing_row + 3 * quarter, 2 * quarter)
    land_back = rows_at(landing, landing_row, quarter)
    land_one = rows_at(landing, landing_row + 5 * quarter, quarter)
    land_two = rows_at(landing, landing_row + 6 * quarter, quarter)
    copy_three = sums.copy(rows_at(total, three, 3 * quarter), land_three, place.near)
    copy_pair = sums.copy(rows_at(total, far_pair, 2 * quarter), land_pair, place.middle)
    outers = rows_at(total, outer_quarter, quarter)
    copy_back = sums.copy(outers, land_back, place.near)
    copy_one = sums.copy(ours, land_one, one)
    copy_two = sums.copy(ours, land_two, two)
    spread_in = sums.copy(ours, ours, place.near)
    spread_out = sums.copy(ours, ours, place.near)
    spread_mid = sums.copy(ours, ours, place.middle)
    forward_mid = sums.copy(outers, outers, place.middle)
    far_rows = rows_at(total, far_pair, 2 * quarter)
    forward_out = sums.copy(far_rows, far_rows, place.near)

    free_three, free_pair, free_back = sums.credit(), sums.credit(), sums.credit()

    def step0():
        @pl.when(place.outer)
        def _():
            copy_three.start()

    def step1():
        @pl.when(place.inner)
        def _():
            copy_three.wait_recv()
            add_rows(total, three, landing, landing_row, 3 * quarter)
            copy_pair.start()

    def step2():
        @pl.when(place.inner)
        def _():
            copy_pair.wait_recv()
            add_rows(total, own_pair, landing, landing_row + 3 * quarter, 2 * quarter)
            copy_back.start()
            copy_one.start()

    def step3():
        @pl.when(place.outer)
        def _():
            copy_back.wait_recv()
            add_rows(total, mine, landing, landing_row, quarter)
            copy_one.start()
            copy_three.wait_send()
            signal(free_three, place.near)

        @pl.when(place.inner)
        def _():
            copy_pair.wait_send()
            signal(free_pair, place.middle)
            copy_back.wait_send()
            signal(free_back, place.near)

    def step4():
        copy_one.wait()
        add_rows(total, mine, landing, landing_row + 5 * quarter, quarter)
        copy_two.start()

    def step5():
        copy_two.wait()
        add_rows(total, mine, landing, landing_row + 6 * quarter, quarter)

        @pl.when(place.outer)
        def _():
            pl.semaphore_wait(free_back, 1)
            spread_in.start()

        @pl.when(place.inner)
        def _():
            pl.semaphore_wait(free_three, 1)
            spread_out.start()
            pl.semaphore_wait(free_pair, 1)
            spread_mid.start()

    def step6():
        @pl.when(place.inner)
        def _():
            spread_in.wait_recv()
            forward_mid.start()

    def step7():
        @pl.when(place.inner)
        def _():
            spread_mid.wait_recv()
            forward_mid.wait_recv()
            forward_out.start()

    def step8():
        @pl.when(place.outer)
        def _():
            spread_out.wait_recv()
            forward_out.wait_recv()
            spread_in.wait_send()

        @pl.when(place.inner)
        def _():
            spread_out.wait_send()
            spread_mid.wait_send()
            forward_mid.wait_send()
            forward_out.wait_send()

        finish()

    return [step0, step1, step2, step3, step4, step5, step6, step7, step8]


def greet(place):
    barrier = pltpu.get_barrier_semaphore()
    for device in (*place.across, place.near, place.sibling):
        pl.semaphore_signal(barrier, inc=1, device_id=device, device_id_type=MESH_ID)

    @pl.when(place.inner)
    def _():
        pl.semaphore_signal(barrier, inc=1, device_id=place.middle, device_id_type=MESH_ID)
        pl.semaphore_wait(barrier, 5)

    @pl.when(place.outer)
    def _():
        pl.semaphore_wait(barrier, 4)


class BackwardInputs(NamedTuple):
    gml: object
    hidden: object
    ff: object
    w_g: object
    w_u: object
    w_d: object
    mlp: object
    attn: object
    tokens: object
    cot: object
    pa: object
    pff: object
    pf: object
    w_o: object
    attended: object
    q_rot: object
    k_rot: object
    values: object
    segments: object
    lse: object
    cosine: object
    sine: object
    normed: object
    w_q: object
    gq: object
    w_kv: object
    gk: object
    gin: object
    gain_pff: object


class Pieces(NamedTuple):
    d: object
    g: object
    u: object
    o: object
    q: object
    k: object
    s: object


PIECE_K, PIECE_S = 5, 6
PARTS = ((0, None),)
PARTS += tuple((piece, block) for block in range(4) for piece in (1, 2))
PARTS += ((3, None), (4, 0), (4, 1), (5, None), (6, None))


class Work(NamedTuple):
    gate: object
    up: object
    part: object
    other: object
    dq: object
    gains: object
    gain_q: object
    gain_k: object
    result: object


def row_loop(count, body, start=0):
    def step(index, carry):
        body(pl.ds(pl.multiple_of(index * ROWS, ROWS), ROWS), index)
        return carry

    lax.fori_loop(start, count, step, 0)


def row_at(segments, index):
    columns = pl.ds(pl.multiple_of(index * ROWS, ROWS), ROWS)
    return segments[:, columns].astype(jnp.float32)


def column_of(row):
    shape = (row.shape[1], row.shape[1])
    diagonal = lax.broadcasted_iota(jnp.int32, shape, 0) == lax.broadcasted_iota(jnp.int32, shape, 1)
    return jnp.sum(jnp.where(diagonal, row, 0.0), axis=1, keepdims=True)


def inverse_rms(values):
    return lax.rsqrt(jnp.mean(values * values, axis=-1, keepdims=True) + EPS)


def rms_back(incoming, gain, normed, inverse):
    scaled = incoming * gain
    return inverse * (scaled - normed * jnp.mean(scaled * normed, axis=-1, keepdims=True))


def add_gain(target, terms):
    width = terms.shape[1]
    target[...] = target[...] + jnp.sum(terms.reshape(-1, 8, width), axis=0)


def gelu_parts(gate):
    inner = 0.7978845608028654 * gate * (1.0 + 0.044715 * gate * gate)
    bent = jnp.tanh(inner)
    half = 0.5 * (1.0 + bent)
    slope = half + 0.5 * gate * (1.0 - bent * bent) * 0.7978845608028654 * (
        1.0 + 0.134145 * gate * gate
    )
    return gate * half, slope


def turn_back(values, cosine, sine):
    half = values.shape[1] // 2
    leading, trailing = values[:, :half], values[:, half:]
    return jnp.concatenate(
        [leading * cosine + trailing * sine, trailing * cosine - leading * sine], axis=1
    )


def backward_kernel(setup, *refs):
    plan, order = setup
    refs = list(refs)
    source = BackwardInputs(*refs[: len(BackwardInputs._fields)])
    refs = refs[len(source) :]
    out_home, token_home, own_k, own_s = refs[:4]
    both = refs[4 : 4 + len(Pieces._fields) - 2]
    refs = refs[4 + len(both) :]
    held = BackwardInputs(*refs[: len(source)])
    refs = refs[len(source) :]
    total = Pieces(*refs[: len(Pieces._fields)])
    refs = refs[len(total) :]
    landing = refs[: len(PARTS)]
    refs = refs[len(PARTS) :]
    swapped_k, swapped_s = refs[:2]
    work = Work(*refs[2 : 2 + len(Work._fields)])
    loads, sends, receives, local, freed, handed = refs[2 + len(work) :]
    place = Place()
    core = place.core
    sums = Sums(place, sends, receives, freed)
    arrivals = BackwardInputs(
        *(
            pltpu.make_async_copy(piece, home, loads.at[index])
            for index, (piece, home) in enumerate(zip(source, held))
        )
    )
    for arrival in arrivals[:2]:
        arrival.start()
    greet(place)
    length = held.attn.shape[0]
    blocks = length // ROWS
    width = held.attn.shape[1]
    head = held.k_rot.shape[1]
    heads = held.q_rot.shape[1] // head
    hidden_columns = held.hidden.shape[1]
    here = set()

    def need(*copies):
        for copy in copies:
            if id(copy) not in here:
                here.add(id(copy))
                copy.wait()

    for gains in (work.gains, work.gain_q, work.gain_k):
        gains[...] = jnp.zeros_like(gains)
    gain_in, gain_pa, gain_pf = (work.gains.at[i] for i in range(3))
    low, part, other = held.gml, work.part, work.other
    leaving = []

    def residual_of(rows):
        attn = held.attn[rows, :]
        inverse = inverse_rms(attn)
        normed = attn * inverse
        return held.tokens[rows, :].astype(jnp.float32) + normed * held.pa[...], normed, inverse

    def down_gradient():
        need(arrivals.gml, arrivals.hidden)
        for arrival in arrivals[2:6]:
            arrival.start()

        def body(columns, _):
            total.d[columns, :] = left_transposed(held.hidden[:, columns], low[...])

        row_loop(hidden_columns // ROWS, body)

    def gate_block(index):
        def run():
            need(arrivals.ff, arrivals.w_g, arrivals.w_u, arrivals.w_d)
            if index == 0:
                for arrival in arrivals[6:]:
                    arrival.start()
            columns = pl.ds(index * ROWS, ROWS)

            def body(rows, _):
                entering = held.ff[rows, :]
                gate = matrix_product(entering, held.w_g[:, columns])
                up = matrix_product(entering, held.w_u[:, columns])
                incoming = right_transposed(low[rows, :], held.w_d[columns, :])
                bent, slope = gelu_parts(gate)
                grad_gate = (incoming * up * slope).astype(jnp.bfloat16)
                grad_up = (incoming * bent).astype(jnp.bfloat16)
                work.gate[rows, :] = grad_gate
                work.up[rows, :] = grad_up
                share = right_transposed(grad_gate, held.w_g[:, columns]) + right_transposed(
                    grad_up, held.w_u[:, columns]
                )
                part[rows, :] = share if index == 0 else part[rows, :] + share

            row_loop(blocks, body)
            total.g[:, columns] = left_transposed(held.ff[...], work.gate[...])
            total.u[:, columns] = left_transposed(held.ff[...], work.up[...])

        return run

    def part_copies():
        first = sums.used
        sums.used += blocks

        def copy(index):
            rows = pl.ds(pl.multiple_of(index * ROWS, ROWS), ROWS)
            return pltpu.make_async_remote_copy(
                src_ref=part.at[rows],
                dst_ref=other.at[rows],
                send_sem=sends.at[first + index],
                recv_sem=receives.at[first + index],
                device_id=place.sibling,
                device_id_type=MESH_ID,
            )

        return copy

    ff_copy, input_copy = part_copies(), part_copies()

    def send_parts(copy):
        row_loop(blocks, lambda rows, index: copy(index).start())

    def residual_back():
        need(arrivals.mlp, arrivals.attn, arrivals.tokens, arrivals.cot, arrivals.pa, arrivals.pff)
        need(arrivals.pf, arrivals.w_o)
        def take_rows(rows, index):
            ff_copy(index).wait_recv()
            residual, normed_attn, inverse_attn = residual_of(rows)
            mlp = held.mlp[rows, :]
            ending = residual + mlp * inverse_rms(mlp) * held.pff[...]
            work.result[rows, :] = ending.astype(jnp.bfloat16)
            incoming = part[rows, :] + other[rows, :]
            inverse = inverse_rms(residual)
            normed = residual * inverse
            add_gain(gain_pf, incoming * normed)
            grad = held.cot[rows, :].astype(jnp.float32) + rms_back(
                incoming, held.pf[...], normed, inverse
            )
            held.mlp[rows, :] = grad
            add_gain(gain_pa, grad * normed_attn)
            low[rows, :] = rms_back(grad, held.pa[...], normed_attn, inverse_attn).astype(
                jnp.bfloat16
            )

        row_loop(blocks, take_rows)
        move = pltpu.make_async_copy(work.result, out_home, local.at[0])
        move.start()
        leaving.append(move)
        row_loop(blocks, lambda rows, index: ff_copy(index).wait_send())
        signal(handed, place.sibling)
        grad_attended = held.ff

        def body(rows, _):
            grad_attended[rows, : heads * head] = right_transposed(
                low[rows, :], held.w_o[...]
            ).astype(jnp.bfloat16)

        row_loop(blocks, body)

    def output_gradient():
        need(arrivals.attended)

        def body(columns, _):
            total.o[columns, :] = left_transposed(held.attended[:, columns], low[...])

        row_loop(heads * head // ROWS, body)

    grad_key = held.attn.at[:, :head]
    grad_value = held.attn.at[:, head : 2 * head]
    grad_query_low = held.hidden.at[:, : heads * head]
    grad_keyvalue_low = held.hidden.at[:, heads * head : heads * head + 2 * head]

    def attention_rows(which, start, stop):
        def run():
            need(arrivals.q_rot, arrivals.k_rot, arrivals.values, arrivals.segments, arrivals.lse, arrivals.cosine, arrivals.sine, arrivals.normed, arrivals.w_q)
            need(arrivals.gq)
            columns = pl.ds(which * head, head)
            if which == 0 and start == 0:
                held.attn[...] = jnp.zeros_like(held.attn)

            def body(rows, index):
                query = held.q_rot[rows, columns]
                grad = held.ff[rows, columns]
                attended = held.attended[rows, columns]
                weight = jnp.sum(
                    grad.astype(jnp.float32) * attended.astype(jnp.float32), axis=1, keepdims=True
                )
                lse = held.lse[which, rows, :]
                segment = column_of(row_at(held.segments, index))
                work.dq[...] = jnp.zeros_like(work.dq)

                def inner(at, carry):
                    others = pl.ds(pl.multiple_of(at * ROWS, ROWS), ROWS)
                    key = held.k_rot[others, :]
                    value = held.values[others, :]
                    scores = right_transposed(query, key)
                    row_index = index * ROWS + lax.broadcasted_iota(jnp.int32, scores.shape, 0)
                    column_index = at * ROWS + lax.broadcasted_iota(jnp.int32, scores.shape, 1)
                    allowed = (segment == row_at(held.segments, at)) & (row_index >= column_index)
                    probs = jnp.where(allowed, jnp.exp(scores - lse), 0.0)
                    grad_probs = right_transposed(grad, value)
                    grad_scores = (probs * (grad_probs - weight)).astype(jnp.bfloat16)
                    work.dq[...] += matrix_product(grad_scores, key)
                    grad_key[others, :] = grad_key[others, :] + left_transposed(grad_scores, query)
                    grad_value[others, :] = grad_value[others, :] + left_transposed(
                        probs.astype(jnp.bfloat16), grad
                    )
                    return carry

                lax.fori_loop(0, index + 1, inner, 0)
                turned = turn_back(work.dq[...], held.cosine[rows, :], held.sine[rows, :])
                turned = turned * head ** (-0.5)
                raw = matrix_product(held.normed[rows, :], held.w_q[:, columns])
                inverse = inverse_rms(raw)
                normed = raw * inverse
                add_gain(work.gain_q, turned * normed)
                grad_query_low[rows, columns] = rms_back(
                    turned, held.gq[...], normed, inverse
                ).astype(jnp.bfloat16)

            row_loop(stop, body, start)

        return run

    def key_back():
        need(arrivals.w_kv, arrivals.gk)

        def body(rows, _):
            turned = turn_back(grad_key[rows, :], held.cosine[rows, :], held.sine[rows, :])
            raw = matrix_product(held.normed[rows, :], held.w_kv[:, :head])
            inverse = inverse_rms(raw)
            normed = raw * inverse
            add_gain(work.gain_k, turned * normed)
            grad_keyvalue_low[rows, :head] = rms_back(
                turned, held.gk[...], normed, inverse
            ).astype(jnp.bfloat16)
            grad_keyvalue_low[rows, head:] = grad_value[rows, :].astype(jnp.bfloat16)

        row_loop(blocks, body)

    def query_gradient(which):
        columns = pl.ds(which * head, head)
        total.q[:, columns] = left_transposed(held.normed[...], grad_query_low[:, columns])

    half_rows = swapped_k.shape[0]
    swap_k, swap_s = [], []

    def keyvalue_gradient():
        for index in range(2 * head // ROWS):
            columns = pl.ds(index * ROWS, ROWS)
            total.k[:, columns] = left_transposed(
                held.normed[...], grad_keyvalue_low[:, columns]
            )
        copy = sums.copy(
            rows_at(total.k, (1 - core) * half_rows, half_rows), swapped_k, place.sibling
        )
        copy.start()
        swap_k.append(copy)

    def input_parts():
        def body(rows, _):
            part[rows, :] = right_transposed(
                grad_query_low[rows, :], held.w_q[...]
            ) + right_transposed(grad_keyvalue_low[rows, :], held.w_kv[...])

        row_loop(blocks, body)
        pl.semaphore_wait(handed, 1)
        send_parts(input_copy)

    def input_back():
        need(arrivals.gin, arrivals.gain_pff)
        def take_rows(rows, index):
            input_copy(index).wait_recv()
            incoming = part[rows, :] + other[rows, :]
            tokens = held.tokens[rows, :].astype(jnp.float32)
            inverse = inverse_rms(tokens)
            normed = tokens * inverse
            add_gain(gain_in, incoming * normed)
            held.mlp[rows, :] = held.mlp[rows, :] + rms_back(
                incoming, held.gin[...], normed, inverse
            )

        row_loop(blocks, take_rows)
        move = pltpu.make_async_copy(held.mlp, token_home, local.at[1])
        move.start()
        leaving.append(move)
        row_loop(blocks, lambda rows, index: input_copy(index).wait_send())
        small = total.s
        small[...] = jnp.zeros_like(small)
        lead = jnp.where(core == 0, 1.0, 0.0)
        row = 0
        for index in range(4):
            rows = work.gains[index] if index < 3 else held.gain_pff[...]
            vector = jnp.sum(rows, axis=0, keepdims=True) * lead
            for at in range(width // 128):
                small[row : row + 1, :] = vector[:, at * 128 : (at + 1) * 128]
                row += 1
        for gains in (work.gain_q, work.gain_k):
            vector = jnp.sum(gains[...], axis=0, keepdims=True)
            for at in range(head // 128):
                small[row : row + 1, :] = vector[:, at * 128 : (at + 1) * 128]
                row += 1
        copy = sums.copy(small, swapped_s, place.sibling)
        copy.start()
        swap_s.append(copy)

    tasks = (
        down_gradient,
        gate_block(0),
        gate_block(1),
        gate_block(2),
        lambda: (gate_block(3)(), send_parts(ff_copy)),
        residual_back,
        output_gradient,
        attention_rows(0, 0, 3),
        attention_rows(0, 3, 4),
        lambda: query_gradient(0),
        attention_rows(1, 0, 3),
        attention_rows(1, 3, 4),
        lambda: query_gradient(1),
        key_back,
        keyvalue_gradient,
        input_parts,
        input_back,
    )
    chunks = []
    slots = 1 + blocks
    for (piece, block), land, parts in zip(PARTS, landing, plan):
        columns = slice(None) if block is None else pl.ds(block * ROWS, ROWS)
        summed = total[piece] if block is None else total[piece].at[:, columns]
        row = 0
        land_row = 0
        base = core * half_rows if piece == PIECE_K else 0
        for line, count, turned in parts:

            def finish(
                piece=piece,
                columns=columns,
                summed=summed,
                row=row,
                base=base,
                count=count,
                slot=slots,
            ):
                done = rows_at(summed, base + row, count)
                if piece == PIECE_S:
                    moves = [pltpu.make_async_copy(done, own_s, local.at[slot])]
                else:
                    if piece == PIECE_K:
                        home = rows_at(own_k, base + row, count)
                    else:
                        home = both[piece].at[core, pl.ds(row, count), columns]
                    moves = [
                        pltpu.make_async_copy(done, home, local.at[slot]),
                        sums.copy(done, home, place.sibling),
                    ]
                for move in moves:
                    move.start()
                leaving.extend(moves)

            build = line_first if line else plane_first
            steps = build(sums, summed, base + row, count, land, land_row, finish, turned)
            if piece >= PIECE_K:
                swap, landed = (swap_k, swapped_k) if piece == PIECE_K else (swap_s, swapped_s)

                def enter(swap=swap, landed=landed, out=total[piece], base=base, first=steps[0]):
                    if swap:
                        swap.pop().wait()
                        add_rows(out, base, landed, 0, landed.shape[0])
                    first()

                steps = [enter] + steps[1:]
            chunks.append(steps)
            slots += 1
            row += count
            land_row += landing_rows(line, count)
    for entry in order:
        if entry < 0:
            tasks[-1 - entry]()
        else:
            chunks[entry // 10][entry % 10]()
    for move in leaving:
        move.wait()


def backward_and_sums(values, shapes):
    length, width = values.tokens.shape
    head = values.k_rot.shape[1]
    full, low = jnp.float32, jnp.bfloat16
    outs = [((length, width), low), ((length, width), full), (shapes.k, full), (shapes.s, full)]
    outs += [((2,) + shape, full) for shape in shapes[:PIECE_K]]
    scratch = [pltpu.VMEM(array.shape, array.dtype) for array in values]
    scratch += [pltpu.VMEM(shape, full) for shape in shapes]
    for (piece, block), parts in zip(PARTS, CUTS):
        columns = shapes[piece][1] if block is None else ROWS
        rows = sum(landing_rows(line, count) for line, count, _ in parts)
        scratch.append(pltpu.VMEM((rows, columns), full))
    scratch += [pltpu.VMEM((shapes.k[0] // 2, shapes.k[1]), full), pltpu.VMEM(shapes.s, full)]
    scratch += Work(
        gate=pltpu.VMEM((length, ROWS), low),
        up=pltpu.VMEM((length, ROWS), low),
        part=pltpu.VMEM((length, width), full),
        other=pltpu.VMEM((length, width), full),
        dq=pltpu.VMEM((ROWS, head), full),
        gains=pltpu.VMEM((3, 8, width), full),
        gain_q=pltpu.VMEM((8, head), full),
        gain_k=pltpu.VMEM((8, head), full),
        result=pltpu.VMEM((length, width), low),
    )
    count = sum(len(parts) for parts in CUTS)
    blocks = length // ROWS
    scratch += [
        pltpu.SemaphoreType.DMA((len(values),)),
        pltpu.SemaphoreType.DMA((count * 11 + 2 * blocks + 4,)),
        pltpu.SemaphoreType.DMA((count * 11 + 2 * blocks + 4,)),
        pltpu.SemaphoreType.DMA((count + blocks + 2,)),
        pltpu.SemaphoreType.REGULAR((count * 3,)),
        pltpu.SemaphoreType.REGULAR,
    ]
    results = pl.pallas_call(
        functools.partial(backward_kernel, (CUTS, ORDER)),
        out_shape=[jax.ShapeDtypeStruct(*out) for out in outs],
        in_specs=[ANYWHERE] * len(values),
        out_specs=[ANYWHERE] * len(outs),
        scratch_shapes=scratch,
        compiler_params=pltpu.CompilerParams(
            collective_id=0, has_side_effects=True, vmem_limit_bytes=67043328
        ),
    )(*values)
    return results[:4], results[4:]


CUTS = (
    ((1, 32, 1), (0, 320, 1), (1, 224, 0), (0, 416, 0), (1, 32, 0),),
    ((0, 640, 0),),
    ((1, 288, 0), (0, 352, 1),),
    ((0, 224, 0), (0, 416, 1),),
    ((1, 544, 0), (0, 96, 0),),
    ((1, 416, 1), (0, 224, 1),),
    ((1, 256, 1), (0, 192, 0), (0, 192, 1),),
    ((0, 640, 1),),
    ((0, 640, 1),),
    ((1, 32, 1), (0, 128, 1), (0, 288, 0), (0, 64, 1),),
    ((0, 64, 1), (0, 576, 0),),
    ((1, 256, 0), (0, 384, 0),),
    ((1, 224, 1), (0, 96, 1),),
    ((0, 32, 0),),
)
ORDER = (
    -1, 10, 30, 20, -2, 0, 70, 50, -3, 40, 60, 90, -4, 160, 120, 110, 11, 41, 21, 31, 100, 80, -5,
    180, 91, 150, 61, 121, 71, 22, 1, 12, 170, -6, 23, -7, 101, 181, 140, 122, 42, 220, 210, -8,
    13, 2, 200, 24, 102, 32, 182, 81, 111, 62, 141, -9, 14, 130, 103, 171, 33, -10, 43, 142, 240,
    123, 82, 190, 230, 183, 25, 161, 211, 104, 72, 92, 51, 3, 15, 143, 124, 34, -11, 184, 26, 212,
    83, -12, 191, 105, 231, -13, 27, 213, 44, 63, 260, 250, 35, -14, 16, 4, 106, -15, 93, 131,
    172, 64, 84, 144, 52, 280, 251, 221, 112, 214, 36, 241, 73, 162, -16, 107, 270, -17, 53, 201,
    151, 74, 252, 113, 261, 163, 173, 192, 215, 65, 222, 281, 114, 271, 185, 145, 54, 132, 85, 75,
    232, 174, 164, 133, 193, 253, 115, 146, 242, 272, 5, 186, 202, 282, 223, 262, 194, 290, 86,
    175, 152, 37, 55, 28, 94, 116, 203, 147, 153, 216, 273, 254, 243, 195, 76, 125, 274, 233, 204,
    154, 283, 224, 95, 126, 244, 291, 284, 176, 134, 108, 45, 187, 165, 205, 155, 66, 263, 255,
    77, 56, 127, 234, 292, 293, 6, 46, 245, 294, 196, 275, 96, 135, 276, 47, 156, 264, 285, 166,
    225, 295, 197, 256, 277, 235, 246, 117, 87, 148, 136, 57, 67, 128, 265, 236, 217, 48, 206,
    177, 7, 296, 97, 266, 226, 257, 286, 167, 297, 237, 68, 198, 227, 17, 137, 207, 278, 8, 157,
    267, 247, 258, 287,
)


def landing_rows(line, count):
    return count // 4 * (7 if line else 5)


FINE = 32


class ForwardInputs(NamedTuple):
    tokens: object
    gin: object
    w_q: object
    a_q: object
    b_q: object
    w_kv: object
    a_kv: object
    b_kv: object
    table: object
    segments: object
    gq: object
    gk: object
    w_o: object
    a_o: object
    b_o: object
    pa: object
    pf: object
    w_gu: object
    a_gu: object
    b_gu: object
    w_d: object
    a_d: object
    b_d: object
    cot: object
    pff: object


class ForwardOutputs(NamedTuple):
    gml: object
    gain_pff: object
    mlp: object
    attn: object
    hidden: object
    ff: object
    w_g: object
    w_u: object
    w_d: object
    w_o: object
    attended: object
    q_rot: object
    k_rot: object
    values: object
    lse: object
    cosine: object
    sine: object
    normed: object
    w_q: object
    w_kv: object


def turn(values, cosine, sine):
    half = values.shape[1] // 2
    leading, trailing = values[:, :half], values[:, half:]
    return jnp.concatenate(
        [leading * cosine - trailing * sine, trailing * cosine + leading * sine], axis=1
    )


def forward_kernel(*refs):
    refs = list(refs)
    source = ForwardInputs(*refs[: len(ForwardInputs._fields)])
    refs = refs[len(source) :]
    target = ForwardOutputs(*refs[: len(ForwardOutputs._fields)])
    refs = refs[len(target) :]
    held = ForwardInputs(*refs[: len(source)])
    refs = refs[len(source) :]
    made = ForwardOutputs(*refs[: len(target)])
    part, other, part_two, other_two, sums_at, rotation = refs[len(target) : len(target) + 6]
    loads, sends, receives, stores = refs[len(target) + 6 :]
    me = lax.axis_index(DP)
    core = lax.axis_index(TENSOR)
    sibling = (me, 1 - core)

    def own_part(ref, home, axis):
        size = home.shape[axis]
        span = pl.ds(pl.multiple_of(core * size, 256), size)
        index = [slice(None)] * len(home.shape)
        index[axis] = span
        return ref.at[tuple(index)]

    pieces = source._replace(
        b_q=own_part(source.b_q, held.b_q, 1),
        a_o=own_part(source.a_o, held.a_o, 0),
        b_gu=own_part(source.b_gu, held.b_gu, 2),
        a_d=own_part(source.a_d, held.a_d, 0),
    )
    arrivals = ForwardInputs(
        *(
            pltpu.make_async_copy(piece, home, loads.at[index])
            for index, (piece, home) in enumerate(zip(pieces, held))
        )
    )
    for arrival in arrivals[:8]:
        arrival.start()
    barrier = pltpu.get_barrier_semaphore()
    signal(barrier, sibling)
    pl.semaphore_wait(barrier, 1)
    leaving = []
    homes = {id(ref): (index, home) for index, (ref, home) in enumerate(zip(made, target))}

    def leave(*arrays):
        for ref in arrays:
            index, home = homes[id(ref)]
            move = pltpu.make_async_copy(ref, home, stores.at[index])
            move.start()
            leaving.append(move)

    def need(*copies):
        for copy in copies:
            copy.wait()

    length, width = held.tokens.shape
    blocks = length // ROWS
    head = held.gq.shape[0]
    heads = held.w_q.shape[1] // head
    rank = held.a_q.shape[1]

    def merge(out, weight, first, second):
        count = weight.shape[0]
        step = 256 if count % 256 == 0 else 320

        def body(index, carry):
            rows = pl.ds(pl.multiple_of(index * step, 64), step)
            out[rows, :] = (
                weight[rows, :].astype(jnp.float32) + matrix_product(first[rows, :], second[...])
            ).astype(jnp.bfloat16)
            return carry

        lax.fori_loop(0, count // step, body, 0)

    need(arrivals.tokens, arrivals.gin, arrivals.w_q, arrivals.a_q, arrivals.b_q)
    for arrival in arrivals[8:]:
        arrival.start()
    merge(made.w_q, held.w_q, held.a_q, held.b_q)
    need(arrivals.w_kv, arrivals.a_kv, arrivals.b_kv)
    for index in range(2):
        columns = pl.ds(index * head, head)
        merge(
            made.w_kv.at[:, columns],
            held.w_kv.at[:, columns],
            held.a_kv.at[:, pl.ds(index * rank, rank)],
            held.b_kv.at[index],
        )
    leave(made.w_q, made.w_kv)
    need(arrivals.table, arrivals.segments, arrivals.gq, arrivals.gk)
    before = jnp.zeros((8, 1), jnp.float32)
    number = lax.broadcasted_iota(jnp.int32, (8, ROWS), 0).astype(jnp.float32)
    for index in range(blocks):
        fewer = jnp.where(row_at(held.segments, index) < number, 1.0, 0.0)
        before = before + jnp.sum(fewer, axis=1, keepdims=True)
    at_token = lax.broadcasted_iota(jnp.int32, (8, length), 1).astype(jnp.float32)
    chosen = jnp.where(at_token == before, 1.0, 0.0)
    half = head // 2
    coarse = length // FINE

    def fill(index, carry):
        rows = pl.ds(pl.multiple_of(index * FINE, FINE), FINE)
        step = held.table[pl.ds(index, 1), :]
        step_cosine, step_sine = step[:, :half], step[:, half:]
        fine = held.table[coarse : coarse + FINE, :]
        fine_cosine, fine_sine = fine[:, :half], fine[:, half:]
        rotation[rows, :half] = fine_cosine * step_cosine - fine_sine * step_sine
        rotation[rows, half:] = fine_sine * step_cosine + fine_cosine * step_sine
        return carry

    lax.fori_loop(0, coarse, fill, 0)
    starts = jnp.dot(
        chosen, rotation[...], precision=lax.Precision.HIGHEST, preferred_element_type=jnp.float32
    )

    def project(rows, index):
        tokens = held.tokens[rows, :].astype(jnp.float32)
        normed = (tokens * inverse_rms(tokens) * held.gin[...]).astype(jnp.bfloat16)
        made.normed[rows, :] = normed
        segment = column_of(row_at(held.segments, index))
        start = starts[3:4, :]
        for document in (2, 1, 0):
            start = jnp.where(segment == document, starts[document : document + 1, :], start)
        start_cosine, start_sine = start[:, :half], start[:, half:]
        here = rotation[rows, :]
        here_cosine, here_sine = here[:, :half], here[:, half:]
        cosine = here_cosine * start_cosine + here_sine * start_sine
        sine = here_sine * start_cosine - here_cosine * start_sine
        made.cosine[rows, :] = cosine
        made.sine[rows, :] = sine
        for at in range(heads):
            columns = pl.ds(at * head, head)
            raw = matrix_product(normed, made.w_q[:, columns])
            query = turn(raw * inverse_rms(raw) * held.gq[...], cosine, sine) * head ** (-0.5)
            made.q_rot[rows, columns] = query.astype(jnp.bfloat16)
        raw = matrix_product(normed, made.w_kv[:, :head])
        key = turn(raw * inverse_rms(raw) * held.gk[...], cosine, sine)
        made.k_rot[rows, :] = key.astype(jnp.bfloat16)
        made.values[rows, :] = matrix_product(normed, made.w_kv[:, head:]).astype(jnp.bfloat16)

    row_loop(blocks, project)
    leave(made.normed, made.cosine, made.sine, made.q_rot, made.k_rot, made.values)
    need(arrivals.w_o, arrivals.a_o, arrivals.b_o)
    merge(made.w_o, held.w_o, held.a_o, held.b_o)
    leave(made.w_o)

    def exchange(key, index, mine, theirs):
        rows = pl.ds(pl.multiple_of(index * ROWS, ROWS), ROWS)
        slot = key * blocks + index
        return pltpu.make_async_remote_copy(
            src_ref=mine.at[rows],
            dst_ref=theirs.at[rows],
            send_sem=sends.at[slot],
            recv_sem=receives.at[slot],
            device_id=sibling,
            device_id_type=MESH_ID,
        )

    def attend(rows, index):
        segment = column_of(row_at(held.segments, index))

        queries = [made.q_rot[rows, at * head : (at + 1) * head] for at in range(heads)]
        sums_at[...] = jnp.zeros_like(sums_at)

        def inner(at, carry):
            others = pl.ds(pl.multiple_of(at * ROWS, ROWS), ROWS)
            key, value = made.k_rot[others, :], made.values[others, :]
            shape = (ROWS, ROWS)
            row_index = index * ROWS + lax.broadcasted_iota(jnp.int32, shape, 0)
            column_index = at * ROWS + lax.broadcasted_iota(jnp.int32, shape, 1)
            allowed = (segment == row_at(held.segments, at)) & (row_index >= column_index)
            after = []
            for which, query in enumerate(queries):
                peak, amount = carry[which]
                scores = jnp.where(allowed, right_transposed(query, key), MASKED)
                higher = jnp.maximum(peak, jnp.max(scores, axis=1, keepdims=True))
                weights = jnp.where(allowed, jnp.exp(scores - higher), 0.0)
                shrink = jnp.exp(peak - higher)
                amount = amount * shrink + jnp.sum(weights, axis=1, keepdims=True)
                sums_at[which] = sums_at[which] * shrink + matrix_product(
                    weights.astype(jnp.bfloat16), value
                )
                after.append((higher, amount))
            return tuple(after)

        first = (jnp.full((ROWS, 1), MASKED, jnp.float32), jnp.zeros((ROWS, 1), jnp.float32))
        final = lax.fori_loop(0, index + 1, inner, (first,) * heads)
        for which, (peak, amount) in enumerate(final):
            columns = pl.ds(which * head, head)
            made.attended[rows, columns] = (sums_at[which] / amount).astype(jnp.bfloat16)
            made.lse[which, rows, :] = peak + jnp.log(amount)
        part[rows, :] = matrix_product(made.attended[rows, :], made.w_o[...])
        exchange(0, index, part, other).start()

    row_loop(blocks, attend)
    leave(made.attended, made.lse)
    need(arrivals.w_gu, arrivals.a_gu, arrivals.b_gu, arrivals.w_d, arrivals.a_d, arrivals.b_d)
    for index, out in enumerate((made.w_g, made.w_u)):
        first = held.a_gu.at[:, pl.ds(index * rank, rank)]
        merge(out, held.w_gu.at[index], first, held.b_gu.at[index])
    merge(made.w_d, held.w_d, held.a_d, held.b_d)
    leave(made.w_g, made.w_u, made.w_d)
    need(arrivals.pa, arrivals.pf)
    hidden_columns = made.hidden.shape[1]

    def feed_forward(rows, index):
        exchange(0, index, part, other).wait_recv()
        attn = part[rows, :] + other[rows, :]
        made.attn[rows, :] = attn
        residual = held.tokens[rows, :].astype(jnp.float32) + attn * inverse_rms(attn) * held.pa[...]
        made.ff[rows, :] = (residual * inverse_rms(residual) * held.pf[...]).astype(jnp.bfloat16)

        def one_block(at, carry):
            for half_at in range(2):
                start = pl.multiple_of((2 * at + half_at) * ROWS, ROWS)
                columns = pl.ds(start, ROWS)
                entering = made.ff[rows, :]
                gate = matrix_product(entering, made.w_g[:, columns])
                up = matrix_product(entering, made.w_u[:, columns])
                bent = 0.5 * gate * (1.0 + jnp.tanh(GELU * gate * (1.0 + 0.044715 * gate * gate)))
                made.hidden[rows, columns] = (bent * up).astype(jnp.bfloat16)
            return carry

        lax.fori_loop(0, hidden_columns // ROWS // 2, one_block, 0)
        part_two[rows, :] = matrix_product(made.hidden[rows, :], made.w_d[...])
        exchange(1, index, part_two, other_two).start()

    row_loop(blocks, feed_forward)
    leave(made.attn, made.ff, made.hidden)

    def add_halves(rows, index):
        exchange(1, index, part_two, other_two).wait_recv()
        mlp = part_two[rows, :] + other_two[rows, :]
        made.mlp[rows, :] = mlp
        inverse = inverse_rms(mlp)
        normed = mlp * inverse
        incoming = held.cot[rows, :].astype(jnp.float32)
        add_gain(made.gain_pff, incoming * normed)
        made.gml[rows, :] = rms_back(incoming, held.pff[...], normed, inverse).astype(jnp.bfloat16)

    made.gain_pff[...] = jnp.zeros_like(made.gain_pff)
    need(arrivals.cot, arrivals.pff)
    row_loop(blocks, add_halves)
    leave(made.gml, made.gain_pff, made.mlp)
    for index in range(blocks):
        exchange(0, index, part, other).wait_send()
        exchange(1, index, part_two, other_two).wait_send()
    for move in leaving:
        move.wait()


def rotation_table(length, head):
    frequency = THETA ** (-np.arange(head // 2, dtype=np.float64) * 2.0 / head)
    positions = np.concatenate([np.arange(0, length, FINE), np.arange(FINE)])
    angles = positions.astype(np.float64)[:, None] * frequency[None, :]
    return jnp.asarray(np.concatenate([np.cos(angles), np.sin(angles)], axis=1).astype(np.float32))


def forward_pass(values):
    length, width = values.tokens.shape
    head = values.gq.shape[0]
    query_columns = values.w_q.shape[1]
    heads = query_columns // head
    hidden_columns = values.w_d.shape[0]
    rank = values.a_q.shape[1]
    low, full = jnp.bfloat16, jnp.float32
    shapes = ForwardOutputs(
        gml=((length, width), low),
        gain_pff=((8, width), full),
        mlp=((length, width), full),
        attn=((length, width), full),
        hidden=((length, hidden_columns), low),
        ff=((length, width), low),
        w_g=((width, hidden_columns), low),
        w_u=((width, hidden_columns), low),
        w_d=((hidden_columns, width), low),
        w_o=((query_columns, width), low),
        attended=((length, query_columns), low),
        q_rot=((length, query_columns), low),
        k_rot=((length, head), low),
        values=((length, head), low),
        lse=((heads, length, 1), full),
        cosine=((length, head // 2), full),
        sine=((length, head // 2), full),
        normed=((length, width), low),
        w_q=((width, query_columns), low),
        w_kv=((width, 2 * head), low),
    )
    sizes = values._replace(
        b_q=jax.ShapeDtypeStruct((rank, query_columns), low),
        a_o=jax.ShapeDtypeStruct((query_columns, rank), low),
        b_gu=jax.ShapeDtypeStruct((2, rank, hidden_columns), low),
        a_d=jax.ShapeDtypeStruct((hidden_columns, rank), low),
    )
    slots = 2 * (length // ROWS)
    results = pl.pallas_call(
        forward_kernel,
        out_shape=[jax.ShapeDtypeStruct(*shape) for shape in shapes],
        in_specs=[ANYWHERE] * len(values),
        out_specs=[ANYWHERE] * len(shapes),
        scratch_shapes=[pltpu.VMEM(array.shape, array.dtype) for array in sizes]
        + [pltpu.VMEM(*shape) for shape in shapes]
        + [pltpu.VMEM((length, width), full)] * 4
        + [
            pltpu.VMEM((heads, ROWS, head), full),
            pltpu.VMEM((length, head), full),
            pltpu.SemaphoreType.DMA((len(values),)),
            pltpu.SemaphoreType.DMA((slots,)),
            pltpu.SemaphoreType.DMA((slots,)),
            pltpu.SemaphoreType.DMA((len(shapes),)),
        ],
        compiler_params=pltpu.CompilerParams(
            collective_id=1, has_side_effects=True, vmem_limit_bytes=67043328
        ),
    )(*values)
    return ForwardOutputs(*results)


class Adapters(NamedTuple):
    down_a: object
    down_b: object
    gateup_a: object
    gateup_b: object
    output_a: object
    output_b: object
    query_a: object
    query_b: object
    keyvalue_a: object
    keyvalue_b: object


class DeriveInputs(NamedTuple):
    down_a: object
    down_b: object
    d: object
    gateup_a: object
    gateup_b: object
    g: object
    u: object
    output_a: object
    output_b: object
    o: object
    query_a: object
    query_b: object
    q: object
    keyvalue_a: object
    keyvalue_b: object
    k: object
    small: object
    result: object
    tokens: object


class DeriveOutputs(NamedTuple):
    down: object
    gateup: object
    output: object
    query: object
    keyvalue: object
    down_a: object
    down_b: object
    gateup_a: object
    gateup_b: object
    output_a: object
    output_b: object
    query_a: object
    query_b: object
    keyvalue_a: object
    keyvalue_b: object
    result: object
    tokens: object
    gain_in: object
    gain_pa: object
    gain_pf: object
    gain_pff: object
    gain_q: object
    gain_k: object


def derive_kernel(*refs):
    refs = list(refs)
    fields = len(DeriveInputs._fields)
    source = DeriveInputs(*refs[:fields])
    refs = refs[fields:]
    target = DeriveOutputs(*refs[: len(DeriveOutputs._fields)])
    refs = refs[len(target) :]
    held = DeriveInputs(*refs[:fields])
    refs = refs[fields:]
    made = Adapters(*refs[: len(Adapters._fields)])
    gains = refs[len(made) : len(made) + 6]
    rounded, loaded, stored = refs[len(made) + 6 :]
    core = lax.axis_index(TENSOR)
    arrivals = DeriveInputs(
        *(
            pltpu.make_async_copy(piece, home, loaded.at[index])
            for index, (piece, home) in enumerate(zip(source, held))
        )
    )
    for arrival in arrivals[:6]:
        arrival.start()
    behind = list(arrivals[6:])
    leaving = []

    def need(*copies):
        for copy in copies:
            copy.wait()
        for arrival in behind[:3]:
            arrival.start()
        del behind[:3]

    def leave(piece, home):
        move = pltpu.make_async_copy(piece, home, stored.at[len(leaving)])
        move.start()
        leaving.append(move)

    def factors(total, first, second, out_first, out_second, add_first=False, add_second=False):
        count, columns = total.shape
        step = 256 if count % 256 == 0 else 320

        def by_rows(index, carry):
            block = pl.ds(pl.multiple_of(index * step, 64), step)
            value = total[block, :].astype(jnp.bfloat16)
            rounded[block, :columns] = value
            product = right_transposed(value, second[...])
            out_first[block, :] = out_first[block, :] + product if add_first else product
            return carry

        lax.fori_loop(0, count // step, by_rows, 0)
        width = 256 if columns == 256 else columns // 2

        def by_columns(index, carry):
            block = pl.ds(pl.multiple_of(index * width, 128), width)
            product = left_transposed(first[...], rounded[:count, block])
            out_second[:, block] = out_second[:, block] + product if add_second else product
            return carry

        if width % 128 == 0:
            lax.fori_loop(0, columns // width, by_columns, 0)
        else:
            product = left_transposed(first[...], rounded[:count, :columns])
            out_second[...] = out_second[...] + product if add_second else product

    rank = made.query_a.shape[1]

    def columns_of(ref, part, size):
        return ref.at[:, pl.ds(part * size, size)]

    def rows_of(ref, part, size):
        return ref.at[pl.ds(part * size, size)]

    need(arrivals.down_a, arrivals.down_b, arrivals.d)
    leave(held.d.at[core], target.down)
    for group in range(2):
        total = held.d.at[group]
        size = total.shape[0]
        first = rows_of(held.down_a, group, size)
        out = rows_of(made.down_a, group, size)
        factors(total, first, held.down_b, out, made.down_b, False, group > 0)
    leave(made.down_a, target.down_a)
    leave(made.down_b, target.down_b)
    need(arrivals.gateup_a, arrivals.gateup_b)
    for part, name in enumerate((held.g, held.u)):
        need((arrivals.g, arrivals.u)[part])
        leave(name.at[core], target.gateup.at[part])
        for group in range(2):
            total = name.at[group]
            size = total.shape[1]
            second = columns_of(held.gateup_b.at[part], group, size)
            first = columns_of(held.gateup_a, part, rank)
            out_first = columns_of(made.gateup_a, part, rank)
            out_second = columns_of(made.gateup_b.at[part], group, size)
            factors(total, first, second, out_first, out_second, group > 0, False)
        leave(made.gateup_b.at[part], target.gateup_b.at[part])
    leave(made.gateup_a, target.gateup_a)
    need(arrivals.output_a, arrivals.output_b, arrivals.o)
    leave(held.o.at[core], target.output)
    for group in range(2):
        total = held.o.at[group]
        size = total.shape[0]
        first = rows_of(held.output_a, group, size)
        out = rows_of(made.output_a, group, size)
        factors(total, first, held.output_b, out, made.output_b, False, group > 0)
    leave(made.output_a, target.output_a)
    leave(made.output_b, target.output_b)
    need(arrivals.query_a, arrivals.query_b, arrivals.q)
    leave(held.q.at[core], target.query)
    for group in range(2):
        total = held.q.at[group]
        size = total.shape[1]
        second = columns_of(held.query_b, group, size)
        out = columns_of(made.query_b, group, size)
        factors(total, held.query_a, second, made.query_a, out, group > 0, False)
    leave(made.query_a, target.query_a)
    leave(made.query_b, target.query_b)
    need(arrivals.keyvalue_a, arrivals.keyvalue_b, arrivals.k)
    leave(held.k, target.keyvalue)
    for part in range(2):
        width = made.keyvalue_b.shape[2]
        total = columns_of(held.k, part, width)
        out = columns_of(made.keyvalue_a, part, rank)
        first = columns_of(held.keyvalue_a, part, rank)
        factors(total, first, held.keyvalue_b.at[part], out, made.keyvalue_b.at[part])
    leave(made.keyvalue_a, target.keyvalue_a)
    leave(made.keyvalue_b, target.keyvalue_b)
    need(arrivals.small, arrivals.result, arrivals.tokens)
    leave(held.result, target.result)
    leave(held.tokens, target.tokens)
    row = 0
    for gain, home in zip(gains, target[-6:]):
        for at in range(gain.shape[0] // 128):
            gain[pl.ds(at * 128, 128)] = held.small[row]
            row += 1
        leave(gain, home)
    for move in leaving:
        move.wait()


def derive_adapters(values, widths):
    made = [getattr(values, name) for name in Adapters._fields]
    shapes = [
        values.d.shape[1:],
        (2,) + values.g.shape[1:],
        values.o.shape[1:],
        values.q.shape[1:],
        values.k.shape,
    ]
    shapes += [array.shape for array in made]
    shapes += [values.result.shape, values.tokens.shape] + [(width,) for width in widths]
    kinds = [jnp.float32] * len(shapes)
    kinds[len(made) + 5] = values.result.dtype
    results = pl.pallas_call(
        derive_kernel,
        out_shape=[jax.ShapeDtypeStruct(*out) for out in zip(shapes, kinds)],
        in_specs=[ANYWHERE] * len(values),
        out_specs=[ANYWHERE] * len(shapes),
        scratch_shapes=[pltpu.VMEM(array.shape, array.dtype) for array in values]
        + [pltpu.VMEM(array.shape, jnp.float32) for array in made]
        + [pltpu.VMEM((width,), jnp.float32) for width in widths]
        + [
            pltpu.VMEM((values.d.shape[1], values.g.shape[2]), jnp.bfloat16),
            pltpu.SemaphoreType.DMA((len(values),)),
            pltpu.SemaphoreType.DMA((len(shapes) + 2,)),
        ],
        compiler_params=pltpu.CompilerParams(vmem_limit_bytes=67043328),
    )(*values)
    return DeriveOutputs(*results)


def on_device_general(
    tokens,
    document_numbers,
    input_norm_gain,
    after_attention_gain,
    before_feedforward_gain,
    after_feedforward_gain,
    query_norm_gain,
    key_norm_gain,
    query_weight,
    keyvalue_weight,
    output_weight,
    gateup_weight,
    down_weight,
    query_adapter_first,
    query_adapter_second,
    keyvalue_adapter_first,
    keyvalue_adapter_second,
    output_adapter_first,
    output_adapter_second,
    gateup_adapter_first,
    gateup_adapter_second,
    down_adapter_first,
    down_adapter_second,
    cotangent,
):
    inputs = tokens[0].astype(jnp.float32)
    segments = document_numbers[0]
    length = inputs.shape[0]
    head_width = keyvalue_adapter_second.shape[2]
    adapter_rank = query_adapter_first.shape[1]
    query_columns = query_weight.shape[1]
    hidden_columns = down_weight.shape[0]
    heads_local = query_columns // head_width
    group_position = lax.axis_index(TENSOR)
    query_piece = lax.dynamic_slice_in_dim(
        query_adapter_second, group_position * query_columns, query_columns, 1
    )
    output_rows = lax.dynamic_slice_in_dim(
        output_adapter_first, group_position * query_columns, query_columns, 0
    )
    gateup_piece = lax.dynamic_slice_in_dim(
        gateup_adapter_second, group_position * hidden_columns, hidden_columns, 2
    )
    down_rows = lax.dynamic_slice_in_dim(
        down_adapter_first, group_position * hidden_columns, hidden_columns, 0
    )
    query_merged = (
        query_weight.astype(jnp.float32) + matrix_product(query_adapter_first, query_piece)
    ).astype(jnp.bfloat16)
    keyvalue_merged = (
        keyvalue_weight.astype(jnp.float32)
        + jnp.concatenate(
            [
                matrix_product(keyvalue_adapter_first[:, :adapter_rank], keyvalue_adapter_second[0]),
                matrix_product(keyvalue_adapter_first[:, adapter_rank:], keyvalue_adapter_second[1]),
            ],
            axis=1,
        )
    ).astype(jnp.bfloat16)
    output_merged = (
        output_weight.astype(jnp.float32) + matrix_product(output_rows, output_adapter_second)
    ).astype(jnp.bfloat16)
    gate_merged = (
        gateup_weight[0].astype(jnp.float32)
        + matrix_product(gateup_adapter_first[:, :adapter_rank], gateup_piece[0])
    ).astype(jnp.bfloat16)
    up_merged = (
        gateup_weight[1].astype(jnp.float32)
        + matrix_product(gateup_adapter_first[:, adapter_rank:], gateup_piece[1])
    ).astype(jnp.bfloat16)
    down_merged = (
        down_weight.astype(jnp.float32) + matrix_product(down_rows, down_adapter_second)
    ).astype(jnp.bfloat16)
    positions = positions_of(segments)
    key_index = jnp.arange(length, dtype=jnp.int32)
    block_rows = min(512, length)
    normalized_rows, in_back = jax.vjp(rms_scale, inputs, input_norm_gain)
    normalized_lowrank = normalized_rows.astype(jnp.bfloat16)
    query_rows = matrix_product(normalized_lowrank, query_merged)
    keyvalue = matrix_product(normalized_lowrank, keyvalue_merged)

    def prepare(q_in, kv_in, q_scale, k_scale):
        q_heads = rms_scale(q_in.reshape(length, heads_local, head_width), q_scale)
        q_out = rotate(q_heads, positions) * head_width ** (-0.5)
        k_out = rotate(rms_scale(kv_in[:, :head_width], k_scale), positions)
        return (q_out, k_out, kv_in[:, head_width:])

    prepared, prepare_back = jax.vjp(prepare, query_rows, keyvalue, query_norm_gain, key_norm_gain)
    q_rot = prepared[0].astype(jnp.bfloat16)
    k_rot = prepared[1].astype(jnp.bfloat16)
    v_low = prepared[2].astype(jnp.bfloat16)

    def scores_of(row_start):
        rows = q_rot[row_start : row_start + block_rows]
        raw = jnp.einsum("qhd,kd->hqk", rows, k_rot, preferred_element_type=jnp.float32)
        row_index = row_start + jnp.arange(block_rows, dtype=jnp.int32)
        allowed = (segments[row_start : row_start + block_rows][:, None] == segments[None, :]) & (
            row_index[:, None] >= key_index[None, :]
        )
        return jnp.where(allowed[None], raw, MASKED)

    outputs = []
    log_totals = []
    for row_start in range(0, length, block_rows):
        scores = scores_of(row_start)
        row_peak = jnp.max(scores, axis=-1, keepdims=True)
        weights = jnp.exp(scores - row_peak)
        row_total = jnp.sum(weights, axis=-1, keepdims=True)
        log_totals.append(row_peak + jnp.log(row_total))
        probs_low = (weights / row_total).astype(jnp.bfloat16)
        outputs.append(
            jnp.einsum("hqk,kd->qhd", probs_low, v_low, preferred_element_type=jnp.float32)
        )
    attended_rows = (
        jnp.concatenate(outputs, axis=0).reshape(length, query_columns).astype(jnp.bfloat16)
    )
    attention_before = lax.psum(matrix_product(attended_rows, output_merged), TENSOR)
    attn_post, post_attn_back = jax.vjp(rms_scale, attention_before, after_attention_gain)
    residual = inputs + attn_post
    normed_ff, pre_ff_back = jax.vjp(rms_scale, residual, before_feedforward_gain)
    feedforward_lowrank = normed_ff.astype(jnp.bfloat16)
    gate_portion = matrix_product(feedforward_lowrank, gate_merged)
    up_portion = matrix_product(feedforward_lowrank, up_merged)
    hidden_full, activate_back = jax.vjp(activate, gate_portion, up_portion)
    hidden_activation = hidden_full.astype(jnp.bfloat16)
    feedforward_before = lax.psum(matrix_product(hidden_activation, down_merged), TENSOR)
    mlp_post, post_ff_back = jax.vjp(rms_scale, feedforward_before, after_feedforward_gain)
    result_value = (residual + mlp_post).astype(jnp.bfloat16)[None]
    grad_out = cotangent[0].astype(jnp.float32)
    grad_mlp_pre, gradient_after_feedforward = post_ff_back(grad_out)
    gradient_feedforward_lowrank = grad_mlp_pre.astype(jnp.bfloat16)
    gradient_down_weight = left_transposed(hidden_activation, gradient_feedforward_lowrank)
    grad_hidden = right_transposed(gradient_feedforward_lowrank, down_merged)
    grad_gate, grad_up = activate_back(grad_hidden)
    gate_lowrank = grad_gate.astype(jnp.bfloat16)
    up_lowrank = grad_up.astype(jnp.bfloat16)
    gradient_gateup_weight = jnp.stack(
        [
            left_transposed(feedforward_lowrank, gate_lowrank),
            left_transposed(feedforward_lowrank, up_lowrank),
        ]
    )
    grad_ff_part = right_transposed(gate_lowrank, gate_merged) + right_transposed(
        up_lowrank, up_merged
    )
    grad_normed_ff = lax.psum(grad_ff_part, TENSOR)
    grad_residual_ff, gradient_before_feedforward = pre_ff_back(grad_normed_ff)
    grad_residual = grad_out + grad_residual_ff
    grad_attn_pre, gradient_after_attention = post_attn_back(grad_residual)
    gradient_attention_lowrank = grad_attn_pre.astype(jnp.bfloat16)
    gradient_output_weight = left_transposed(attended_rows, gradient_attention_lowrank)
    grad_attended = right_transposed(gradient_attention_lowrank, output_merged).astype(jnp.bfloat16)
    grad_attended = grad_attended.reshape(length, heads_local, head_width)
    grad_q_blocks = []
    grad_k_rot = jnp.zeros((length, head_width), jnp.float32)
    grad_values = jnp.zeros((length, head_width), jnp.float32)
    for block_index, row_start in enumerate(range(0, length, block_rows)):
        scores = scores_of(row_start)
        probs = jnp.exp(scores - log_totals[block_index])
        grad_rows = grad_attended[row_start : row_start + block_rows]
        grad_probs = jnp.einsum("qhd,kd->hqk", grad_rows, v_low, preferred_element_type=jnp.float32)
        grad_scores = (
            probs * (grad_probs - jnp.sum(probs * grad_probs, axis=-1, keepdims=True))
        ).astype(jnp.bfloat16)
        grad_q_blocks.append(
            jnp.einsum("hqk,kd->qhd", grad_scores, k_rot, preferred_element_type=jnp.float32)
        )
        grad_k_rot = grad_k_rot + jnp.einsum(
            "hqk,qhd->kd",
            grad_scores,
            q_rot[row_start : row_start + block_rows],
            preferred_element_type=jnp.float32,
        )
        grad_values = grad_values + jnp.einsum(
            "hqk,qhd->kd", probs.astype(jnp.bfloat16), grad_rows, preferred_element_type=jnp.float32
        )
    grad_queries, grad_keyvalue, gradient_query_norm_gain, gradient_key_norm_gain = prepare_back(
        (jnp.concatenate(grad_q_blocks, axis=0), grad_k_rot, grad_values)
    )
    query_low = grad_queries.astype(jnp.bfloat16)
    keyvalue_gradient_lowrank = grad_keyvalue.astype(jnp.bfloat16)
    gradient_query_weight = left_transposed(normalized_lowrank, query_low)
    gradient_keyvalue_weight = left_transposed(normalized_lowrank, keyvalue_gradient_lowrank)
    grad_in_part = right_transposed(query_low, query_merged) + right_transposed(
        keyvalue_gradient_lowrank, keyvalue_merged
    )
    grad_normed = lax.psum(grad_in_part, TENSOR)
    grad_inputs_add, gradient_input_gain = in_back(grad_normed)
    gradient_token_input = (grad_residual + grad_inputs_add)[None]
    lead_mask = (group_position == 0).astype(jnp.float32)
    lead_in = gradient_input_gain * lead_mask
    lead_post_attn = gradient_after_attention * lead_mask
    lead_pre_ff = gradient_before_feedforward * lead_mask
    lead_post_ff = gradient_after_feedforward * lead_mask
    sum_w_query, sum_w_out, sum_w_gate_up, sum_w_down = lax.psum(
        (
            gradient_query_weight,
            gradient_output_weight,
            gradient_gateup_weight,
            gradient_down_weight,
        ),
        DP,
    )
    (
        sum_gain_in,
        sum_post_attn,
        sum_pre_ff,
        sum_post_ff,
        sum_query_gain,
        sum_key_gain,
        sum_w_keyvalue,
    ) = lax.psum(
        (
            lead_in,
            lead_post_attn,
            lead_pre_ff,
            lead_post_ff,
            gradient_query_norm_gain,
            gradient_key_norm_gain,
            gradient_keyvalue_weight,
        ),
        (DP, TENSOR),
    )
    rows_rows = ((0,), (0,))
    columns_columns = ((1,), (1,))
    sum_kv_b = jnp.stack(
        [
            exact_product(
                sum_w_keyvalue[:, i * head_width : (i + 1) * head_width],
                keyvalue_adapter_first[:, i * adapter_rank : (i + 1) * adapter_rank],
                rows_rows,
            ).T
            for i in range(2)
        ]
    )
    sum_kv_a = jnp.concatenate(
        [
            exact_product(
                sum_w_keyvalue[:, i * head_width : (i + 1) * head_width],
                keyvalue_adapter_second[i],
                columns_columns,
            )
            for i in range(2)
        ],
        axis=1,
    )
    part_q_b = exact_product(sum_w_query, query_adapter_first, rows_rows).T
    part_q_a = exact_product(sum_w_query, query_piece, columns_columns)
    part_o_a = exact_product(sum_w_out, output_adapter_second, columns_columns)
    part_o_b = exact_product(sum_w_out, output_rows, rows_rows).T
    part_gu_b = jnp.stack(
        [
            exact_product(
                sum_w_gate_up[i],
                gateup_adapter_first[:, i * adapter_rank : (i + 1) * adapter_rank],
                rows_rows,
            ).T
            for i in range(2)
        ]
    )
    part_gu_a = jnp.concatenate(
        [exact_product(sum_w_gate_up[i], gateup_piece[i], columns_columns) for i in range(2)],
        axis=1,
    )
    part_d_a = exact_product(sum_w_down, down_adapter_second, columns_columns)
    part_d_b = exact_product(sum_w_down, down_rows, rows_rows).T
    sum_q_a, sum_o_b, sum_gu_a, sum_d_b = lax.psum(
        (part_q_a, part_o_b, part_gu_a, part_d_b), TENSOR
    )
    sum_q_b = lax.all_gather(part_q_b, TENSOR, axis=1, tiled=True)
    sum_o_a = lax.all_gather(part_o_a, TENSOR, axis=0, tiled=True)
    sum_gu_b = lax.all_gather(part_gu_b, TENSOR, axis=2, tiled=True)
    sum_d_a = lax.all_gather(part_d_a, TENSOR, axis=0, tiled=True)
    return (
        result_value,
        gradient_token_input,
        sum_gain_in,
        sum_post_attn,
        sum_pre_ff,
        sum_post_ff,
        sum_query_gain,
        sum_key_gain,
        sum_w_query,
        sum_w_keyvalue,
        sum_w_out,
        sum_w_gate_up,
        sum_w_down,
        sum_q_a,
        sum_q_b,
        sum_kv_a,
        sum_kv_b,
        sum_o_a,
        sum_o_b,
        sum_gu_a,
        sum_gu_b,
        sum_d_a,
        sum_d_b,
    )


def on_device_fast(
    tokens,
    document_numbers,
    input_norm_gain,
    after_attention_gain,
    before_feedforward_gain,
    after_feedforward_gain,
    query_norm_gain,
    key_norm_gain,
    query_weight,
    keyvalue_weight,
    output_weight,
    gateup_weight,
    down_weight,
    query_adapter_first,
    query_adapter_second,
    keyvalue_adapter_first,
    keyvalue_adapter_second,
    output_adapter_first,
    output_adapter_second,
    gateup_adapter_first,
    gateup_adapter_second,
    down_adapter_first,
    down_adapter_second,
    cotangent,
):
    length = document_numbers.shape[1]
    head_width = keyvalue_adapter_second.shape[2]
    width = input_norm_gain.shape[0]
    ahead = forward_pass(
        ForwardInputs(
            tokens=tokens[0],
            gin=input_norm_gain,
            w_q=query_weight,
            a_q=query_adapter_first,
            b_q=query_adapter_second,
            w_kv=keyvalue_weight,
            a_kv=keyvalue_adapter_first,
            b_kv=keyvalue_adapter_second,
            table=rotation_table(length, head_width),
            segments=document_numbers,
            gq=query_norm_gain,
            gk=key_norm_gain,
            w_o=output_weight,
            a_o=output_adapter_first,
            b_o=output_adapter_second,
            pa=after_attention_gain,
            pf=before_feedforward_gain,
            w_gu=gateup_weight,
            a_gu=gateup_adapter_first,
            b_gu=gateup_adapter_second,
            w_d=down_weight,
            a_d=down_adapter_first,
            b_d=down_adapter_second,
            cot=cotangent[0],
            pff=after_feedforward_gain,
        )
    )
    shapes = Pieces(
        d=down_weight.shape,
        g=gateup_weight.shape[1:],
        u=gateup_weight.shape[1:],
        o=output_weight.shape,
        q=query_weight.shape,
        k=keyvalue_weight.shape,
        s=(32, 128),
    )
    values = BackwardInputs(
        tokens=tokens[0],
        cot=cotangent[0],
        pa=after_attention_gain,
        pff=after_feedforward_gain,
        pf=before_feedforward_gain,
        segments=document_numbers,
        gq=query_norm_gain,
        gk=key_norm_gain,
        gin=input_norm_gain,
        **ahead._asdict(),
    )
    (result, grad_tokens, sum_k, sum_s), both = backward_and_sums(values, shapes)
    sum_d, sum_g, sum_u, sum_o, sum_q = both
    derived = derive_adapters(
        DeriveInputs(
            down_a=down_adapter_first,
            down_b=down_adapter_second,
            d=sum_d,
            gateup_a=gateup_adapter_first,
            gateup_b=gateup_adapter_second,
            g=sum_g,
            u=sum_u,
            output_a=output_adapter_first,
            output_b=output_adapter_second,
            o=sum_o,
            query_a=query_adapter_first,
            query_b=query_adapter_second,
            q=sum_q,
            keyvalue_a=keyvalue_adapter_first,
            keyvalue_b=keyvalue_adapter_second,
            k=sum_k,
            small=sum_s,
            result=result,
            tokens=grad_tokens,
        ),
        (width,) * 4 + (head_width,) * 2,
    )
    return (
        derived.result[None],
        derived.tokens[None],
        derived.gain_in,
        derived.gain_pa,
        derived.gain_pf,
        derived.gain_pff,
        derived.gain_q,
        derived.gain_k,
        derived.query,
        derived.keyvalue,
        derived.output,
        derived.gateup,
        derived.down,
        derived.query_a,
        derived.query_b,
        derived.keyvalue_a,
        derived.keyvalue_b,
        derived.output_a,
        derived.output_b,
        derived.gateup_a,
        derived.gateup_b,
        derived.down_a,
        derived.down_b,
    )


def solution(mesh):
    in_specs = (
        P(DP, None, None),
        P(DP, None),
        P(),
        P(),
        P(),
        P(),
        P(),
        P(),
        P(None, TENSOR),
        P(),
        P(TENSOR, None),
        P(None, None, TENSOR),
        P(TENSOR, None),
        P(),
        P(),
        P(),
        P(),
        P(),
        P(),
        P(),
        P(),
        P(),
        P(),
        P(DP, None, None),
    )
    out_specs = (
        P(DP, None, None),
        P(DP, None, None),
        P(),
        P(),
        P(),
        P(),
        P(),
        P(),
        P(None, TENSOR),
        P(),
        P(TENSOR, None),
        P(None, None, TENSOR),
        P(TENSOR, None),
        P(),
        P(),
        P(),
        P(),
        P(),
        P(),
        P(),
        P(),
        P(),
        P(),
    )
    fast = mesh.shape[DP] == 16 and mesh.shape[TENSOR] == 2
    return jax.shard_map(
        on_device_fast if fast else on_device_general,
        mesh=mesh, in_specs=in_specs, out_specs=out_specs, check_vma=False
    )
```

```python
import functools
from typing import NamedTuple

import jax
import jax.numpy as jnp
import numpy as np
from jax import lax
from jax.experimental import pallas as pl
from jax.experimental.pallas import tpu as pltpu
from jax.sharding import PartitionSpec as P

EPS = 1e-06
THETA = 1000000.0
MASKED = -1e30
GELU = 0.7978845608028654
DP, TENSOR = "dp", "tensor"
ROWS = 256
MESH_ID = pl.DeviceIdType.MESH
ANYWHERE = pl.BlockSpec(memory_space=pl.ANY)


def matrix_product(left_side, right_side):
    return jnp.dot(left_side, right_side, preferred_element_type=jnp.float32)


def left_transposed(left_side, right_side):
    return lax.dot_general(
        left_side, right_side, (((0,), (0,)), ((), ())), preferred_element_type=jnp.float32
    )


def right_transposed(left_side, right_side):
    return lax.dot_general(
        left_side, right_side, (((1,), (1,)), ((), ())), preferred_element_type=jnp.float32
    )


def rms_scale(values, scale_gain):
    return values * lax.rsqrt(jnp.mean(values * values, axis=-1, keepdims=True) + EPS) * scale_gain


def positions_of(segments):
    length = segments.shape[0]
    indices = jnp.arange(length, dtype=jnp.int32)
    before = jnp.concatenate([jnp.full((1,), -1, jnp.int32), segments[:-1]])
    starts = lax.cummax(jnp.where(segments != before, indices, jnp.zeros_like(indices)), axis=0)
    return indices - starts


def rotate(values, positions):
    half_dim = values.shape[-1] // 2
    frequency = THETA ** (-jnp.arange(half_dim, dtype=jnp.float32) * 2.0 / values.shape[-1])
    angles = positions.astype(jnp.float32)[:, None] * frequency[None, :]
    cosine = jnp.cos(angles)
    sine_part = jnp.sin(angles)
    if values.ndim == 3:
        cosine = cosine[:, None, :]
        sine_part = sine_part[:, None, :]
    leading = values[..., :half_dim]
    trailing = values[..., half_dim:]
    return jnp.concatenate(
        [leading * cosine - trailing * sine_part, trailing * cosine + leading * sine_part], axis=-1
    )


def exact_product(left_side, right_side, contract):
    return lax.dot_general(
        left_side,
        right_side.astype(jnp.float32),
        (contract, ((), ())),
        precision=lax.Precision.HIGHEST,
        preferred_element_type=jnp.float32,
    )


def activate(gate_in, up_in):
    return jax.nn.gelu(gate_in, approximate=True) * up_in


class Place:
    def __init__(self):
        me = lax.axis_index(DP)
        core = lax.axis_index(TENSOR)
        bit_x = lax.rem(me, 2)
        bit_y = lax.rem(me // 2, 2)
        level = me // 4
        across_x = me + 1 - 2 * bit_x
        across_y = me + 2 - 4 * bit_y
        self.core = core
        self.side = level // 2
        self.level = level
        self.outer = jnp.logical_or(level == 0, level == 3)
        self.inner = jnp.logical_not(self.outer)
        self.bits = (jnp.where(core == 0, bit_x, bit_y), jnp.where(core == 0, bit_y, bit_x))
        self.across = (
            (jnp.where(core == 0, across_x, across_y), core),
            (jnp.where(core == 0, across_y, across_x), core),
        )
        column = lax.rem(me, 4)
        self.near = ((level + 1 - 2 * lax.rem(level, 2)) * 4 + column, core)
        self.middle = ((3 - level) * 4 + column, core)
        self.sibling = (me, 1 - core)


def add_rows(target, target_row, extra, extra_row, count):
    step = 32 if count % 32 == 0 else (16 if count % 16 == 0 else 8)

    def body(index, carry):
        rows = pl.ds(pl.multiple_of(target_row + index * step, 8), step)
        target[rows] = target[rows] + extra[pl.ds(pl.multiple_of(extra_row + index * step, 8), step)]
        return carry

    lax.fori_loop(0, count // step, body, 0)


class Sums:
    def __init__(self, place, sends, receives, freed):
        self.place = place
        self.sends = sends
        self.receives = receives
        self.freed = freed
        self.used = 0
        self.credits = 0

    def credit(self):
        self.credits += 1
        return self.freed.at[self.credits - 1]

    def slot(self):
        self.used += 1
        return self.used - 1

    def copy(self, source, target, device, slot=None):
        slot = self.slot() if slot is None else slot
        return pltpu.make_async_remote_copy(
            src_ref=source,
            dst_ref=target,
            send_sem=self.sends.at[slot],
            recv_sem=self.receives.at[slot],
            device_id=device,
            device_id_type=MESH_ID,
        )


def signal(semaphore, device):
    pl.semaphore_signal(semaphore, inc=1, device_id=device, device_id_type=MESH_ID)


def rows_at(ref, start, count):
    return ref.at[pl.ds(pl.multiple_of(start, 8), count)]


def plane_first(sums, total, row, count, landing, landing_row, finish, turned):
    place = sums.place
    half, quarter = count // 2, count // 4
    bit_one, bit_two = place.bits[turned], place.bits[1 - turned]
    one, two = place.across[turned], place.across[1 - turned]
    kept = row + bit_one * half
    given = row + (1 - bit_one) * half
    mine = kept + bit_two * quarter
    other = kept + (1 - bit_two) * quarter
    land_one = rows_at(landing, landing_row, half)
    land_two = rows_at(landing, landing_row + half, quarter)
    land_near = rows_at(landing, landing_row + half + quarter, quarter)
    land_mid = rows_at(landing, landing_row + 2 * half, quarter)
    ours = rows_at(total, mine, quarter)
    slot_one, slot_two, slot_near = sums.slot(), sums.slot(), sums.slot()
    copy_one = sums.copy(rows_at(total, given, half), land_one, one, slot_one)
    copy_two = sums.copy(rows_at(total, other, quarter), land_two, two, slot_two)
    copy_in = sums.copy(ours, land_near, place.near, slot_near)
    copy_mid = sums.copy(ours, land_mid, place.middle)
    copy_out = sums.copy(ours, ours, place.near, slot_near)
    back_two = sums.copy(ours, ours, two, slot_two)
    back_one = sums.copy(rows_at(total, kept, half), rows_at(total, kept, half), one, slot_one)

    free_one, free_two, free_in = sums.credit(), sums.credit(), sums.credit()

    def step0():
        copy_one.start()

    def step1():
        copy_one.wait_recv()
        add_rows(total, kept, landing, landing_row, half)
        copy_two.start()

    def step2():
        copy_two.wait_recv()
        add_rows(total, mine, landing, landing_row + half, quarter)

        @pl.when(place.outer)
        def _():
            copy_in.start()

        copy_one.wait_send()
        signal(free_one, one)

    def step3():
        @pl.when(place.inner)
        def _():
            copy_in.wait_recv()
            add_rows(total, mine, landing, landing_row + half + quarter, quarter)
            copy_mid.start()

        copy_two.wait_send()
        signal(free_two, two)

        @pl.when(place.outer)
        def _():
            copy_in.wait_send()
            signal(free_in, place.near)

    def step4():
        @pl.when(place.inner)
        def _():
            copy_mid.wait()
            add_rows(total, mine, landing, landing_row + 2 * half, quarter)
            pl.semaphore_wait(free_in, 1)
            copy_out.start()
            pl.semaphore_wait(free_two, 1)
            back_two.start()

    def step5():
        @pl.when(place.outer)
        def _():
            copy_out.wait_recv()
            pl.semaphore_wait(free_two, 1)
            back_two.start()

    def step6():
        back_two.wait_recv()
        pl.semaphore_wait(free_one, 1)
        back_one.start()

    def step7():
        back_one.wait_recv()
        back_two.wait_send()
        back_one.wait_send()

        @pl.when(place.inner)
        def _():
            copy_out.wait_send()

        finish()

    return [step0, step1, step2, step3, step4, step5, step6, step7]


def line_first(sums, total, row, count, landing, landing_row, finish, turned):
    place = sums.place
    one, two = place.across[turned], place.across[1 - turned]
    quarter = count // 4
    side = place.side
    three = row + (1 - side) * quarter
    far_pair = row + (1 - side) * 2 * quarter
    own_pair = row + side * 2 * quarter
    outer_quarter = row + 3 * side * quarter
    mine = row + place.level * quarter
    ours = rows_at(total, mine, quarter)
    land_three = rows_at(landing, landing_row, 3 * quarter)
    land_pair = rows_at(landing, landing_row + 3 * quarter, 2 * quarter)
    land_back = rows_at(landing, landing_row, quarter)
    land_one = rows_at(landing, landing_row + 5 * quarter, quarter)
    land_two = rows_at(landing, landing_row + 6 * quarter, quarter)
    slot_near, slot_middle, slot_spread = sums.slot(), sums.slot(), sums.slot()
    copy_three = sums.copy(rows_at(total, three, 3 * quarter), land_three, place.near, slot_near)
    copy_pair = sums.copy(
        rows_at(total, far_pair, 2 * quarter), land_pair, place.middle, slot_middle
    )
    outers = rows_at(total, outer_quarter, quarter)
    copy_back = sums.copy(outers, land_back, place.near, slot_near)
    copy_one = sums.copy(ours, land_one, one)
    copy_two = sums.copy(ours, land_two, two)
    spread_in = sums.copy(ours, ours, place.near, slot_spread)
    spread_out = sums.copy(ours, ours, place.near, slot_spread)
    spread_mid = sums.copy(ours, ours, place.middle, slot_middle)
    forward_mid = sums.copy(outers, outers, place.middle)
    far_rows = rows_at(total, far_pair, 2 * quarter)
    forward_out = sums.copy(far_rows, far_rows, place.near, slot_near)

    free_near, free_pair = sums.credit(), sums.credit()

    def step0():
        @pl.when(place.outer)
        def _():
            copy_three.start()

    def step1():
        @pl.when(place.inner)
        def _():
            copy_three.wait_recv()
            add_rows(total, three, landing, landing_row, 3 * quarter)
            copy_pair.start()

    def step2():
        @pl.when(place.inner)
        def _():
            copy_pair.wait_recv()
            add_rows(total, own_pair, landing, landing_row + 3 * quarter, 2 * quarter)
            copy_back.start()
            copy_one.start()

    def step3():
        @pl.when(place.outer)
        def _():
            copy_back.wait_recv()
            add_rows(total, mine, landing, landing_row, quarter)
            copy_one.start()
            copy_three.wait_send()
            signal(free_near, place.near)

        @pl.when(place.inner)
        def _():
            copy_pair.wait_send()
            signal(free_pair, place.middle)
            copy_back.wait_send()
            signal(free_near, place.near)

    def step4():
        copy_one.wait()
        add_rows(total, mine, landing, landing_row + 5 * quarter, quarter)
        copy_two.start()

    def step5():
        copy_two.wait()
        add_rows(total, mine, landing, landing_row + 6 * quarter, quarter)

        @pl.when(place.outer)
        def _():
            pl.semaphore_wait(free_near, 1)
            spread_in.start()

        @pl.when(place.inner)
        def _():
            pl.semaphore_wait(free_near, 1)
            spread_out.start()
            pl.semaphore_wait(free_pair, 1)
            spread_mid.start()

    def step6():
        @pl.when(place.inner)
        def _():
            spread_in.wait_recv()
            forward_mid.start()

    def step7():
        @pl.when(place.inner)
        def _():
            spread_mid.wait_recv()
            forward_mid.wait_recv()
            forward_out.start()

    def step8():
        @pl.when(place.outer)
        def _():
            spread_out.wait_recv()
            forward_out.wait_recv()
            spread_in.wait_send()

        @pl.when(place.inner)
        def _():
            spread_out.wait_send()
            spread_mid.wait_send()
            forward_mid.wait_send()
            forward_out.wait_send()

        finish()

    return [step0, step1, step2, step3, step4, step5, step6, step7, step8]


def greet(place):
    barrier = pltpu.get_barrier_semaphore()
    for device in (*place.across, place.near, place.sibling):
        pl.semaphore_signal(barrier, inc=1, device_id=device, device_id_type=MESH_ID)

    @pl.when(place.inner)
    def _():
        pl.semaphore_signal(barrier, inc=1, device_id=place.middle, device_id_type=MESH_ID)
        pl.semaphore_wait(barrier, 5)

    @pl.when(place.outer)
    def _():
        pl.semaphore_wait(barrier, 4)


class BackwardInputs(NamedTuple):
    gml: object
    hidden: object
    ff: object
    w_g: object
    w_u: object
    w_d: object
    mlp: object
    attn: object
    tokens: object
    cot: object
    pa: object
    pff: object
    pf: object
    w_o: object
    attended: object
    q_rot: object
    k_rot: object
    values: object
    segments: object
    lse: object
    cosine: object
    sine: object
    normed: object
    w_q: object
    gq: object
    w_kv: object
    gk: object
    gin: object
    gain_pff: object


class Pieces(NamedTuple):
    d: object
    g: object
    u: object
    o: object
    q: object
    k: object
    s: object


PIECE_K, PIECE_S = 5, 6
PARTS = ((0, None),)
PARTS += tuple((piece, block) for block in range(4) for piece in (1, 2))
PARTS += ((3, None), (4, 0), (4, 1), (5, None), (6, None))


class Work(NamedTuple):
    gate: object
    up: object
    part: object
    other: object
    dq: object
    gains: object
    gain_q: object
    gain_k: object
    result: object


def row_loop(count, body, start=0):
    def step(index, carry):
        body(pl.ds(pl.multiple_of(index * ROWS, ROWS), ROWS), index)
        return carry

    lax.fori_loop(start, count, step, 0)


def row_at(segments, index):
    columns = pl.ds(pl.multiple_of(index * ROWS, ROWS), ROWS)
    return segments[:, columns].astype(jnp.float32)


def column_of(row):
    shape = (row.shape[1], row.shape[1])
    diagonal = lax.broadcasted_iota(jnp.int32, shape, 0) == lax.broadcasted_iota(jnp.int32, shape, 1)
    return jnp.sum(jnp.where(diagonal, row, 0.0), axis=1, keepdims=True)


def inverse_rms(values):
    return lax.rsqrt(jnp.mean(values * values, axis=-1, keepdims=True) + EPS)


def rms_back(incoming, gain, normed, inverse):
    scaled = incoming * gain
    return inverse * (scaled - normed * jnp.mean(scaled * normed, axis=-1, keepdims=True))


def add_gain(target, terms):
    width = terms.shape[1]
    target[...] = target[...] + jnp.sum(terms.reshape(-1, 8, width), axis=0)


def gelu_parts(gate):
    inner = 0.7978845608028654 * gate * (1.0 + 0.044715 * gate * gate)
    bent = jnp.tanh(inner)
    half = 0.5 * (1.0 + bent)
    slope = half + 0.5 * gate * (1.0 - bent * bent) * 0.7978845608028654 * (
        1.0 + 0.134145 * gate * gate
    )
    return gate * half, slope


def turn_back(values, cosine, sine):
    half = values.shape[1] // 2
    leading, trailing = values[:, :half], values[:, half:]
    return jnp.concatenate(
        [leading * cosine + trailing * sine, trailing * cosine - leading * sine], axis=1
    )


def backward_kernel(setup, *refs):
    plan, order = setup
    refs = list(refs)
    source = BackwardInputs(*refs[: len(BackwardInputs._fields)])
    refs = refs[len(source) :]
    out_home, token_home, own_k, own_s = refs[:4]
    both = refs[4 : 4 + len(Pieces._fields) - 2]
    refs = refs[4 + len(both) :]
    held = BackwardInputs(*refs[: len(source)])
    refs = refs[len(source) :]
    total = Pieces(*refs[: len(Pieces._fields)])
    refs = refs[len(total) :]
    landing = refs[: len(PARTS)]
    refs = refs[len(PARTS) :]
    swapped_k, swapped_s = refs[:2]
    work = Work(*refs[2 : 2 + len(Work._fields)])
    loads, sends, receives, local, freed, handed = refs[2 + len(work) :]
    place = Place()
    core = place.core
    sums = Sums(place, sends, receives, freed)
    arrivals = BackwardInputs(
        *(
            pltpu.make_async_copy(piece, home, loads.at[index])
            for index, (piece, home) in enumerate(zip(source, held))
        )
    )
    for arrival in arrivals[:2]:
        arrival.start()
    greet(place)
    length = held.attn.shape[0]
    blocks = length // ROWS
    width = held.attn.shape[1]
    head = held.k_rot.shape[1]
    heads = held.q_rot.shape[1] // head
    hidden_columns = held.hidden.shape[1]
    here = set()

    def need(*copies):
        for copy in copies:
            if id(copy) not in here:
                here.add(id(copy))
                copy.wait()

    for gains in (work.gains, work.gain_q, work.gain_k):
        gains[...] = jnp.zeros_like(gains)
    gain_in, gain_pa, gain_pf = (work.gains.at[i] for i in range(3))
    low, part, other = held.gml, work.part, work.other
    leaving = []

    def residual_of(rows):
        attn = held.attn[rows, :]
        inverse = inverse_rms(attn)
        normed = attn * inverse
        return held.tokens[rows, :].astype(jnp.float32) + normed * held.pa[...], normed, inverse

    def down_gradient():
        need(arrivals.gml, arrivals.hidden)
        for arrival in arrivals[2:6]:
            arrival.start()

        def body(columns, _):
            total.d[columns, :] = left_transposed(held.hidden[:, columns], low[...])

        row_loop(hidden_columns // ROWS, body)

    def gate_block(index):
        def run():
            need(arrivals.ff, arrivals.w_g, arrivals.w_u, arrivals.w_d)
            if index == 0:
                for arrival in arrivals[6:]:
                    arrival.start()
            columns = pl.ds(index * ROWS, ROWS)

            def body(rows, _):
                entering = held.ff[rows, :]
                gate = matrix_product(entering, held.w_g[:, columns])
                up = matrix_product(entering, held.w_u[:, columns])
                incoming = right_transposed(low[rows, :], held.w_d[columns, :])
                bent, slope = gelu_parts(gate)
                grad_gate = (incoming * up * slope).astype(jnp.bfloat16)
                grad_up = (incoming * bent).astype(jnp.bfloat16)
                work.gate[rows, :] = grad_gate
                work.up[rows, :] = grad_up
                share = right_transposed(grad_gate, held.w_g[:, columns]) + right_transposed(
                    grad_up, held.w_u[:, columns]
                )
                part[rows, :] = share if index == 0 else part[rows, :] + share

            row_loop(blocks, body)
            total.g[:, columns] = left_transposed(held.ff[...], work.gate[...])
            total.u[:, columns] = left_transposed(held.ff[...], work.up[...])

        return run

    def part_copies():
        first = sums.used
        sums.used += blocks

        def copy(index):
            rows = pl.ds(pl.multiple_of(index * ROWS, ROWS), ROWS)
            return pltpu.make_async_remote_copy(
                src_ref=part.at[rows],
                dst_ref=other.at[rows],
                send_sem=sends.at[first + index],
                recv_sem=receives.at[first + index],
                device_id=place.sibling,
                device_id_type=MESH_ID,
            )

        return copy

    ff_copy, input_copy = part_copies(), part_copies()

    def send_parts(copy):
        row_loop(blocks, lambda rows, index: copy(index).start())

    def residual_back():
        need(arrivals.mlp, arrivals.attn, arrivals.tokens, arrivals.cot, arrivals.pa, arrivals.pff)
        need(arrivals.pf, arrivals.w_o)
        def take_rows(rows, index):
            ff_copy(index).wait_recv()
            residual, normed_attn, inverse_attn = residual_of(rows)
            mlp = held.mlp[rows, :]
            ending = residual + mlp * inverse_rms(mlp) * held.pff[...]
            work.result[rows, :] = ending.astype(jnp.bfloat16)
            incoming = part[rows, :] + other[rows, :]
            inverse = inverse_rms(residual)
            normed = residual * inverse
            add_gain(gain_pf, incoming * normed)
            grad = held.cot[rows, :].astype(jnp.float32) + rms_back(
                incoming, held.pf[...], normed, inverse
            )
            held.mlp[rows, :] = grad
            add_gain(gain_pa, grad * normed_attn)
            low[rows, :] = rms_back(grad, held.pa[...], normed_attn, inverse_attn).astype(
                jnp.bfloat16
            )

        row_loop(blocks, take_rows)
        move = pltpu.make_async_copy(work.result, out_home, local.at[0])
        move.start()
        leaving.append(move)
        row_loop(blocks, lambda rows, index: ff_copy(index).wait_send())
        signal(handed, place.sibling)
        grad_attended = held.ff

        def body(rows, _):
            grad_attended[rows, : heads * head] = right_transposed(
                low[rows, :], held.w_o[...]
            ).astype(jnp.bfloat16)

        row_loop(blocks, body)

    def output_gradient():
        need(arrivals.attended)

        def body(columns, _):
            total.o[columns, :] = left_transposed(held.attended[:, columns], low[...])

        row_loop(heads * head // ROWS, body)

    grad_key = held.attn.at[:, :head]
    grad_value = held.attn.at[:, head : 2 * head]
    grad_query_low = held.hidden.at[:, : heads * head]
    grad_keyvalue_low = held.hidden.at[:, heads * head : heads * head + 2 * head]

    def attention_rows(which, start, stop):
        def run():
            need(arrivals.q_rot, arrivals.k_rot, arrivals.values, arrivals.segments, arrivals.lse, arrivals.cosine, arrivals.sine, arrivals.normed, arrivals.w_q)
            need(arrivals.gq)
            columns = pl.ds(which * head, head)
            if which == 0 and start == 0:
                held.attn[...] = jnp.zeros_like(held.attn)

            def body(rows, index):
                query = held.q_rot[rows, columns]
                grad = held.ff[rows, columns]
                attended = held.attended[rows, columns]
                weight = jnp.sum(
                    grad.astype(jnp.float32) * attended.astype(jnp.float32), axis=1, keepdims=True
                )
                lse = held.lse[which, rows, :]
                segment = column_of(row_at(held.segments, index))
                work.dq[...] = jnp.zeros_like(work.dq)

                def inner(at, carry):
                    others = pl.ds(pl.multiple_of(at * ROWS, ROWS), ROWS)
                    key = held.k_rot[others, :]
                    value = held.values[others, :]
                    scores = right_transposed(query, key)
                    row_index = index * ROWS + lax.broadcasted_iota(jnp.int32, scores.shape, 0)
                    column_index = at * ROWS + lax.broadcasted_iota(jnp.int32, scores.shape, 1)
                    allowed = (segment == row_at(held.segments, at)) & (row_index >= column_index)
                    probs = jnp.where(allowed, jnp.exp(scores - lse), 0.0)
                    grad_probs = right_transposed(grad, value)
                    grad_scores = (probs * (grad_probs - weight)).astype(jnp.bfloat16)
                    work.dq[...] += matrix_product(grad_scores, key)
                    grad_key[others, :] = grad_key[others, :] + left_transposed(grad_scores, query)
                    grad_value[others, :] = grad_value[others, :] + left_transposed(
                        probs.astype(jnp.bfloat16), grad
                    )
                    return carry

                lax.fori_loop(0, index + 1, inner, 0)
                turned = turn_back(work.dq[...], held.cosine[rows, :], held.sine[rows, :])
                turned = turned * head ** (-0.5)
                raw = matrix_product(held.normed[rows, :], held.w_q[:, columns])
                inverse = inverse_rms(raw)
                normed = raw * inverse
                add_gain(work.gain_q, turned * normed)
                grad_query_low[rows, columns] = rms_back(
                    turned, held.gq[...], normed, inverse
                ).astype(jnp.bfloat16)

            row_loop(stop, body, start)

        return run

    def key_back():
        need(arrivals.w_kv, arrivals.gk)

        def body(rows, _):
            turned = turn_back(grad_key[rows, :], held.cosine[rows, :], held.sine[rows, :])
            raw = matrix_product(held.normed[rows, :], held.w_kv[:, :head])
            inverse = inverse_rms(raw)
            normed = raw * inverse
            add_gain(work.gain_k, turned * normed)
            grad_keyvalue_low[rows, :head] = rms_back(
                turned, held.gk[...], normed, inverse
            ).astype(jnp.bfloat16)
            grad_keyvalue_low[rows, head:] = grad_value[rows, :].astype(jnp.bfloat16)

        row_loop(blocks, body)

    def query_gradient(which):
        columns = pl.ds(which * head, head)
        total.q[:, columns] = left_transposed(held.normed[...], grad_query_low[:, columns])

    half_rows = swapped_k.shape[0]
    swap_k, swap_s = [], []

    def keyvalue_gradient():
        for index in range(2 * head // ROWS):
            columns = pl.ds(index * ROWS, ROWS)
            total.k[:, columns] = left_transposed(
                held.normed[...], grad_keyvalue_low[:, columns]
            )
        copy = sums.copy(
            rows_at(total.k, (1 - core) * half_rows, half_rows), swapped_k, place.sibling
        )
        copy.start()
        swap_k.append(copy)

    def input_parts():
        def body(rows, _):
            part[rows, :] = right_transposed(
                grad_query_low[rows, :], held.w_q[...]
            ) + right_transposed(grad_keyvalue_low[rows, :], held.w_kv[...])

        row_loop(blocks, body)
        pl.semaphore_wait(handed, 1)
        send_parts(input_copy)

    def input_back():
        need(arrivals.gin, arrivals.gain_pff)
        def take_rows(rows, index):
            input_copy(index).wait_recv()
            incoming = part[rows, :] + other[rows, :]
            tokens = held.tokens[rows, :].astype(jnp.float32)
            inverse = inverse_rms(tokens)
            normed = tokens * inverse
            add_gain(gain_in, incoming * normed)
            held.mlp[rows, :] = held.mlp[rows, :] + rms_back(
                incoming, held.gin[...], normed, inverse
            )

        row_loop(blocks, take_rows)
        move = pltpu.make_async_copy(held.mlp, token_home, local.at[1])
        move.start()
        leaving.append(move)
        row_loop(blocks, lambda rows, index: input_copy(index).wait_send())
        small = total.s
        small[...] = jnp.zeros_like(small)
        lead = jnp.where(core == 0, 1.0, 0.0)
        row = 0
        for index in range(4):
            rows = work.gains[index] if index < 3 else held.gain_pff[...]
            vector = jnp.sum(rows, axis=0, keepdims=True) * lead
            for at in range(width // 128):
                small[row : row + 1, :] = vector[:, at * 128 : (at + 1) * 128]
                row += 1
        for gains in (work.gain_q, work.gain_k):
            vector = jnp.sum(gains[...], axis=0, keepdims=True)
            for at in range(head // 128):
                small[row : row + 1, :] = vector[:, at * 128 : (at + 1) * 128]
                row += 1
        copy = sums.copy(small, swapped_s, place.sibling)
        copy.start()
        swap_s.append(copy)

    tasks = (
        down_gradient,
        gate_block(0),
        gate_block(1),
        gate_block(2),
        lambda: (gate_block(3)(), send_parts(ff_copy)),
        residual_back,
        output_gradient,
        attention_rows(0, 0, 3),
        attention_rows(0, 3, 4),
        lambda: query_gradient(0),
        attention_rows(1, 0, 3),
        attention_rows(1, 3, 4),
        lambda: query_gradient(1),
        key_back,
        keyvalue_gradient,
        input_parts,
        input_back,
    )
    chunks = []
    slots = 2
    for (piece, block), land, parts in zip(PARTS, landing, plan):
        columns = slice(None) if block is None else pl.ds(block * ROWS, ROWS)
        summed = total[piece] if block is None else total[piece].at[:, columns]
        row = 0
        land_row = 0
        base = core * half_rows if piece == PIECE_K else 0
        for line, count, turned in parts:

            def finish(
                piece=piece,
                columns=columns,
                summed=summed,
                row=row,
                base=base,
                count=count,
                slot=slots,
            ):
                done = rows_at(summed, base + row, count)
                if piece == PIECE_S:
                    moves = [pltpu.make_async_copy(done, own_s, local.at[slot])]
                else:
                    if piece == PIECE_K:
                        home = rows_at(own_k, base + row, count)
                    else:
                        home = both[piece].at[core, pl.ds(row, count), columns]
                    moves = [
                        pltpu.make_async_copy(done, home, local.at[slot]),
                        sums.copy(done, home, place.sibling),
                    ]
                for move in moves:
                    move.start()
                leaving.extend(moves)

            build = line_first if line else plane_first
            steps = build(sums, summed, base + row, count, land, land_row, finish, turned)
            if piece >= PIECE_K:
                swap, landed = (swap_k, swapped_k) if piece == PIECE_K else (swap_s, swapped_s)

                def enter(swap=swap, landed=landed, out=total[piece], base=base, first=steps[0]):
                    if swap:
                        swap.pop().wait()
                        add_rows(out, base, landed, 0, landed.shape[0])
                    first()

                steps = [enter] + steps[1:]
            chunks.append(steps)
            slots += 1
            row += count
            land_row += landing_rows(line, count)
    for entry in order:
        if entry < 0:
            tasks[-1 - entry]()
        else:
            chunks[entry // 10][entry % 10]()
    for move in leaving:
        move.wait()


def backward_and_sums(values, shapes):
    length, width = values.tokens.shape
    head = values.k_rot.shape[1]
    full, low = jnp.float32, jnp.bfloat16
    outs = [((length, width), low), ((length, width), full), (shapes.k, full), (shapes.s, full)]
    outs += [((2,) + shape, full) for shape in shapes[:PIECE_K]]
    scratch = [pltpu.VMEM(array.shape, array.dtype) for array in values]
    scratch += [pltpu.VMEM(shape, full) for shape in shapes]
    for (piece, block), parts in zip(PARTS, CUTS):
        columns = shapes[piece][1] if block is None else ROWS
        rows = sum(landing_rows(line, count) for line, count, _ in parts)
        scratch.append(pltpu.VMEM((rows, columns), full))
    scratch += [pltpu.VMEM((shapes.k[0] // 2, shapes.k[1]), full), pltpu.VMEM(shapes.s, full)]
    scratch += Work(
        gate=pltpu.VMEM((length, ROWS), low),
        up=pltpu.VMEM((length, ROWS), low),
        part=pltpu.VMEM((length, width), full),
        other=pltpu.VMEM((length, width), full),
        dq=pltpu.VMEM((ROWS, head), full),
        gains=pltpu.VMEM((3, 8, width), full),
        gain_q=pltpu.VMEM((8, head), full),
        gain_k=pltpu.VMEM((8, head), full),
        result=pltpu.VMEM((length, width), low),
    )
    kinds = [line for parts in CUTS for line, _, _ in parts]
    count = len(kinds)
    blocks = length // ROWS
    slots = 2 * blocks + 2 + count + sum(6 if line else 4 for line in kinds)
    scratch += [
        pltpu.SemaphoreType.DMA((len(values),)),
        pltpu.SemaphoreType.DMA((slots,)),
        pltpu.SemaphoreType.DMA((slots,)),
        pltpu.SemaphoreType.DMA((count + 2,)),
        pltpu.SemaphoreType.REGULAR((sum(2 if line else 3 for line in kinds),)),
        pltpu.SemaphoreType.REGULAR,
    ]
    results = pl.pallas_call(
        functools.partial(backward_kernel, (CUTS, ORDER)),
        out_shape=[jax.ShapeDtypeStruct(*out) for out in outs],
        in_specs=[ANYWHERE] * len(values),
        out_specs=[ANYWHERE] * len(outs),
        scratch_shapes=scratch,
        compiler_params=pltpu.CompilerParams(
            collective_id=0, has_side_effects=True, vmem_limit_bytes=67043328
        ),
    )(*values)
    return results[:4], results[4:]


CUTS = (
    ((0, 64, 1), (1, 224, 0), (0, 480, 0), (1, 256, 1),),
    ((0, 96, 1), (0, 544, 1),),
    ((0, 640, 0),),
    ((0, 640, 1),),
    ((0, 96, 1), (0, 544, 0),),
    ((0, 32, 1), (1, 576, 1), (0, 32, 1),),
    ((0, 64, 0), (0, 576, 1),),
    ((0, 640, 0),),
    ((0, 32, 0), (0, 288, 1), (1, 320, 0),),
    ((1, 160, 1), (0, 160, 0), (0, 32, 1), (0, 160, 1),),
    ((0, 224, 0), (0, 416, 1),),
    ((0, 640, 0),),
    ((1, 224, 1), (0, 96, 1),),
    ((0, 32, 0),),
)
ORDER = (
    -1, 20, 30, 0, -2, 50, 60, -3, 10, 70, 90, -4, 21, 110, 51, 31, -5, 140, 11, 150, -6, 22, 61,
    40, 32, 130, -7, 200, 111, 170, 71, 180, -8, 141, 23, 62, 33, 112, 210, 220, 12, -9, 160, 72,
    190, 181, 171, -10, 80, 34, 113, 24, 142, 63, 151, 230, 13, 91, 73, 182, -11, 35, 41, 114,
    221, 25, 191, 131, 1, 74, -12, 143, 52, 183, 115, 161, 240, -13, 172, 250, 211, 2, 64, 42, 53,
    92, 192, 75, -14, 116, 201, 231, 152, 100, 144, 241, 65, -15, 120, 54, 222, 173, 270, 3, 81,
    260, 117, 14, 145, 93, 251, 212, 184, 153, 76, 121, 55, 174, 223, 232, 4, 66, 94, -16, 15,
    122, 132, 154, 261, 271, -17, 101, 280, 26, 43, 82, 16, 133, 213, 224, 193, 281, 272, 242,
    202, 185, 95, 273, 194, 102, 162, 262, 56, 5, 17, 175, 203, 233, 243, 123, 274, 204, 163, 263,
    103, 252, 146, 282, 186, 214, 134, 225, 96, 253, 44, 234, 164, 283, 83, 155, 18, 244, 205,
    124, 104, 264, 165, 36, 215, 226, 195, 57, 45, 284, 125, 254, 67, 275, 156, 84, 285, 196, 135,
    105, 245, 176, 37, 6, 197, 265, 136, 255, 106, 85, 286, 266, 206, 118, 27, 77, 235, 287, 276,
    166, 216, 187, 256, 46, 86, 126, 157, 167, 207, 227, 246, 198, 267, 147, 7, 177, 217, 97, 277,
    137, 47, 236, 107, 188, 87, 257, 127, 247, 38, 268, 237,
)


def landing_rows(line, count):
    return count // 4 * (7 if line else 5)


FINE = 32


class ForwardInputs(NamedTuple):
    tokens: object
    gin: object
    w_q: object
    a_q: object
    b_q: object
    w_kv: object
    a_kv: object
    b_kv: object
    table: object
    segments: object
    gq: object
    gk: object
    w_o: object
    a_o: object
    b_o: object
    pa: object
    pf: object
    w_gu: object
    a_gu: object
    b_gu: object
    w_d: object
    a_d: object
    b_d: object
    cot: object
    pff: object


class ForwardOutputs(NamedTuple):
    gml: object
    gain_pff: object
    mlp: object
    attn: object
    hidden: object
    ff: object
    w_g: object
    w_u: object
    w_d: object
    w_o: object
    attended: object
    q_rot: object
    k_rot: object
    values: object
    lse: object
    cosine: object
    sine: object
    normed: object
    w_q: object
    w_kv: object


def turn(values, cosine, sine):
    half = values.shape[1] // 2
    leading, trailing = values[:, :half], values[:, half:]
    return jnp.concatenate(
        [leading * cosine - trailing * sine, trailing * cosine + leading * sine], axis=1
    )


def forward_kernel(*refs):
    refs = list(refs)
    source = ForwardInputs(*refs[: len(ForwardInputs._fields)])
    refs = refs[len(source) :]
    target = ForwardOutputs(*refs[: len(ForwardOutputs._fields)])
    refs = refs[len(target) :]
    held = ForwardInputs(*refs[: len(source)])
    refs = refs[len(source) :]
    made = ForwardOutputs(*refs[: len(target)])
    part, other, part_two, other_two, sums_at, rotation = refs[len(target) : len(target) + 6]
    loads, sends, receives, stores = refs[len(target) + 6 :]
    me = lax.axis_index(DP)
    core = lax.axis_index(TENSOR)
    sibling = (me, 1 - core)

    def own_part(ref, home, axis):
        size = home.shape[axis]
        span = pl.ds(pl.multiple_of(core * size, 256), size)
        index = [slice(None)] * len(home.shape)
        index[axis] = span
        return ref.at[tuple(index)]

    pieces = source._replace(
        b_q=own_part(source.b_q, held.b_q, 1),
        a_o=own_part(source.a_o, held.a_o, 0),
        b_gu=own_part(source.b_gu, held.b_gu, 2),
        a_d=own_part(source.a_d, held.a_d, 0),
    )
    arrivals = ForwardInputs(
        *(
            pltpu.make_async_copy(piece, home, loads.at[index])
            for index, (piece, home) in enumerate(zip(pieces, held))
        )
    )
    for arrival in arrivals[:8]:
        arrival.start()
    barrier = pltpu.get_barrier_semaphore()
    signal(barrier, sibling)
    pl.semaphore_wait(barrier, 1)
    leaving = []
    homes = {id(ref): (index, home) for index, (ref, home) in enumerate(zip(made, target))}

    def leave(*arrays):
        for ref in arrays:
            index, home = homes[id(ref)]
            move = pltpu.make_async_copy(ref, home, stores.at[index])
            move.start()
            leaving.append(move)

    def need(*copies):
        for copy in copies:
            copy.wait()

    length, width = held.tokens.shape
    blocks = length // ROWS
    head = held.gq.shape[0]
    heads = held.w_q.shape[1] // head
    rank = held.a_q.shape[1]

    def merge(out, weight, first, second):
        count = weight.shape[0]
        step = 256 if count % 256 == 0 else 320

        def body(index, carry):
            rows = pl.ds(pl.multiple_of(index * step, 64), step)
            out[rows, :] = (
                weight[rows, :].astype(jnp.float32) + matrix_product(first[rows, :], second[...])
            ).astype(jnp.bfloat16)
            return carry

        lax.fori_loop(0, count // step, body, 0)

    need(arrivals.tokens, arrivals.gin, arrivals.w_q, arrivals.a_q, arrivals.b_q)
    for arrival in arrivals[8:]:
        arrival.start()
    merge(made.w_q, held.w_q, held.a_q, held.b_q)
    need(arrivals.w_kv, arrivals.a_kv, arrivals.b_kv)
    for index in range(2):
        columns = pl.ds(index * head, head)
        merge(
            made.w_kv.at[:, columns],
            held.w_kv.at[:, columns],
            held.a_kv.at[:, pl.ds(index * rank, rank)],
            held.b_kv.at[index],
        )
    leave(made.w_q, made.w_kv)
    need(arrivals.table, arrivals.segments, arrivals.gq, arrivals.gk)
    before = jnp.zeros((8, 1), jnp.float32)
    number = lax.broadcasted_iota(jnp.int32, (8, ROWS), 0).astype(jnp.float32)
    for index in range(blocks):
        fewer = jnp.where(row_at(held.segments, index) < number, 1.0, 0.0)
        before = before + jnp.sum(fewer, axis=1, keepdims=True)
    at_token = lax.broadcasted_iota(jnp.int32, (8, length), 1).astype(jnp.float32)
    chosen = jnp.where(at_token == before, 1.0, 0.0)
    half = head // 2
    coarse = length // FINE

    def fill(index, carry):
        rows = pl.ds(pl.multiple_of(index * FINE, FINE), FINE)
        step = held.table[pl.ds(index, 1), :]
        step_cosine, step_sine = step[:, :half], step[:, half:]
        fine = held.table[coarse : coarse + FINE, :]
        fine_cosine, fine_sine = fine[:, :half], fine[:, half:]
        rotation[rows, :half] = fine_cosine * step_cosine - fine_sine * step_sine
        rotation[rows, half:] = fine_sine * step_cosine + fine_cosine * step_sine
        return carry

    lax.fori_loop(0, coarse, fill, 0)
    starts = jnp.dot(
        chosen, rotation[...], precision=lax.Precision.HIGHEST, preferred_element_type=jnp.float32
    )

    def project(rows, index):
        tokens = held.tokens[rows, :].astype(jnp.float32)
        normed = (tokens * inverse_rms(tokens) * held.gin[...]).astype(jnp.bfloat16)
        made.normed[rows, :] = normed
        segment = column_of(row_at(held.segments, index))
        start = starts[3:4, :]
        for document in (2, 1, 0):
            start = jnp.where(segment == document, starts[document : document + 1, :], start)
        start_cosine, start_sine = start[:, :half], start[:, half:]
        here = rotation[rows, :]
        here_cosine, here_sine = here[:, :half], here[:, half:]
        cosine = here_cosine * start_cosine + here_sine * start_sine
        sine = here_sine * start_cosine - here_cosine * start_sine
        made.cosine[rows, :] = cosine
        made.sine[rows, :] = sine
        for at in range(heads):
            columns = pl.ds(at * head, head)
            raw = matrix_product(normed, made.w_q[:, columns])
            query = turn(raw * inverse_rms(raw) * held.gq[...], cosine, sine) * head ** (-0.5)
            made.q_rot[rows, columns] = query.astype(jnp.bfloat16)
        raw = matrix_product(normed, made.w_kv[:, :head])
        key = turn(raw * inverse_rms(raw) * held.gk[...], cosine, sine)
        made.k_rot[rows, :] = key.astype(jnp.bfloat16)
        made.values[rows, :] = matrix_product(normed, made.w_kv[:, head:]).astype(jnp.bfloat16)

    row_loop(blocks, project)
    leave(made.normed, made.cosine, made.sine, made.q_rot, made.k_rot, made.values)
    need(arrivals.w_o, arrivals.a_o, arrivals.b_o)
    merge(made.w_o, held.w_o, held.a_o, held.b_o)
    leave(made.w_o)

    def exchange(key, index, mine, theirs):
        rows = pl.ds(pl.multiple_of(index * ROWS, ROWS), ROWS)
        slot = key * blocks + index
        return pltpu.make_async_remote_copy(
            src_ref=mine.at[rows],
            dst_ref=theirs.at[rows],
            send_sem=sends.at[slot],
            recv_sem=receives.at[slot],
            device_id=sibling,
            device_id_type=MESH_ID,
        )

    def attend(rows, index):
        segment = column_of(row_at(held.segments, index))

        queries = [made.q_rot[rows, at * head : (at + 1) * head] for at in range(heads)]
        sums_at[...] = jnp.zeros_like(sums_at)

        def inner(at, carry):
            others = pl.ds(pl.multiple_of(at * ROWS, ROWS), ROWS)
            key, value = made.k_rot[others, :], made.values[others, :]
            shape = (ROWS, ROWS)
            row_index = index * ROWS + lax.broadcasted_iota(jnp.int32, shape, 0)
            column_index = at * ROWS + lax.broadcasted_iota(jnp.int32, shape, 1)
            allowed = (segment == row_at(held.segments, at)) & (row_index >= column_index)
            after = []
            for which, query in enumerate(queries):
                peak, amount = carry[which]
                scores = jnp.where(allowed, right_transposed(query, key), MASKED)
                higher = jnp.maximum(peak, jnp.max(scores, axis=1, keepdims=True))
                weights = jnp.where(allowed, jnp.exp(scores - higher), 0.0)
                shrink = jnp.exp(peak - higher)
                amount = amount * shrink + jnp.sum(weights, axis=1, keepdims=True)
                sums_at[which] = sums_at[which] * shrink + matrix_product(
                    weights.astype(jnp.bfloat16), value
                )
                after.append((higher, amount))
            return tuple(after)

        first = (jnp.full((ROWS, 1), MASKED, jnp.float32), jnp.zeros((ROWS, 1), jnp.float32))
        final = lax.fori_loop(0, index + 1, inner, (first,) * heads)
        for which, (peak, amount) in enumerate(final):
            columns = pl.ds(which * head, head)
            made.attended[rows, columns] = (sums_at[which] / amount).astype(jnp.bfloat16)
            made.lse[which, rows, :] = peak + jnp.log(amount)
        part[rows, :] = matrix_product(made.attended[rows, :], made.w_o[...])
        exchange(0, index, part, other).start()

    row_loop(blocks, attend)
    leave(made.attended, made.lse)
    need(arrivals.w_gu, arrivals.a_gu, arrivals.b_gu, arrivals.w_d, arrivals.a_d, arrivals.b_d)
    for index, out in enumerate((made.w_g, made.w_u)):
        first = held.a_gu.at[:, pl.ds(index * rank, rank)]
        merge(out, held.w_gu.at[index], first, held.b_gu.at[index])
    merge(made.w_d, held.w_d, held.a_d, held.b_d)
    leave(made.w_g, made.w_u, made.w_d)
    need(arrivals.pa, arrivals.pf)
    hidden_columns = made.hidden.shape[1]

    def feed_forward(rows, index):
        exchange(0, index, part, other).wait_recv()
        attn = part[rows, :] + other[rows, :]
        made.attn[rows, :] = attn
        residual = held.tokens[rows, :].astype(jnp.float32) + attn * inverse_rms(attn) * held.pa[...]
        made.ff[rows, :] = (residual * inverse_rms(residual) * held.pf[...]).astype(jnp.bfloat16)

        def one_block(at, carry):
            for piece in range(4):
                start = pl.multiple_of((4 * at + piece) * ROWS, ROWS)
                columns = pl.ds(start, ROWS)
                entering = made.ff[rows, :]
                gate = matrix_product(entering, made.w_g[:, columns])
                up = matrix_product(entering, made.w_u[:, columns])
                bent = 0.5 * gate * (1.0 + jnp.tanh(GELU * gate * (1.0 + 0.044715 * gate * gate)))
                made.hidden[rows, columns] = (bent * up).astype(jnp.bfloat16)
            return carry

        lax.fori_loop(0, hidden_columns // ROWS // 4, one_block, 0)
        part_two[rows, :] = matrix_product(made.hidden[rows, :], made.w_d[...])
        exchange(1, index, part_two, other_two).start()

    row_loop(blocks, feed_forward)
    leave(made.attn, made.ff, made.hidden)

    def add_halves(rows, index):
        exchange(1, index, part_two, other_two).wait_recv()
        mlp = part_two[rows, :] + other_two[rows, :]
        made.mlp[rows, :] = mlp
        inverse = inverse_rms(mlp)
        normed = mlp * inverse
        incoming = held.cot[rows, :].astype(jnp.float32)
        add_gain(made.gain_pff, incoming * normed)
        made.gml[rows, :] = rms_back(incoming, held.pff[...], normed, inverse).astype(jnp.bfloat16)

    made.gain_pff[...] = jnp.zeros_like(made.gain_pff)
    need(arrivals.cot, arrivals.pff)
    row_loop(blocks, add_halves)
    leave(made.gml, made.gain_pff, made.mlp)
    for index in range(blocks):
        exchange(0, index, part, other).wait_send()
        exchange(1, index, part_two, other_two).wait_send()
    for move in leaving:
        move.wait()


def rotation_table(length, head):
    frequency = THETA ** (-np.arange(head // 2, dtype=np.float64) * 2.0 / head)
    positions = np.concatenate([np.arange(0, length, FINE), np.arange(FINE)])
    angles = positions.astype(np.float64)[:, None] * frequency[None, :]
    return jnp.asarray(np.concatenate([np.cos(angles), np.sin(angles)], axis=1).astype(np.float32))


def forward_pass(values):
    length, width = values.tokens.shape
    head = values.gq.shape[0]
    query_columns = values.w_q.shape[1]
    heads = query_columns // head
    hidden_columns = values.w_d.shape[0]
    rank = values.a_q.shape[1]
    low, full = jnp.bfloat16, jnp.float32
    shapes = ForwardOutputs(
        gml=((length, width), low),
        gain_pff=((8, width), full),
        mlp=((length, width), full),
        attn=((length, width), full),
        hidden=((length, hidden_columns), low),
        ff=((length, width), low),
        w_g=((width, hidden_columns), low),
        w_u=((width, hidden_columns), low),
        w_d=((hidden_columns, width), low),
        w_o=((query_columns, width), low),
        attended=((length, query_columns), low),
        q_rot=((length, query_columns), low),
        k_rot=((length, head), low),
        values=((length, head), low),
        lse=((heads, length, 1), full),
        cosine=((length, head // 2), full),
        sine=((length, head // 2), full),
        normed=((length, width), low),
        w_q=((width, query_columns), low),
        w_kv=((width, 2 * head), low),
    )
    sizes = values._replace(
        b_q=jax.ShapeDtypeStruct((rank, query_columns), low),
        a_o=jax.ShapeDtypeStruct((query_columns, rank), low),
        b_gu=jax.ShapeDtypeStruct((2, rank, hidden_columns), low),
        a_d=jax.ShapeDtypeStruct((hidden_columns, rank), low),
    )
    slots = 2 * (length // ROWS)
    results = pl.pallas_call(
        forward_kernel,
        out_shape=[jax.ShapeDtypeStruct(*shape) for shape in shapes],
        in_specs=[ANYWHERE] * len(values),
        out_specs=[ANYWHERE] * len(shapes),
        scratch_shapes=[pltpu.VMEM(array.shape, array.dtype) for array in sizes]
        + [pltpu.VMEM(*shape) for shape in shapes]
        + [pltpu.VMEM((length, width), full)] * 4
        + [
            pltpu.VMEM((heads, ROWS, head), full),
            pltpu.VMEM((length, head), full),
            pltpu.SemaphoreType.DMA((len(values),)),
            pltpu.SemaphoreType.DMA((slots,)),
            pltpu.SemaphoreType.DMA((slots,)),
            pltpu.SemaphoreType.DMA((len(shapes),)),
        ],
        compiler_params=pltpu.CompilerParams(
            collective_id=1, has_side_effects=True, vmem_limit_bytes=67043328
        ),
    )(*values)
    return ForwardOutputs(*results)


class Adapters(NamedTuple):
    down_a: object
    down_b: object
    gateup_a: object
    gateup_b: object
    output_a: object
    output_b: object
    query_a: object
    query_b: object
    keyvalue_a: object
    keyvalue_b: object


class DeriveInputs(NamedTuple):
    down_a: object
    down_b: object
    d: object
    gateup_a: object
    gateup_b: object
    g: object
    u: object
    output_a: object
    output_b: object
    o: object
    query_a: object
    query_b: object
    q: object
    keyvalue_a: object
    keyvalue_b: object
    k: object
    small: object
    result: object
    tokens: object


class DeriveOutputs(NamedTuple):
    down: object
    gateup: object
    output: object
    query: object
    keyvalue: object
    down_a: object
    down_b: object
    gateup_a: object
    gateup_b: object
    output_a: object
    output_b: object
    query_a: object
    query_b: object
    keyvalue_a: object
    keyvalue_b: object
    result: object
    tokens: object
    gain_in: object
    gain_pa: object
    gain_pf: object
    gain_pff: object
    gain_q: object
    gain_k: object


def derive_kernel(*refs):
    refs = list(refs)
    fields = len(DeriveInputs._fields)
    source = DeriveInputs(*refs[:fields])
    refs = refs[fields:]
    target = DeriveOutputs(*refs[: len(DeriveOutputs._fields)])
    refs = refs[len(target) :]
    held = DeriveInputs(*refs[:fields])
    refs = refs[fields:]
    made = Adapters(*refs[: len(Adapters._fields)])
    gains = refs[len(made) : len(made) + 6]
    rounded, loaded, stored = refs[len(made) + 6 :]
    core = lax.axis_index(TENSOR)
    arrivals = DeriveInputs(
        *(
            pltpu.make_async_copy(piece, home, loaded.at[index])
            for index, (piece, home) in enumerate(zip(source, held))
        )
    )
    for arrival in arrivals[:6]:
        arrival.start()
    behind = list(arrivals[6:])
    leaving = []

    def need(*copies):
        for copy in copies:
            copy.wait()
        for arrival in behind[:3]:
            arrival.start()
        del behind[:3]

    def leave(piece, home):
        move = pltpu.make_async_copy(piece, home, stored.at[len(leaving)])
        move.start()
        leaving.append(move)

    def factors(total, first, second, out_first, out_second, add_first=False, add_second=False):
        count, columns = total.shape
        step = 256 if count % 256 == 0 else 320

        def by_rows(index, carry):
            block = pl.ds(pl.multiple_of(index * step, 64), step)
            value = total[block, :].astype(jnp.bfloat16)
            rounded[block, :columns] = value
            product = right_transposed(value, second[...])
            out_first[block, :] = out_first[block, :] + product if add_first else product
            return carry

        lax.fori_loop(0, count // step, by_rows, 0)
        width = 256 if columns == 256 else columns // 2

        def by_columns(index, carry):
            block = pl.ds(pl.multiple_of(index * width, 128), width)
            product = left_transposed(first[...], rounded[:count, block])
            out_second[:, block] = out_second[:, block] + product if add_second else product
            return carry

        if width % 128 == 0:
            lax.fori_loop(0, columns // width, by_columns, 0)
        else:
            product = left_transposed(first[...], rounded[:count, :columns])
            out_second[...] = out_second[...] + product if add_second else product

    rank = made.query_a.shape[1]

    def columns_of(ref, part, size):
        return ref.at[:, pl.ds(part * size, size)]

    def rows_of(ref, part, size):
        return ref.at[pl.ds(part * size, size)]

    need(arrivals.down_a, arrivals.down_b, arrivals.d)
    leave(held.d.at[core], target.down)
    for group in range(2):
        total = held.d.at[group]
        size = total.shape[0]
        first = rows_of(held.down_a, group, size)
        out = rows_of(made.down_a, group, size)
        factors(total, first, held.down_b, out, made.down_b, False, group > 0)
    leave(made.down_a, target.down_a)
    leave(made.down_b, target.down_b)
    need(arrivals.gateup_a, arrivals.gateup_b)
    for part, name in enumerate((held.g, held.u)):
        need((arrivals.g, arrivals.u)[part])
        leave(name.at[core], target.gateup.at[part])
        for group in range(2):
            total = name.at[group]
            size = total.shape[1]
            second = columns_of(held.gateup_b.at[part], group, size)
            first = columns_of(held.gateup_a, part, rank)
            out_first = columns_of(made.gateup_a, part, rank)
            out_second = columns_of(made.gateup_b.at[part], group, size)
            factors(total, first, second, out_first, out_second, group > 0, False)
        leave(made.gateup_b.at[part], target.gateup_b.at[part])
    leave(made.gateup_a, target.gateup_a)
    need(arrivals.output_a, arrivals.output_b, arrivals.o)
    leave(held.o.at[core], target.output)
    for group in range(2):
        total = held.o.at[group]
        size = total.shape[0]
        first = rows_of(held.output_a, group, size)
        out = rows_of(made.output_a, group, size)
        factors(total, first, held.output_b, out, made.output_b, False, group > 0)
    leave(made.output_a, target.output_a)
    leave(made.output_b, target.output_b)
    need(arrivals.query_a, arrivals.query_b, arrivals.q)
    leave(held.q.at[core], target.query)
    for group in range(2):
        total = held.q.at[group]
        size = total.shape[1]
        second = columns_of(held.query_b, group, size)
        out = columns_of(made.query_b, group, size)
        factors(total, held.query_a, second, made.query_a, out, group > 0, False)
    leave(made.query_a, target.query_a)
    leave(made.query_b, target.query_b)
    need(arrivals.keyvalue_a, arrivals.keyvalue_b, arrivals.k)
    leave(held.k, target.keyvalue)
    for part in range(2):
        width = made.keyvalue_b.shape[2]
        total = columns_of(held.k, part, width)
        out = columns_of(made.keyvalue_a, part, rank)
        first = columns_of(held.keyvalue_a, part, rank)
        factors(total, first, held.keyvalue_b.at[part], out, made.keyvalue_b.at[part])
    leave(made.keyvalue_a, target.keyvalue_a)
    leave(made.keyvalue_b, target.keyvalue_b)
    need(arrivals.small, arrivals.result, arrivals.tokens)
    leave(held.result, target.result)
    leave(held.tokens, target.tokens)
    row = 0
    for gain, home in zip(gains, target[-6:]):
        for at in range(gain.shape[0] // 128):
            gain[pl.ds(at * 128, 128)] = held.small[row]
            row += 1
        leave(gain, home)
    for move in leaving:
        move.wait()


def derive_adapters(values, widths):
    made = [getattr(values, name) for name in Adapters._fields]
    shapes = [
        values.d.shape[1:],
        (2,) + values.g.shape[1:],
        values.o.shape[1:],
        values.q.shape[1:],
        values.k.shape,
    ]
    shapes += [array.shape for array in made]
    shapes += [values.result.shape, values.tokens.shape] + [(width,) for width in widths]
    kinds = [jnp.float32] * len(shapes)
    kinds[len(made) + 5] = values.result.dtype
    results = pl.pallas_call(
        derive_kernel,
        out_shape=[jax.ShapeDtypeStruct(*out) for out in zip(shapes, kinds)],
        in_specs=[ANYWHERE] * len(values),
        out_specs=[ANYWHERE] * len(shapes),
        scratch_shapes=[pltpu.VMEM(array.shape, array.dtype) for array in values]
        + [pltpu.VMEM(array.shape, jnp.float32) for array in made]
        + [pltpu.VMEM((width,), jnp.float32) for width in widths]
        + [
            pltpu.VMEM((values.d.shape[1], values.g.shape[2]), jnp.bfloat16),
            pltpu.SemaphoreType.DMA((len(values),)),
            pltpu.SemaphoreType.DMA((len(shapes) + 2,)),
        ],
        compiler_params=pltpu.CompilerParams(vmem_limit_bytes=67043328),
    )(*values)
    return DeriveOutputs(*results)


def on_device_general(
    tokens,
    document_numbers,
    input_norm_gain,
    after_attention_gain,
    before_feedforward_gain,
    after_feedforward_gain,
    query_norm_gain,
    key_norm_gain,
    query_weight,
    keyvalue_weight,
    output_weight,
    gateup_weight,
    down_weight,
    query_adapter_first,
    query_adapter_second,
    keyvalue_adapter_first,
    keyvalue_adapter_second,
    output_adapter_first,
    output_adapter_second,
    gateup_adapter_first,
    gateup_adapter_second,
    down_adapter_first,
    down_adapter_second,
    cotangent,
):
    inputs = tokens[0].astype(jnp.float32)
    segments = document_numbers[0]
    length = inputs.shape[0]
    head_width = keyvalue_adapter_second.shape[2]
    adapter_rank = query_adapter_first.shape[1]
    query_columns = query_weight.shape[1]
    hidden_columns = down_weight.shape[0]
    heads_local = query_columns // head_width
    group_position = lax.axis_index(TENSOR)
    query_piece = lax.dynamic_slice_in_dim(
        query_adapter_second, group_position * query_columns, query_columns, 1
    )
    output_rows = lax.dynamic_slice_in_dim(
        output_adapter_first, group_position * query_columns, query_columns, 0
    )
    gateup_piece = lax.dynamic_slice_in_dim(
        gateup_adapter_second, group_position * hidden_columns, hidden_columns, 2
    )
    down_rows = lax.dynamic_slice_in_dim(
        down_adapter_first, group_position * hidden_columns, hidden_columns, 0
    )
    query_merged = (
        query_weight.astype(jnp.float32) + matrix_product(query_adapter_first, query_piece)
    ).astype(jnp.bfloat16)
    keyvalue_merged = (
        keyvalue_weight.astype(jnp.float32)
        + jnp.concatenate(
            [
                matrix_product(keyvalue_adapter_first[:, :adapter_rank], keyvalue_adapter_second[0]),
                matrix_product(keyvalue_adapter_first[:, adapter_rank:], keyvalue_adapter_second[1]),
            ],
            axis=1,
        )
    ).astype(jnp.bfloat16)
    output_merged = (
        output_weight.astype(jnp.float32) + matrix_product(output_rows, output_adapter_second)
    ).astype(jnp.bfloat16)
    gate_merged = (
        gateup_weight[0].astype(jnp.float32)
        + matrix_product(gateup_adapter_first[:, :adapter_rank], gateup_piece[0])
    ).astype(jnp.bfloat16)
    up_merged = (
        gateup_weight[1].astype(jnp.float32)
        + matrix_product(gateup_adapter_first[:, adapter_rank:], gateup_piece[1])
    ).astype(jnp.bfloat16)
    down_merged = (
        down_weight.astype(jnp.float32) + matrix_product(down_rows, down_adapter_second)
    ).astype(jnp.bfloat16)
    positions = positions_of(segments)
    key_index = jnp.arange(length, dtype=jnp.int32)
    block_rows = min(512, length)
    normalized_rows, in_back = jax.vjp(rms_scale, inputs, input_norm_gain)
    normalized_lowrank = normalized_rows.astype(jnp.bfloat16)
    query_rows = matrix_product(normalized_lowrank, query_merged)
    keyvalue = matrix_product(normalized_lowrank, keyvalue_merged)

    def prepare(q_in, kv_in, q_scale, k_scale):
        q_heads = rms_scale(q_in.reshape(length, heads_local, head_width), q_scale)
        q_out = rotate(q_heads, positions) * head_width ** (-0.5)
        k_out = rotate(rms_scale(kv_in[:, :head_width], k_scale), positions)
        return (q_out, k_out, kv_in[:, head_width:])

    prepared, prepare_back = jax.vjp(prepare, query_rows, keyvalue, query_norm_gain, key_norm_gain)
    q_rot = prepared[0].astype(jnp.bfloat16)
    k_rot = prepared[1].astype(jnp.bfloat16)
    v_low = prepared[2].astype(jnp.bfloat16)

    def scores_of(row_start):
        rows = q_rot[row_start : row_start + block_rows]
        raw = jnp.einsum("qhd,kd->hqk", rows, k_rot, preferred_element_type=jnp.float32)
        row_index = row_start + jnp.arange(block_rows, dtype=jnp.int32)
        allowed = (segments[row_start : row_start + block_rows][:, None] == segments[None, :]) & (
            row_index[:, None] >= key_index[None, :]
        )
        return jnp.where(allowed[None], raw, MASKED)

    outputs = []
    log_totals = []
    for row_start in range(0, length, block_rows):
        scores = scores_of(row_start)
        row_peak = jnp.max(scores, axis=-1, keepdims=True)
        weights = jnp.exp(scores - row_peak)
        row_total = jnp.sum(weights, axis=-1, keepdims=True)
        log_totals.append(row_peak + jnp.log(row_total))
        probs_low = (weights / row_total).astype(jnp.bfloat16)
        outputs.append(
            jnp.einsum("hqk,kd->qhd", probs_low, v_low, preferred_element_type=jnp.float32)
        )
    attended_rows = (
        jnp.concatenate(outputs, axis=0).reshape(length, query_columns).astype(jnp.bfloat16)
    )
    attention_before = lax.psum(matrix_product(attended_rows, output_merged), TENSOR)
    attn_post, post_attn_back = jax.vjp(rms_scale, attention_before, after_attention_gain)
    residual = inputs + attn_post
    normed_ff, pre_ff_back = jax.vjp(rms_scale, residual, before_feedforward_gain)
    feedforward_lowrank = normed_ff.astype(jnp.bfloat16)
    gate_portion = matrix_product(feedforward_lowrank, gate_merged)
    up_portion = matrix_product(feedforward_lowrank, up_merged)
    hidden_full, activate_back = jax.vjp(activate, gate_portion, up_portion)
    hidden_activation = hidden_full.astype(jnp.bfloat16)
    feedforward_before = lax.psum(matrix_product(hidden_activation, down_merged), TENSOR)
    mlp_post, post_ff_back = jax.vjp(rms_scale, feedforward_before, after_feedforward_gain)
    result_value = (residual + mlp_post).astype(jnp.bfloat16)[None]
    grad_out = cotangent[0].astype(jnp.float32)
    grad_mlp_pre, gradient_after_feedforward = post_ff_back(grad_out)
    gradient_feedforward_lowrank = grad_mlp_pre.astype(jnp.bfloat16)
    gradient_down_weight = left_transposed(hidden_activation, gradient_feedforward_lowrank)
    grad_hidden = right_transposed(gradient_feedforward_lowrank, down_merged)
    grad_gate, grad_up = activate_back(grad_hidden)
    gate_lowrank = grad_gate.astype(jnp.bfloat16)
    up_lowrank = grad_up.astype(jnp.bfloat16)
    gradient_gateup_weight = jnp.stack(
        [
            left_transposed(feedforward_lowrank, gate_lowrank),
            left_transposed(feedforward_lowrank, up_lowrank),
        ]
    )
    grad_ff_part = right_transposed(gate_lowrank, gate_merged) + right_transposed(
        up_lowrank, up_merged
    )
    grad_normed_ff = lax.psum(grad_ff_part, TENSOR)
    grad_residual_ff, gradient_before_feedforward = pre_ff_back(grad_normed_ff)
    grad_residual = grad_out + grad_residual_ff
    grad_attn_pre, gradient_after_attention = post_attn_back(grad_residual)
    gradient_attention_lowrank = grad_attn_pre.astype(jnp.bfloat16)
    gradient_output_weight = left_transposed(attended_rows, gradient_attention_lowrank)
    grad_attended = right_transposed(gradient_attention_lowrank, output_merged).astype(jnp.bfloat16)
    grad_attended = grad_attended.reshape(length, heads_local, head_width)
    grad_q_blocks = []
    grad_k_rot = jnp.zeros((length, head_width), jnp.float32)
    grad_values = jnp.zeros((length, head_width), jnp.float32)
    for block_index, row_start in enumerate(range(0, length, block_rows)):
        scores = scores_of(row_start)
        probs = jnp.exp(scores - log_totals[block_index])
        grad_rows = grad_attended[row_start : row_start + block_rows]
        grad_probs = jnp.einsum("qhd,kd->hqk", grad_rows, v_low, preferred_element_type=jnp.float32)
        grad_scores = (
            probs * (grad_probs - jnp.sum(probs * grad_probs, axis=-1, keepdims=True))
        ).astype(jnp.bfloat16)
        grad_q_blocks.append(
            jnp.einsum("hqk,kd->qhd", grad_scores, k_rot, preferred_element_type=jnp.float32)
        )
        grad_k_rot = grad_k_rot + jnp.einsum(
            "hqk,qhd->kd",
            grad_scores,
            q_rot[row_start : row_start + block_rows],
            preferred_element_type=jnp.float32,
        )
        grad_values = grad_values + jnp.einsum(
            "hqk,qhd->kd", probs.astype(jnp.bfloat16), grad_rows, preferred_element_type=jnp.float32
        )
    grad_queries, grad_keyvalue, gradient_query_norm_gain, gradient_key_norm_gain = prepare_back(
        (jnp.concatenate(grad_q_blocks, axis=0), grad_k_rot, grad_values)
    )
    query_low = grad_queries.astype(jnp.bfloat16)
    keyvalue_gradient_lowrank = grad_keyvalue.astype(jnp.bfloat16)
    gradient_query_weight = left_transposed(normalized_lowrank, query_low)
    gradient_keyvalue_weight = left_transposed(normalized_lowrank, keyvalue_gradient_lowrank)
    grad_in_part = right_transposed(query_low, query_merged) + right_transposed(
        keyvalue_gradient_lowrank, keyvalue_merged
    )
    grad_normed = lax.psum(grad_in_part, TENSOR)
    grad_inputs_add, gradient_input_gain = in_back(grad_normed)
    gradient_token_input = (grad_residual + grad_inputs_add)[None]
    lead_mask = (group_position == 0).astype(jnp.float32)
    lead_in = gradient_input_gain * lead_mask
    lead_post_attn = gradient_after_attention * lead_mask
    lead_pre_ff = gradient_before_feedforward * lead_mask
    lead_post_ff = gradient_after_feedforward * lead_mask
    sum_w_query, sum_w_out, sum_w_gate_up, sum_w_down = lax.psum(
        (
            gradient_query_weight,
            gradient_output_weight,
            gradient_gateup_weight,
            gradient_down_weight,
        ),
        DP,
    )
    (
        sum_gain_in,
        sum_post_attn,
        sum_pre_ff,
        sum_post_ff,
        sum_query_gain,
        sum_key_gain,
        sum_w_keyvalue,
    ) = lax.psum(
        (
            lead_in,
            lead_post_attn,
            lead_pre_ff,
            lead_post_ff,
            gradient_query_norm_gain,
            gradient_key_norm_gain,
            gradient_keyvalue_weight,
        ),
        (DP, TENSOR),
    )
    rows_rows = ((0,), (0,))
    columns_columns = ((1,), (1,))
    sum_kv_b = jnp.stack(
        [
            exact_product(
                sum_w_keyvalue[:, i * head_width : (i + 1) * head_width],
                keyvalue_adapter_first[:, i * adapter_rank : (i + 1) * adapter_rank],
                rows_rows,
            ).T
            for i in range(2)
        ]
    )
    sum_kv_a = jnp.concatenate(
        [
            exact_product(
                sum_w_keyvalue[:, i * head_width : (i + 1) * head_width],
                keyvalue_adapter_second[i],
                columns_columns,
            )
            for i in range(2)
        ],
        axis=1,
    )
    part_q_b = exact_product(sum_w_query, query_adapter_first, rows_rows).T
    part_q_a = exact_product(sum_w_query, query_piece, columns_columns)
    part_o_a = exact_product(sum_w_out, output_adapter_second, columns_columns)
    part_o_b = exact_product(sum_w_out, output_rows, rows_rows).T
    part_gu_b = jnp.stack(
        [
            exact_product(
                sum_w_gate_up[i],
                gateup_adapter_first[:, i * adapter_rank : (i + 1) * adapter_rank],
                rows_rows,
            ).T
            for i in range(2)
        ]
    )
    part_gu_a = jnp.concatenate(
        [exact_product(sum_w_gate_up[i], gateup_piece[i], columns_columns) for i in range(2)],
        axis=1,
    )
    part_d_a = exact_product(sum_w_down, down_adapter_second, columns_columns)
    part_d_b = exact_product(sum_w_down, down_rows, rows_rows).T
    sum_q_a, sum_o_b, sum_gu_a, sum_d_b = lax.psum(
        (part_q_a, part_o_b, part_gu_a, part_d_b), TENSOR
    )
    sum_q_b = lax.all_gather(part_q_b, TENSOR, axis=1, tiled=True)
    sum_o_a = lax.all_gather(part_o_a, TENSOR, axis=0, tiled=True)
    sum_gu_b = lax.all_gather(part_gu_b, TENSOR, axis=2, tiled=True)
    sum_d_a = lax.all_gather(part_d_a, TENSOR, axis=0, tiled=True)
    return (
        result_value,
        gradient_token_input,
        sum_gain_in,
        sum_post_attn,
        sum_pre_ff,
        sum_post_ff,
        sum_query_gain,
        sum_key_gain,
        sum_w_query,
        sum_w_keyvalue,
        sum_w_out,
        sum_w_gate_up,
        sum_w_down,
        sum_q_a,
        sum_q_b,
        sum_kv_a,
        sum_kv_b,
        sum_o_a,
        sum_o_b,
        sum_gu_a,
        sum_gu_b,
        sum_d_a,
        sum_d_b,
    )


def on_device_fast(
    tokens,
    document_numbers,
    input_norm_gain,
    after_attention_gain,
    before_feedforward_gain,
    after_feedforward_gain,
    query_norm_gain,
    key_norm_gain,
    query_weight,
    keyvalue_weight,
    output_weight,
    gateup_weight,
    down_weight,
    query_adapter_first,
    query_adapter_second,
    keyvalue_adapter_first,
    keyvalue_adapter_second,
    output_adapter_first,
    output_adapter_second,
    gateup_adapter_first,
    gateup_adapter_second,
    down_adapter_first,
    down_adapter_second,
    cotangent,
):
    length = document_numbers.shape[1]
    head_width = keyvalue_adapter_second.shape[2]
    width = input_norm_gain.shape[0]
    ahead = forward_pass(
        ForwardInputs(
            tokens=tokens[0],
            gin=input_norm_gain,
            w_q=query_weight,
            a_q=query_adapter_first,
            b_q=query_adapter_second,
            w_kv=keyvalue_weight,
            a_kv=keyvalue_adapter_first,
            b_kv=keyvalue_adapter_second,
            table=rotation_table(length, head_width),
            segments=document_numbers,
            gq=query_norm_gain,
            gk=key_norm_gain,
            w_o=output_weight,
            a_o=output_adapter_first,
            b_o=output_adapter_second,
            pa=after_attention_gain,
            pf=before_feedforward_gain,
            w_gu=gateup_weight,
            a_gu=gateup_adapter_first,
            b_gu=gateup_adapter_second,
            w_d=down_weight,
            a_d=down_adapter_first,
            b_d=down_adapter_second,
            cot=cotangent[0],
            pff=after_feedforward_gain,
        )
    )
    shapes = Pieces(
        d=down_weight.shape,
        g=gateup_weight.shape[1:],
        u=gateup_weight.shape[1:],
        o=output_weight.shape,
        q=query_weight.shape,
        k=keyvalue_weight.shape,
        s=(32, 128),
    )
    values = BackwardInputs(
        tokens=tokens[0],
        cot=cotangent[0],
        pa=after_attention_gain,
        pff=after_feedforward_gain,
        pf=before_feedforward_gain,
        segments=document_numbers,
        gq=query_norm_gain,
        gk=key_norm_gain,
        gin=input_norm_gain,
        **ahead._asdict(),
    )
    (result, grad_tokens, sum_k, sum_s), both = backward_and_sums(values, shapes)
    sum_d, sum_g, sum_u, sum_o, sum_q = both
    derived = derive_adapters(
        DeriveInputs(
            down_a=down_adapter_first,
            down_b=down_adapter_second,
            d=sum_d,
            gateup_a=gateup_adapter_first,
            gateup_b=gateup_adapter_second,
            g=sum_g,
            u=sum_u,
            output_a=output_adapter_first,
            output_b=output_adapter_second,
            o=sum_o,
            query_a=query_adapter_first,
            query_b=query_adapter_second,
            q=sum_q,
            keyvalue_a=keyvalue_adapter_first,
            keyvalue_b=keyvalue_adapter_second,
            k=sum_k,
            small=sum_s,
            result=result,
            tokens=grad_tokens,
        ),
        (width,) * 4 + (head_width,) * 2,
    )
    return (
        derived.result[None],
        derived.tokens[None],
        derived.gain_in,
        derived.gain_pa,
        derived.gain_pf,
        derived.gain_pff,
        derived.gain_q,
        derived.gain_k,
        derived.query,
        derived.keyvalue,
        derived.output,
        derived.gateup,
        derived.down,
        derived.query_a,
        derived.query_b,
        derived.keyvalue_a,
        derived.keyvalue_b,
        derived.output_a,
        derived.output_b,
        derived.gateup_a,
        derived.gateup_b,
        derived.down_a,
        derived.down_b,
    )


def solution(mesh):
    in_specs = (
        P(DP, None, None),
        P(DP, None),
        P(),
        P(),
        P(),
        P(),
        P(),
        P(),
        P(None, TENSOR),
        P(),
        P(TENSOR, None),
        P(None, None, TENSOR),
        P(TENSOR, None),
        P(),
        P(),
        P(),
        P(),
        P(),
        P(),
        P(),
        P(),
        P(),
        P(),
        P(DP, None, None),
    )
    out_specs = (
        P(DP, None, None),
        P(DP, None, None),
        P(),
        P(),
        P(),
        P(),
        P(),
        P(),
        P(None, TENSOR),
        P(),
        P(TENSOR, None),
        P(None, None, TENSOR),
        P(TENSOR, None),
        P(),
        P(),
        P(),
        P(),
        P(),
        P(),
        P(),
        P(),
        P(),
        P(),
    )
    fast = mesh.shape[DP] == 16 and mesh.shape[TENSOR] == 2
    return jax.shard_map(
        on_device_fast if fast else on_device_general,
        mesh=mesh, in_specs=in_specs, out_specs=out_specs, check_vma=False
    )
```

```python
import functools
from typing import NamedTuple

import jax
import jax.numpy as jnp
import numpy as np
from jax import lax
from jax.experimental import pallas as pl
from jax.experimental.pallas import tpu as pltpu
from jax.sharding import PartitionSpec as P

EPS = 1e-06
THETA = 1000000.0
MASKED = -1e30
GELU = 0.7978845608028654
DP, TENSOR = "dp", "tensor"
ROWS = 256
MESH_ID = pl.DeviceIdType.MESH
ANYWHERE = pl.BlockSpec(memory_space=pl.ANY)


def matrix_product(left_side, right_side):
    return jnp.dot(left_side, right_side, preferred_element_type=jnp.float32)


def left_transposed(left_side, right_side):
    return lax.dot_general(
        left_side, right_side, (((0,), (0,)), ((), ())), preferred_element_type=jnp.float32
    )


def right_transposed(left_side, right_side):
    return lax.dot_general(
        left_side, right_side, (((1,), (1,)), ((), ())), preferred_element_type=jnp.float32
    )


def rms_scale(values, scale_gain):
    return values * lax.rsqrt(jnp.mean(values * values, axis=-1, keepdims=True) + EPS) * scale_gain


def positions_of(segments):
    length = segments.shape[0]
    indices = jnp.arange(length, dtype=jnp.int32)
    before = jnp.concatenate([jnp.full((1,), -1, jnp.int32), segments[:-1]])
    starts = lax.cummax(jnp.where(segments != before, indices, jnp.zeros_like(indices)), axis=0)
    return indices - starts


def rotate(values, positions):
    half_dim = values.shape[-1] // 2
    frequency = THETA ** (-jnp.arange(half_dim, dtype=jnp.float32) * 2.0 / values.shape[-1])
    angles = positions.astype(jnp.float32)[:, None] * frequency[None, :]
    cosine = jnp.cos(angles)
    sine_part = jnp.sin(angles)
    if values.ndim == 3:
        cosine = cosine[:, None, :]
        sine_part = sine_part[:, None, :]
    leading = values[..., :half_dim]
    trailing = values[..., half_dim:]
    return jnp.concatenate(
        [leading * cosine - trailing * sine_part, trailing * cosine + leading * sine_part], axis=-1
    )


def exact_product(left_side, right_side, contract):
    return lax.dot_general(
        left_side,
        right_side.astype(jnp.float32),
        (contract, ((), ())),
        precision=lax.Precision.HIGHEST,
        preferred_element_type=jnp.float32,
    )


def activate(gate_in, up_in):
    return jax.nn.gelu(gate_in, approximate=True) * up_in


class Place:
    def __init__(self):
        me = lax.axis_index(DP)
        core = lax.axis_index(TENSOR)
        bit_x = lax.rem(me, 2)
        bit_y = lax.rem(me // 2, 2)
        level = me // 4
        across_x = me + 1 - 2 * bit_x
        across_y = me + 2 - 4 * bit_y
        self.core = core
        self.side = level // 2
        self.level = level
        self.outer = jnp.logical_or(level == 0, level == 3)
        self.inner = jnp.logical_not(self.outer)
        self.bits = (jnp.where(core == 0, bit_x, bit_y), jnp.where(core == 0, bit_y, bit_x))
        self.across = (
            (jnp.where(core == 0, across_x, across_y), core),
            (jnp.where(core == 0, across_y, across_x), core),
        )
        column = lax.rem(me, 4)
        self.near = ((level + 1 - 2 * lax.rem(level, 2)) * 4 + column, core)
        self.middle = ((3 - level) * 4 + column, core)
        self.sibling = (me, 1 - core)


def add_rows(target, target_row, extra, extra_row, count):
    step = 32 if count % 32 == 0 else (16 if count % 16 == 0 else 8)

    def body(index, carry):
        rows = pl.ds(pl.multiple_of(target_row + index * step, 8), step)
        target[rows] = target[rows] + extra[pl.ds(pl.multiple_of(extra_row + index * step, 8), step)]
        return carry

    lax.fori_loop(0, count // step, body, 0)


class Sums:
    def __init__(self, place, sends, receives, freed):
        self.place = place
        self.sends = sends
        self.receives = receives
        self.freed = freed
        self.used = 0
        self.credits = 0

    def credit(self):
        self.credits += 1
        return self.freed.at[self.credits - 1]

    def slot(self):
        self.used += 1
        return self.used - 1

    def copy(self, source, target, device, slot=None):
        slot = self.slot() if slot is None else slot
        return pltpu.make_async_remote_copy(
            src_ref=source,
            dst_ref=target,
            send_sem=self.sends.at[slot],
            recv_sem=self.receives.at[slot],
            device_id=device,
            device_id_type=MESH_ID,
        )


def signal(semaphore, device):
    pl.semaphore_signal(semaphore, inc=1, device_id=device, device_id_type=MESH_ID)


def rows_at(ref, start, count):
    return ref.at[pl.ds(pl.multiple_of(start, 8), count)]


def plane_first(sums, total, row, count, landing, landing_row, finish, turned):
    place = sums.place
    half, quarter = count // 2, count // 4
    bit_one, bit_two = place.bits[turned], place.bits[1 - turned]
    one, two = place.across[turned], place.across[1 - turned]
    kept = row + bit_one * half
    given = row + (1 - bit_one) * half
    mine = kept + bit_two * quarter
    other = kept + (1 - bit_two) * quarter
    land_one = rows_at(landing, landing_row, half)
    land_two = rows_at(landing, landing_row + half, quarter)
    land_near = rows_at(landing, landing_row + half + quarter, quarter)
    land_mid = rows_at(landing, landing_row + 2 * half, quarter)
    ours = rows_at(total, mine, quarter)
    slot_one, slot_two, slot_near = sums.slot(), sums.slot(), sums.slot()
    copy_one = sums.copy(rows_at(total, given, half), land_one, one, slot_one)
    copy_two = sums.copy(rows_at(total, other, quarter), land_two, two, slot_two)
    copy_in = sums.copy(ours, land_near, place.near, slot_near)
    copy_mid = sums.copy(ours, land_mid, place.middle)
    copy_out = sums.copy(ours, ours, place.near, slot_near)
    back_two = sums.copy(ours, ours, two, slot_two)
    back_one = sums.copy(rows_at(total, kept, half), rows_at(total, kept, half), one, slot_one)

    free_one, free_two, free_in = sums.credit(), sums.credit(), sums.credit()

    def step0():
        copy_one.start()

    def step1():
        copy_one.wait_recv()
        add_rows(total, kept, landing, landing_row, half)
        copy_two.start()

    def step2():
        copy_two.wait_recv()
        add_rows(total, mine, landing, landing_row + half, quarter)

        @pl.when(place.outer)
        def _():
            copy_in.start()

        copy_one.wait_send()
        signal(free_one, one)

    def step3():
        @pl.when(place.inner)
        def _():
            copy_in.wait_recv()
            add_rows(total, mine, landing, landing_row + half + quarter, quarter)
            copy_mid.start()

        copy_two.wait_send()
        signal(free_two, two)

        @pl.when(place.outer)
        def _():
            copy_in.wait_send()
            signal(free_in, place.near)

    def step4():
        @pl.when(place.inner)
        def _():
            copy_mid.wait()
            add_rows(total, mine, landing, landing_row + 2 * half, quarter)
            pl.semaphore_wait(free_in, 1)
            copy_out.start()
            pl.semaphore_wait(free_two, 1)
            back_two.start()

    def step5():
        @pl.when(place.outer)
        def _():
            copy_out.wait_recv()
            pl.semaphore_wait(free_two, 1)
            back_two.start()

    def step6():
        back_two.wait_recv()
        pl.semaphore_wait(free_one, 1)
        back_one.start()

    def step7():
        back_one.wait_recv()
        back_two.wait_send()
        back_one.wait_send()

        @pl.when(place.inner)
        def _():
            copy_out.wait_send()

        finish()

    return [step0, step1, step2, step3, step4, step5, step6, step7]


def line_first(sums, total, row, count, landing, landing_row, finish, turned):
    place = sums.place
    one, two = place.across[turned], place.across[1 - turned]
    quarter = count // 4
    side = place.side
    three = row + (1 - side) * quarter
    far_pair = row + (1 - side) * 2 * quarter
    own_pair = row + side * 2 * quarter
    outer_quarter = row + 3 * side * quarter
    mine = row + place.level * quarter
    ours = rows_at(total, mine, quarter)
    land_three = rows_at(landing, landing_row, 3 * quarter)
    land_pair = rows_at(landing, landing_row + 3 * quarter, 2 * quarter)
    land_back = rows_at(landing, landing_row, quarter)
    land_one = rows_at(landing, landing_row + 5 * quarter, quarter)
    land_two = rows_at(landing, landing_row + 6 * quarter, quarter)
    slot_near, slot_middle, slot_spread = sums.slot(), sums.slot(), sums.slot()
    copy_three = sums.copy(rows_at(total, three, 3 * quarter), land_three, place.near, slot_near)
    copy_pair = sums.copy(
        rows_at(total, far_pair, 2 * quarter), land_pair, place.middle, slot_middle
    )
    outers = rows_at(total, outer_quarter, quarter)
    copy_back = sums.copy(outers, land_back, place.near, slot_near)
    copy_one = sums.copy(ours, land_one, one)
    copy_two = sums.copy(ours, land_two, two)
    spread_in = sums.copy(ours, ours, place.near, slot_spread)
    spread_out = sums.copy(ours, ours, place.near, slot_spread)
    spread_mid = sums.copy(ours, ours, place.middle, slot_middle)
    forward_mid = sums.copy(outers, outers, place.middle)
    far_rows = rows_at(total, far_pair, 2 * quarter)
    forward_out = sums.copy(far_rows, far_rows, place.near, slot_near)

    free_near, free_pair = sums.credit(), sums.credit()

    def step0():
        @pl.when(place.outer)
        def _():
            copy_three.start()

    def step1():
        @pl.when(place.inner)
        def _():
            copy_three.wait_recv()
            add_rows(total, three, landing, landing_row, 3 * quarter)
            copy_pair.start()

    def step2():
        @pl.when(place.inner)
        def _():
            copy_pair.wait_recv()
            add_rows(total, own_pair, landing, landing_row + 3 * quarter, 2 * quarter)
            copy_back.start()
            copy_one.start()

    def step3():
        @pl.when(place.outer)
        def _():
            copy_back.wait_recv()
            add_rows(total, mine, landing, landing_row, quarter)
            copy_one.start()
            copy_three.wait_send()
            signal(free_near, place.near)

        @pl.when(place.inner)
        def _():
            copy_pair.wait_send()
            signal(free_pair, place.middle)
            copy_back.wait_send()
            signal(free_near, place.near)

    def step4():
        copy_one.wait()
        add_rows(total, mine, landing, landing_row + 5 * quarter, quarter)
        copy_two.start()

    def step5():
        copy_two.wait()
        add_rows(total, mine, landing, landing_row + 6 * quarter, quarter)

        @pl.when(place.outer)
        def _():
            pl.semaphore_wait(free_near, 1)
            spread_in.start()

        @pl.when(place.inner)
        def _():
            pl.semaphore_wait(free_near, 1)
            spread_out.start()
            pl.semaphore_wait(free_pair, 1)
            spread_mid.start()

    def step6():
        @pl.when(place.inner)
        def _():
            spread_in.wait_recv()
            forward_mid.start()

    def step7():
        @pl.when(place.inner)
        def _():
            spread_mid.wait_recv()
            forward_mid.wait_recv()
            forward_out.start()

    def step8():
        @pl.when(place.outer)
        def _():
            spread_out.wait_recv()
            forward_out.wait_recv()
            spread_in.wait_send()

        @pl.when(place.inner)
        def _():
            spread_out.wait_send()
            spread_mid.wait_send()
            forward_mid.wait_send()
            forward_out.wait_send()

        finish()

    return [step0, step1, step2, step3, step4, step5, step6, step7, step8]


def greet(place):
    barrier = pltpu.get_barrier_semaphore()
    for device in (*place.across, place.near, place.sibling):
        pl.semaphore_signal(barrier, inc=1, device_id=device, device_id_type=MESH_ID)

    @pl.when(place.inner)
    def _():
        pl.semaphore_signal(barrier, inc=1, device_id=place.middle, device_id_type=MESH_ID)
        pl.semaphore_wait(barrier, 5)

    @pl.when(place.outer)
    def _():
        pl.semaphore_wait(barrier, 4)


class BackwardInputs(NamedTuple):
    gml: object
    hidden: object
    ff: object
    w_g: object
    w_u: object
    w_d: object
    mlp: object
    attn: object
    tokens: object
    cot: object
    pa: object
    pff: object
    pf: object
    w_o: object
    attended: object
    q_rot: object
    k_rot: object
    values: object
    segments: object
    lse: object
    cosine: object
    sine: object
    normed: object
    w_q: object
    gq: object
    w_kv: object
    gk: object
    gin: object
    gain_pff: object


class Pieces(NamedTuple):
    d: object
    g: object
    u: object
    o: object
    q: object
    k: object
    s: object


PIECE_K, PIECE_S = 5, 6
PARTS = ((0, None),)
PARTS += tuple((piece, block) for block in range(4) for piece in (1, 2))
PARTS += ((3, None), (4, 0), (4, 1), (5, None), (6, None))


class Work(NamedTuple):
    gate: object
    up: object
    part: object
    other: object
    dq: object
    gains: object
    gain_q: object
    gain_k: object
    result: object


def row_loop(count, body, start=0):
    def step(index, carry):
        body(pl.ds(pl.multiple_of(index * ROWS, ROWS), ROWS), index)
        return carry

    lax.fori_loop(start, count, step, 0)


def row_at(segments, index):
    columns = pl.ds(pl.multiple_of(index * ROWS, ROWS), ROWS)
    return segments[:, columns].astype(jnp.float32)


def column_of(row):
    shape = (row.shape[1], row.shape[1])
    diagonal = lax.broadcasted_iota(jnp.int32, shape, 0) == lax.broadcasted_iota(jnp.int32, shape, 1)
    return jnp.sum(jnp.where(diagonal, row, 0.0), axis=1, keepdims=True)


def inverse_rms(values):
    return lax.rsqrt(jnp.mean(values * values, axis=-1, keepdims=True) + EPS)


def rms_back(incoming, gain, normed, inverse):
    scaled = incoming * gain
    return inverse * (scaled - normed * jnp.mean(scaled * normed, axis=-1, keepdims=True))


def add_gain(target, terms):
    width = terms.shape[1]
    target[...] = target[...] + jnp.sum(terms.reshape(-1, 8, width), axis=0)


def gelu_parts(gate):
    inner = 0.7978845608028654 * gate * (1.0 + 0.044715 * gate * gate)
    bent = jnp.tanh(inner)
    half = 0.5 * (1.0 + bent)
    slope = half + 0.5 * gate * (1.0 - bent * bent) * 0.7978845608028654 * (
        1.0 + 0.134145 * gate * gate
    )
    return gate * half, slope


def turn_back(values, cosine, sine):
    half = values.shape[1] // 2
    leading, trailing = values[:, :half], values[:, half:]
    return jnp.concatenate(
        [leading * cosine + trailing * sine, trailing * cosine - leading * sine], axis=1
    )


def backward_kernel(setup, *refs):
    plan, order = setup
    refs = list(refs)
    source = BackwardInputs(*refs[: len(BackwardInputs._fields)])
    refs = refs[len(source) :]
    out_home, token_home, own_k, own_s = refs[:4]
    both = refs[4 : 4 + len(Pieces._fields) - 2]
    refs = refs[4 + len(both) :]
    held = BackwardInputs(*refs[: len(source)])
    refs = refs[len(source) :]
    total = Pieces(*refs[: len(Pieces._fields)])
    refs = refs[len(total) :]
    landing = refs[: len(PARTS)]
    refs = refs[len(PARTS) :]
    swapped_k, swapped_s = refs[:2]
    work = Work(*refs[2 : 2 + len(Work._fields)])
    loads, sends, receives, local, freed, handed = refs[2 + len(work) :]
    place = Place()
    core = place.core
    sums = Sums(place, sends, receives, freed)
    arrivals = BackwardInputs(
        *(
            pltpu.make_async_copy(piece, home, loads.at[index])
            for index, (piece, home) in enumerate(zip(source, held))
        )
    )
    for arrival in arrivals[:2]:
        arrival.start()
    greet(place)
    length = held.attn.shape[0]
    blocks = length // ROWS
    width = held.attn.shape[1]
    head = held.k_rot.shape[1]
    heads = held.q_rot.shape[1] // head
    hidden_columns = held.hidden.shape[1]
    here = set()

    def need(*copies):
        for copy in copies:
            if id(copy) not in here:
                here.add(id(copy))
                copy.wait()

    for gains in (work.gains, work.gain_q, work.gain_k):
        gains[...] = jnp.zeros_like(gains)
    gain_in, gain_pa, gain_pf = (work.gains.at[i] for i in range(3))
    low, part, other = held.gml, work.part, work.other
    leaving = []

    def residual_of(rows):
        attn = held.attn[rows, :]
        inverse = inverse_rms(attn)
        normed = attn * inverse
        return held.tokens[rows, :].astype(jnp.float32) + normed * held.pa[...], normed, inverse

    def down_gradient():
        need(arrivals.gml, arrivals.hidden)
        for arrival in arrivals[2:6]:
            arrival.start()

        def body(columns, _):
            total.d[columns, :] = left_transposed(held.hidden[:, columns], low[...])

        row_loop(hidden_columns // ROWS, body)

    def gate_block(index):
        def run():
            need(arrivals.ff, arrivals.w_g, arrivals.w_u, arrivals.w_d)
            if index == 0:
                for arrival in arrivals[6:]:
                    arrival.start()
            columns = pl.ds(index * ROWS, ROWS)

            def body(rows, _):
                entering = held.ff[rows, :]
                gate = matrix_product(entering, held.w_g[:, columns])
                up = matrix_product(entering, held.w_u[:, columns])
                incoming = right_transposed(low[rows, :], held.w_d[columns, :])
                bent, slope = gelu_parts(gate)
                grad_gate = (incoming * up * slope).astype(jnp.bfloat16)
                grad_up = (incoming * bent).astype(jnp.bfloat16)
                work.gate[rows, :] = grad_gate
                work.up[rows, :] = grad_up
                share = right_transposed(grad_gate, held.w_g[:, columns]) + right_transposed(
                    grad_up, held.w_u[:, columns]
                )
                part[rows, :] = share if index == 0 else part[rows, :] + share

            row_loop(blocks, body)
            total.g[:, columns] = left_transposed(held.ff[...], work.gate[...])
            total.u[:, columns] = left_transposed(held.ff[...], work.up[...])

        return run

    def part_copies():
        first = sums.used
        sums.used += blocks

        def copy(index):
            rows = pl.ds(pl.multiple_of(index * ROWS, ROWS), ROWS)
            return pltpu.make_async_remote_copy(
                src_ref=part.at[rows],
                dst_ref=other.at[rows],
                send_sem=sends.at[first + index],
                recv_sem=receives.at[first + index],
                device_id=place.sibling,
                device_id_type=MESH_ID,
            )

        return copy

    ff_copy, input_copy = part_copies(), part_copies()

    def send_parts(copy):
        row_loop(blocks, lambda rows, index: copy(index).start())

    def residual_back():
        need(arrivals.mlp, arrivals.attn, arrivals.tokens, arrivals.cot, arrivals.pa, arrivals.pff)
        need(arrivals.pf, arrivals.w_o)
        def take_rows(rows, index):
            ff_copy(index).wait_recv()
            residual, normed_attn, inverse_attn = residual_of(rows)
            mlp = held.mlp[rows, :]
            ending = residual + mlp * inverse_rms(mlp) * held.pff[...]
            work.result[rows, :] = ending.astype(jnp.bfloat16)
            incoming = part[rows, :] + other[rows, :]
            inverse = inverse_rms(residual)
            normed = residual * inverse
            add_gain(gain_pf, incoming * normed)
            grad = held.cot[rows, :].astype(jnp.float32) + rms_back(
                incoming, held.pf[...], normed, inverse
            )
            held.mlp[rows, :] = grad
            add_gain(gain_pa, grad * normed_attn)
            low[rows, :] = rms_back(grad, held.pa[...], normed_attn, inverse_attn).astype(
                jnp.bfloat16
            )

        row_loop(blocks, take_rows)
        move = pltpu.make_async_copy(work.result, out_home, local.at[0])
        move.start()
        leaving.append(move)
        row_loop(blocks, lambda rows, index: ff_copy(index).wait_send())
        signal(handed, place.sibling)
        grad_attended = held.ff

        def body(rows, _):
            grad_attended[rows, : heads * head] = right_transposed(
                low[rows, :], held.w_o[...]
            ).astype(jnp.bfloat16)

        row_loop(blocks, body)

    def output_gradient():
        need(arrivals.attended)

        def body(columns, _):
            total.o[columns, :] = left_transposed(held.attended[:, columns], low[...])

        row_loop(heads * head // ROWS, body)

    grad_key = held.attn.at[:, :head]
    grad_value = held.attn.at[:, head : 2 * head]
    grad_query_low = held.hidden.at[:, : heads * head]
    grad_keyvalue_low = held.hidden.at[:, heads * head : heads * head + 2 * head]

    def attention_rows(which, start, stop):
        def run():
            need(arrivals.q_rot, arrivals.k_rot, arrivals.values, arrivals.segments, arrivals.lse, arrivals.cosine, arrivals.sine, arrivals.normed, arrivals.w_q)
            need(arrivals.gq)
            columns = pl.ds(which * head, head)
            if which == 0 and start == 0:
                held.attn[...] = jnp.zeros_like(held.attn)

            def body(rows, index):
                query = held.q_rot[rows, columns]
                grad = held.ff[rows, columns]
                attended = held.attended[rows, columns]
                weight = jnp.sum(
                    grad.astype(jnp.float32) * attended.astype(jnp.float32), axis=1, keepdims=True
                )
                lse = held.lse[which, rows, :]
                segment = column_of(row_at(held.segments, index))
                work.dq[...] = jnp.zeros_like(work.dq)

                def inner(at, carry):
                    others = pl.ds(pl.multiple_of(at * ROWS, ROWS), ROWS)
                    key = held.k_rot[others, :]
                    value = held.values[others, :]
                    scores = right_transposed(query, key)
                    row_index = index * ROWS + lax.broadcasted_iota(jnp.int32, scores.shape, 0)
                    column_index = at * ROWS + lax.broadcasted_iota(jnp.int32, scores.shape, 1)
                    allowed = (segment == row_at(held.segments, at)) & (row_index >= column_index)
                    probs = jnp.where(allowed, jnp.exp(scores - lse), 0.0)
                    grad_probs = right_transposed(grad, value)
                    grad_scores = (probs * (grad_probs - weight)).astype(jnp.bfloat16)
                    work.dq[...] += matrix_product(grad_scores, key)
                    grad_key[others, :] = grad_key[others, :] + left_transposed(grad_scores, query)
                    grad_value[others, :] = grad_value[others, :] + left_transposed(
                        probs.astype(jnp.bfloat16), grad
                    )
                    return carry

                lax.fori_loop(0, index + 1, inner, 0)
                turned = turn_back(work.dq[...], held.cosine[rows, :], held.sine[rows, :])
                turned = turned * head ** (-0.5)
                raw = matrix_product(held.normed[rows, :], held.w_q[:, columns])
                inverse = inverse_rms(raw)
                normed = raw * inverse
                add_gain(work.gain_q, turned * normed)
                grad_query_low[rows, columns] = rms_back(
                    turned, held.gq[...], normed, inverse
                ).astype(jnp.bfloat16)

            row_loop(stop, body, start)

        return run

    def key_back():
        need(arrivals.w_kv, arrivals.gk)

        def body(rows, _):
            turned = turn_back(grad_key[rows, :], held.cosine[rows, :], held.sine[rows, :])
            raw = matrix_product(held.normed[rows, :], held.w_kv[:, :head])
            inverse = inverse_rms(raw)
            normed = raw * inverse
            add_gain(work.gain_k, turned * normed)
            grad_keyvalue_low[rows, :head] = rms_back(
                turned, held.gk[...], normed, inverse
            ).astype(jnp.bfloat16)
            grad_keyvalue_low[rows, head:] = grad_value[rows, :].astype(jnp.bfloat16)

        row_loop(blocks, body)

    def query_gradient(which):
        columns = pl.ds(which * head, head)
        total.q[:, columns] = left_transposed(held.normed[...], grad_query_low[:, columns])

    half_rows = swapped_k.shape[0]
    swap_k, swap_s = [], []

    def keyvalue_gradient():
        for index in range(2 * head // ROWS):
            columns = pl.ds(index * ROWS, ROWS)
            total.k[:, columns] = left_transposed(
                held.normed[...], grad_keyvalue_low[:, columns]
            )
        copy = sums.copy(
            rows_at(total.k, (1 - core) * half_rows, half_rows), swapped_k, place.sibling
        )
        copy.start()
        swap_k.append(copy)

    def input_parts():
        def body(rows, _):
            part[rows, :] = right_transposed(
                grad_query_low[rows, :], held.w_q[...]
            ) + right_transposed(grad_keyvalue_low[rows, :], held.w_kv[...])

        row_loop(blocks, body)
        pl.semaphore_wait(handed, 1)
        send_parts(input_copy)

    def input_back():
        need(arrivals.gin, arrivals.gain_pff)
        def take_rows(rows, index):
            input_copy(index).wait_recv()
            incoming = part[rows, :] + other[rows, :]
            tokens = held.tokens[rows, :].astype(jnp.float32)
            inverse = inverse_rms(tokens)
            normed = tokens * inverse
            add_gain(gain_in, incoming * normed)
            held.mlp[rows, :] = held.mlp[rows, :] + rms_back(
                incoming, held.gin[...], normed, inverse
            )

        row_loop(blocks, take_rows)
        move = pltpu.make_async_copy(held.mlp, token_home, local.at[1])
        move.start()
        leaving.append(move)
        row_loop(blocks, lambda rows, index: input_copy(index).wait_send())
        small = total.s
        small[...] = jnp.zeros_like(small)
        lead = jnp.where(core == 0, 1.0, 0.0)
        row = 0
        for index in range(4):
            rows = work.gains[index] if index < 3 else held.gain_pff[...]
            vector = jnp.sum(rows, axis=0, keepdims=True) * lead
            for at in range(width // 128):
                small[row : row + 1, :] = vector[:, at * 128 : (at + 1) * 128]
                row += 1
        for gains in (work.gain_q, work.gain_k):
            vector = jnp.sum(gains[...], axis=0, keepdims=True)
            for at in range(head // 128):
                small[row : row + 1, :] = vector[:, at * 128 : (at + 1) * 128]
                row += 1
        copy = sums.copy(small, swapped_s, place.sibling)
        copy.start()
        swap_s.append(copy)

    tasks = (
        down_gradient,
        gate_block(0),
        gate_block(1),
        gate_block(2),
        lambda: (gate_block(3)(), send_parts(ff_copy)),
        residual_back,
        output_gradient,
        attention_rows(0, 0, 3),
        attention_rows(0, 3, 4),
        lambda: query_gradient(0),
        attention_rows(1, 0, 3),
        attention_rows(1, 3, 4),
        lambda: query_gradient(1),
        key_back,
        keyvalue_gradient,
        input_parts,
        input_back,
    )
    chunks = []
    slots = 2
    for (piece, block), land, parts in zip(PARTS, landing, plan):
        columns = slice(None) if block is None else pl.ds(block * ROWS, ROWS)
        summed = total[piece] if block is None else total[piece].at[:, columns]
        row = 0
        land_row = 0
        base = core * half_rows if piece == PIECE_K else 0
        for line, count, turned in parts:

            def finish(
                piece=piece,
                columns=columns,
                summed=summed,
                row=row,
                base=base,
                count=count,
                slot=slots,
            ):
                done = rows_at(summed, base + row, count)
                if piece == PIECE_S:
                    moves = [pltpu.make_async_copy(done, own_s, local.at[slot])]
                else:
                    if piece == PIECE_K:
                        home = rows_at(own_k, base + row, count)
                    else:
                        home = both[piece].at[core, pl.ds(row, count), columns]
                    moves = [
                        pltpu.make_async_copy(done, home, local.at[slot]),
                        sums.copy(done, home, place.sibling),
                    ]
                for move in moves:
                    move.start()
                leaving.extend(moves)

            build = line_first if line else plane_first
            steps = build(sums, summed, base + row, count, land, land_row, finish, turned)
            if piece >= PIECE_K:
                swap, landed = (swap_k, swapped_k) if piece == PIECE_K else (swap_s, swapped_s)

                def enter(swap=swap, landed=landed, out=total[piece], base=base, first=steps[0]):
                    if swap:
                        swap.pop().wait()
                        add_rows(out, base, landed, 0, landed.shape[0])
                    first()

                steps = [enter] + steps[1:]
            chunks.append(steps)
            slots += 1
            row += count
            land_row += landing_rows(line, count)
    for entry in order:
        if entry < 0:
            tasks[-1 - entry]()
        else:
            chunks[entry // 10][entry % 10]()
    for move in leaving:
        move.wait()


def backward_and_sums(values, shapes):
    length, width = values.tokens.shape
    head = values.k_rot.shape[1]
    full, low = jnp.float32, jnp.bfloat16
    outs = [((length, width), low), ((length, width), full), (shapes.k, full), (shapes.s, full)]
    outs += [((2,) + shape, full) for shape in shapes[:PIECE_K]]
    scratch = [pltpu.VMEM(array.shape, array.dtype) for array in values]
    scratch += [pltpu.VMEM(shape, full) for shape in shapes]
    for (piece, block), parts in zip(PARTS, CUTS):
        columns = shapes[piece][1] if block is None else ROWS
        rows = sum(landing_rows(line, count) for line, count, _ in parts)
        scratch.append(pltpu.VMEM((rows, columns), full))
    scratch += [pltpu.VMEM((shapes.k[0] // 2, shapes.k[1]), full), pltpu.VMEM(shapes.s, full)]
    scratch += Work(
        gate=pltpu.VMEM((length, ROWS), low),
        up=pltpu.VMEM((length, ROWS), low),
        part=pltpu.VMEM((length, width), full),
        other=pltpu.VMEM((length, width), full),
        dq=pltpu.VMEM((ROWS, head), full),
        gains=pltpu.VMEM((3, 8, width), full),
        gain_q=pltpu.VMEM((8, head), full),
        gain_k=pltpu.VMEM((8, head), full),
        result=pltpu.VMEM((length, width), low),
    )
    kinds = [line for parts in CUTS for line, _, _ in parts]
    count = len(kinds)
    blocks = length // ROWS
    slots = 2 * blocks + 2 + count + sum(6 if line else 4 for line in kinds)
    scratch += [
        pltpu.SemaphoreType.DMA((len(values),)),
        pltpu.SemaphoreType.DMA((slots,)),
        pltpu.SemaphoreType.DMA((slots,)),
        pltpu.SemaphoreType.DMA((count + 2,)),
        pltpu.SemaphoreType.REGULAR((sum(2 if line else 3 for line in kinds),)),
        pltpu.SemaphoreType.REGULAR,
    ]
    results = pl.pallas_call(
        functools.partial(backward_kernel, (CUTS, ORDER)),
        out_shape=[jax.ShapeDtypeStruct(*out) for out in outs],
        in_specs=[ANYWHERE] * len(values),
        out_specs=[ANYWHERE] * len(outs),
        scratch_shapes=scratch,
        compiler_params=pltpu.CompilerParams(
            collective_id=0, has_side_effects=True, vmem_limit_bytes=67043328
        ),
    )(*values)
    return results[:4], results[4:]


CUTS = (
    ((0, 64, 1), (1, 224, 0), (0, 480, 0), (1, 256, 1),),
    ((0, 96, 1), (0, 544, 1),),
    ((0, 640, 0),),
    ((0, 640, 1),),
    ((0, 96, 1), (0, 544, 0),),
    ((0, 32, 1), (1, 576, 1), (0, 32, 1),),
    ((0, 64, 0), (0, 576, 1),),
    ((0, 640, 0),),
    ((0, 32, 0), (0, 288, 1), (1, 320, 0),),
    ((1, 160, 1), (0, 160, 0), (0, 32, 1), (0, 160, 1),),
    ((0, 224, 0), (0, 416, 1),),
    ((0, 640, 0),),
    ((1, 224, 1), (0, 96, 1),),
    ((0, 32, 0),),
)
ORDER = (
    -1, 20, 30, 0, -2, 50, 60, -3, 10, 70, 90, -4, 21, 110, 51, 31, -5, 140, 11, 150, -6, 22, 61,
    40, 32, 130, -7, 200, 111, 170, 71, 180, -8, 141, 23, 62, 33, 112, 210, 220, 12, -9, 160, 72,
    190, 181, 171, -10, 80, 34, 113, 24, 142, 63, 151, 230, 13, 91, 73, 182, -11, 35, 41, 114,
    221, 25, 191, 131, 1, 74, -12, 143, 52, 183, 115, 161, 240, -13, 172, 250, 211, 2, 64, 42, 53,
    92, 192, 75, -14, 116, 201, 231, 152, 100, 144, 241, 65, -15, 120, 54, 222, 173, 270, 3, 81,
    260, 117, 14, 145, 93, 251, 212, 184, 153, 76, 121, 55, 174, 223, 232, 4, 66, 94, -16, 15,
    122, 132, 154, 261, 271, -17, 101, 280, 26, 43, 82, 16, 133, 213, 224, 193, 281, 272, 242,
    202, 185, 95, 273, 194, 102, 162, 262, 56, 5, 17, 175, 203, 233, 243, 123, 274, 204, 163, 263,
    103, 252, 146, 282, 186, 214, 134, 225, 96, 253, 44, 234, 164, 283, 83, 155, 18, 244, 205,
    124, 104, 264, 165, 36, 215, 226, 195, 57, 45, 284, 125, 254, 67, 275, 156, 84, 285, 196, 135,
    105, 245, 176, 37, 6, 197, 265, 136, 255, 106, 85, 286, 266, 206, 118, 27, 77, 235, 287, 276,
    166, 216, 187, 256, 46, 86, 126, 157, 167, 207, 227, 246, 198, 267, 147, 7, 177, 217, 97, 277,
    137, 47, 236, 107, 188, 87, 257, 127, 247, 38, 268, 237,
)


def landing_rows(line, count):
    return count // 4 * (7 if line else 5)


FINE = 32


class ForwardInputs(NamedTuple):
    tokens: object
    gin: object
    w_q: object
    a_q: object
    b_q: object
    w_kv: object
    a_kv: object
    b_kv: object
    table: object
    segments: object
    gq: object
    gk: object
    w_o: object
    a_o: object
    b_o: object
    pa: object
    pf: object
    w_gu: object
    a_gu: object
    b_gu: object
    w_d: object
    a_d: object
    b_d: object
    cot: object
    pff: object


class ForwardOutputs(NamedTuple):
    gml: object
    gain_pff: object
    mlp: object
    attn: object
    hidden: object
    ff: object
    w_g: object
    w_u: object
    w_d: object
    w_o: object
    attended: object
    q_rot: object
    k_rot: object
    values: object
    lse: object
    cosine: object
    sine: object
    normed: object
    w_q: object
    w_kv: object


def turn(values, cosine, sine):
    half = values.shape[1] // 2
    leading, trailing = values[:, :half], values[:, half:]
    return jnp.concatenate(
        [leading * cosine - trailing * sine, trailing * cosine + leading * sine], axis=1
    )


def forward_kernel(*refs):
    refs = list(refs)
    source = ForwardInputs(*refs[: len(ForwardInputs._fields)])
    refs = refs[len(source) :]
    target = ForwardOutputs(*refs[: len(ForwardOutputs._fields)])
    refs = refs[len(target) :]
    held = ForwardInputs(*refs[: len(source)])
    refs = refs[len(source) :]
    made = ForwardOutputs(*refs[: len(target)])
    part, other, part_two, other_two, sums_at, rotation = refs[len(target) : len(target) + 6]
    loads, sends, receives, stores = refs[len(target) + 6 :]
    me = lax.axis_index(DP)
    core = lax.axis_index(TENSOR)
    sibling = (me, 1 - core)

    def own_part(ref, home, axis):
        size = home.shape[axis]
        span = pl.ds(pl.multiple_of(core * size, 256), size)
        index = [slice(None)] * len(home.shape)
        index[axis] = span
        return ref.at[tuple(index)]

    pieces = source._replace(
        b_q=own_part(source.b_q, held.b_q, 1),
        a_o=own_part(source.a_o, held.a_o, 0),
        b_gu=own_part(source.b_gu, held.b_gu, 2),
        a_d=own_part(source.a_d, held.a_d, 0),
    )
    arrivals = ForwardInputs(
        *(
            pltpu.make_async_copy(piece, home, loads.at[index])
            for index, (piece, home) in enumerate(zip(pieces, held))
        )
    )
    for arrival in arrivals[:8]:
        arrival.start()
    barrier = pltpu.get_barrier_semaphore()
    signal(barrier, sibling)
    pl.semaphore_wait(barrier, 1)
    leaving = []
    homes = {id(ref): (index, home) for index, (ref, home) in enumerate(zip(made, target))}

    def leave(*arrays):
        for ref in arrays:
            index, home = homes[id(ref)]
            move = pltpu.make_async_copy(ref, home, stores.at[index])
            move.start()
            leaving.append(move)

    def need(*copies):
        for copy in copies:
            copy.wait()

    length, width = held.tokens.shape
    blocks = length // ROWS
    head = held.gq.shape[0]
    heads = held.w_q.shape[1] // head
    rank = held.a_q.shape[1]

    def merge(out, weight, first, second):
        count = weight.shape[0]
        step = 256 if count % 256 == 0 else 320

        def body(index, carry):
            rows = pl.ds(pl.multiple_of(index * step, 64), step)
            out[rows, :] = (
                weight[rows, :].astype(jnp.float32) + matrix_product(first[rows, :], second[...])
            ).astype(jnp.bfloat16)
            return carry

        lax.fori_loop(0, count // step, body, 0)

    need(arrivals.tokens, arrivals.gin, arrivals.w_q, arrivals.a_q, arrivals.b_q)
    for arrival in arrivals[8:]:
        arrival.start()
    merge(made.w_q, held.w_q, held.a_q, held.b_q)
    need(arrivals.w_kv, arrivals.a_kv, arrivals.b_kv)
    for index in range(2):
        columns = pl.ds(index * head, head)
        merge(
            made.w_kv.at[:, columns],
            held.w_kv.at[:, columns],
            held.a_kv.at[:, pl.ds(index * rank, rank)],
            held.b_kv.at[index],
        )
    leave(made.w_q, made.w_kv)
    need(arrivals.table, arrivals.segments, arrivals.gq, arrivals.gk)
    before = jnp.zeros((8, 1), jnp.float32)
    number = lax.broadcasted_iota(jnp.int32, (8, ROWS), 0).astype(jnp.float32)
    for index in range(blocks):
        fewer = jnp.where(row_at(held.segments, index) < number, 1.0, 0.0)
        before = before + jnp.sum(fewer, axis=1, keepdims=True)
    at_token = lax.broadcasted_iota(jnp.int32, (8, length), 1).astype(jnp.float32)
    chosen = jnp.where(at_token == before, 1.0, 0.0)
    half = head // 2
    coarse = length // FINE

    def fill(index, carry):
        rows = pl.ds(pl.multiple_of(index * FINE, FINE), FINE)
        step = held.table[pl.ds(index, 1), :]
        step_cosine, step_sine = step[:, :half], step[:, half:]
        fine = held.table[coarse : coarse + FINE, :]
        fine_cosine, fine_sine = fine[:, :half], fine[:, half:]
        rotation[rows, :half] = fine_cosine * step_cosine - fine_sine * step_sine
        rotation[rows, half:] = fine_sine * step_cosine + fine_cosine * step_sine
        return carry

    lax.fori_loop(0, coarse, fill, 0)
    starts = jnp.dot(
        chosen, rotation[...], precision=lax.Precision.HIGHEST, preferred_element_type=jnp.float32
    )

    def project(rows, index):
        tokens = held.tokens[rows, :].astype(jnp.float32)
        normed = (tokens * inverse_rms(tokens) * held.gin[...]).astype(jnp.bfloat16)
        made.normed[rows, :] = normed
        segment = column_of(row_at(held.segments, index))
        start = starts[3:4, :]
        for document in (2, 1, 0):
            start = jnp.where(segment == document, starts[document : document + 1, :], start)
        start_cosine, start_sine = start[:, :half], start[:, half:]
        here = rotation[rows, :]
        here_cosine, here_sine = here[:, :half], here[:, half:]
        cosine = here_cosine * start_cosine + here_sine * start_sine
        sine = here_sine * start_cosine - here_cosine * start_sine
        made.cosine[rows, :] = cosine
        made.sine[rows, :] = sine
        for at in range(heads):
            columns = pl.ds(at * head, head)
            raw = matrix_product(normed, made.w_q[:, columns])
            query = turn(raw * inverse_rms(raw) * held.gq[...], cosine, sine) * head ** (-0.5)
            made.q_rot[rows, columns] = query.astype(jnp.bfloat16)
        raw = matrix_product(normed, made.w_kv[:, :head])
        key = turn(raw * inverse_rms(raw) * held.gk[...], cosine, sine)
        made.k_rot[rows, :] = key.astype(jnp.bfloat16)
        made.values[rows, :] = matrix_product(normed, made.w_kv[:, head:]).astype(jnp.bfloat16)

    row_loop(blocks, project)
    leave(made.normed, made.cosine, made.sine, made.q_rot, made.k_rot, made.values)
    need(arrivals.w_o, arrivals.a_o, arrivals.b_o)
    merge(made.w_o, held.w_o, held.a_o, held.b_o)
    leave(made.w_o)

    def exchange(key, index, mine, theirs):
        rows = pl.ds(pl.multiple_of(index * ROWS, ROWS), ROWS)
        slot = key * blocks + index
        return pltpu.make_async_remote_copy(
            src_ref=mine.at[rows],
            dst_ref=theirs.at[rows],
            send_sem=sends.at[slot],
            recv_sem=receives.at[slot],
            device_id=sibling,
            device_id_type=MESH_ID,
        )

    def attend(rows, index):
        segment = column_of(row_at(held.segments, index))

        queries = [made.q_rot[rows, at * head : (at + 1) * head] for at in range(heads)]
        sums_at[...] = jnp.zeros_like(sums_at)

        def inner(at, carry):
            others = pl.ds(pl.multiple_of(at * ROWS, ROWS), ROWS)
            key, value = made.k_rot[others, :], made.values[others, :]
            shape = (ROWS, ROWS)
            row_index = index * ROWS + lax.broadcasted_iota(jnp.int32, shape, 0)
            column_index = at * ROWS + lax.broadcasted_iota(jnp.int32, shape, 1)
            allowed = (segment == row_at(held.segments, at)) & (row_index >= column_index)
            after = []
            for which, query in enumerate(queries):
                peak, amount = carry[which]
                scores = jnp.where(allowed, right_transposed(query, key), MASKED)
                higher = jnp.maximum(peak, jnp.max(scores, axis=1, keepdims=True))
                weights = jnp.exp(scores - higher)
                shrink = jnp.exp(peak - higher)
                amount = amount * shrink + jnp.sum(weights, axis=1, keepdims=True)
                sums_at[which] = sums_at[which] * shrink + matrix_product(
                    weights.astype(jnp.bfloat16), value
                )
                after.append((higher, amount))
            return tuple(after)

        first = (jnp.full((ROWS, 1), MASKED, jnp.float32), jnp.zeros((ROWS, 1), jnp.float32))
        final = lax.fori_loop(0, index + 1, inner, (first,) * heads)
        for which, (peak, amount) in enumerate(final):
            columns = pl.ds(which * head, head)
            made.attended[rows, columns] = (sums_at[which] / amount).astype(jnp.bfloat16)
            made.lse[which, rows, :] = peak + jnp.log(amount)
        part[rows, :] = matrix_product(made.attended[rows, :], made.w_o[...])
        exchange(0, index, part, other).start()

    row_loop(blocks, attend)
    leave(made.attended, made.lse)
    need(arrivals.w_gu, arrivals.a_gu, arrivals.b_gu, arrivals.w_d, arrivals.a_d, arrivals.b_d)
    for index, out in enumerate((made.w_g, made.w_u)):
        first = held.a_gu.at[:, pl.ds(index * rank, rank)]
        merge(out, held.w_gu.at[index], first, held.b_gu.at[index])
    merge(made.w_d, held.w_d, held.a_d, held.b_d)
    leave(made.w_g, made.w_u, made.w_d)
    need(arrivals.pa, arrivals.pf)
    hidden_columns = made.hidden.shape[1]

    def feed_forward(rows, index):
        exchange(0, index, part, other).wait_recv()
        attn = part[rows, :] + other[rows, :]
        made.attn[rows, :] = attn
        residual = held.tokens[rows, :].astype(jnp.float32) + attn * inverse_rms(attn) * held.pa[...]
        made.ff[rows, :] = (residual * inverse_rms(residual) * held.pf[...]).astype(jnp.bfloat16)

        def one_block(at, carry):
            for piece in range(4):
                start = pl.multiple_of((4 * at + piece) * ROWS, ROWS)
                columns = pl.ds(start, ROWS)
                entering = made.ff[rows, :]
                gate = matrix_product(entering, made.w_g[:, columns])
                up = matrix_product(entering, made.w_u[:, columns])
                bent = 0.5 * gate * (1.0 + jnp.tanh(GELU * gate * (1.0 + 0.044715 * gate * gate)))
                made.hidden[rows, columns] = (bent * up).astype(jnp.bfloat16)
            return carry

        lax.fori_loop(0, hidden_columns // ROWS // 4, one_block, 0)
        part_two[rows, :] = matrix_product(made.hidden[rows, :], made.w_d[...])
        exchange(1, index, part_two, other_two).start()

    row_loop(blocks, feed_forward)
    leave(made.attn, made.ff, made.hidden)

    def add_halves(rows, index):
        exchange(1, index, part_two, other_two).wait_recv()
        mlp = part_two[rows, :] + other_two[rows, :]
        made.mlp[rows, :] = mlp
        inverse = inverse_rms(mlp)
        normed = mlp * inverse
        incoming = held.cot[rows, :].astype(jnp.float32)
        add_gain(made.gain_pff, incoming * normed)
        made.gml[rows, :] = rms_back(incoming, held.pff[...], normed, inverse).astype(jnp.bfloat16)

    made.gain_pff[...] = jnp.zeros_like(made.gain_pff)
    need(arrivals.cot, arrivals.pff)
    row_loop(blocks, add_halves)
    leave(made.gml, made.gain_pff, made.mlp)
    for index in range(blocks):
        exchange(0, index, part, other).wait_send()
        exchange(1, index, part_two, other_two).wait_send()
    for move in leaving:
        move.wait()


def rotation_table(length, head):
    frequency = THETA ** (-np.arange(head // 2, dtype=np.float64) * 2.0 / head)
    positions = np.concatenate([np.arange(0, length, FINE), np.arange(FINE)])
    angles = positions.astype(np.float64)[:, None] * frequency[None, :]
    return jnp.asarray(np.concatenate([np.cos(angles), np.sin(angles)], axis=1).astype(np.float32))


def forward_pass(values):
    length, width = values.tokens.shape
    head = values.gq.shape[0]
    query_columns = values.w_q.shape[1]
    heads = query_columns // head
    hidden_columns = values.w_d.shape[0]
    rank = values.a_q.shape[1]
    low, full = jnp.bfloat16, jnp.float32
    shapes = ForwardOutputs(
        gml=((length, width), low),
        gain_pff=((8, width), full),
        mlp=((length, width), full),
        attn=((length, width), full),
        hidden=((length, hidden_columns), low),
        ff=((length, width), low),
        w_g=((width, hidden_columns), low),
        w_u=((width, hidden_columns), low),
        w_d=((hidden_columns, width), low),
        w_o=((query_columns, width), low),
        attended=((length, query_columns), low),
        q_rot=((length, query_columns), low),
        k_rot=((length, head), low),
        values=((length, head), low),
        lse=((heads, length, 1), full),
        cosine=((length, head // 2), full),
        sine=((length, head // 2), full),
        normed=((length, width), low),
        w_q=((width, query_columns), low),
        w_kv=((width, 2 * head), low),
    )
    sizes = values._replace(
        b_q=jax.ShapeDtypeStruct((rank, query_columns), low),
        a_o=jax.ShapeDtypeStruct((query_columns, rank), low),
        b_gu=jax.ShapeDtypeStruct((2, rank, hidden_columns), low),
        a_d=jax.ShapeDtypeStruct((hidden_columns, rank), low),
    )
    slots = 2 * (length // ROWS)
    results = pl.pallas_call(
        forward_kernel,
        out_shape=[jax.ShapeDtypeStruct(*shape) for shape in shapes],
        in_specs=[ANYWHERE] * len(values),
        out_specs=[ANYWHERE] * len(shapes),
        scratch_shapes=[pltpu.VMEM(array.shape, array.dtype) for array in sizes]
        + [pltpu.VMEM(*shape) for shape in shapes]
        + [pltpu.VMEM((length, width), full)] * 4
        + [
            pltpu.VMEM((heads, ROWS, head), full),
            pltpu.VMEM((length, head), full),
            pltpu.SemaphoreType.DMA((len(values),)),
            pltpu.SemaphoreType.DMA((slots,)),
            pltpu.SemaphoreType.DMA((slots,)),
            pltpu.SemaphoreType.DMA((len(shapes),)),
        ],
        compiler_params=pltpu.CompilerParams(
            collective_id=1, has_side_effects=True, vmem_limit_bytes=67043328
        ),
    )(*values)
    return ForwardOutputs(*results)


class Adapters(NamedTuple):
    down_a: object
    down_b: object
    gateup_a: object
    gateup_b: object
    output_a: object
    output_b: object
    query_a: object
    query_b: object
    keyvalue_a: object
    keyvalue_b: object


class DeriveInputs(NamedTuple):
    down_a: object
    down_b: object
    d: object
    gateup_a: object
    gateup_b: object
    g: object
    u: object
    output_a: object
    output_b: object
    o: object
    query_a: object
    query_b: object
    q: object
    keyvalue_a: object
    keyvalue_b: object
    k: object
    small: object
    result: object
    tokens: object


class DeriveOutputs(NamedTuple):
    down: object
    gateup: object
    output: object
    query: object
    keyvalue: object
    down_a: object
    down_b: object
    gateup_a: object
    gateup_b: object
    output_a: object
    output_b: object
    query_a: object
    query_b: object
    keyvalue_a: object
    keyvalue_b: object
    result: object
    tokens: object
    gain_in: object
    gain_pa: object
    gain_pf: object
    gain_pff: object
    gain_q: object
    gain_k: object


def derive_kernel(*refs):
    refs = list(refs)
    fields = len(DeriveInputs._fields)
    source = DeriveInputs(*refs[:fields])
    refs = refs[fields:]
    target = DeriveOutputs(*refs[: len(DeriveOutputs._fields)])
    refs = refs[len(target) :]
    held = DeriveInputs(*refs[:fields])
    refs = refs[fields:]
    made = Adapters(*refs[: len(Adapters._fields)])
    gains = refs[len(made) : len(made) + 6]
    rounded, loaded, stored = refs[len(made) + 6 :]
    core = lax.axis_index(TENSOR)
    arrivals = DeriveInputs(
        *(
            pltpu.make_async_copy(piece, home, loaded.at[index])
            for index, (piece, home) in enumerate(zip(source, held))
        )
    )
    for arrival in arrivals[:6]:
        arrival.start()
    behind = list(arrivals[6:])
    leaving = []

    def need(*copies):
        for copy in copies:
            copy.wait()
        for arrival in behind[:3]:
            arrival.start()
        del behind[:3]

    def leave(piece, home):
        move = pltpu.make_async_copy(piece, home, stored.at[len(leaving)])
        move.start()
        leaving.append(move)

    def factors(total, first, second, out_first, out_second, add_first=False, add_second=False):
        count, columns = total.shape
        step = 256 if count % 256 == 0 else 320

        def by_rows(index, carry):
            block = pl.ds(pl.multiple_of(index * step, 64), step)
            value = total[block, :].astype(jnp.bfloat16)
            rounded[block, :columns] = value
            product = right_transposed(value, second[...])
            out_first[block, :] = out_first[block, :] + product if add_first else product
            return carry

        lax.fori_loop(0, count // step, by_rows, 0)
        width = 256 if columns == 256 else columns // 2

        def by_columns(index, carry):
            block = pl.ds(pl.multiple_of(index * width, 128), width)
            product = left_transposed(first[...], rounded[:count, block])
            out_second[:, block] = out_second[:, block] + product if add_second else product
            return carry

        if width % 128 == 0:
            lax.fori_loop(0, columns // width, by_columns, 0)
        else:
            product = left_transposed(first[...], rounded[:count, :columns])
            out_second[...] = out_second[...] + product if add_second else product

    rank = made.query_a.shape[1]

    def columns_of(ref, part, size):
        return ref.at[:, pl.ds(part * size, size)]

    def rows_of(ref, part, size):
        return ref.at[pl.ds(part * size, size)]

    need(arrivals.down_a, arrivals.down_b, arrivals.d)
    leave(held.d.at[core], target.down)
    for group in range(2):
        total = held.d.at[group]
        size = total.shape[0]
        first = rows_of(held.down_a, group, size)
        out = rows_of(made.down_a, group, size)
        factors(total, first, held.down_b, out, made.down_b, False, group > 0)
    leave(made.down_a, target.down_a)
    leave(made.down_b, target.down_b)
    need(arrivals.gateup_a, arrivals.gateup_b)
    for part, name in enumerate((held.g, held.u)):
        need((arrivals.g, arrivals.u)[part])
        leave(name.at[core], target.gateup.at[part])
        for group in range(2):
            total = name.at[group]
            size = total.shape[1]
            second = columns_of(held.gateup_b.at[part], group, size)
            first = columns_of(held.gateup_a, part, rank)
            out_first = columns_of(made.gateup_a, part, rank)
            out_second = columns_of(made.gateup_b.at[part], group, size)
            factors(total, first, second, out_first, out_second, group > 0, False)
        leave(made.gateup_b.at[part], target.gateup_b.at[part])
    leave(made.gateup_a, target.gateup_a)
    need(arrivals.output_a, arrivals.output_b, arrivals.o)
    leave(held.o.at[core], target.output)
    for group in range(2):
        total = held.o.at[group]
        size = total.shape[0]
        first = rows_of(held.output_a, group, size)
        out = rows_of(made.output_a, group, size)
        factors(total, first, held.output_b, out, made.output_b, False, group > 0)
    leave(made.output_a, target.output_a)
    leave(made.output_b, target.output_b)
    need(arrivals.query_a, arrivals.query_b, arrivals.q)
    leave(held.q.at[core], target.query)
    for group in range(2):
        total = held.q.at[group]
        size = total.shape[1]
        second = columns_of(held.query_b, group, size)
        out = columns_of(made.query_b, group, size)
        factors(total, held.query_a, second, made.query_a, out, group > 0, False)
    leave(made.query_a, target.query_a)
    leave(made.query_b, target.query_b)
    need(arrivals.keyvalue_a, arrivals.keyvalue_b, arrivals.k)
    leave(held.k, target.keyvalue)
    for part in range(2):
        width = made.keyvalue_b.shape[2]
        total = columns_of(held.k, part, width)
        out = columns_of(made.keyvalue_a, part, rank)
        first = columns_of(held.keyvalue_a, part, rank)
        factors(total, first, held.keyvalue_b.at[part], out, made.keyvalue_b.at[part])
    leave(made.keyvalue_a, target.keyvalue_a)
    leave(made.keyvalue_b, target.keyvalue_b)
    need(arrivals.small, arrivals.result, arrivals.tokens)
    leave(held.result, target.result)
    leave(held.tokens, target.tokens)
    row = 0
    for gain, home in zip(gains, target[-6:]):
        for at in range(gain.shape[0] // 128):
            gain[pl.ds(at * 128, 128)] = held.small[row]
            row += 1
        leave(gain, home)
    for move in leaving:
        move.wait()


def derive_adapters(values, widths):
    made = [getattr(values, name) for name in Adapters._fields]
    shapes = [
        values.d.shape[1:],
        (2,) + values.g.shape[1:],
        values.o.shape[1:],
        values.q.shape[1:],
        values.k.shape,
    ]
    shapes += [array.shape for array in made]
    shapes += [values.result.shape, values.tokens.shape] + [(width,) for width in widths]
    kinds = [jnp.float32] * len(shapes)
    kinds[len(made) + 5] = values.result.dtype
    results = pl.pallas_call(
        derive_kernel,
        out_shape=[jax.ShapeDtypeStruct(*out) for out in zip(shapes, kinds)],
        in_specs=[ANYWHERE] * len(values),
        out_specs=[ANYWHERE] * len(shapes),
        scratch_shapes=[pltpu.VMEM(array.shape, array.dtype) for array in values]
        + [pltpu.VMEM(array.shape, jnp.float32) for array in made]
        + [pltpu.VMEM((width,), jnp.float32) for width in widths]
        + [
            pltpu.VMEM((values.d.shape[1], values.g.shape[2]), jnp.bfloat16),
            pltpu.SemaphoreType.DMA((len(values),)),
            pltpu.SemaphoreType.DMA((len(shapes) + 2,)),
        ],
        compiler_params=pltpu.CompilerParams(vmem_limit_bytes=67043328),
    )(*values)
    return DeriveOutputs(*results)


def on_device_general(
    tokens,
    document_numbers,
    input_norm_gain,
    after_attention_gain,
    before_feedforward_gain,
    after_feedforward_gain,
    query_norm_gain,
    key_norm_gain,
    query_weight,
    keyvalue_weight,
    output_weight,
    gateup_weight,
    down_weight,
    query_adapter_first,
    query_adapter_second,
    keyvalue_adapter_first,
    keyvalue_adapter_second,
    output_adapter_first,
    output_adapter_second,
    gateup_adapter_first,
    gateup_adapter_second,
    down_adapter_first,
    down_adapter_second,
    cotangent,
):
    inputs = tokens[0].astype(jnp.float32)
    segments = document_numbers[0]
    length = inputs.shape[0]
    head_width = keyvalue_adapter_second.shape[2]
    adapter_rank = query_adapter_first.shape[1]
    query_columns = query_weight.shape[1]
    hidden_columns = down_weight.shape[0]
    heads_local = query_columns // head_width
    group_position = lax.axis_index(TENSOR)
    query_piece = lax.dynamic_slice_in_dim(
        query_adapter_second, group_position * query_columns, query_columns, 1
    )
    output_rows = lax.dynamic_slice_in_dim(
        output_adapter_first, group_position * query_columns, query_columns, 0
    )
    gateup_piece = lax.dynamic_slice_in_dim(
        gateup_adapter_second, group_position * hidden_columns, hidden_columns, 2
    )
    down_rows = lax.dynamic_slice_in_dim(
        down_adapter_first, group_position * hidden_columns, hidden_columns, 0
    )
    query_merged = (
        query_weight.astype(jnp.float32) + matrix_product(query_adapter_first, query_piece)
    ).astype(jnp.bfloat16)
    keyvalue_merged = (
        keyvalue_weight.astype(jnp.float32)
        + jnp.concatenate(
            [
                matrix_product(keyvalue_adapter_first[:, :adapter_rank], keyvalue_adapter_second[0]),
                matrix_product(keyvalue_adapter_first[:, adapter_rank:], keyvalue_adapter_second[1]),
            ],
            axis=1,
        )
    ).astype(jnp.bfloat16)
    output_merged = (
        output_weight.astype(jnp.float32) + matrix_product(output_rows, output_adapter_second)
    ).astype(jnp.bfloat16)
    gate_merged = (
        gateup_weight[0].astype(jnp.float32)
        + matrix_product(gateup_adapter_first[:, :adapter_rank], gateup_piece[0])
    ).astype(jnp.bfloat16)
    up_merged = (
        gateup_weight[1].astype(jnp.float32)
        + matrix_product(gateup_adapter_first[:, adapter_rank:], gateup_piece[1])
    ).astype(jnp.bfloat16)
    down_merged = (
        down_weight.astype(jnp.float32) + matrix_product(down_rows, down_adapter_second)
    ).astype(jnp.bfloat16)
    positions = positions_of(segments)
    key_index = jnp.arange(length, dtype=jnp.int32)
    block_rows = min(512, length)
    normalized_rows, in_back = jax.vjp(rms_scale, inputs, input_norm_gain)
    normalized_lowrank = normalized_rows.astype(jnp.bfloat16)
    query_rows = matrix_product(normalized_lowrank, query_merged)
    keyvalue = matrix_product(normalized_lowrank, keyvalue_merged)

    def prepare(q_in, kv_in, q_scale, k_scale):
        q_heads = rms_scale(q_in.reshape(length, heads_local, head_width), q_scale)
        q_out = rotate(q_heads, positions) * head_width ** (-0.5)
        k_out = rotate(rms_scale(kv_in[:, :head_width], k_scale), positions)
        return (q_out, k_out, kv_in[:, head_width:])

    prepared, prepare_back = jax.vjp(prepare, query_rows, keyvalue, query_norm_gain, key_norm_gain)
    q_rot = prepared[0].astype(jnp.bfloat16)
    k_rot = prepared[1].astype(jnp.bfloat16)
    v_low = prepared[2].astype(jnp.bfloat16)

    def scores_of(row_start):
        rows = q_rot[row_start : row_start + block_rows]
        raw = jnp.einsum("qhd,kd->hqk", rows, k_rot, preferred_element_type=jnp.float32)
        row_index = row_start + jnp.arange(block_rows, dtype=jnp.int32)
        allowed = (segments[row_start : row_start + block_rows][:, None] == segments[None, :]) & (
            row_index[:, None] >= key_index[None, :]
        )
        return jnp.where(allowed[None], raw, MASKED)

    outputs = []
    log_totals = []
    for row_start in range(0, length, block_rows):
        scores = scores_of(row_start)
        row_peak = jnp.max(scores, axis=-1, keepdims=True)
        weights = jnp.exp(scores - row_peak)
        row_total = jnp.sum(weights, axis=-1, keepdims=True)
        log_totals.append(row_peak + jnp.log(row_total))
        probs_low = (weights / row_total).astype(jnp.bfloat16)
        outputs.append(
            jnp.einsum("hqk,kd->qhd", probs_low, v_low, preferred_element_type=jnp.float32)
        )
    attended_rows = (
        jnp.concatenate(outputs, axis=0).reshape(length, query_columns).astype(jnp.bfloat16)
    )
    attention_before = lax.psum(matrix_product(attended_rows, output_merged), TENSOR)
    attn_post, post_attn_back = jax.vjp(rms_scale, attention_before, after_attention_gain)
    residual = inputs + attn_post
    normed_ff, pre_ff_back = jax.vjp(rms_scale, residual, before_feedforward_gain)
    feedforward_lowrank = normed_ff.astype(jnp.bfloat16)
    gate_portion = matrix_product(feedforward_lowrank, gate_merged)
    up_portion = matrix_product(feedforward_lowrank, up_merged)
    hidden_full, activate_back = jax.vjp(activate, gate_portion, up_portion)
    hidden_activation = hidden_full.astype(jnp.bfloat16)
    feedforward_before = lax.psum(matrix_product(hidden_activation, down_merged), TENSOR)
    mlp_post, post_ff_back = jax.vjp(rms_scale, feedforward_before, after_feedforward_gain)
    result_value = (residual + mlp_post).astype(jnp.bfloat16)[None]
    grad_out = cotangent[0].astype(jnp.float32)
    grad_mlp_pre, gradient_after_feedforward = post_ff_back(grad_out)
    gradient_feedforward_lowrank = grad_mlp_pre.astype(jnp.bfloat16)
    gradient_down_weight = left_transposed(hidden_activation, gradient_feedforward_lowrank)
    grad_hidden = right_transposed(gradient_feedforward_lowrank, down_merged)
    grad_gate, grad_up = activate_back(grad_hidden)
    gate_lowrank = grad_gate.astype(jnp.bfloat16)
    up_lowrank = grad_up.astype(jnp.bfloat16)
    gradient_gateup_weight = jnp.stack(
        [
            left_transposed(feedforward_lowrank, gate_lowrank),
            left_transposed(feedforward_lowrank, up_lowrank),
        ]
    )
    grad_ff_part = right_transposed(gate_lowrank, gate_merged) + right_transposed(
        up_lowrank, up_merged
    )
    grad_normed_ff = lax.psum(grad_ff_part, TENSOR)
    grad_residual_ff, gradient_before_feedforward = pre_ff_back(grad_normed_ff)
    grad_residual = grad_out + grad_residual_ff
    grad_attn_pre, gradient_after_attention = post_attn_back(grad_residual)
    gradient_attention_lowrank = grad_attn_pre.astype(jnp.bfloat16)
    gradient_output_weight = left_transposed(attended_rows, gradient_attention_lowrank)
    grad_attended = right_transposed(gradient_attention_lowrank, output_merged).astype(jnp.bfloat16)
    grad_attended = grad_attended.reshape(length, heads_local, head_width)
    grad_q_blocks = []
    grad_k_rot = jnp.zeros((length, head_width), jnp.float32)
    grad_values = jnp.zeros((length, head_width), jnp.float32)
    for block_index, row_start in enumerate(range(0, length, block_rows)):
        scores = scores_of(row_start)
        probs = jnp.exp(scores - log_totals[block_index])
        grad_rows = grad_attended[row_start : row_start + block_rows]
        grad_probs = jnp.einsum("qhd,kd->hqk", grad_rows, v_low, preferred_element_type=jnp.float32)
        grad_scores = (
            probs * (grad_probs - jnp.sum(probs * grad_probs, axis=-1, keepdims=True))
        ).astype(jnp.bfloat16)
        grad_q_blocks.append(
            jnp.einsum("hqk,kd->qhd", grad_scores, k_rot, preferred_element_type=jnp.float32)
        )
        grad_k_rot = grad_k_rot + jnp.einsum(
            "hqk,qhd->kd",
            grad_scores,
            q_rot[row_start : row_start + block_rows],
            preferred_element_type=jnp.float32,
        )
        grad_values = grad_values + jnp.einsum(
            "hqk,qhd->kd", probs.astype(jnp.bfloat16), grad_rows, preferred_element_type=jnp.float32
        )
    grad_queries, grad_keyvalue, gradient_query_norm_gain, gradient_key_norm_gain = prepare_back(
        (jnp.concatenate(grad_q_blocks, axis=0), grad_k_rot, grad_values)
    )
    query_low = grad_queries.astype(jnp.bfloat16)
    keyvalue_gradient_lowrank = grad_keyvalue.astype(jnp.bfloat16)
    gradient_query_weight = left_transposed(normalized_lowrank, query_low)
    gradient_keyvalue_weight = left_transposed(normalized_lowrank, keyvalue_gradient_lowrank)
    grad_in_part = right_transposed(query_low, query_merged) + right_transposed(
        keyvalue_gradient_lowrank, keyvalue_merged
    )
    grad_normed = lax.psum(grad_in_part, TENSOR)
    grad_inputs_add, gradient_input_gain = in_back(grad_normed)
    gradient_token_input = (grad_residual + grad_inputs_add)[None]
    lead_mask = (group_position == 0).astype(jnp.float32)
    lead_in = gradient_input_gain * lead_mask
    lead_post_attn = gradient_after_attention * lead_mask
    lead_pre_ff = gradient_before_feedforward * lead_mask
    lead_post_ff = gradient_after_feedforward * lead_mask
    sum_w_query, sum_w_out, sum_w_gate_up, sum_w_down = lax.psum(
        (
            gradient_query_weight,
            gradient_output_weight,
            gradient_gateup_weight,
            gradient_down_weight,
        ),
        DP,
    )
    (
        sum_gain_in,
        sum_post_attn,
        sum_pre_ff,
        sum_post_ff,
        sum_query_gain,
        sum_key_gain,
        sum_w_keyvalue,
    ) = lax.psum(
        (
            lead_in,
            lead_post_attn,
            lead_pre_ff,
            lead_post_ff,
            gradient_query_norm_gain,
            gradient_key_norm_gain,
            gradient_keyvalue_weight,
        ),
        (DP, TENSOR),
    )
    rows_rows = ((0,), (0,))
    columns_columns = ((1,), (1,))
    sum_kv_b = jnp.stack(
        [
            exact_product(
                sum_w_keyvalue[:, i * head_width : (i + 1) * head_width],
                keyvalue_adapter_first[:, i * adapter_rank : (i + 1) * adapter_rank],
                rows_rows,
            ).T
            for i in range(2)
        ]
    )
    sum_kv_a = jnp.concatenate(
        [
            exact_product(
                sum_w_keyvalue[:, i * head_width : (i + 1) * head_width],
                keyvalue_adapter_second[i],
                columns_columns,
            )
            for i in range(2)
        ],
        axis=1,
    )
    part_q_b = exact_product(sum_w_query, query_adapter_first, rows_rows).T
    part_q_a = exact_product(sum_w_query, query_piece, columns_columns)
    part_o_a = exact_product(sum_w_out, output_adapter_second, columns_columns)
    part_o_b = exact_product(sum_w_out, output_rows, rows_rows).T
    part_gu_b = jnp.stack(
        [
            exact_product(
                sum_w_gate_up[i],
                gateup_adapter_first[:, i * adapter_rank : (i + 1) * adapter_rank],
                rows_rows,
            ).T
            for i in range(2)
        ]
    )
    part_gu_a = jnp.concatenate(
        [exact_product(sum_w_gate_up[i], gateup_piece[i], columns_columns) for i in range(2)],
        axis=1,
    )
    part_d_a = exact_product(sum_w_down, down_adapter_second, columns_columns)
    part_d_b = exact_product(sum_w_down, down_rows, rows_rows).T
    sum_q_a, sum_o_b, sum_gu_a, sum_d_b = lax.psum(
        (part_q_a, part_o_b, part_gu_a, part_d_b), TENSOR
    )
    sum_q_b = lax.all_gather(part_q_b, TENSOR, axis=1, tiled=True)
    sum_o_a = lax.all_gather(part_o_a, TENSOR, axis=0, tiled=True)
    sum_gu_b = lax.all_gather(part_gu_b, TENSOR, axis=2, tiled=True)
    sum_d_a = lax.all_gather(part_d_a, TENSOR, axis=0, tiled=True)
    return (
        result_value,
        gradient_token_input,
        sum_gain_in,
        sum_post_attn,
        sum_pre_ff,
        sum_post_ff,
        sum_query_gain,
        sum_key_gain,
        sum_w_query,
        sum_w_keyvalue,
        sum_w_out,
        sum_w_gate_up,
        sum_w_down,
        sum_q_a,
        sum_q_b,
        sum_kv_a,
        sum_kv_b,
        sum_o_a,
        sum_o_b,
        sum_gu_a,
        sum_gu_b,
        sum_d_a,
        sum_d_b,
    )


def on_device_fast(
    tokens,
    document_numbers,
    input_norm_gain,
    after_attention_gain,
    before_feedforward_gain,
    after_feedforward_gain,
    query_norm_gain,
    key_norm_gain,
    query_weight,
    keyvalue_weight,
    output_weight,
    gateup_weight,
    down_weight,
    query_adapter_first,
    query_adapter_second,
    keyvalue_adapter_first,
    keyvalue_adapter_second,
    output_adapter_first,
    output_adapter_second,
    gateup_adapter_first,
    gateup_adapter_second,
    down_adapter_first,
    down_adapter_second,
    cotangent,
):
    length = document_numbers.shape[1]
    head_width = keyvalue_adapter_second.shape[2]
    width = input_norm_gain.shape[0]
    ahead = forward_pass(
        ForwardInputs(
            tokens=tokens[0],
            gin=input_norm_gain,
            w_q=query_weight,
            a_q=query_adapter_first,
            b_q=query_adapter_second,
            w_kv=keyvalue_weight,
            a_kv=keyvalue_adapter_first,
            b_kv=keyvalue_adapter_second,
            table=rotation_table(length, head_width),
            segments=document_numbers,
            gq=query_norm_gain,
            gk=key_norm_gain,
            w_o=output_weight,
            a_o=output_adapter_first,
            b_o=output_adapter_second,
            pa=after_attention_gain,
            pf=before_feedforward_gain,
            w_gu=gateup_weight,
            a_gu=gateup_adapter_first,
            b_gu=gateup_adapter_second,
            w_d=down_weight,
            a_d=down_adapter_first,
            b_d=down_adapter_second,
            cot=cotangent[0],
            pff=after_feedforward_gain,
        )
    )
    shapes = Pieces(
        d=down_weight.shape,
        g=gateup_weight.shape[1:],
        u=gateup_weight.shape[1:],
        o=output_weight.shape,
        q=query_weight.shape,
        k=keyvalue_weight.shape,
        s=(32, 128),
    )
    values = BackwardInputs(
        tokens=tokens[0],
        cot=cotangent[0],
        pa=after_attention_gain,
        pff=after_feedforward_gain,
        pf=before_feedforward_gain,
        segments=document_numbers,
        gq=query_norm_gain,
        gk=key_norm_gain,
        gin=input_norm_gain,
        **ahead._asdict(),
    )
    (result, grad_tokens, sum_k, sum_s), both = backward_and_sums(values, shapes)
    sum_d, sum_g, sum_u, sum_o, sum_q = both
    derived = derive_adapters(
        DeriveInputs(
            down_a=down_adapter_first,
            down_b=down_adapter_second,
            d=sum_d,
            gateup_a=gateup_adapter_first,
            gateup_b=gateup_adapter_second,
            g=sum_g,
            u=sum_u,
            output_a=output_adapter_first,
            output_b=output_adapter_second,
            o=sum_o,
            query_a=query_adapter_first,
            query_b=query_adapter_second,
            q=sum_q,
            keyvalue_a=keyvalue_adapter_first,
            keyvalue_b=keyvalue_adapter_second,
            k=sum_k,
            small=sum_s,
            result=result,
            tokens=grad_tokens,
        ),
        (width,) * 4 + (head_width,) * 2,
    )
    return (
        derived.result[None],
        derived.tokens[None],
        derived.gain_in,
        derived.gain_pa,
        derived.gain_pf,
        derived.gain_pff,
        derived.gain_q,
        derived.gain_k,
        derived.query,
        derived.keyvalue,
        derived.output,
        derived.gateup,
        derived.down,
        derived.query_a,
        derived.query_b,
        derived.keyvalue_a,
        derived.keyvalue_b,
        derived.output_a,
        derived.output_b,
        derived.gateup_a,
        derived.gateup_b,
        derived.down_a,
        derived.down_b,
    )


def solution(mesh):
    in_specs = (
        P(DP, None, None),
        P(DP, None),
        P(),
        P(),
        P(),
        P(),
        P(),
        P(),
        P(None, TENSOR),
        P(),
        P(TENSOR, None),
        P(None, None, TENSOR),
        P(TENSOR, None),
        P(),
        P(),
        P(),
        P(),
        P(),
        P(),
        P(),
        P(),
        P(),
        P(),
        P(DP, None, None),
    )
    out_specs = (
        P(DP, None, None),
        P(DP, None, None),
        P(),
        P(),
        P(),
        P(),
        P(),
        P(),
        P(None, TENSOR),
        P(),
        P(TENSOR, None),
        P(None, None, TENSOR),
        P(TENSOR, None),
        P(),
        P(),
        P(),
        P(),
        P(),
        P(),
        P(),
        P(),
        P(),
        P(),
    )
    fast = mesh.shape[DP] == 16 and mesh.shape[TENSOR] == 2
    return jax.shard_map(
        on_device_fast if fast else on_device_general,
        mesh=mesh, in_specs=in_specs, out_specs=out_specs, check_vma=False
    )
```
